32 devices in a mesh: rep: 4 (over z), shard: 8 (over y, x, core).
Axes of the slice: x: 2, y: 2, z: 4, core: 2. Of those that a mesh axis runs over, the one named last changes fastest.
Arguments:
- tokens: bfloat16 [4096, 2048], P(('rep', 'shard')), may hold values from -6 to 6
- attn_gain: float32 [2048], replicated, may hold values from 0.5 to 1.5
- query_weight: bfloat16 [2048, 2048], P('shard'), may hold values from -0.5 to 0.5
- key_weight: bfloat16 [2048, 512], P('shard'), may hold values from -0.5 to 0.5
- value_weight: bfloat16 [2048, 512], P('shard'), may hold values from -0.5 to 0.5
- output_weight: bfloat16 [2048, 2048], P('shard'), may hold values from -1 to 1
- ffn_gain: float32 [2048], replicated, may hold values from 0.5 to 1.5
- gate_weight: bfloat16 [2048, 8192], P('shard'), may hold values from -0.125 to 0.125
- up_weight: bfloat16 [2048, 8192], P('shard'), may hold values from -0.125 to 0.125
- down_weight: bfloat16 [8192, 2048], P('shard'), may hold values from -0.25 to 0.25
- dealing: int32 [4, 1024], P('rep'), may hold values from 0 to 1023, each once within a row
- lengths: int32 [4, 3], P('rep'), may hold values from 1 to 768, 1024 in all within a row
- cotangent: bfloat16 [4096, 2048], P(('rep', 'shard')), may hold values from -6 to 6
Outputs:
- layer_output: bfloat16 [4096, 2048], P(('rep', 'shard'))
- tokens_grad: float32 [4096, 2048], P(('rep', 'shard'))
- attn_gain_grad: float32 [2048], replicated
- query_weight_grad: float32 [2048, 2048], P('shard')
- key_weight_grad: float32 [2048, 512], P('shard')
- value_weight_grad: float32 [2048, 512], P('shard')
- output_weight_grad: float32 [2048, 2048], P('shard')
- ffn_gain_grad: float32 [2048], replicated
- gate_weight_grad: float32 [2048, 8192], P('shard')
- up_weight_grad: float32 [2048, 8192], P('shard')
- down_weight_grad: float32 [8192, 2048], P('shard')
The draws below stay inside these ranges and needn't reach their ends.
Inputs may be any that keep to these rules, and one draw needn't show every extreme that they name: Each row of dealing is a permutation of 0 to 1023. Each row of lengths sums to 1024 and holds one length of exactly 768.
All inputs are finite; a program needn't handle non-finite values.
Results may differ from the reference program's by a relative error of at most 0.023.
Values may be sent and summed in bfloat16 or wider, within the bound.
A program may use at most 640 MiB of HBM per device.

```python
import math
import jax
import jax.numpy as jnp
import numpy as np
from jax import lax

D = 2048
FF = 8192
HEADS = 32
KV_HEADS = 8
HEAD = 64
SEQS = 3
GROUP_TOK = 1024
LONGEST = 768
TOKENS = 4096
N_REP = 4


def levels(rng, dims, pieces, least, high):
    gain, own = 1.0, jax.random.fold_in(rng, 6)
    for dim, parts in pieces:
        heights = jnp.exp(jax.random.uniform(jax.random.fold_in(own, dim), (parts,), jnp.float32, least / len(pieces), high / len(pieces)))
        gain = gain * jnp.repeat(heights, dims[dim] // parts).reshape([-1 if axis == dim else 1 for axis in range(len(dims))])
    return gain


def length_profile(count, total, limit, lean):
    portions = [(1 << 20) // math.isqrt(grade ** lean) + 1 for grade in range(2, count + 1)]
    spare, counts = total - limit - (count - 1), [1] * (count - 1)
    while spare > 0:
        free = [i for i in range(count - 1) if counts[i] < limit]
        pool, remaining = sum([portions[i] for i in free]), spare
        for i in free:
            addition = min(limit - counts[i], max(1, remaining * portions[i] // pool), spare)
            counts[i] = counts[i] + addition
            spare = spare - addition
    return np.array([limit] + counts)


def ragged_sizes(stream_key, count, total, reach, slope):
    if count == 2:
        one = jax.random.randint(stream_key, (), max(1, total - reach), min(reach, total - 1) + 1)
        return jnp.stack([one, total - one])
    tallies = jnp.asarray(length_profile(count, total, reach, slope), jnp.int32)
    pairs = (count - 1) // 2
    donor, sink = tallies[1:1 + 2 * pairs:2], tallies[2:2 + 2 * pairs:2]
    margin = jnp.minimum(donor - 1, reach - sink)
    passed = jax.random.randint(jax.random.fold_in(stream_key, 1), (pairs,), 0, 1 << 20) % (margin + 1)
    tallies = tallies.at[1:1 + 2 * pairs:2].set(donor - passed).at[2:2 + 2 * pairs:2].set(sink + passed)
    return tallies[jax.random.permutation(jax.random.fold_in(stream_key, 2), count)]


def noise(rng, shape, spread, reach, pieces=(), kind=jnp.bfloat16):
    array = spread * jax.random.normal(rng, shape, jnp.float32)
    if pieces:
        array = array * levels(rng, shape, pieces, -0.22, 0.18)
    return jnp.clip(array, -reach, reach).astype(kind)


def setup_inputs(seed: int = 0) -> dict:
    key_of = jax.random.split(jax.random.key(seed), 14)
    return {
        "tokens": noise(key_of[0], (TOKENS, D), 1.0, 6.0, ((0, 32),)),
        "attn_gain": jnp.clip(1.0 + 0.1 * jax.random.normal(key_of[1], (D,), jnp.float32), 0.5, 1.5),
        "query_weight": noise(key_of[2], (D, D), (D // 16) ** -0.5, 0.5, ((0, 8),)),
        "key_weight": noise(key_of[3], (D, KV_HEADS * HEAD), (D // 16) ** -0.5, 0.5, ((0, 8),)),
        "value_weight": noise(key_of[4], (D, KV_HEADS * HEAD), (D // 16) ** -0.5, 0.5, ((0, 8),)),
        "output_weight": noise(key_of[5], (D, D), (D // 64) ** -0.5, 1.0, ((0, 8),)),
        "ffn_gain": jnp.clip(1.0 + 0.1 * jax.random.normal(key_of[6], (D,), jnp.float32), 0.5, 1.5),
        "gate_weight": noise(key_of[7], (D, FF), D ** -0.5, 0.125, ((0, 8),)),
        "up_weight": noise(key_of[8], (D, FF), D ** -0.5, 0.125, ((0, 8),)),
        "down_weight": noise(key_of[9], (FF, D), (FF // 16) ** -0.5, 0.25, ((0, 8),)),
        "dealing": jax.vmap(lambda own: jax.random.permutation(own, GROUP_TOK))(jax.random.split(key_of[10], N_REP)).reshape((N_REP, GROUP_TOK)).astype(jnp.int32),
        "lengths": jax.vmap(lambda own: ragged_sizes(own, SEQS, GROUP_TOK, LONGEST, 2))(jax.random.split(key_of[11], N_REP)).reshape((N_REP, SEQS)).astype(jnp.int32),
        "cotangent": noise(key_of[12], (TOKENS, D), 1.0, 6.0, ((0, 32),)),
    }


@jax.custom_vjp
def low(v):
    return lax.optimization_barrier(v.astype(jnp.bfloat16)).astype(jnp.float32)

@jax.custom_vjp
def low_back(v):
    return v

def low_keep(v):
    return (low(v), None)

def low_pass(kept, grad):
    return (grad,)

def back_keep(v):
    return (v, None)

def back_low(kept, grad):
    return (low(grad),)
low.defvjp(low_keep, low_pass)
low_back.defvjp(back_keep, back_low)
EPSILON = 1e-05
RESIDUAL_SCALE = 0.22
SCORE_SCALE = 0.015625
ROPE_BASE = 10000000.0
MASKED = -1e+30

def matmul_high(left_side, right_side):
    return jnp.dot(left_side, right_side, precision=lax.Precision.HIGHEST, preferred_element_type=jnp.float32)

def rms_scale(hidden, gain_vector):
    return hidden * lax.rsqrt(lax.optimization_barrier(jnp.mean(hidden * hidden, axis=-1, keepdims=True)) + EPSILON) * gain_vector

def places(packed_index, seq_lengths):
    seq_ends = jnp.cumsum(seq_lengths).astype(jnp.int32)
    starts = (seq_ends - seq_lengths).astype(jnp.int32)
    segment = lax.optimization_barrier(jnp.sum((packed_index[:, None] >= seq_ends[None, :]).astype(jnp.int32), axis=1)).astype(jnp.int32)
    chosen = segment[:, None] == jnp.arange(seq_lengths.shape[0], dtype=jnp.int32)[None, :]
    position = packed_index - lax.optimization_barrier(jnp.sum(jnp.where(chosen, starts[None, :], 0), axis=1)).astype(jnp.int32)
    return (segment, position.astype(jnp.int32))

def angles(position, half_width):
    frequency = ROPE_BASE ** (-(jnp.arange(half_width, dtype=jnp.float32) * 2.0) / (2.0 * half_width))
    turned = position.astype(jnp.float32)[:, None] * frequency[None, :]
    return (jnp.cos(turned)[:, None, :], jnp.sin(turned)[:, None, :])

def rotate(values, cosine, sine_table):
    half_width = values.shape[-1] // 2
    first_half = values[..., :half_width]
    second = values[..., half_width:]
    return jnp.concatenate([first_half * cosine - second * sine_table, second * cosine + first_half * sine_table], axis=-1)

def group_layer(hidden, attn_gain, query_weight, key_weight, value_weight, output_weight, ffn_gain, gate_weight, up_weight, down_weight, seq_lengths):
    packed_index = jnp.arange(GROUP_TOK, dtype=jnp.int32)
    segment, position = places(packed_index, seq_lengths)
    cosine, sine_table = angles(position, HEAD // 2)
    normed = low(rms_scale(hidden, attn_gain))
    query_pre = low_back(matmul_high(normed, query_weight)).reshape(GROUP_TOK, HEADS, HEAD)
    key_pre = low_back(matmul_high(normed, key_weight)).reshape(GROUP_TOK, KV_HEADS, HEAD)
    values = low(low_back(matmul_high(normed, value_weight))).reshape(GROUP_TOK, KV_HEADS, HEAD)
    queries = low(rotate(query_pre, cosine, sine_table))
    key_rows = low(rotate(key_pre, cosine, sine_table))
    block_rows = math.gcd(GROUP_TOK, 512)
    block_count = GROUP_TOK // block_rows
    query_blocks = queries.reshape(block_count, block_rows, KV_HEADS, HEADS // KV_HEADS, HEAD)

    def attend(block_item):
        query_block, query_segment, query_position = block_item
        raw_scores = jnp.einsum('bkgd,ckd->kgbc', query_block, key_rows, precision=lax.Precision.HIGHEST)
        scores = low_back(SCORE_SCALE * raw_scores)
        allowed = (segment[None, :] == query_segment[:, None]) & (position[None, :] <= query_position[:, None])
        probabilities = jax.nn.softmax(jnp.where(allowed, scores, MASKED), axis=-1)
        mixture = jnp.einsum('kgbc,ckd->bkgd', low(probabilities), values, precision=lax.Precision.HIGHEST)
        return low(low_back(mixture))
    attention = lax.map(jax.checkpoint(attend), (query_blocks, segment.reshape(block_count, block_rows), position.reshape(block_count, block_rows)))
    attention = attention.reshape(GROUP_TOK, D)
    middle = hidden + RESIDUAL_SCALE * low_back(matmul_high(attention, output_weight))
    normed_ffn = low(rms_scale(middle, ffn_gain))
    gate = low_back(matmul_high(normed_ffn, gate_weight))
    up_proj = low_back(matmul_high(normed_ffn, up_weight))
    activated = low(jax.nn.silu(gate) * up_proj)
    return middle + RESIDUAL_SCALE * low_back(matmul_high(activated, down_weight))

def reference(tokens, attn_gain, query_weight, key_weight, value_weight, output_weight, ffn_gain, gate_weight, up_weight, down_weight, dealing, lengths, cotangent):
    floats = (tokens.astype(jnp.float32), attn_gain.astype(jnp.float32), query_weight.astype(jnp.float32), key_weight.astype(jnp.float32), value_weight.astype(jnp.float32), output_weight.astype(jnp.float32), ffn_gain.astype(jnp.float32), gate_weight.astype(jnp.float32), up_weight.astype(jnp.float32), down_weight.astype(jnp.float32))

    def forward(hidden_all, gain_first, weight_query, weight_key, weight_value, weight_output, gain_second, weight_gate, weight_up, weight_down):

        def group_step(running, group_item):
            group_hidden, group_lengths, group_order = group_item
            layer_out = group_layer(group_hidden, gain_first, weight_query, weight_key, weight_value, weight_output, gain_second, weight_gate, weight_up, weight_down, group_lengths)
            return (running, jnp.take(layer_out, group_order, axis=0))
        unused_carry, dealt = lax.scan(jax.checkpoint(group_step), jnp.zeros((), jnp.float32), (hidden_all.reshape(N_REP, GROUP_TOK, D), lengths, dealing))
        return dealt.reshape(TOKENS, D)
    layer_out, pull_back = jax.vjp(forward, *floats)
    grads = pull_back(cotangent.astype(jnp.float32))
    return (layer_out.astype(jnp.bfloat16), grads[0], grads[1], grads[2], grads[3], grads[4], grads[5], grads[6], grads[7], grads[8], grads[9])
```

```python
import functools

import jax
import jax.numpy as jnp
from jax import lax
from jax.experimental import pallas as pl
from jax.experimental.pallas import tpu as pltpu
from jax.sharding import PartitionSpec as P

HEADS = 32
KV_HEADS = 8
HEAD = 64
EPSILON = 1e-05
RESIDUAL_SCALE = 0.22
SCORE_SCALE = 0.015625
ROPE_BASE = 10000000.0
MASKED = -1e30
BF16 = jnp.bfloat16
F32 = jnp.float32


def mm(a, b):
    return jnp.dot(a, b, preferred_element_type=F32)


def mm_t(a, b):
    return lax.dot_general(a, b, (((1,), (1,)), ((), ())), preferred_element_type=F32)


def t_mm(a, b):
    return lax.dot_general(a, b, (((0,), (0,)), ((), ())), preferred_element_type=F32)


def rms_scale(hidden, gain_vector):
    return (
        hidden
        * lax.rsqrt(jnp.mean(hidden * hidden, axis=-1, keepdims=True) + EPSILON)
        * gain_vector
    )


def places(packed_index, seq_lengths):
    seq_ends = jnp.cumsum(seq_lengths)
    starts = seq_ends - seq_lengths
    segment = jnp.sum((packed_index[:, None] >= seq_ends[None, :]).astype(jnp.int32), axis=1)
    chosen = segment[:, None] == jnp.arange(seq_lengths.shape[0], dtype=jnp.int32)[None, :]
    position = packed_index - jnp.sum(jnp.where(chosen, starts[None, :], 0), axis=1)
    return segment, position


def rope_tables(position, width):
    half = HEAD // 2
    frequency = ROPE_BASE ** (-(jnp.arange(half, dtype=F32) * 2.0) / (2.0 * half))
    turned = position.astype(F32)[:, None] * frequency[None, :]
    cosine, sine = jnp.cos(turned), jnp.sin(turned)
    cos_full = jnp.concatenate([cosine, cosine], axis=-1)
    sin_full = jnp.concatenate([-sine, sine], axis=-1)
    return jnp.tile(cos_full, (1, width // HEAD)), jnp.tile(sin_full, (1, width // HEAD))


def swap_halves(x):
    rows, width = x.shape
    half = HEAD // 2
    y = x.reshape(rows, width // HEAD, 2, half)
    return jnp.concatenate([y[:, :, 1:], y[:, :, :1]], axis=2).reshape(rows, width)


def rotate(x, cos_full, sin_full):
    return x * cos_full + swap_halves(x) * sin_full


def unrotate(x, cos_full, sin_full):
    return x * cos_full - swap_halves(x) * sin_full


def softmax_block(q, k, allowed):
    scores = SCORE_SCALE * lax.dot_general(
        q, k, (((1,), (1,)), ((), ())), preferred_element_type=F32
    )
    scores = jnp.where(allowed, scores, MASKED)
    top = jnp.max(scores, axis=-1, keepdims=True)
    weight = jnp.exp(scores - top)
    return weight * (1.0 / jnp.sum(weight, axis=-1, keepdims=True))


def allowed_block(row0, rows, cols, seg_q, seg_k):
    q_index = row0 + lax.broadcasted_iota(jnp.int32, (rows, cols), 0)
    k_index = lax.broadcasted_iota(jnp.int32, (rows, cols), 1)
    return (seg_q == seg_k) & (k_index <= q_index)


def attention_kernel(heads, block, q_ref, k_ref, v_ref, segc_ref, segr_ref, o_ref):
    total = k_ref.shape[0]
    for i in range(total // block):
        cols = (i + 1) * block
        rows = pl.ds(i * block, block)
        allowed = allowed_block(i * block, block, cols, segc_ref[rows, :], segr_ref[:, :cols])
        k, v = k_ref[:cols, :], v_ref[:cols, :]
        for h in range(heads):
            lanes = slice(h * HEAD, (h + 1) * HEAD)
            probs = softmax_block(q_ref[rows, lanes], k, allowed)
            out = jnp.dot(probs.astype(BF16), v, preferred_element_type=F32)
            o_ref[rows, lanes] = out.astype(BF16)


def attention_forward(q, k, v, seg_col, seg_row):
    total, width = q.shape
    heads = width // HEAD
    return pl.pallas_call(
        functools.partial(attention_kernel, heads, 256),
        out_shape=jax.ShapeDtypeStruct((total, width), BF16),
        compiler_params=pltpu.CompilerParams(vmem_limit_bytes=40 << 20),
        cost_estimate=pl.CostEstimate(
            flops=2 * total * total * width, bytes_accessed=4 * total * width, transcendentals=heads * total * total // 2
        ),
        name="attention_forward",
    )(q, k, v, seg_col, seg_row)


def attention_backward_kernel(
    heads, block, q_ref, k_ref, v_ref, g_ref, segc_ref, segr_ref, dq_ref, dk_ref, dv_ref
):
    total = k_ref.shape[0]
    dk_ref[...] = jnp.zeros_like(dk_ref)
    dv_ref[...] = jnp.zeros_like(dv_ref)
    for i in range(total // block):
        cols = (i + 1) * block
        rows = pl.ds(i * block, block)
        allowed = allowed_block(i * block, block, cols, segc_ref[rows, :], segr_ref[:, :cols])
        k, v = k_ref[:cols, :], v_ref[:cols, :]
        for h in range(heads):
            lanes = slice(h * HEAD, (h + 1) * HEAD)
            q, g = q_ref[rows, lanes], g_ref[rows, lanes]
            probs = softmax_block(q, k, allowed)
            probs_grad = lax.dot_general(
                g, v, (((1,), (1,)), ((), ())), preferred_element_type=F32
            )
            delta = jnp.sum(probs * probs_grad, axis=-1, keepdims=True)
            score_grad = (probs * (probs_grad - delta)).astype(BF16)
            dq_ref[rows, lanes] = SCORE_SCALE * jnp.dot(
                score_grad, k, preferred_element_type=F32
            )
            dk_ref[:cols, :] += SCORE_SCALE * lax.dot_general(
                score_grad, q, (((0,), (0,)), ((), ())), preferred_element_type=F32
            )
            dv_ref[:cols, :] += lax.dot_general(
                probs.astype(BF16), g, (((0,), (0,)), ((), ())), preferred_element_type=F32
            )


def attention_backward(q, k, v, g, seg_col, seg_row):
    total, width = q.shape
    heads = width // HEAD
    return pl.pallas_call(
        functools.partial(attention_backward_kernel, heads, 256),
        out_shape=(
            jax.ShapeDtypeStruct((total, width), F32),
            jax.ShapeDtypeStruct((total, HEAD), F32),
            jax.ShapeDtypeStruct((total, HEAD), F32),
        ),
        compiler_params=pltpu.CompilerParams(vmem_limit_bytes=40 << 20),
        cost_estimate=pl.CostEstimate(
            flops=5 * total * total * width, bytes_accessed=10 * total * width, transcendentals=heads * total * total // 2
        ),
        name="attention_backward",
    )(q, k, v, g, seg_col, seg_row)


def gather_rows(x):
    return lax.all_gather(x, "shard", axis=0, tiled=True)


def scatter_rows(x):
    return lax.psum_scatter(x, "shard", scatter_dimension=0, tiled=True)


def exchange(blocks):
    return lax.all_to_all(blocks, "shard", split_axis=0, concat_axis=0, tiled=True)


def rep_sum(x):
    count = lax.axis_size("rep")
    where = lax.axis_index("rep")
    half = count // 2
    for hop in range(half - 1):
        moved = lax.ppermute(
            x, "rep", [(hop, hop + 1), (count - 1 - hop, count - 2 - hop)]
        )
        x = (x.astype(F32) + moved.astype(F32)).astype(BF16)
    moved = lax.ppermute(x, "rep", [(half - 1, half), (half, half - 1)])
    x = (x.astype(F32) + moved.astype(F32)).astype(BF16)
    for hop in range(half - 1):
        near, far = half - 1 - hop, half + hop
        moved = lax.ppermute(x, "rep", [(near, near - 1), (far, far + 1)])
        x = jnp.where((where == near - 1) | (where == far + 1), moved, x)
    return x


def per_device(
    tokens,
    attn_gain,
    query_weight,
    key_weight,
    value_weight,
    output_weight,
    ffn_gain,
    gate_weight,
    up_weight,
    down_weight,
    dealing,
    lengths,
    cotangent,
):
    n = lax.axis_size("shard")
    here = lax.axis_index("shard")
    local, width = tokens.shape
    total = local * n
    rows = query_weight.shape[0]
    ff_cols = gate_weight.shape[1] // n
    q_cols = query_weight.shape[1] // n
    copies = n // KV_HEADS
    own = here * local

    packed = jnp.arange(total, dtype=jnp.int32)
    segment, position = places(packed, lengths[0])
    seg_col, seg_row = segment[:, None], segment[None, :]
    cos_q, sin_q = rope_tables(position, q_cols)
    cos_k, sin_k = cos_q[:, :HEAD], sin_q[:, :HEAD]
    dealt = (dealing[0][:, None] == packed[None, :]).astype(BF16)

    def column_blocks(weight, cols):
        return weight.reshape(rows, n, cols).transpose(1, 0, 2)

    def head_blocks(weight):
        blocks = weight.reshape(rows, KV_HEADS, HEAD).transpose(1, 0, 2)
        return jnp.repeat(blocks, copies, axis=0)

    hidden = tokens.astype(F32)
    normed = gather_rows(rms_scale(hidden, attn_gain).astype(BF16))
    qkv = exchange(
        jnp.concatenate(
            [column_blocks(query_weight, q_cols), head_blocks(key_weight), head_blocks(value_weight)],
            axis=2,
        )
    ).reshape(width, q_cols + 2 * HEAD)
    gate_cols = exchange(column_blocks(gate_weight, ff_cols)).reshape(width, ff_cols)
    up_cols = exchange(column_blocks(up_weight, ff_cols)).reshape(width, ff_cols)
    spread_cotangent = gather_rows(cotangent)

    pre = mm(normed, qkv)
    queries = rotate(pre[:, :q_cols], cos_q, sin_q).astype(BF16)
    keys = rotate(pre[:, q_cols : q_cols + HEAD], cos_k, sin_k).astype(BF16)
    values = pre[:, q_cols + HEAD :].astype(BF16)
    attention = attention_forward(queries, keys, values, seg_col, seg_row)
    branch = scatter_rows(mm(attention, output_weight).astype(BF16))
    middle = hidden + RESIDUAL_SCALE * branch.astype(F32)
    normed_ffn = gather_rows(rms_scale(middle, ffn_gain).astype(BF16))

    out_grad_all = t_mm(dealt, spread_cotangent)
    down_grad = (RESIDUAL_SCALE * out_grad_all).astype(BF16)
    out_grad = lax.dynamic_slice_in_dim(out_grad_all, own, local)
    act_grad = mm_t(down_grad, down_weight)

    gate = mm(normed_ffn, gate_cols)
    up = mm(normed_ffn, up_cols)
    sigmoid = jax.nn.sigmoid(gate)
    activated = (gate * sigmoid * up).astype(BF16)
    gate_grad = (act_grad * up * sigmoid * (1.0 + gate * (1.0 - sigmoid))).astype(BF16)
    up_grad = (act_grad * gate * sigmoid).astype(BF16)

    down_part = rep_sum(t_mm(activated, down_grad).astype(BF16))
    gate_part = rep_sum(exchange(t_mm(normed_ffn, gate_grad).astype(BF16).reshape(n, rows, ff_cols)))
    up_part = rep_sum(exchange(t_mm(normed_ffn, up_grad).astype(BF16).reshape(n, rows, ff_cols)))

    own_columns = lax.dynamic_slice_in_dim(dealt, own, local, axis=1)
    layer_output = scatter_rows(
        (
            RESIDUAL_SCALE * mm(mm(dealt, activated).astype(BF16), down_weight)
            + mm(own_columns, middle.astype(BF16))
        ).astype(BF16)
    )

    normed_ffn_grad = scatter_rows(
        (mm_t(gate_grad, gate_cols) + mm_t(up_grad, up_cols)).astype(BF16)
    ).astype(F32)
    unused_norm, ffn_pull = jax.vjp(rms_scale, middle, ffn_gain)
    middle_part, ffn_gain_part = ffn_pull(normed_ffn_grad)
    middle_grad = out_grad + middle_part
    branch_grad = gather_rows((RESIDUAL_SCALE * middle_grad).astype(BF16))
    output_part = rep_sum(t_mm(attention, branch_grad).astype(BF16))
    attention_grad = mm_t(branch_grad, output_weight).astype(BF16)
    dq, dk, dv = attention_backward(queries, keys, values, attention_grad, seg_col, seg_row)
    pre_grad = jnp.concatenate(
        [
            unrotate(dq, cos_q, sin_q).astype(BF16),
            unrotate(dk, cos_k, sin_k).astype(BF16),
            dv.astype(BF16),
        ],
        axis=1,
    )
    qkv_part = rep_sum(exchange(t_mm(normed, pre_grad).astype(BF16).reshape(n, rows, q_cols + 2 * HEAD)))
    normed_grad = scatter_rows(mm_t(pre_grad, qkv).astype(BF16)).astype(F32)
    unused_first, attn_pull = jax.vjp(rms_scale, hidden, attn_gain)
    hidden_part, attn_gain_part = attn_pull(normed_grad)
    tokens_grad = middle_grad + hidden_part

    def join(blocks):
        return blocks.transpose(1, 0, 2).reshape(rows, -1).astype(F32)

    def join_heads(blocks):
        blocks = blocks.astype(F32).reshape(KV_HEADS, copies, rows, HEAD).sum(axis=1)
        return blocks.transpose(1, 0, 2).reshape(rows, KV_HEADS * HEAD)

    attn_gain_grad, ffn_gain_grad = lax.psum((attn_gain_part, ffn_gain_part), ("rep", "shard"))
    return (
        layer_output,
        tokens_grad,
        attn_gain_grad,
        join(qkv_part[:, :, :q_cols]),
        join_heads(qkv_part[:, :, q_cols : q_cols + HEAD]),
        join_heads(qkv_part[:, :, q_cols + HEAD :]),
        output_part.astype(F32),
        ffn_gain_grad,
        join(gate_part),
        join(up_part),
        down_part.astype(F32),
    )


def solution(mesh):
    both = P(("rep", "shard"), None)
    rowed = P("shard", None)
    return jax.shard_map(
        per_device,
        mesh=mesh,
        in_specs=(
            both, P(), rowed, rowed, rowed, rowed, P(), rowed, rowed, rowed,
            P("rep", None), P("rep", None), both,
        ),
        out_specs=(both, both, P(), rowed, rowed, rowed, rowed, P(), rowed, rowed, rowed),
        check_vma=False,
    )
```

```python
import functools

import jax
import jax.numpy as jnp
from jax import lax
from jax.experimental import pallas as pl
from jax.experimental.pallas import tpu as pltpu
from jax.sharding import PartitionSpec as P

HEADS = 32
KV_HEADS = 8
HEAD = 64
EPSILON = 1e-05
RESIDUAL_SCALE = 0.22
SCORE_SCALE = 0.015625
ROPE_BASE = 10000000.0
MASKED = -1e30
BF16 = jnp.bfloat16
F32 = jnp.float32


def mm(a, b):
    return jnp.dot(a, b, preferred_element_type=F32)


def mm_t(a, b):
    return lax.dot_general(a, b, (((1,), (1,)), ((), ())), preferred_element_type=F32)


def t_mm(a, b):
    return lax.dot_general(a, b, (((0,), (0,)), ((), ())), preferred_element_type=F32)


def rms_scale(hidden, gain_vector):
    return (
        hidden
        * lax.rsqrt(jnp.mean(hidden * hidden, axis=-1, keepdims=True) + EPSILON)
        * gain_vector
    )


def places(packed_index, seq_lengths):
    seq_ends = jnp.cumsum(seq_lengths)
    starts = seq_ends - seq_lengths
    segment = jnp.sum((packed_index[:, None] >= seq_ends[None, :]).astype(jnp.int32), axis=1)
    chosen = segment[:, None] == jnp.arange(seq_lengths.shape[0], dtype=jnp.int32)[None, :]
    position = packed_index - jnp.sum(jnp.where(chosen, starts[None, :], 0), axis=1)
    return segment, position


def rope_tables(position, width):
    half = HEAD // 2
    frequency = ROPE_BASE ** (-(jnp.arange(half, dtype=F32) * 2.0) / (2.0 * half))
    turned = position.astype(F32)[:, None] * frequency[None, :]
    cosine, sine = jnp.cos(turned), jnp.sin(turned)
    cos_full = jnp.concatenate([cosine, cosine], axis=-1)
    sin_full = jnp.concatenate([-sine, sine], axis=-1)
    return jnp.tile(cos_full, (1, width // HEAD)), jnp.tile(sin_full, (1, width // HEAD))


def swap_halves(x):
    rows, width = x.shape
    half = HEAD // 2
    y = x.reshape(rows, width // HEAD, 2, half)
    return jnp.concatenate([y[:, :, 1:], y[:, :, :1]], axis=2).reshape(rows, width)


def rotate(x, cos_full, sin_full):
    return x * cos_full + swap_halves(x) * sin_full


def unrotate(x, cos_full, sin_full):
    return x * cos_full - swap_halves(x) * sin_full


def softmax_block(q, k, allowed):
    scores = SCORE_SCALE * lax.dot_general(
        q, k, (((1,), (1,)), ((), ())), preferred_element_type=F32
    )
    scores = jnp.where(allowed, scores, MASKED)
    top = jnp.max(scores, axis=-1, keepdims=True)
    weight = jnp.exp(scores - top)
    return weight * (1.0 / jnp.sum(weight, axis=-1, keepdims=True))


def allowed_block(row0, rows, cols, seg_q, seg_k):
    q_index = row0 + lax.broadcasted_iota(jnp.int32, (rows, cols), 0)
    k_index = lax.broadcasted_iota(jnp.int32, (rows, cols), 1)
    return (seg_q == seg_k) & (k_index <= q_index)


def attention_kernel(heads, block, q_ref, k_ref, v_ref, segc_ref, segr_ref, o_ref):
    total = k_ref.shape[0]
    for i in range(total // block):
        cols = (i + 1) * block
        rows = pl.ds(i * block, block)
        allowed = allowed_block(i * block, block, cols, segc_ref[rows, :], segr_ref[:, :cols])
        k, v = k_ref[:cols, :], v_ref[:cols, :]
        for h in range(heads):
            lanes = slice(h * HEAD, (h + 1) * HEAD)
            probs = softmax_block(q_ref[rows, lanes], k, allowed)
            out = jnp.dot(probs.astype(BF16), v, preferred_element_type=F32)
            o_ref[rows, lanes] = out.astype(BF16)


def attention_forward(q, k, v, seg_col, seg_row):
    total, width = q.shape
    heads = width // HEAD
    return pl.pallas_call(
        functools.partial(attention_kernel, heads, 256),
        out_shape=jax.ShapeDtypeStruct((total, width), BF16),
        compiler_params=pltpu.CompilerParams(vmem_limit_bytes=40 << 20),
        cost_estimate=pl.CostEstimate(
            flops=2 * total * total * width, bytes_accessed=4 * total * width, transcendentals=heads * total * total // 2
        ),
        name="attention_forward",
    )(q, k, v, seg_col, seg_row)


def attention_backward_kernel(
    heads, block, q_ref, k_ref, v_ref, g_ref, segc_ref, segr_ref, dq_ref, dk_ref, dv_ref
):
    total = k_ref.shape[0]
    dk_ref[...] = jnp.zeros_like(dk_ref)
    dv_ref[...] = jnp.zeros_like(dv_ref)
    for i in range(total // block):
        cols = (i + 1) * block
        rows = pl.ds(i * block, block)
        allowed = allowed_block(i * block, block, cols, segc_ref[rows, :], segr_ref[:, :cols])
        k, v = k_ref[:cols, :], v_ref[:cols, :]
        for h in range(heads):
            lanes = slice(h * HEAD, (h + 1) * HEAD)
            q, g = q_ref[rows, lanes], g_ref[rows, lanes]
            probs = softmax_block(q, k, allowed)
            probs_grad = lax.dot_general(
                g, v, (((1,), (1,)), ((), ())), preferred_element_type=F32
            )
            delta = jnp.sum(probs * probs_grad, axis=-1, keepdims=True)
            score_grad = (probs * (probs_grad - delta)).astype(BF16)
            dq_ref[rows, lanes] = SCORE_SCALE * jnp.dot(
                score_grad, k, preferred_element_type=F32
            )
            dk_ref[:cols, :] += SCORE_SCALE * lax.dot_general(
                score_grad, q, (((0,), (0,)), ((), ())), preferred_element_type=F32
            )
            dv_ref[:cols, :] += lax.dot_general(
                probs.astype(BF16), g, (((0,), (0,)), ((), ())), preferred_element_type=F32
            )


def attention_backward(q, k, v, g, seg_col, seg_row):
    total, width = q.shape
    heads = width // HEAD
    return pl.pallas_call(
        functools.partial(attention_backward_kernel, heads, 256),
        out_shape=(
            jax.ShapeDtypeStruct((total, width), F32),
            jax.ShapeDtypeStruct((total, HEAD), F32),
            jax.ShapeDtypeStruct((total, HEAD), F32),
        ),
        compiler_params=pltpu.CompilerParams(vmem_limit_bytes=40 << 20),
        cost_estimate=pl.CostEstimate(
            flops=5 * total * total * width, bytes_accessed=10 * total * width, transcendentals=heads * total * total // 2
        ),
        name="attention_backward",
    )(q, k, v, g, seg_col, seg_row)


def gather_rows(x):
    return lax.all_gather(x, "shard", axis=0, tiled=True)


def scatter_rows(x):
    return lax.psum_scatter(x, "shard", scatter_dimension=0, tiled=True)


def exchange(blocks):
    return lax.all_to_all(blocks, "shard", split_axis=0, concat_axis=0, tiled=True)


def rep_sum(x):
    count = lax.axis_size("rep")
    where = lax.axis_index("rep")
    half = count // 2
    for hop in range(half - 1):
        moved = lax.ppermute(
            x, "rep", [(hop, hop + 1), (count - 1 - hop, count - 2 - hop)]
        )
        x = (x.astype(F32) + moved.astype(F32)).astype(BF16)
    moved = lax.ppermute(x, "rep", [(half - 1, half), (half, half - 1)])
    x = (x.astype(F32) + moved.astype(F32)).astype(BF16)
    for hop in range(half - 1):
        near, far = half - 1 - hop, half + hop
        moved = lax.ppermute(x, "rep", [(near, near - 1), (far, far + 1)])
        x = jnp.where((where == near - 1) | (where == far + 1), moved, x)
    return x


MESH = pl.DeviceIdType.MESH


def flip(index, bits):
    for weight in (1, 2, 4):
        if bits & weight:
            index = index + weight - 2 * weight * lax.rem(lax.div(index, weight), 2)
    return index


def send(src, dst, sems, k, target):
    return pltpu.make_async_remote_copy(
        src_ref=src,
        dst_ref=dst,
        send_sem=sems.at[0, k],
        recv_sem=sems.at[1, k],
        device_id={"shard": target},
        device_id_type=MESH,
    )


def greet(me, masks):
    barrier = pltpu.get_barrier_semaphore()
    for mask in masks:
        pl.semaphore_signal(
            barrier, inc=1, device_id={"shard": flip(me, mask)}, device_id_type=MESH
        )
    pl.semaphore_wait(barrier, len(masks))


GATHER_SEMS = 13


def gather_blocks(me, out, sems):
    core, px, py, diag = (flip(me, mask) for mask in (1, 2, 4, 6))
    half = out.shape[1] // 2
    low, high, whole = pl.ds(0, half), pl.ds(half, half), pl.ds(0, 2 * half)

    def move(k, block, rows, target):
        ref = out.at[block, rows]
        copy = send(ref, ref, sems, k, target)
        copy.start()
        return copy

    x_low, y_high = move(0, me, low, px), move(1, me, high, py)
    own = move(2, me, whole, core)
    x_high, y_low = move(3, me, high, px), move(4, me, low, py)
    x_low.wait_recv()
    diag_low = move(5, px, low, py)
    pieces = [own, move(6, px, low, core)]
    y_high.wait_recv()
    diag_high = move(7, py, high, px)
    pieces.append(move(8, py, high, core))
    x_high.wait_recv()
    pieces.append(move(9, px, high, core))
    y_low.wait_recv()
    pieces.append(move(10, py, low, core))
    diag_low.wait_recv()
    pieces.append(move(11, diag, low, core))
    diag_high.wait_recv()
    pieces.append(move(12, diag, high, core))
    for copy in pieces:
        copy.wait_recv()
    for copy in [x_low, y_high, x_high, y_low, diag_low, diag_high] + pieces:
        copy.wait_send()


SCATTER_SEMS = 10


def scatter_blocks(me, partial, sib_out, sib_in, acc, x_out, x_in, y_out, y_in, sems):
    core, px, py = (flip(me, mask) for mask in (1, 2, 4))
    half = acc.shape[1] // 2
    masks = (6, 2, 4, 0)
    low, high = pl.ds(0, half), pl.ds(half, half)
    copies = []

    def move(src, dst, k, target):
        copy = send(src, dst, sems, k, target)
        copy.start()
        copies.append(copy)
        return copy

    inside = []
    for i, mask in enumerate(masks):
        sib_out[i] = partial(flip(core, mask)).astype(BF16)
        inside.append(move(sib_out.at[i], sib_in.at[i], i, core))
    for i, mask in enumerate(masks):
        term = partial(flip(me, mask))
        inside[i].wait_recv()
        acc[i] = term + sib_in[i].astype(F32)
        if mask == 6:
            x_out[0] = acc[i, low].astype(BF16)
            x_diag = move(x_out.at[0], x_in.at[0], 4, px)
            y_out[0] = acc[i, high].astype(BF16)
            y_diag = move(y_out.at[0], y_in.at[0], 5, py)
        if mask == 2:
            x_out[1] = acc[i, low].astype(BF16)
            x_near = move(x_out.at[1], x_in.at[1], 6, px)
        if mask == 4:
            y_out[1] = acc[i, high].astype(BF16)
            y_near = move(y_out.at[1], y_in.at[1], 7, py)
    x_diag.wait_recv()
    y_out[2] = (acc[2, low] + x_in[0].astype(F32)).astype(BF16)
    y_last = move(y_out.at[2], y_in.at[2], 8, py)
    y_diag.wait_recv()
    x_out[2] = (acc[1, high] + y_in[0].astype(F32)).astype(BF16)
    x_last = move(x_out.at[2], x_in.at[2], 9, px)
    x_near.wait_recv()
    y_near.wait_recv()
    y_last.wait_recv()
    acc[3, low] = acc[3, low] + x_in[1].astype(F32) + y_in[2].astype(F32)
    x_last.wait_recv()
    acc[3, high] = acc[3, high] + y_in[1].astype(F32) + x_in[2].astype(F32)
    for copy in copies:
        copy.wait_send()
    return acc[3]


def scatter_scratch(rows, width):
    half = rows // 2
    return [
        pltpu.VMEM((4, rows, width), BF16),
        pltpu.VMEM((4, rows, width), BF16),
        pltpu.VMEM((4, rows, width), F32),
        pltpu.VMEM((3, half, width), BF16),
        pltpu.VMEM((3, half, width), BF16),
        pltpu.VMEM((3, half, width), BF16),
        pltpu.VMEM((3, half, width), BF16),
        pltpu.SemaphoreType.DMA((2, SCATTER_SEMS)),
    ]


VMEM = pl.BlockSpec(memory_space=pltpu.VMEM)


def comm_params(collective_id, mebibytes):
    return pltpu.CompilerParams(
        collective_id=collective_id, has_side_effects=True, vmem_limit_bytes=mebibytes << 20
    )


def norm_gather(x, gain, normalise, collective_id):
    rows, width = x.shape

    def kernel(x_ref, gain_ref, out, sems):
        me = lax.axis_index("shard")
        block = x_ref[...]
        if normalise:
            block = rms_scale(block.astype(F32), gain_ref[...]).astype(BF16)
        out[me] = block
        greet(me, (1, 2, 4))
        gather_blocks(me, out, sems)

    return pl.pallas_call(
        kernel,
        out_shape=jax.ShapeDtypeStruct((8, rows, width), BF16),
        in_specs=[VMEM, VMEM],
        out_specs=VMEM,
        scratch_shapes=[pltpu.SemaphoreType.DMA((2, GATHER_SEMS))],
        compiler_params=comm_params(collective_id, 20),
        cost_estimate=pl.CostEstimate(
            flops=8 * rows * width, bytes_accessed=18 * rows * width, transcendentals=rows
        ),
        name="gather_kernel",
    )(x, gain[None, :]).reshape(8 * rows, width)


def branch_middle_gather(attention, weight, hidden, gain, collective_id):
    rows, width = hidden.shape

    def kernel(a_ref, w_ref, h_ref, gain_ref, mid, out, *scratch):
        me = lax.axis_index("shard")
        *buffers, scatter_sems, sems = scratch
        greet(me, (1, 2, 4))

        def partial(d):
            return jnp.dot(
                a_ref[pl.ds(pl.multiple_of(d * rows, rows), rows), :],
                w_ref[...],
                preferred_element_type=F32,
            )

        branch = scatter_blocks(me, partial, *buffers, scatter_sems)
        middle = h_ref[...].astype(F32) + RESIDUAL_SCALE * branch
        mid[...] = middle
        out[me] = rms_scale(middle, gain_ref[...]).astype(BF16)
        gather_blocks(me, out, sems)

    return pl.pallas_call(
        kernel,
        out_shape=(
            jax.ShapeDtypeStruct((rows, width), F32),
            jax.ShapeDtypeStruct((8, rows, width), BF16),
        ),
        in_specs=[VMEM] * 4,
        out_specs=[VMEM] * 2,
        scratch_shapes=scatter_scratch(rows, width)
        + [pltpu.SemaphoreType.DMA((2, GATHER_SEMS))],
        compiler_params=comm_params(collective_id, 40),
        cost_estimate=pl.CostEstimate(
            flops=2 * 8 * rows * width * weight.shape[0], bytes_accessed=40 * rows * width, transcendentals=rows
        ),
        name="branch_middle_gather",
    )(attention, weight, hidden, gain[None, :])


def norm_pull(x, gain, grad):
    scale = lax.rsqrt(jnp.mean(x * x, axis=-1, keepdims=True) + EPSILON)
    pulled = gain * grad
    rows_part = scale * pulled - x * (
        scale * scale * scale * jnp.mean(pulled * x, axis=-1, keepdims=True)
    )
    return rows_part, jnp.sum(grad * x * scale, axis=0, keepdims=True)


def pull_gather(part, middle, gain, out_grad, collective_id):
    rows, width = middle.shape

    def kernel(p_ref, m_ref, gain_ref, g_ref, mg_ref, gain_part, out, *scratch):
        me = lax.axis_index("shard")
        *buffers, scatter_sems, sems = scratch
        greet(me, (1, 2, 4))
        grad = scatter_blocks(
            me,
            lambda d: p_ref[pl.ds(pl.multiple_of(d * rows, rows), rows), :].astype(F32),
            *buffers,
            scatter_sems,
        )
        rows_part, gain_row = norm_pull(m_ref[...], gain_ref[...], grad)
        gain_part[...] = gain_row
        middle_grad = g_ref[...] + rows_part
        mg_ref[...] = middle_grad
        out[me] = (RESIDUAL_SCALE * middle_grad).astype(BF16)
        gather_blocks(me, out, sems)

    return pl.pallas_call(
        kernel,
        out_shape=(
            jax.ShapeDtypeStruct((rows, width), F32),
            jax.ShapeDtypeStruct((1, width), F32),
            jax.ShapeDtypeStruct((8, rows, width), BF16),
        ),
        in_specs=[VMEM] * 4,
        out_specs=[VMEM] * 3,
        scratch_shapes=scatter_scratch(rows, width)
        + [pltpu.SemaphoreType.DMA((2, GATHER_SEMS))],
        compiler_params=comm_params(collective_id, 44),
        cost_estimate=pl.CostEstimate(
            flops=40 * rows * width, bytes_accessed=50 * rows * width, transcendentals=rows
        ),
        name="pull_gather",
    )(part, middle, gain[None, :], out_grad)


def pull_tokens(part, hidden, gain, middle_grad, collective_id):
    rows, width = middle_grad.shape

    def kernel(p_ref, h_ref, gain_ref, mg_ref, out, gain_part, *scratch):
        me = lax.axis_index("shard")
        *buffers, scatter_sems = scratch
        greet(me, (1, 2, 4))
        grad = scatter_blocks(
            me,
            lambda d: p_ref[pl.ds(pl.multiple_of(d * rows, rows), rows), :].astype(F32),
            *buffers,
            scatter_sems,
        )
        rows_part, gain_row = norm_pull(h_ref[...].astype(F32), gain_ref[...], grad)
        gain_part[...] = gain_row
        out[...] = mg_ref[...] + rows_part

    return pl.pallas_call(
        kernel,
        out_shape=(
            jax.ShapeDtypeStruct((rows, width), F32),
            jax.ShapeDtypeStruct((1, width), F32),
        ),
        in_specs=[VMEM] * 4,
        out_specs=[VMEM] * 2,
        scratch_shapes=scatter_scratch(rows, width),
        compiler_params=comm_params(collective_id, 40),
        cost_estimate=pl.CostEstimate(
            flops=40 * rows * width, bytes_accessed=50 * rows * width, transcendentals=rows
        ),
        name="pull_tokens",
    )(part, hidden, gain[None, :], middle_grad)


def per_device(
    tokens,
    attn_gain,
    query_weight,
    key_weight,
    value_weight,
    output_weight,
    ffn_gain,
    gate_weight,
    up_weight,
    down_weight,
    dealing,
    lengths,
    cotangent,
):
    n = lax.axis_size("shard")
    here = lax.axis_index("shard")
    local, width = tokens.shape
    total = local * n
    rows = query_weight.shape[0]
    ff_cols = gate_weight.shape[1] // n
    q_cols = query_weight.shape[1] // n
    copies = n // KV_HEADS
    own = here * local

    packed = jnp.arange(total, dtype=jnp.int32)
    segment, position = places(packed, lengths[0])
    seg_col, seg_row = segment[:, None], segment[None, :]
    cos_q, sin_q = rope_tables(position, q_cols)
    cos_k, sin_k = cos_q[:, :HEAD], sin_q[:, :HEAD]
    dealt = (dealing[0][:, None] == packed[None, :]).astype(BF16)

    def column_blocks(weight, cols):
        return weight.reshape(rows, n, cols).transpose(1, 0, 2)

    def head_blocks(weight):
        blocks = weight.reshape(rows, KV_HEADS, HEAD).transpose(1, 0, 2)
        return jnp.repeat(blocks, copies, axis=0)

    fast = n == 8

    spread_cotangent = lax.all_gather(cotangent, ("rep", "shard"), axis=0, tiled=True)
    all_dealing = lax.all_gather(dealing, "rep", axis=0, tiled=True)
    qkv = exchange(
        jnp.concatenate(
            [column_blocks(query_weight, q_cols), head_blocks(key_weight), head_blocks(value_weight)],
            axis=2,
        )
    ).reshape(width, q_cols + 2 * HEAD)
    gate_cols = exchange(column_blocks(gate_weight, ff_cols)).reshape(width, ff_cols)
    up_cols = exchange(column_blocks(up_weight, ff_cols)).reshape(width, ff_cols)

    if fast:
        normed = norm_gather(tokens, attn_gain, True, 0)
    else:
        normed = gather_rows(rms_scale(tokens.astype(F32), attn_gain).astype(BF16))
    pre = mm(normed, qkv)
    queries = rotate(pre[:, :q_cols], cos_q, sin_q).astype(BF16)
    keys = rotate(pre[:, q_cols : q_cols + HEAD], cos_k, sin_k).astype(BF16)
    values = pre[:, q_cols + HEAD :].astype(BF16)
    attention = attention_forward(queries, keys, values, seg_col, seg_row)
    if fast:
        middle, normed_ffn = branch_middle_gather(attention, output_weight, tokens, ffn_gain, 1)
        normed_ffn = normed_ffn.reshape(total, width)
    else:
        branch = scatter_rows(mm(attention, output_weight).astype(BF16))
        middle = tokens.astype(F32) + RESIDUAL_SCALE * branch.astype(F32)
        normed_ffn = gather_rows(rms_scale(middle, ffn_gain).astype(BF16))
    own_normed = lax.dynamic_slice_in_dim(normed_ffn, own, local)
    all_normed = lax.all_gather(own_normed, ("rep", "shard"), axis=0, tiled=True)

    reps = lax.axis_size("rep")
    group = lax.axis_index("rep")
    deals = (all_dealing[:, :, None] == packed[None, None, :]).astype(BF16)
    out_grad_all = lax.dot_general(
        deals,
        spread_cotangent.reshape(reps, total, width),
        (((1,), (1,)), ((0,), (0,))),
        preferred_element_type=F32,
    ).reshape(reps * total, width)
    down_grad_all = (RESIDUAL_SCALE * out_grad_all).astype(BF16)
    out_grad = lax.dynamic_slice_in_dim(out_grad_all, group * total + own, local)
    act_grad_all = mm_t(down_grad_all, down_weight)

    def ffn(rows_in, act_grad):
        gate = mm(rows_in, gate_cols)
        up = mm(rows_in, up_cols)
        sigmoid = jax.nn.sigmoid(gate)
        activated = (gate * sigmoid * up).astype(BF16)
        gate_grad = (act_grad * up * sigmoid * (1.0 + gate * (1.0 - sigmoid))).astype(BF16)
        up_grad = (act_grad * gate * sigmoid).astype(BF16)
        return activated, gate_grad, up_grad

    activated, gate_grad, up_grad = ffn(
        normed_ffn, lax.dynamic_slice_in_dim(act_grad_all, group * total, total)
    )
    normed_ffn_part = (mm_t(gate_grad, gate_cols) + mm_t(up_grad, up_cols)).astype(BF16)
    if fast:
        middle_grad, ffn_gain_part, branch_grad = pull_gather(
            normed_ffn_part, middle, ffn_gain, out_grad, 2
        )
        branch_grad = branch_grad.reshape(total, width)
    else:
        middle_part, ffn_gain_part = norm_pull(
            middle, ffn_gain, scatter_rows(normed_ffn_part).astype(F32)
        )
        middle_grad = out_grad + middle_part
        branch_grad = gather_rows((RESIDUAL_SCALE * middle_grad).astype(BF16))

    own_columns = lax.dynamic_slice_in_dim(dealt, own, local, axis=1)
    layer_output = scatter_rows(
        (
            RESIDUAL_SCALE * mm(mm(dealt, activated).astype(BF16), down_weight)
            + mm(own_columns, middle.astype(BF16))
        ).astype(BF16)
    )

    attention_grad = mm_t(branch_grad, output_weight).astype(BF16)
    dq, dk, dv = attention_backward(queries, keys, values, attention_grad, seg_col, seg_row)
    pre_grad = jnp.concatenate(
        [
            unrotate(dq, cos_q, sin_q).astype(BF16),
            unrotate(dk, cos_k, sin_k).astype(BF16),
            dv.astype(BF16),
        ],
        axis=1,
    )
    normed_part = mm_t(pre_grad, qkv).astype(BF16)
    if fast:
        tokens_grad, attn_gain_part = pull_tokens(normed_part, tokens, attn_gain, middle_grad, 3)
    else:
        hidden_part, attn_gain_part = norm_pull(
            tokens.astype(F32), attn_gain, scatter_rows(normed_part).astype(F32)
        )
        tokens_grad = middle_grad + hidden_part

    activated, gate_grad, up_grad = ffn(all_normed, act_grad_all)
    gate_part = exchange(t_mm(all_normed, gate_grad).astype(BF16).reshape(n, rows, ff_cols))
    up_part = exchange(t_mm(all_normed, up_grad).astype(BF16).reshape(n, rows, ff_cols))
    down_part = t_mm(activated, down_grad_all)
    output_part = rep_sum(t_mm(attention, branch_grad).astype(BF16))
    qkv_part = rep_sum(exchange(t_mm(normed, pre_grad).astype(BF16).reshape(n, rows, q_cols + 2 * HEAD)))

    def join(blocks):
        return blocks.transpose(1, 0, 2).reshape(rows, -1).astype(F32)

    def join_heads(blocks):
        blocks = blocks.astype(F32).reshape(KV_HEADS, copies, rows, HEAD).sum(axis=1)
        return blocks.transpose(1, 0, 2).reshape(rows, KV_HEADS * HEAD)

    gain_grads = lax.psum(jnp.concatenate([attn_gain_part, ffn_gain_part]), ("rep", "shard"))
    return (
        layer_output,
        tokens_grad,
        gain_grads[0],
        join(qkv_part[:, :, :q_cols]),
        join_heads(qkv_part[:, :, q_cols : q_cols + HEAD]),
        join_heads(qkv_part[:, :, q_cols + HEAD :]),
        output_part.astype(F32),
        gain_grads[1],
        join(gate_part),
        join(up_part),
        down_part,
    )


def solution(mesh):
    both = P(("rep", "shard"), None)
    rowed = P("shard", None)
    return jax.shard_map(
        per_device,
        mesh=mesh,
        in_specs=(
            both, P(), rowed, rowed, rowed, rowed, P(), rowed, rowed, rowed,
            P("rep", None), P("rep", None), both,
        ),
        out_specs=(both, both, P(), rowed, rowed, rowed, rowed, P(), rowed, rowed, rowed),
        check_vma=False,
    )
```

```python
import functools

import jax
import jax.numpy as jnp
from jax import lax
from jax.experimental import pallas as pl
from jax.experimental.pallas import tpu as pltpu
from jax.sharding import PartitionSpec as P

HEADS = 32
KV_HEADS = 8
HEAD = 64
EPSILON = 1e-05
RESIDUAL_SCALE = 0.22
SCORE_SCALE = 0.015625
ROPE_BASE = 10000000.0
MASKED = -1e30
BF16 = jnp.bfloat16
F32 = jnp.float32


def mm(a, b):
    return jnp.dot(a, b, preferred_element_type=F32)


def mm_t(a, b):
    return lax.dot_general(a, b, (((1,), (1,)), ((), ())), preferred_element_type=F32)


def t_mm(a, b):
    return lax.dot_general(a, b, (((0,), (0,)), ((), ())), preferred_element_type=F32)


def rms_scale(hidden, gain_vector):
    return (
        hidden
        * lax.rsqrt(jnp.mean(hidden * hidden, axis=-1, keepdims=True) + EPSILON)
        * gain_vector
    )


def places(packed_index, seq_lengths):
    seq_ends = jnp.cumsum(seq_lengths)
    starts = seq_ends - seq_lengths
    segment = jnp.sum((packed_index[:, None] >= seq_ends[None, :]).astype(jnp.int32), axis=1)
    chosen = segment[:, None] == jnp.arange(seq_lengths.shape[0], dtype=jnp.int32)[None, :]
    position = packed_index - jnp.sum(jnp.where(chosen, starts[None, :], 0), axis=1)
    return segment, position


def rope_tables(position, width):
    half = HEAD // 2
    frequency = ROPE_BASE ** (-(jnp.arange(half, dtype=F32) * 2.0) / (2.0 * half))
    turned = position.astype(F32)[:, None] * frequency[None, :]
    cosine, sine = jnp.cos(turned), jnp.sin(turned)
    cos_full = jnp.concatenate([cosine, cosine], axis=-1)
    sin_full = jnp.concatenate([-sine, sine], axis=-1)
    return jnp.tile(cos_full, (1, width // HEAD)), jnp.tile(sin_full, (1, width // HEAD))


def swap_halves(x):
    rows, width = x.shape
    half = HEAD // 2
    y = x.reshape(rows, width // HEAD, 2, half)
    return jnp.concatenate([y[:, :, 1:], y[:, :, :1]], axis=2).reshape(rows, width)


def rotate(x, cos_full, sin_full):
    return x * cos_full + swap_halves(x) * sin_full


def unrotate(x, cos_full, sin_full):
    return x * cos_full - swap_halves(x) * sin_full


def gather_rows(x):
    return lax.all_gather(x, "shard", axis=0, tiled=True)


def scatter_rows(x):
    return lax.psum_scatter(x, "shard", scatter_dimension=0, tiled=True)


def exchange(blocks):
    return lax.all_to_all(blocks, "shard", split_axis=0, concat_axis=0, tiled=True)


def rep_sum(x):
    count = lax.axis_size("rep")
    where = lax.axis_index("rep")
    half = count // 2
    for hop in range(half - 1):
        moved = lax.ppermute(
            x, "rep", [(hop, hop + 1), (count - 1 - hop, count - 2 - hop)]
        )
        x = (x.astype(F32) + moved.astype(F32)).astype(BF16)
    moved = lax.ppermute(x, "rep", [(half - 1, half), (half, half - 1)])
    x = (x.astype(F32) + moved.astype(F32)).astype(BF16)
    for hop in range(half - 1):
        near, far = half - 1 - hop, half + hop
        moved = lax.ppermute(x, "rep", [(near, near - 1), (far, far + 1)])
        x = jnp.where((where == near - 1) | (where == far + 1), moved, x)
    return x


MESH = pl.DeviceIdType.MESH


def flip(index, bits):
    for weight in (1, 2, 4):
        if bits & weight:
            index = index + weight - 2 * weight * lax.rem(lax.div(index, weight), 2)
    return index


def send(src, dst, sems, k, target):
    return pltpu.make_async_remote_copy(
        src_ref=src,
        dst_ref=dst,
        send_sem=sems.at[0, k],
        recv_sem=sems.at[1, k],
        device_id={"shard": target},
        device_id_type=MESH,
    )


def greet(me, masks):
    barrier = pltpu.get_barrier_semaphore()
    for mask in masks:
        pl.semaphore_signal(
            barrier, inc=1, device_id={"shard": flip(me, mask)}, device_id_type=MESH
        )
    pl.semaphore_wait(barrier, len(masks))


GATHER_SEMS = 13


def gather_steps(me, out, sems):
    core, px, py, diag = (flip(me, mask) for mask in (1, 2, 4, 6))
    half = out.shape[1] // 2
    low, high, whole = pl.ds(0, half), pl.ds(half, half), pl.ds(0, 2 * half)

    def move(k, block, rows, target):
        ref = out.at[block, rows]
        copy = send(ref, ref, sems, k, target)
        copy.start()
        return copy

    x_low, y_high = move(0, me, low, px), move(1, me, high, py)
    own = move(2, me, whole, core)
    x_high, y_low = move(3, me, high, px), move(4, me, low, py)
    yield
    x_low.wait_recv()
    diag_low = move(5, px, low, py)
    pieces = [own, move(6, px, low, core)]
    yield
    y_high.wait_recv()
    diag_high = move(7, py, high, px)
    pieces.append(move(8, py, high, core))
    yield
    x_high.wait_recv()
    pieces.append(move(9, px, high, core))
    yield
    y_low.wait_recv()
    pieces.append(move(10, py, low, core))
    yield
    diag_low.wait_recv()
    pieces.append(move(11, diag, low, core))
    diag_high.wait_recv()
    pieces.append(move(12, diag, high, core))
    yield
    for copy in pieces:
        copy.wait_recv()
    for copy in [x_low, y_high, x_high, y_low, diag_low, diag_high] + pieces:
        copy.wait_send()


def gather_blocks(me, out, sems):
    for unused_step in gather_steps(me, out, sems):
        pass


SCATTER_SEMS = 10


def scatter_blocks(
    me, partial, sib_out, sib_in, acc, x_out, x_in, y_out, y_in, sems, meanwhile=None
):
    core, px, py = (flip(me, mask) for mask in (1, 2, 4))
    half = acc.shape[1] // 2
    masks = (6, 2, 4, 0)
    low, high = pl.ds(0, half), pl.ds(half, half)
    copies = []

    def move(src, dst, k, target):
        copy = send(src, dst, sems, k, target)
        copy.start()
        copies.append(copy)
        return copy

    inside = []
    for i, mask in enumerate(masks):
        sib_out[i] = partial(flip(core, mask)).astype(BF16)
        inside.append(move(sib_out.at[i], sib_in.at[i], i, core))
    for i, mask in enumerate(masks):
        term = partial(flip(me, mask))
        inside[i].wait_recv()
        acc[i] = term + sib_in[i].astype(F32)
        if mask == 6:
            x_out[0] = acc[i, low].astype(BF16)
            x_diag = move(x_out.at[0], x_in.at[0], 4, px)
            y_out[0] = acc[i, high].astype(BF16)
            y_diag = move(y_out.at[0], y_in.at[0], 5, py)
        if mask == 2:
            x_out[1] = acc[i, low].astype(BF16)
            x_near = move(x_out.at[1], x_in.at[1], 6, px)
        if mask == 4:
            y_out[1] = acc[i, high].astype(BF16)
            y_near = move(y_out.at[1], y_in.at[1], 7, py)
    x_diag.wait_recv()
    y_out[2] = (acc[2, low] + x_in[0].astype(F32)).astype(BF16)
    y_last = move(y_out.at[2], y_in.at[2], 8, py)
    y_diag.wait_recv()
    x_out[2] = (acc[1, high] + y_in[0].astype(F32)).astype(BF16)
    x_last = move(x_out.at[2], x_in.at[2], 9, px)
    if meanwhile is not None:
        meanwhile()
    x_near.wait_recv()
    y_near.wait_recv()
    y_last.wait_recv()
    acc[3, low] = acc[3, low] + x_in[1].astype(F32) + y_in[2].astype(F32)
    x_last.wait_recv()
    acc[3, high] = acc[3, high] + y_in[1].astype(F32) + x_in[2].astype(F32)
    for copy in copies:
        copy.wait_send()
    return acc[3]


def scatter_scratch(rows, width):
    half = rows // 2
    return [
        pltpu.VMEM((4, rows, width), BF16),
        pltpu.VMEM((4, rows, width), BF16),
        pltpu.VMEM((4, rows, width), F32),
        pltpu.VMEM((3, half, width), BF16),
        pltpu.VMEM((3, half, width), BF16),
        pltpu.VMEM((3, half, width), BF16),
        pltpu.VMEM((3, half, width), BF16),
        pltpu.SemaphoreType.DMA((2, SCATTER_SEMS)),
    ]


VMEM = pl.BlockSpec(memory_space=pltpu.VMEM)
SMEM = pl.BlockSpec(memory_space=pltpu.SMEM)
ANY = pl.BlockSpec(memory_space=pl.ANY)


def comm_params(collective_id, mebibytes):
    return pltpu.CompilerParams(
        collective_id=collective_id, has_side_effects=True, vmem_limit_bytes=mebibytes << 20
    )


def front(
    tokens, attn_gain, query_weight, key_weight, value_weight, output_weight, ffn_gain,
    gate_weight, up_weight, dealing, lengths, cotangent, freq, replicas,
):
    local, width = tokens.shape
    total = 8 * local
    shard_rows = query_weight.shape[0]
    q_cols = query_weight.shape[1] // 8
    ff_cols = gate_weight.shape[1] // 8
    block = 256
    others = (1, 2, 3, 4, 5, 6, 7)

    def kernel(
        tok_ref, gain_ref, wq_hbm, wk_ref, wv_ref, wo_ref, fgain_ref, wg_hbm, wu_hbm,
        deal_ref, len_ref, cot_ref, freq_ref,
        n_ref, q_ref, kv_ref, att_ref, qw_ref, kvw_ref, wg_out, wu_out, mid_ref, nf_ref, dg_out, cot_out,
        kv_stage, c_all, dg_own,
        sib_out, sib_in, acc, x_out, x_in, y_out, y_in, scatter_sems,
        n_sems, c_sems, nf_sems, qkv_sems, bulk_sems, ring_sems, pair_sems, local_sems,
    ):
        me = lax.axis_index("shard")
        group = lax.axis_index("rep")
        core = lax.rem(me, 2)
        after = lax.rem(group + 1, replicas)
        before = lax.rem(group + replicas - 1, replicas)

        barrier = pltpu.get_barrier_semaphore()
        for mask in others:
            pl.semaphore_signal(
                barrier, inc=1, device_id={"shard": flip(me, mask)}, device_id_type=MESH
            )
        for neighbour in (after, before):
            pl.semaphore_signal(
                barrier, inc=1, device_id={"rep": neighbour}, device_id_type=MESH
            )
        n_ref[me] = rms_scale(tok_ref[...].astype(F32), gain_ref[...]).astype(BF16)
        c_all[me] = cot_ref[...]
        for d in range(8):
            lanes = slice(d * HEAD, (d + 1) * HEAD)
            kv_stage[d] = jnp.concatenate([wk_ref[:, lanes], wv_ref[:, lanes]], axis=1)
        pl.semaphore_wait(barrier, len(others) + 2)

        gather_n = gather_steps(me, n_ref, n_sems)
        next(gather_n)
        weights = []
        for mask in others:
            peer = flip(me, mask)
            columns = pl.ds(pl.multiple_of(peer * q_cols, q_cols), q_cols)
            weights.append(send(wq_hbm.at[:, columns], qw_ref.at[me], qkv_sems, 2 * mask - 2, peer))
            weights.append(send(kv_stage.at[peer], kvw_ref.at[me], qkv_sems, 2 * mask - 1, peer))
        gather_c = gather_steps(me, c_all, c_sems)
        for copy in weights:
            copy.start()
        next(gather_c)
        bulk = []
        for i, (source, target) in enumerate(((wg_hbm, wg_out), (wu_hbm, wu_out))):
            for mask in others:
                peer = flip(me, mask)
                columns = pl.ds(pl.multiple_of(peer * ff_cols, ff_cols), ff_cols)
                bulk.append(
                    send(source.at[:, columns], target.at[me], bulk_sems, 7 * i + mask - 1, peer)
                )
        for copy in bulk:
            copy.start()
        own_columns = pl.ds(pl.multiple_of(me * ff_cols, ff_cols), ff_cols)
        own_q = pl.ds(pl.multiple_of(me * q_cols, q_cols), q_cols)
        kept = [
            pltpu.make_async_copy(wg_hbm.at[:, own_columns], wg_out.at[me], local_sems.at[0]),
            pltpu.make_async_copy(wu_hbm.at[:, own_columns], wu_out.at[me], local_sems.at[1]),
            pltpu.make_async_copy(wq_hbm.at[:, own_q], qw_ref.at[me], local_sems.at[2]),
        ]
        for copy in kept:
            copy.start()
        kvw_ref[me] = kv_stage[me]
        for unused in range(5):
            next(gather_n)
            next(gather_c)
        for unused in gather_n:
            pass
        for unused in gather_c:
            pass

        for i in range(total // block):
            rows = pl.ds(i * block, block)
            packed = i * block + lax.broadcasted_iota(jnp.int32, (block, total), 0)
            chosen = (deal_ref[...] == packed).astype(BF16)
            dealt = mm(chosen, c_all[...].reshape(total, width))
            dg_own[rows, :] = (RESIDUAL_SCALE * dealt).astype(BF16)
        packed = me * local + lax.broadcasted_iota(jnp.int32, (local, total), 0)
        chosen = (deal_ref[...] == packed).astype(BF16)
        cot_out[...] = mm(chosen, c_all[...].reshape(total, width)).astype(BF16)
        half = pl.ds(pl.multiple_of(core * (total // 2), total // 2), total // 2)
        store = pltpu.make_async_copy(dg_own, dg_out.at[group], local_sems.at[3])
        store.start()

        def ring(hop):
            held = lax.rem(group + replicas - hop, replicas)
            ref = dg_out.at[held, half]
            copy = pltpu.make_async_remote_copy(
                src_ref=dg_own.at[half] if hop == 0 else ref,
                dst_ref=ref,
                send_sem=ring_sems.at[0, hop],
                recv_sem=ring_sems.at[1, hop],
                device_id={"rep": after},
                device_id_type=MESH,
            )
            copy.start()
            return copy

        def share(hop):
            held = lax.rem(group + replicas - hop, replicas)
            ref = dg_out.at[held, half]
            copy = send(ref, ref, pair_sems, hop - 1, flip(me, 1))
            copy.start()
            return copy

        hops, shares = [ring(0)], []

        for copy in kept[2:]:
            copy.wait()
        for copy in weights:
            copy.wait_recv()
        for i in range(total // block):
            rows = pl.ds(i * block, block)
            x = n_ref[pl.ds(i * block // local, block // local)].reshape(block, width)
            cosine, sine = lane_rope(i * block, block, freq_ref[...], len_ref)
            pre = mm(x, qw_ref[...].reshape(width, q_cols))
            for j in range(q_cols // (2 * HEAD)):
                lanes = slice(j * 2 * HEAD, (j + 1) * 2 * HEAD)
                y = pre[:, lanes]
                q_ref[rows, lanes] = (y * cosine + lane_swap(y) * sine).astype(BF16)
            cosine, sine = keys_only(cosine, sine)
            y = mm(x, kvw_ref[...].reshape(width, 2 * HEAD))
            kv_ref[rows, :] = (y * cosine + lane_swap(y) * sine).astype(BF16)
        attend(q_cols // HEAD, block, q_ref, kv_ref, len_ref, att_ref)

        def partial(d):
            return mm(att_ref[pl.ds(pl.multiple_of(d * local, local), local), :], wo_ref[...])

        def next_hop():
            hop = len(hops)
            hops[-1].wait_recv()
            if hop < replicas - 1:
                hops.append(ring(hop))
            shares.append(share(hop))

        branch = scatter_blocks(
            me, partial, sib_out, sib_in, acc, x_out, x_in, y_out, y_in, scatter_sems, next_hop
        )
        middle = tok_ref[...].astype(F32) + RESIDUAL_SCALE * branch
        mid_ref[...] = middle
        nf_ref[me] = rms_scale(middle, fgain_ref[...]).astype(BF16)
        gather_blocks(me, nf_ref, nf_sems)
        while len(shares) < replicas - 1:
            next_hop()
        for copy in kept[:2] + [store]:
            copy.wait()
        for copy in bulk + shares:
            copy.wait_recv()
        for copy in weights + bulk + hops + shares:
            copy.wait_send()

    rows8 = jax.ShapeDtypeStruct((8, local, width), BF16)
    half_sems = pltpu.SemaphoreType.DMA
    outs = pl.pallas_call(
        kernel,
        out_shape=(
            rows8,
            jax.ShapeDtypeStruct((total, q_cols), BF16),
            jax.ShapeDtypeStruct((total, 2 * HEAD), BF16),
            jax.ShapeDtypeStruct((total, q_cols), BF16),
            jax.ShapeDtypeStruct((8, shard_rows, q_cols), BF16),
            jax.ShapeDtypeStruct((8, shard_rows, 2 * HEAD), BF16),
            jax.ShapeDtypeStruct((8, shard_rows, ff_cols), BF16),
            jax.ShapeDtypeStruct((8, shard_rows, ff_cols), BF16),
            jax.ShapeDtypeStruct((local, width), F32),
            rows8,
            jax.ShapeDtypeStruct((replicas, total, width), BF16),
            jax.ShapeDtypeStruct((local, width), BF16),
        ),
        in_specs=[VMEM, VMEM, ANY, VMEM, VMEM, VMEM, VMEM, ANY, ANY, VMEM, SMEM, VMEM, VMEM],
        out_specs=[VMEM] * 6 + [ANY, ANY, VMEM, VMEM, ANY, VMEM],
        scratch_shapes=[
            pltpu.VMEM((8, shard_rows, 2 * HEAD), BF16),
            pltpu.VMEM((8, local, width), BF16),
            pltpu.VMEM((total, width), BF16),
        ]
        + scatter_scratch(local, width)
        + [
            half_sems((2, GATHER_SEMS)),
            half_sems((2, GATHER_SEMS)),
            half_sems((2, GATHER_SEMS)),
            half_sems((2, 14)),
            half_sems((2, 14)),
            half_sems((2, replicas)),
            half_sems((2, replicas)),
            half_sems((4,)),
        ],
        compiler_params=comm_params(0, 56),
        cost_estimate=pl.CostEstimate(
            flops=150_000_000_000, bytes_accessed=50 << 20, transcendentals=total * total
        ),
        name="front",
    )(
        tokens, attn_gain[None, :], query_weight, key_weight, value_weight, output_weight,
        ffn_gain[None, :], gate_weight, up_weight, dealing, lengths, cotangent, freq,
    )
    normed, q, kv, attention, qw, kvw, wg, wu, middle, nf, dg, cot = outs
    return (
        normed.reshape(total, width), q, kv, attention,
        qw.reshape(width, q_cols), kvw.reshape(width, 2 * HEAD),
        wg.reshape(width, ff_cols), wu.reshape(width, ff_cols),
        middle, nf.reshape(total, width), dg, cot,
    )


def norm_pull(x, gain, grad):
    scale = lax.rsqrt(jnp.mean(x * x, axis=-1, keepdims=True) + EPSILON)
    pulled = gain * grad
    rows_part = scale * pulled - x * (
        scale * scale * scale * jnp.mean(pulled * x, axis=-1, keepdims=True)
    )
    return rows_part, jnp.sum(grad * x * scale, axis=0, keepdims=True)


def pull_gather(part, middle, gain, out_grad, collective_id):
    rows, width = middle.shape

    def kernel(p_ref, m_ref, gain_ref, g_ref, mg_ref, gain_part, out, *scratch):
        me = lax.axis_index("shard")
        *buffers, scatter_sems, sems = scratch
        greet(me, (1, 2, 4))
        grad = scatter_blocks(
            me,
            lambda d: p_ref[pl.ds(pl.multiple_of(d * rows, rows), rows), :].astype(F32),
            *buffers,
            scatter_sems,
        )
        rows_part, gain_row = norm_pull(m_ref[...], gain_ref[...], grad)
        gain_part[...] = gain_row
        middle_grad = g_ref[...].astype(F32) + rows_part
        mg_ref[...] = middle_grad
        out[me] = (RESIDUAL_SCALE * middle_grad).astype(BF16)
        gather_blocks(me, out, sems)

    return pl.pallas_call(
        kernel,
        out_shape=(
            jax.ShapeDtypeStruct((rows, width), F32),
            jax.ShapeDtypeStruct((1, width), F32),
            jax.ShapeDtypeStruct((8, rows, width), BF16),
        ),
        in_specs=[VMEM] * 4,
        out_specs=[VMEM] * 3,
        scratch_shapes=scatter_scratch(rows, width)
        + [pltpu.SemaphoreType.DMA((2, GATHER_SEMS))],
        compiler_params=comm_params(collective_id, 44),
        cost_estimate=pl.CostEstimate(
            flops=40 * rows * width, bytes_accessed=50 * rows * width, transcendentals=rows
        ),
        name="pull_gather",
    )(part, middle, gain[None, :], out_grad)


def pull_tokens(part, hidden, gain, middle_grad, collective_id):
    rows, width = middle_grad.shape

    def kernel(p_ref, h_ref, gain_ref, mg_ref, out, gain_part, *scratch):
        me = lax.axis_index("shard")
        *buffers, scatter_sems = scratch
        greet(me, (1, 2, 4))
        grad = scatter_blocks(
            me,
            lambda d: p_ref[pl.ds(pl.multiple_of(d * rows, rows), rows), :].astype(F32),
            *buffers,
            scatter_sems,
        )
        rows_part, gain_row = norm_pull(h_ref[...].astype(F32), gain_ref[...], grad)
        gain_part[...] = gain_row
        out[...] = mg_ref[...] + rows_part

    return pl.pallas_call(
        kernel,
        out_shape=(
            jax.ShapeDtypeStruct((rows, width), F32),
            jax.ShapeDtypeStruct((1, width), F32),
        ),
        in_specs=[VMEM] * 4,
        out_specs=[VMEM] * 2,
        scratch_shapes=scatter_scratch(rows, width),
        compiler_params=comm_params(collective_id, 40),
        cost_estimate=pl.CostEstimate(
            flops=40 * rows * width, bytes_accessed=50 * rows * width, transcendentals=rows
        ),
        name="pull_tokens",
    )(part, hidden, gain[None, :], middle_grad)


def softmax_block(q, k, allowed):
    scores = SCORE_SCALE * mm_t(q, k)
    scores = jnp.where(allowed, scores, MASKED)
    top = jnp.max(scores, axis=-1, keepdims=True)
    weight = jnp.exp(scores - top)
    return weight * (1.0 / jnp.sum(weight, axis=-1, keepdims=True))


def allowed_block(row0, cols, start):
    shape = (start.shape[0], cols)
    query = row0 + lax.broadcasted_iota(jnp.int32, shape, 0)
    key = lax.broadcasted_iota(jnp.int32, shape, 1)
    return (key >= start) & (key <= query)


def sequence_starts(row0, shape, lengths_ref):
    row = row0 + lax.broadcasted_iota(jnp.int32, shape, 0)
    start = jnp.zeros(shape, jnp.int32)
    end = 0
    for i in range(lengths_ref.shape[1]):
        length = lengths_ref[0, i]
        end = end + length
        start = start + jnp.where(row >= end, length, 0)
    return start


def attend(heads, block, q_ref, kv_ref, lengths_ref, o_ref):
    total = kv_ref.shape[0]
    for i in range(total // block):
        cols = (i + 1) * block
        rows = pl.ds(i * block, block)
        allowed = allowed_block(
            i * block, cols, sequence_starts(i * block, (block, 1), lengths_ref)
        )
        kv = kv_ref[:cols, :]
        k, v = kv[:, :HEAD], kv[:, HEAD:]
        for h in range(heads):
            lanes = slice(h * HEAD, (h + 1) * HEAD)
            probs = softmax_block(q_ref[rows, lanes], k, allowed)
            o_ref[rows, lanes] = mm(probs.astype(BF16), v).astype(BF16)


def attend_back(heads, block, q_ref, kv_ref, g_ref, lengths_ref, dq_ref, dk_ref, dv_ref):
    total = kv_ref.shape[0]
    dk_ref[...] = jnp.zeros_like(dk_ref)
    dv_ref[...] = jnp.zeros_like(dv_ref)
    for i in range(total // block):
        cols = (i + 1) * block
        rows = pl.ds(i * block, block)
        allowed = allowed_block(
            i * block, cols, sequence_starts(i * block, (block, 1), lengths_ref)
        )
        kv = kv_ref[:cols, :]
        k, v = kv[:, :HEAD], kv[:, HEAD:]
        for h in range(heads):
            lanes = slice(h * HEAD, (h + 1) * HEAD)
            q, g = q_ref[rows, lanes], g_ref[rows, lanes]
            probs = softmax_block(q, k, allowed)
            probs_grad = mm_t(g, v)
            delta = jnp.sum(probs * probs_grad, axis=-1, keepdims=True)
            score_grad = (probs * (probs_grad - delta)).astype(BF16)
            dq_ref[rows, lanes] = SCORE_SCALE * mm(score_grad, k)
            dk_ref[:cols, :] += SCORE_SCALE * t_mm(score_grad, q)
            dv_ref[:cols, :] += t_mm(probs.astype(BF16), g)


def attention_forward(q, kv, lengths):
    total, width = q.shape

    def kernel(q_ref, kv_ref, lengths_ref, o_ref):
        attend(width // HEAD, 256, q_ref, kv_ref, lengths_ref, o_ref)

    return pl.pallas_call(
        kernel,
        out_shape=jax.ShapeDtypeStruct((total, width), BF16),
        in_specs=[VMEM, VMEM, SMEM],
        out_specs=VMEM,
        compiler_params=pltpu.CompilerParams(vmem_limit_bytes=40 << 20),
        name="attention_forward",
    )(q, kv, lengths)


def attention_gradients(q, kv, grad, lengths):
    total, width = q.shape

    def kernel(q_ref, kv_ref, g_ref, lengths_ref, dq_ref, dk_ref, dv_ref):
        attend_back(width // HEAD, 256, q_ref, kv_ref, g_ref, lengths_ref, dq_ref, dk_ref, dv_ref)

    return pl.pallas_call(
        kernel,
        out_shape=(
            jax.ShapeDtypeStruct((total, width), F32),
            jax.ShapeDtypeStruct((total, HEAD), F32),
            jax.ShapeDtypeStruct((total, HEAD), F32),
        ),
        in_specs=[VMEM, VMEM, VMEM, SMEM],
        out_specs=[VMEM] * 3,
        compiler_params=pltpu.CompilerParams(vmem_limit_bytes=40 << 20),
        name="attention_gradients",
    )(q, kv, grad, lengths)


def lane_rope(row0, rows, freq, lengths_ref):
    shape = (rows, 2 * HEAD)
    row = row0 + lax.broadcasted_iota(jnp.int32, shape, 0)
    position = row - sequence_starts(row0, shape, lengths_ref)
    turned = position.astype(F32) * freq
    lane = lax.broadcasted_iota(jnp.int32, shape, 1)
    first = lax.rem(lane, HEAD) < HEAD // 2
    sine = jnp.sin(turned)
    return jnp.cos(turned), jnp.where(first, -sine, sine)


def lane_swap(x):
    half = HEAD // 2
    lane = lax.broadcasted_iota(jnp.int32, x.shape, 1)
    first = lax.rem(lane, HEAD) < half
    return jnp.where(first, pltpu.roll(x, 2 * HEAD - half, 1), pltpu.roll(x, half, 1))


def keys_only(cosine, sine):
    lane = lax.broadcasted_iota(jnp.int32, cosine.shape, 1)
    return jnp.where(lane < HEAD, cosine, 1.0), jnp.where(lane < HEAD, sine, 0.0)


def attention_backward(
    branch_grad, output_weight, attention, q, kv, normed, q_weight, kv_weight, lengths, freq
):
    total, q_cols = q.shape
    width = normed.shape[1]
    block = 256

    def kernel(
        bg_ref, wo_ref, a_ref, q_ref, kv_ref, n_ref, qw_ref, kvw_ref, len_ref, freq_ref,
        dn_ref, dqw_ref, dkvw_ref, dwo_ref, g_ref, dq_ref, dk_ref, dv_ref, pq_ref, pkv_ref,
    ):
        for i in range(total // block):
            rows = pl.ds(i * block, block)
            g_ref[rows, :] = mm_t(bg_ref[rows, :], wo_ref[...]).astype(BF16)
        attend_back(
            q_cols // HEAD, block, q_ref, kv_ref, g_ref, len_ref, dq_ref, dk_ref, dv_ref
        )
        for i in range(total // block):
            rows = pl.ds(i * block, block)
            cosine, sine = lane_rope(i * block, block, freq_ref[...], len_ref)
            for j in range(q_cols // (2 * HEAD)):
                lanes = slice(j * 2 * HEAD, (j + 1) * 2 * HEAD)
                x = dq_ref[rows, lanes]
                pq_ref[rows, lanes] = (x * cosine - lane_swap(x) * sine).astype(BF16)
            cosine, sine = keys_only(cosine, sine)
            x = jnp.concatenate([dk_ref[rows, :], dv_ref[rows, :]], axis=1)
            pkv_ref[rows, :] = (x * cosine - lane_swap(x) * sine).astype(BF16)
            dn_ref[rows, :] = (
                mm_t(pq_ref[rows, :], qw_ref[...]) + mm_t(pkv_ref[rows, :], kvw_ref[...])
            ).astype(BF16)
        for i in range(width // 512):
            cols = slice(i * 512, (i + 1) * 512)
            dqw_ref[cols, :] = t_mm(n_ref[:, cols], pq_ref[...]).astype(BF16)
            dkvw_ref[cols, :] = t_mm(n_ref[:, cols], pkv_ref[...]).astype(BF16)
            dwo_ref[:, cols] = t_mm(a_ref[...], bg_ref[:, cols]).astype(BF16)

    return pl.pallas_call(
        kernel,
        out_shape=(
            jax.ShapeDtypeStruct((total, width), BF16),
            jax.ShapeDtypeStruct((width, q_cols), BF16),
            jax.ShapeDtypeStruct((width, 2 * HEAD), BF16),
            jax.ShapeDtypeStruct((q_cols, width), BF16),
        ),
        in_specs=[VMEM] * 8 + [SMEM, VMEM],
        out_specs=[VMEM] * 4,
        scratch_shapes=[
            pltpu.VMEM((total, q_cols), BF16),
            pltpu.VMEM((total, q_cols), F32),
            pltpu.VMEM((total, HEAD), F32),
            pltpu.VMEM((total, HEAD), F32),
            pltpu.VMEM((total, q_cols), BF16),
            pltpu.VMEM((total, 2 * HEAD), BF16),
        ],
        compiler_params=pltpu.CompilerParams(vmem_limit_bytes=56 << 20),
        cost_estimate=pl.CostEstimate(flops=30_000_000_000, bytes_accessed=30 << 20, transcendentals=total * total),
        name="attention_backward",
    )(branch_grad, output_weight, attention, q, kv, normed, q_weight, kv_weight, lengths, freq)


def ffn_rows(nf, dg, wg, wu, wd):
    gate, up, act_grad = mm(nf, wg), mm(nf, wu), mm_t(dg, wd)
    sigmoid = 1.0 / (1.0 + jnp.exp(-gate))
    silu = gate * sigmoid
    activated = (silu * up).astype(BF16)
    gate_grad = (act_grad * up * sigmoid * (1.0 + gate * (1.0 - sigmoid))).astype(BF16)
    return activated, gate_grad, (act_grad * silu).astype(BF16)


def ffn_own(group, nf, dg_all, wg, wu, wd, groups):
    total, width = nf.shape
    cols = wg.shape[1]
    block = 256

    def kernel(g_ref, nf_ref, dg_ref, wg_ref, wu_ref, wd_ref, na_ref, act_ref, gg_ref, ug_ref, dn_ref):
        nf = nf_ref[...]
        act, gg, ug = ffn_rows(nf, dg_ref[0], wg_ref[...], wu_ref[...], wd_ref[...])
        na_ref[0], act_ref[0], gg_ref[0], ug_ref[0] = nf, act, gg, ug
        dn_ref[...] = (mm_t(gg, wg_ref[...]) + mm_t(ug, wu_ref[...])).astype(BF16)

    mine = pl.BlockSpec((1, block, width), lambda i, g: (g[0], i, 0))
    hid = pl.BlockSpec((1, block, cols), lambda i, g: (g[0], i, 0))
    plain = pl.BlockSpec((block, width), lambda i, g: (i, 0))
    whole = [
        pl.BlockSpec(w.shape, lambda i, g: (0, 0), pipeline_mode=pl.Buffered(1)) for w in (wg, wu, wd)
    ]
    hidden = jax.ShapeDtypeStruct((groups, total, cols), BF16)
    return pl.pallas_call(
        kernel,
        grid_spec=pltpu.PrefetchScalarGridSpec(
            num_scalar_prefetch=1,
            grid=(total // block,),
            in_specs=[plain, mine] + whole,
            out_specs=[mine, hid, hid, hid, plain],
        ),
        out_shape=(
            jax.ShapeDtypeStruct((groups, total, width), BF16),
            hidden,
            hidden,
            hidden,
            jax.ShapeDtypeStruct((total, width), BF16),
        ),
        compiler_params=pltpu.CompilerParams(vmem_limit_bytes=56 << 20),
        cost_estimate=pl.CostEstimate(
            flops=10 * total * width * cols, bytes_accessed=40 << 20, transcendentals=total * cols
        ),
        name="ffn_own",
    )(group, nf, dg_all, wg, wu, wd)


def ffn_other(where, held, fetched, dg_all, wg, wu, wd, filled):
    groups, total, width = dg_all.shape
    cols = wg.shape[1]
    block = 256
    per_half = total // 2 // block

    def kernel(
        w_ref, held_ref, fetched_ref, dg_ref, wg_ref, wu_ref, wd_ref, *rest
    ):
        na_ref, act_ref, gg_ref, ug_ref, nf_ref = rest[4:]
        i = pl.program_id(0)

        @pl.when(i < per_half)
        def _():
            nf_ref[...] = held_ref[...]

        @pl.when(i >= per_half)
        def _():
            nf_ref[...] = fetched_ref[...]

        nf = nf_ref[...]
        act, gg, ug = ffn_rows(nf, dg_ref[0], wg_ref[...], wu_ref[...], wd_ref[...])
        na_ref[0], act_ref[0], gg_ref[0], ug_ref[0] = nf, act, gg, ug

    def row(i, w):
        half = jnp.where(i < per_half, w[1], 1 - w[1])
        return half * per_half + lax.rem(i, per_half)

    mine = pl.BlockSpec((1, block, width), lambda i, w: (w[0], row(i, w), 0))
    hid = pl.BlockSpec((1, block, cols), lambda i, w: (w[0], row(i, w), 0))
    first = pl.BlockSpec((block, width), lambda i, w: (jnp.minimum(i, per_half - 1), 0))
    last = pl.BlockSpec((block, width), lambda i, w: (jnp.maximum(i - per_half, 0), 0))
    whole = [
        pl.BlockSpec(w.shape, lambda i, g: (0, 0), pipeline_mode=pl.Buffered(1)) for w in (wg, wu, wd)
    ]
    hidden = jax.ShapeDtypeStruct((groups, total, cols), BF16)
    return pl.pallas_call(
        kernel,
        grid_spec=pltpu.PrefetchScalarGridSpec(
            num_scalar_prefetch=1,
            grid=(2 * per_half,),
            in_specs=[first, last, mine] + whole + [pl.BlockSpec(memory_space=pl.ANY)] * 4,
            out_specs=[mine, hid, hid, hid],
            scratch_shapes=[pltpu.VMEM((block, width), BF16)],
        ),
        out_shape=(jax.ShapeDtypeStruct((groups, total, width), BF16), hidden, hidden, hidden),
        input_output_aliases={7: 0, 8: 1, 9: 2, 10: 3},
        compiler_params=pltpu.CompilerParams(vmem_limit_bytes=56 << 20),
        cost_estimate=pl.CostEstimate(
            flops=6 * total * width * cols, bytes_accessed=40 << 20, transcendentals=total * cols
        ),
        name="ffn_other",
    )(where, held, fetched, dg_all, wg, wu, wd, *filled)


def weight_grad(left, right):
    groups, total, m = left.shape
    n = right.shape[2]
    block = 512
    steps = groups * total // block

    def kernel(l_ref, r_ref, o_ref, acc):
        k = pl.program_id(0)
        term = t_mm(l_ref[...], r_ref[...])

        @pl.when(k == 0)
        def _():
            acc[...] = term

        @pl.when(k > 0)
        def _():
            acc[...] += term

        @pl.when(k == steps - 1)
        def _():
            o_ref[...] = acc[...].astype(o_ref.dtype)

    return pl.pallas_call(
        kernel,
        grid=(steps,),
        in_specs=[
            pl.BlockSpec((block, m), lambda k: (k, 0)),
            pl.BlockSpec((block, n), lambda k: (k, 0)),
        ],
        out_specs=pl.BlockSpec((m, n), lambda k: (0, 0), pipeline_mode=pl.Buffered(1)),
        out_shape=jax.ShapeDtypeStruct((m, n), BF16),
        scratch_shapes=[pltpu.VMEM((m, n), F32)],
        compiler_params=pltpu.CompilerParams(vmem_limit_bytes=56 << 20),
        cost_estimate=pl.CostEstimate(
            flops=2 * groups * total * m * n, bytes_accessed=2 * groups * total * (m + n), transcendentals=0
        ),
        name="weight_grad",
    )(left.reshape(groups * total, m), right.reshape(groups * total, n))


def per_device_plane(
    tokens, attn_gain, query_weight, key_weight, value_weight, output_weight, ffn_gain,
    gate_weight, up_weight, down_weight, dealing, lengths, cotangent,
):
    n = 8
    here = lax.axis_index("shard")
    group = lax.axis_index("rep")
    replicas = lax.axis_size("rep")
    local, width = tokens.shape
    total = local * n
    rows = query_weight.shape[0]
    q_cols = query_weight.shape[1] // n
    ff_cols = gate_weight.shape[1] // n
    core = lax.rem(here, 2)
    half = HEAD // 2
    freq = ROPE_BASE ** (-(jnp.arange(half, dtype=F32) * 2.0) / (2.0 * half))
    freq = jnp.tile(freq, 4)[None, :]

    (
        normed, q, kv, attention, q_weight, kv_weight, gate_cols, up_cols,
        middle, normed_ffn, down_grads, cot_own,
    ) = front(
        tokens, attn_gain, query_weight, key_weight, value_weight, output_weight, ffn_gain,
        gate_weight, up_weight, dealing, lengths, cotangent, freq, replicas,
    )

    held = lax.dynamic_slice_in_dim(normed_ffn, core * (total // 2), total // 2)
    onward = [(i, (i + 1) % replicas) for i in range(replicas)]
    beside = [(i, i ^ 1) for i in range(n)]
    arrivals = []
    for hop in range(1, replicas):
        held = lax.ppermute(held, "rep", onward)
        where = jnp.stack([lax.rem(group + replicas - hop, replicas), core]).astype(jnp.int32)
        arrivals.append((where, held, lax.ppermute(held, "shard", beside)))

    *filled, normed_ffn_part = ffn_own(
        group.astype(jnp.int32)[None], normed_ffn, down_grads, gate_cols, up_cols, down_weight, replicas
    )
    activated = lax.dynamic_index_in_dim(filled[1], group, keepdims=False)
    middle_grad, ffn_gain_part, branch_grad = pull_gather(
        normed_ffn_part, middle, ffn_gain, cot_own, 2
    )
    branch_grad = branch_grad.reshape(total, width)
    for where, from_ring, from_core in arrivals:
        filled = ffn_other(
            where, from_ring, from_core, down_grads, gate_cols, up_cols, down_weight, filled
        )
    all_normed, all_activated, all_gate_grad, all_up_grad = filled

    normed_part, q_grad, kv_grad, output_grad = attention_backward(
        branch_grad, output_weight, attention, q, kv, normed, q_weight, kv_weight, lengths, freq
    )
    tokens_grad, attn_gain_part = pull_tokens(normed_part, tokens, attn_gain, middle_grad, 3)

    packed = jnp.arange(total, dtype=jnp.int32)
    dealt = (dealing[0][:, None] == packed[None, :]).astype(BF16)
    own_rows = (packed[:, None] - here * local == jnp.arange(local, dtype=jnp.int32)[None, :]).astype(BF16)
    layer_output = scatter_rows(
        mm(
            dealt,
            (
                RESIDUAL_SCALE * mm(activated, down_weight)
                + mm(own_rows, middle.astype(BF16))
            ).astype(BF16),
        ).astype(BF16)
    )

    gate_part = exchange(weight_grad(all_normed, all_gate_grad).reshape(n, rows, ff_cols))
    up_part = exchange(weight_grad(all_normed, all_up_grad).reshape(n, rows, ff_cols))
    down_part = weight_grad(all_activated, down_grads)
    output_part = rep_sum(output_grad)
    qkv_part = rep_sum(
        exchange(jnp.concatenate([q_grad, kv_grad], axis=1).reshape(n, rows, q_cols + 2 * HEAD))
    )

    def join(blocks):
        return blocks.transpose(1, 0, 2).reshape(rows, -1).astype(F32)

    gains = lax.all_gather(
        jnp.concatenate([attn_gain_part, ffn_gain_part]), ("rep", "shard"), axis=0
    ).sum(axis=0)
    return (
        layer_output,
        tokens_grad,
        gains[0],
        join(qkv_part[:, :, :q_cols]),
        join(qkv_part[:, :, q_cols : q_cols + HEAD]),
        join(qkv_part[:, :, q_cols + HEAD :]),
        output_part.astype(F32),
        gains[1],
        join(gate_part),
        join(up_part),
        down_part.astype(F32),
    )


def per_device(
    tokens,
    attn_gain,
    query_weight,
    key_weight,
    value_weight,
    output_weight,
    ffn_gain,
    gate_weight,
    up_weight,
    down_weight,
    dealing,
    lengths,
    cotangent,
):
    n = lax.axis_size("shard")
    here = lax.axis_index("shard")
    local, width = tokens.shape
    total = local * n
    rows = query_weight.shape[0]
    ff_cols = gate_weight.shape[1] // n
    q_cols = query_weight.shape[1] // n
    copies = n // KV_HEADS
    own = here * local

    packed = jnp.arange(total, dtype=jnp.int32)
    segment, position = places(packed, lengths[0])
    cos_q, sin_q = rope_tables(position, q_cols)
    cos_k, sin_k = cos_q[:, :HEAD], sin_q[:, :HEAD]
    dealt = (dealing[0][:, None] == packed[None, :]).astype(BF16)

    def column_blocks(weight, cols):
        return weight.reshape(rows, n, cols).transpose(1, 0, 2)

    def head_blocks(weight):
        blocks = weight.reshape(rows, KV_HEADS, HEAD).transpose(1, 0, 2)
        return jnp.repeat(blocks, copies, axis=0)

    spread_cotangent = lax.all_gather(cotangent, ("rep", "shard"), axis=0, tiled=True)
    all_dealing = lax.all_gather(dealing, "rep", axis=0, tiled=True)
    qkv = exchange(
        jnp.concatenate(
            [column_blocks(query_weight, q_cols), head_blocks(key_weight), head_blocks(value_weight)],
            axis=2,
        )
    ).reshape(width, q_cols + 2 * HEAD)
    gate_cols = exchange(column_blocks(gate_weight, ff_cols)).reshape(width, ff_cols)
    up_cols = exchange(column_blocks(up_weight, ff_cols)).reshape(width, ff_cols)

    normed = gather_rows(rms_scale(tokens.astype(F32), attn_gain).astype(BF16))
    pre = mm(normed, qkv)
    queries = rotate(pre[:, :q_cols], cos_q, sin_q).astype(BF16)
    keys = rotate(pre[:, q_cols : q_cols + HEAD], cos_k, sin_k).astype(BF16)
    values = pre[:, q_cols + HEAD :].astype(BF16)
    attention = attention_forward(queries, jnp.concatenate([keys, values], axis=1), lengths)
    branch = scatter_rows(mm(attention, output_weight).astype(BF16))
    middle = tokens.astype(F32) + RESIDUAL_SCALE * branch.astype(F32)
    normed_ffn = gather_rows(rms_scale(middle, ffn_gain).astype(BF16))
    own_normed = lax.dynamic_slice_in_dim(normed_ffn, own, local)
    all_normed = lax.all_gather(own_normed, ("rep", "shard"), axis=0, tiled=True)

    reps = lax.axis_size("rep")
    group = lax.axis_index("rep")
    deals = (all_dealing[:, :, None] == packed[None, None, :]).astype(BF16)
    out_grad_all = lax.dot_general(
        deals,
        spread_cotangent.reshape(reps, total, width),
        (((1,), (1,)), ((0,), (0,))),
        preferred_element_type=F32,
    ).reshape(reps * total, width)
    down_grad_all = (RESIDUAL_SCALE * out_grad_all).astype(BF16)
    out_grad = lax.dynamic_slice_in_dim(out_grad_all, group * total + own, local)
    act_grad_all = mm_t(down_grad_all, down_weight)

    def ffn(rows_in, act_grad):
        gate = mm(rows_in, gate_cols)
        up = mm(rows_in, up_cols)
        sigmoid = jax.nn.sigmoid(gate)
        activated = (gate * sigmoid * up).astype(BF16)
        gate_grad = (act_grad * up * sigmoid * (1.0 + gate * (1.0 - sigmoid))).astype(BF16)
        up_grad = (act_grad * gate * sigmoid).astype(BF16)
        return activated, gate_grad, up_grad

    activated, gate_grad, up_grad = ffn(
        normed_ffn, lax.dynamic_slice_in_dim(act_grad_all, group * total, total)
    )
    normed_ffn_part = (mm_t(gate_grad, gate_cols) + mm_t(up_grad, up_cols)).astype(BF16)
    middle_part, ffn_gain_part = norm_pull(
        middle, ffn_gain, scatter_rows(normed_ffn_part).astype(F32)
    )
    middle_grad = out_grad + middle_part
    branch_grad = gather_rows((RESIDUAL_SCALE * middle_grad).astype(BF16))

    own_columns = lax.dynamic_slice_in_dim(dealt, own, local, axis=1)
    layer_output = scatter_rows(
        (
            RESIDUAL_SCALE * mm(mm(dealt, activated).astype(BF16), down_weight)
            + mm(own_columns, middle.astype(BF16))
        ).astype(BF16)
    )

    attention_grad = mm_t(branch_grad, output_weight).astype(BF16)
    dq, dk, dv = attention_gradients(
        queries, jnp.concatenate([keys, values], axis=1), attention_grad, lengths
    )
    pre_grad = jnp.concatenate(
        [
            unrotate(dq, cos_q, sin_q).astype(BF16),
            unrotate(dk, cos_k, sin_k).astype(BF16),
            dv.astype(BF16),
        ],
        axis=1,
    )
    normed_part = mm_t(pre_grad, qkv).astype(BF16)
    hidden_part, attn_gain_part = norm_pull(
        tokens.astype(F32), attn_gain, scatter_rows(normed_part).astype(F32)
    )
    tokens_grad = middle_grad + hidden_part

    activated, gate_grad, up_grad = ffn(all_normed, act_grad_all)
    gate_part = exchange(t_mm(all_normed, gate_grad).astype(BF16).reshape(n, rows, ff_cols))
    up_part = exchange(t_mm(all_normed, up_grad).astype(BF16).reshape(n, rows, ff_cols))
    down_part = t_mm(activated, down_grad_all)
    output_part = rep_sum(t_mm(attention, branch_grad).astype(BF16))
    qkv_part = rep_sum(exchange(t_mm(normed, pre_grad).astype(BF16).reshape(n, rows, q_cols + 2 * HEAD)))

    def join(blocks):
        return blocks.transpose(1, 0, 2).reshape(rows, -1).astype(F32)

    def join_heads(blocks):
        blocks = blocks.astype(F32).reshape(KV_HEADS, copies, rows, HEAD).sum(axis=1)
        return blocks.transpose(1, 0, 2).reshape(rows, KV_HEADS * HEAD)

    gain_grads = lax.psum(jnp.concatenate([attn_gain_part, ffn_gain_part]), ("rep", "shard"))
    return (
        layer_output,
        tokens_grad,
        gain_grads[0],
        join(qkv_part[:, :, :q_cols]),
        join_heads(qkv_part[:, :, q_cols : q_cols + HEAD]),
        join_heads(qkv_part[:, :, q_cols + HEAD :]),
        output_part.astype(F32),
        gain_grads[1],
        join(gate_part),
        join(up_part),
        down_part,
    )


def solution(mesh):
    both = P(("rep", "shard"), None)
    rowed = P("shard", None)
    return jax.shard_map(
        per_device_plane if mesh.shape["shard"] == 8 else per_device,
        mesh=mesh,
        in_specs=(
            both, P(), rowed, rowed, rowed, rowed, P(), rowed, rowed, rowed,
            P("rep", None), P("rep", None), both,
        ),
        out_specs=(both, both, P(), rowed, rowed, rowed, rowed, P(), rowed, rowed, rowed),
        check_vma=False,
    )
```

```python
import functools

import jax
import jax.numpy as jnp
from jax import lax
from jax.experimental import pallas as pl
from jax.experimental.pallas import tpu as pltpu
from jax.sharding import PartitionSpec as P

HEADS = 32
KV_HEADS = 8
HEAD = 64
EPSILON = 1e-05
RESIDUAL_SCALE = 0.22
SCORE_SCALE = 0.015625
ROPE_BASE = 10000000.0
MASKED = -1e30
BF16 = jnp.bfloat16
F32 = jnp.float32


def mm(a, b):
    return jnp.dot(a, b, preferred_element_type=F32)


def mm_t(a, b):
    return lax.dot_general(a, b, (((1,), (1,)), ((), ())), preferred_element_type=F32)


def t_mm(a, b):
    return lax.dot_general(a, b, (((0,), (0,)), ((), ())), preferred_element_type=F32)


def rms_scale(hidden, gain_vector):
    return (
        hidden
        * lax.rsqrt(jnp.mean(hidden * hidden, axis=-1, keepdims=True) + EPSILON)
        * gain_vector
    )


def places(packed_index, seq_lengths):
    seq_ends = jnp.cumsum(seq_lengths)
    starts = seq_ends - seq_lengths
    segment = jnp.sum((packed_index[:, None] >= seq_ends[None, :]).astype(jnp.int32), axis=1)
    chosen = segment[:, None] == jnp.arange(seq_lengths.shape[0], dtype=jnp.int32)[None, :]
    position = packed_index - jnp.sum(jnp.where(chosen, starts[None, :], 0), axis=1)
    return segment, position


def rope_tables(position, width):
    half = HEAD // 2
    frequency = ROPE_BASE ** (-(jnp.arange(half, dtype=F32) * 2.0) / (2.0 * half))
    turned = position.astype(F32)[:, None] * frequency[None, :]
    cosine, sine = jnp.cos(turned), jnp.sin(turned)
    cos_full = jnp.concatenate([cosine, cosine], axis=-1)
    sin_full = jnp.concatenate([-sine, sine], axis=-1)
    return jnp.tile(cos_full, (1, width // HEAD)), jnp.tile(sin_full, (1, width // HEAD))


def swap_halves(x):
    rows, width = x.shape
    half = HEAD // 2
    y = x.reshape(rows, width // HEAD, 2, half)
    return jnp.concatenate([y[:, :, 1:], y[:, :, :1]], axis=2).reshape(rows, width)


def rotate(x, cos_full, sin_full):
    return x * cos_full + swap_halves(x) * sin_full


def unrotate(x, cos_full, sin_full):
    return x * cos_full - swap_halves(x) * sin_full


def gather_rows(x):
    return lax.all_gather(x, "shard", axis=0, tiled=True)


def scatter_rows(x):
    return lax.psum_scatter(x, "shard", scatter_dimension=0, tiled=True)


def exchange(blocks):
    return lax.all_to_all(blocks, "shard", split_axis=0, concat_axis=0, tiled=True)


def rep_sum(x):
    count = lax.axis_size("rep")
    where = lax.axis_index("rep")
    half = count // 2
    for hop in range(half - 1):
        moved = lax.ppermute(
            x, "rep", [(hop, hop + 1), (count - 1 - hop, count - 2 - hop)]
        )
        x = (x.astype(F32) + moved.astype(F32)).astype(BF16)
    moved = lax.ppermute(x, "rep", [(half - 1, half), (half, half - 1)])
    x = (x.astype(F32) + moved.astype(F32)).astype(BF16)
    for hop in range(half - 1):
        near, far = half - 1 - hop, half + hop
        moved = lax.ppermute(x, "rep", [(near, near - 1), (far, far + 1)])
        x = jnp.where((where == near - 1) | (where == far + 1), moved, x)
    return x


MESH = pl.DeviceIdType.MESH


def flip(index, bits):
    for weight in (1, 2, 4):
        if bits & weight:
            index = index + weight - 2 * weight * lax.rem(lax.div(index, weight), 2)
    return index


def send(src, dst, sems, k, target):
    return pltpu.make_async_remote_copy(
        src_ref=src,
        dst_ref=dst,
        send_sem=sems.at[0, k],
        recv_sem=sems.at[1, k],
        device_id={"shard": target},
        device_id_type=MESH,
    )


def greet(me, masks):
    barrier = pltpu.get_barrier_semaphore()
    for mask in masks:
        pl.semaphore_signal(
            barrier, inc=1, device_id={"shard": flip(me, mask)}, device_id_type=MESH
        )
    pl.semaphore_wait(barrier, len(masks))


GATHER_SEMS = 13
BULK = (12, 2, 2)


def gather_steps(me, out, sems):
    core, px, py, diag = (flip(me, mask) for mask in (1, 2, 4, 6))
    half = out.shape[1] // 2
    low, high, whole = pl.ds(0, half), pl.ds(half, half), pl.ds(0, 2 * half)

    def move(k, block, rows, target):
        ref = out.at[block, rows]
        copy = send(ref, ref, sems, k, target)
        copy.start()
        return copy

    x_low, y_high = move(0, me, low, px), move(1, me, high, py)
    own = move(2, me, whole, core)
    x_high, y_low = move(3, me, high, px), move(4, me, low, py)
    yield
    x_low.wait_recv()
    diag_low = move(5, px, low, py)
    pieces = [own, move(6, px, low, core)]
    yield
    y_high.wait_recv()
    diag_high = move(7, py, high, px)
    pieces.append(move(8, py, high, core))
    yield
    x_high.wait_recv()
    pieces.append(move(9, px, high, core))
    yield
    y_low.wait_recv()
    pieces.append(move(10, py, low, core))
    yield
    diag_low.wait_recv()
    pieces.append(move(11, diag, low, core))
    diag_high.wait_recv()
    pieces.append(move(12, diag, high, core))
    yield
    for copy in pieces:
        copy.wait_recv()
    for copy in [x_low, y_high, x_high, y_low, diag_low, diag_high] + pieces:
        copy.wait_send()


def gather_blocks(me, out, sems):
    for unused_step in gather_steps(me, out, sems):
        pass


SCATTER_SEMS = 10


def scatter_steps(me, partial, sib_out, sib_in, acc, x_out, x_in, y_out, y_in, sems):
    core, px, py = (flip(me, mask) for mask in (1, 2, 4))
    half = acc.shape[1] // 2
    masks = (6, 2, 4, 0)
    low, high = pl.ds(0, half), pl.ds(half, half)
    copies = []

    def move(src, dst, k, target):
        copy = send(src, dst, sems, k, target)
        copy.start()
        copies.append(copy)
        return copy

    inside = []
    for i, mask in enumerate(masks):
        sib_out[i] = partial(flip(core, mask)).astype(BF16)
        inside.append(move(sib_out.at[i], sib_in.at[i], i, core))
    yield
    for i, mask in enumerate(masks):
        term = partial(flip(me, mask))
        inside[i].wait_recv()
        acc[i] = term + sib_in[i].astype(F32)
        if mask == 6:
            x_out[0] = acc[i, low].astype(BF16)
            x_diag = move(x_out.at[0], x_in.at[0], 4, px)
            y_out[0] = acc[i, high].astype(BF16)
            y_diag = move(y_out.at[0], y_in.at[0], 5, py)
        if mask == 2:
            x_out[1] = acc[i, low].astype(BF16)
            x_near = move(x_out.at[1], x_in.at[1], 6, px)
        if mask == 4:
            y_out[1] = acc[i, high].astype(BF16)
            y_near = move(y_out.at[1], y_in.at[1], 7, py)
    yield
    x_diag.wait_recv()
    y_out[2] = (acc[2, low] + x_in[0].astype(F32)).astype(BF16)
    y_last = move(y_out.at[2], y_in.at[2], 8, py)
    y_diag.wait_recv()
    x_out[2] = (acc[1, high] + y_in[0].astype(F32)).astype(BF16)
    x_last = move(x_out.at[2], x_in.at[2], 9, px)
    yield
    x_near.wait_recv()
    y_near.wait_recv()
    y_last.wait_recv()
    acc[3, low] = acc[3, low] + x_in[1].astype(F32) + y_in[2].astype(F32)
    x_last.wait_recv()
    acc[3, high] = acc[3, high] + y_in[1].astype(F32) + x_in[2].astype(F32)
    yield
    for copy in copies:
        copy.wait_send()


def scatter_blocks(me, partial, *buffers):
    for unused_step in scatter_steps(me, partial, *buffers):
        pass
    return buffers[2][3]


def scatter_scratch(rows, width):
    half = rows // 2
    return [
        pltpu.VMEM((4, rows, width), BF16),
        pltpu.VMEM((4, rows, width), BF16),
        pltpu.VMEM((4, rows, width), F32),
        pltpu.VMEM((3, half, width), BF16),
        pltpu.VMEM((3, half, width), BF16),
        pltpu.VMEM((3, half, width), BF16),
        pltpu.VMEM((3, half, width), BF16),
        pltpu.SemaphoreType.DMA((2, SCATTER_SEMS)),
    ]


VMEM = pl.BlockSpec(memory_space=pltpu.VMEM)
SMEM = pl.BlockSpec(memory_space=pltpu.SMEM)
ANY = pl.BlockSpec(memory_space=pl.ANY)


def comm_params(collective_id, mebibytes):
    return pltpu.CompilerParams(
        collective_id=collective_id, has_side_effects=True, vmem_limit_bytes=mebibytes << 20
    )


def front(
    tokens, attn_gain, query_weight, key_weight, value_weight, output_weight, ffn_gain,
    gate_weight, up_weight, down_weight, dealing, lengths, cotangent, freq, replicas,
):
    local, width = tokens.shape
    total = 8 * local
    shard_rows = query_weight.shape[0]
    q_cols = query_weight.shape[1] // 8
    ff_cols = gate_weight.shape[1] // 8
    block = 256
    others = (1, 2, 3, 4, 5, 6, 7)

    def kernel(
        tok_ref, gain_ref, wq_hbm, wk_ref, wv_ref, wo_ref, fgain_ref, wg_hbm, wu_hbm,
        wd_ref, deal_ref, len_ref, cot_ref, freq_ref,
        n_ref, q_ref, kv_ref, att_ref, qw_ref, kvw_ref, wg_out, wu_out, mid_ref, nf_ref, dg_out, ag_out, cot_out,
        kv_stage, c_all, dg_own, ag_stage,
        sib_out, sib_in, acc, x_out, x_in, y_out, y_in, scatter_sems,
        n_sems, c_sems, nf_sems, qkv_sems, bulk_sems, ring_sems, pair_sems, local_sems,
    ):
        me = lax.axis_index("shard")
        group = lax.axis_index("rep")
        core = lax.rem(me, 2)
        after = lax.rem(group + 1, replicas)
        before = lax.rem(group + replicas - 1, replicas)

        barrier = pltpu.get_barrier_semaphore()
        for mask in others:
            pl.semaphore_signal(
                barrier, inc=1, device_id={"shard": flip(me, mask)}, device_id_type=MESH
            )
        for neighbour in (after, before):
            pl.semaphore_signal(
                barrier, inc=1, device_id={"rep": neighbour}, device_id_type=MESH
            )
        n_ref[me] = rms_scale(tok_ref[...].astype(F32), gain_ref[...]).astype(BF16)
        c_all[me] = cot_ref[...]
        for d in range(8):
            lanes = slice(d * HEAD, (d + 1) * HEAD)
            kv_stage[d] = jnp.concatenate([wk_ref[:, lanes], wv_ref[:, lanes]], axis=1)
        pl.semaphore_wait(barrier, len(others) + 2)

        gather_c = gather_steps(me, c_all, c_sems)
        next(gather_c)
        gather_n = gather_steps(me, n_ref, n_sems)
        next(gather_n)
        weights = []
        for mask in others:
            peer = flip(me, mask)
            columns = pl.ds(pl.multiple_of(peer * q_cols, q_cols), q_cols)
            weights.append(send(wq_hbm.at[:, columns], qw_ref.at[me], qkv_sems, 2 * mask - 2, peer))
            weights.append(send(kv_stage.at[peer], kvw_ref.at[me], qkv_sems, 2 * mask - 1, peer))
        for copy in weights:
            copy.start()
        own_columns = pl.ds(pl.multiple_of(me * ff_cols, ff_cols), ff_cols)
        own_q = pl.ds(pl.multiple_of(me * q_cols, q_cols), q_cols)
        gate_slot, up_slot = ag_stage.at[:shard_rows], ag_stage.at[pl.ds(shard_rows, shard_rows)]
        kept = [
            pltpu.make_async_copy(wg_hbm.at[:, own_columns], gate_slot, local_sems.at[0]),
            pltpu.make_async_copy(wu_hbm.at[:, own_columns], up_slot, local_sems.at[1]),
            pltpu.make_async_copy(wq_hbm.at[:, own_q], qw_ref.at[me], local_sems.at[2]),
        ]
        for copy in kept:
            copy.start()
        kvw_ref[me] = kv_stage[me]

        bulk, waiting = [], []
        for source, target in ((wg_hbm, wg_out), (wu_hbm, wu_out)):
            for part in range(2):
                rows = pl.ds(part * (shard_rows // 2), shard_rows // 2)
                for mask in (2, 4, 6, 3, 5, 7, 1):
                    waiting.append((source, target, rows, mask))

        def more(count):
            for unused in range(min(count, len(waiting))):
                source, target, rows, mask = waiting.pop(0)
                peer = flip(me, mask)
                columns = pl.ds(pl.multiple_of(peer * ff_cols, ff_cols), ff_cols)
                copy = send(
                    source.at[rows, columns], target.at[me, rows], bulk_sems, len(bulk), peer
                )
                copy.start()
                bulk.append(copy)

        for unused in gather_c:
            pass

        def permute(first):
            for i in range(total // 2 // block):
                row0 = pl.multiple_of(first + i * block, block)
                packed = row0 + lax.broadcasted_iota(jnp.int32, (block, total), 0)
                chosen = (deal_ref[...] == packed).astype(BF16)
                dealt = mm(chosen, c_all[...].reshape(total, width))
                dg_own[pl.ds(row0, block), :] = (RESIDUAL_SCALE * dealt).astype(BF16)

        near = pl.multiple_of(core * (total // 2), total // 2)
        far = pl.multiple_of((1 - core) * (total // 2), total // 2)
        half = pl.ds(near, total // 2)

        def ring(hop):
            held = lax.rem(group + replicas - hop, replicas)
            ref = dg_out.at[held, half]
            copy = pltpu.make_async_remote_copy(
                src_ref=dg_own.at[half] if hop == 0 else ref,
                dst_ref=ref,
                send_sem=ring_sems.at[0, hop],
                recv_sem=ring_sems.at[1, hop],
                device_id={"rep": after},
                device_id_type=MESH,
            )
            copy.start()
            return copy

        def share(hop):
            held = lax.rem(group + replicas - hop, replicas)
            ref = dg_out.at[held, half]
            copy = send(ref, ref, pair_sems, hop - 1, flip(me, 1))
            copy.start()
            return copy

        permute(near)
        hops, shares = [ring(0)], []
        for unused in range(4):
            next(gather_n)
        permute(far)
        packed = me * local + lax.broadcasted_iota(jnp.int32, (local, total), 0)
        chosen = (deal_ref[...] == packed).astype(BF16)
        cot_out[...] = mm(chosen, c_all[...].reshape(total, width)).astype(BF16)
        store = pltpu.make_async_copy(dg_own, dg_out.at[group], local_sems.at[3])
        store.start()
        for unused in gather_n:
            pass
        for copy in kept:
            copy.wait()
        kept = [
            pltpu.make_async_copy(gate_slot, wg_out.at[me], local_sems.at[0]),
            pltpu.make_async_copy(up_slot, wu_out.at[me], local_sems.at[1]),
        ]
        for copy in kept:
            copy.start()
        for copy in weights:
            copy.wait_recv()
        more(BULK[0])
        for i in range(total // block):
            rows = pl.ds(i * block, block)
            x = n_ref[pl.ds(i * block // local, block // local)].reshape(block, width)
            cosine, sine = lane_rope(i * block, block, freq_ref[...], len_ref)
            pre = mm(x, qw_ref[...].reshape(width, q_cols))
            for j in range(q_cols // (2 * HEAD)):
                lanes = slice(j * 2 * HEAD, (j + 1) * 2 * HEAD)
                y = pre[:, lanes]
                q_ref[rows, lanes] = (y * cosine + lane_swap(y) * sine).astype(BF16)
            cosine, sine = keys_only(cosine, sine)
            y = mm(x, kvw_ref[...].reshape(width, 2 * HEAD))
            kv_ref[rows, :] = (y * cosine + lane_swap(y) * sine).astype(BF16)
        attend(q_cols // HEAD, block, q_ref, kv_ref, len_ref, att_ref)

        def partial(d):
            return mm(att_ref[pl.ds(pl.multiple_of(d * local, local), local), :], wo_ref[...])

        def next_hop():
            hop = len(hops)
            hops[-1].wait_recv()
            if hop < replicas - 1:
                hops.append(ring(hop))
            shares.append(share(hop))

        def act_grad(held, source):
            for i in range(total // block):
                rows = pl.ds(i * block, block)
                ag_stage[rows, :] = mm_t(source[rows, :], wd_ref[...]).astype(BF16)
            copy = pltpu.make_async_copy(ag_stage, ag_out.at[held], local_sems.at[3])
            copy.start()
            copy.wait()

        next_hop()
        scatter = scatter_steps(
            me, partial, sib_out, sib_in, acc, x_out, x_in, y_out, y_in, scatter_sems
        )
        next(scatter)
        more(BULK[1])
        for unused in scatter:
            pass
        branch = acc[3]
        middle = tok_ref[...].astype(F32) + RESIDUAL_SCALE * branch
        mid_ref[...] = middle
        nf_ref[me] = rms_scale(middle, fgain_ref[...]).astype(BF16)
        gather_nf = gather_steps(me, nf_ref, nf_sems)
        next(gather_nf)
        more(BULK[2])
        for unused in gather_nf:
            pass
        more(len(waiting))
        store.wait()
        for copy in kept:
            copy.wait()
        act_grad(group, dg_own)
        hops[0].wait_send()
        if len(shares) < replicas - 1:
            next_hop()
        for done in range(replicas - 1):
            if len(shares) < done + 1:
                next_hop()
            held = lax.rem(group + replicas - 1 - done, replicas)
            shares[done].wait_recv()
            load = pltpu.make_async_copy(dg_out.at[held], dg_own, local_sems.at[3])
            load.start()
            load.wait()
            act_grad(held, dg_own)
        for copy in bulk:
            copy.wait_recv()
        for copy in weights + bulk + hops[1:] + shares:
            copy.wait_send()

    rows8 = jax.ShapeDtypeStruct((8, local, width), BF16)
    half_sems = pltpu.SemaphoreType.DMA
    outs = pl.pallas_call(
        kernel,
        out_shape=(
            rows8,
            jax.ShapeDtypeStruct((total, q_cols), BF16),
            jax.ShapeDtypeStruct((total, 2 * HEAD), BF16),
            jax.ShapeDtypeStruct((total, q_cols), BF16),
            jax.ShapeDtypeStruct((8, shard_rows, q_cols), BF16),
            jax.ShapeDtypeStruct((8, shard_rows, 2 * HEAD), BF16),
            jax.ShapeDtypeStruct((8, shard_rows, ff_cols), BF16),
            jax.ShapeDtypeStruct((8, shard_rows, ff_cols), BF16),
            jax.ShapeDtypeStruct((local, width), F32),
            rows8,
            jax.ShapeDtypeStruct((replicas, total, width), BF16),
            jax.ShapeDtypeStruct((replicas, total, ff_cols), BF16),
            jax.ShapeDtypeStruct((local, width), BF16),
        ),
        in_specs=[VMEM, VMEM, ANY, VMEM, VMEM, VMEM, VMEM, ANY, ANY, VMEM, VMEM, SMEM, VMEM, VMEM],
        out_specs=[VMEM] * 6 + [ANY, ANY, VMEM, VMEM, ANY, ANY, VMEM],
        scratch_shapes=[
            pltpu.VMEM((8, shard_rows, 2 * HEAD), BF16),
            pltpu.VMEM((8, local, width), BF16),
            pltpu.VMEM((total, width), BF16),
            pltpu.VMEM((total, ff_cols), BF16),
        ]
        + scatter_scratch(local, width)
        + [
            half_sems((2, GATHER_SEMS)),
            half_sems((2, GATHER_SEMS)),
            half_sems((2, GATHER_SEMS)),
            half_sems((2, 14)),
            half_sems((2, 28)),
            half_sems((2, replicas)),
            half_sems((2, replicas)),
            half_sems((4,)),
        ],
        compiler_params=comm_params(0, 56),
        cost_estimate=pl.CostEstimate(
            flops=200_000_000_000, bytes_accessed=50 << 20, transcendentals=total * total
        ),
        name="front",
    )(
        tokens, attn_gain[None, :], query_weight, key_weight, value_weight, output_weight,
        ffn_gain[None, :], gate_weight, up_weight, down_weight, dealing, lengths, cotangent, freq,
    )
    normed, q, kv, attention, qw, kvw, wg, wu, middle, nf, dg, ag, cot = outs
    return (
        normed.reshape(total, width), q, kv, attention,
        qw.reshape(width, q_cols), kvw.reshape(width, 2 * HEAD),
        wg.reshape(width, ff_cols), wu.reshape(width, ff_cols),
        middle, nf.reshape(total, width), dg, ag, cot,
    )


def norm_pull(x, gain, grad):
    scale = lax.rsqrt(jnp.mean(x * x, axis=-1, keepdims=True) + EPSILON)
    pulled = gain * grad
    rows_part = scale * pulled - x * (
        scale * scale * scale * jnp.mean(pulled * x, axis=-1, keepdims=True)
    )
    return rows_part, jnp.sum(grad * x * scale, axis=0, keepdims=True)


def pull_gather(part, middle, gain, out_grad, collective_id):
    rows, width = middle.shape

    def kernel(p_ref, m_ref, gain_ref, g_ref, mg_ref, gain_part, out, *scratch):
        me = lax.axis_index("shard")
        *buffers, scatter_sems, sems = scratch
        greet(me, (1, 2, 4))
        grad = scatter_blocks(
            me,
            lambda d: p_ref[pl.ds(pl.multiple_of(d * rows, rows), rows), :].astype(F32),
            *buffers,
            scatter_sems,
        )
        rows_part, gain_row = norm_pull(m_ref[...], gain_ref[...], grad)
        gain_part[...] = gain_row
        middle_grad = g_ref[...].astype(F32) + rows_part
        mg_ref[...] = middle_grad
        out[me] = (RESIDUAL_SCALE * middle_grad).astype(BF16)
        gather_blocks(me, out, sems)

    return pl.pallas_call(
        kernel,
        out_shape=(
            jax.ShapeDtypeStruct((rows, width), F32),
            jax.ShapeDtypeStruct((1, width), F32),
            jax.ShapeDtypeStruct((8, rows, width), BF16),
        ),
        in_specs=[VMEM] * 4,
        out_specs=[VMEM] * 3,
        scratch_shapes=scatter_scratch(rows, width)
        + [pltpu.SemaphoreType.DMA((2, GATHER_SEMS))],
        compiler_params=comm_params(collective_id, 44),
        cost_estimate=pl.CostEstimate(
            flops=50_000_000_000, bytes_accessed=50 * rows * width, transcendentals=rows
        ),
        name="pull_gather",
    )(part, middle, gain[None, :], out_grad)


def pull_tokens(part, out_part, hidden, gain, middle_grad, other_gain, replicas, collective_id):
    rows, width = middle_grad.shape
    levels = [("shard", 1), ("shard", 2), ("shard", 4)]
    level = 1
    while level < replicas:
        levels.append(("rep", level))
        level *= 2

    def kernel(
        p_ref, o_ref, h_ref, gain_ref, mg_ref, og_ref, out, lay, gains, gain_in, gain_out, gain_sems, *scratch
    ):
        me = lax.axis_index("shard")
        group = lax.axis_index("rep")
        first, second = scratch[:8], scratch[8:]
        barrier = pltpu.get_barrier_semaphore()
        peers = []
        for axis, weight in levels:
            index = me if axis == "shard" else group
            peers.append({axis: index + weight - 2 * weight * lax.rem(lax.div(index, weight), 2)})
        for peer in peers:
            pl.semaphore_signal(barrier, inc=1, device_id=peer, device_id_type=MESH)
        pl.semaphore_wait(barrier, len(peers))

        def blocks_of(ref):
            return lambda d: ref[pl.ds(pl.multiple_of(d * rows, rows), rows), :].astype(F32)

        grads = scatter_steps(me, blocks_of(p_ref), *first)
        outputs = scatter_steps(me, blocks_of(o_ref), *second)
        next(grads)
        next(grads)
        next(outputs)
        next(grads)
        next(outputs)
        next(grads)
        rows_part, gain_row = norm_pull(h_ref[...].astype(F32), gain_ref[...], first[2][3])
        out[...] = mg_ref[...] + rows_part
        total = jnp.concatenate([gain_row, og_ref[...]], axis=0)
        for i, peer in enumerate(peers):
            gain_out[i] = total
            copy = pltpu.make_async_remote_copy(
                src_ref=gain_out.at[i],
                dst_ref=gain_in.at[i],
                send_sem=gain_sems.at[0, i],
                recv_sem=gain_sems.at[1, i],
                device_id=peer,
                device_id_type=MESH,
            )
            copy.start()
            if i == 1:
                next(outputs)
            copy.wait()
            total = total + gain_in[i]
        gains[...] = total
        next(outputs)
        lay[...] = second[2][3].astype(BF16)
        for steps in (grads, outputs):
            for unused in steps:
                pass

    return pl.pallas_call(
        kernel,
        out_shape=(
            jax.ShapeDtypeStruct((rows, width), F32),
            jax.ShapeDtypeStruct((rows, width), BF16),
            jax.ShapeDtypeStruct((2, width), F32),
        ),
        in_specs=[VMEM] * 6,
        out_specs=[VMEM] * 3,
        scratch_shapes=[
            pltpu.VMEM((len(levels), 2, width), F32),
            pltpu.VMEM((len(levels), 2, width), F32),
            pltpu.SemaphoreType.DMA((2, len(levels))),
        ]
        + scatter_scratch(rows, width)
        + scatter_scratch(rows, width),
        compiler_params=comm_params(collective_id, 52),
        cost_estimate=pl.CostEstimate(
            flops=50_000_000_000, bytes_accessed=50 * rows * width, transcendentals=rows
        ),
        name="pull_tokens",
    )(part, out_part, hidden, gain[None, :], middle_grad, other_gain)


def softmax_block(q, k, allowed):
    scores = SCORE_SCALE * mm_t(q, k)
    scores = jnp.where(allowed, scores, MASKED)
    top = jnp.max(scores, axis=-1, keepdims=True)
    weight = jnp.exp(scores - top)
    return weight * (1.0 / jnp.sum(weight, axis=-1, keepdims=True))


def allowed_block(row0, cols, start):
    shape = (start.shape[0], cols)
    query = row0 + lax.broadcasted_iota(jnp.int32, shape, 0)
    key = lax.broadcasted_iota(jnp.int32, shape, 1)
    return (key >= start) & (key <= query)


def sequence_starts(row0, shape, lengths_ref):
    row = row0 + lax.broadcasted_iota(jnp.int32, shape, 0)
    start = jnp.zeros(shape, jnp.int32)
    end = 0
    for i in range(lengths_ref.shape[1]):
        length = lengths_ref[0, i]
        end = end + length
        start = start + jnp.where(row >= end, length, 0)
    return start


def attend(heads, block, q_ref, kv_ref, lengths_ref, o_ref):
    total = kv_ref.shape[0]
    for i in range(total // block):
        cols = (i + 1) * block
        rows = pl.ds(i * block, block)
        allowed = allowed_block(
            i * block, cols, sequence_starts(i * block, (block, 1), lengths_ref)
        )
        kv = kv_ref[:cols, :]
        k, v = kv[:, :HEAD], kv[:, HEAD:]
        for h in range(heads):
            lanes = slice(h * HEAD, (h + 1) * HEAD)
            probs = softmax_block(q_ref[rows, lanes], k, allowed)
            o_ref[rows, lanes] = mm(probs.astype(BF16), v).astype(BF16)


def attend_back(heads, block, q_ref, kv_ref, g_ref, lengths_ref, dq_ref, dk_ref, dv_ref):
    total = kv_ref.shape[0]
    dk_ref[...] = jnp.zeros_like(dk_ref)
    dv_ref[...] = jnp.zeros_like(dv_ref)
    for i in range(total // block):
        cols = (i + 1) * block
        rows = pl.ds(i * block, block)
        allowed = allowed_block(
            i * block, cols, sequence_starts(i * block, (block, 1), lengths_ref)
        )
        kv = kv_ref[:cols, :]
        k, v = kv[:, :HEAD], kv[:, HEAD:]
        for h in range(heads):
            lanes = slice(h * HEAD, (h + 1) * HEAD)
            q, g = q_ref[rows, lanes], g_ref[rows, lanes]
            probs = softmax_block(q, k, allowed)
            probs_grad = mm_t(g, v)
            delta = jnp.sum(probs * probs_grad, axis=-1, keepdims=True)
            score_grad = (probs * (probs_grad - delta)).astype(BF16)
            dq_ref[rows, lanes] = SCORE_SCALE * mm(score_grad, k)
            dk_ref[:cols, :] += SCORE_SCALE * t_mm(score_grad, q)
            dv_ref[:cols, :] += t_mm(probs.astype(BF16), g)


def attention_forward(q, kv, lengths):
    total, width = q.shape

    def kernel(q_ref, kv_ref, lengths_ref, o_ref):
        attend(width // HEAD, 256, q_ref, kv_ref, lengths_ref, o_ref)

    return pl.pallas_call(
        kernel,
        out_shape=jax.ShapeDtypeStruct((total, width), BF16),
        in_specs=[VMEM, VMEM, SMEM],
        out_specs=VMEM,
        compiler_params=pltpu.CompilerParams(vmem_limit_bytes=40 << 20),
        name="attention_forward",
    )(q, kv, lengths)


def attention_gradients(q, kv, grad, lengths):
    total, width = q.shape

    def kernel(q_ref, kv_ref, g_ref, lengths_ref, dq_ref, dk_ref, dv_ref):
        attend_back(width // HEAD, 256, q_ref, kv_ref, g_ref, lengths_ref, dq_ref, dk_ref, dv_ref)

    return pl.pallas_call(
        kernel,
        out_shape=(
            jax.ShapeDtypeStruct((total, width), F32),
            jax.ShapeDtypeStruct((total, HEAD), F32),
            jax.ShapeDtypeStruct((total, HEAD), F32),
        ),
        in_specs=[VMEM, VMEM, VMEM, SMEM],
        out_specs=[VMEM] * 3,
        compiler_params=pltpu.CompilerParams(vmem_limit_bytes=40 << 20),
        name="attention_gradients",
    )(q, kv, grad, lengths)


def lane_rope(row0, rows, freq, lengths_ref):
    shape = (rows, 2 * HEAD)
    row = row0 + lax.broadcasted_iota(jnp.int32, shape, 0)
    position = row - sequence_starts(row0, shape, lengths_ref)
    turned = position.astype(F32) * freq
    lane = lax.broadcasted_iota(jnp.int32, shape, 1)
    first = lax.rem(lane, HEAD) < HEAD // 2
    sine = jnp.sin(turned)
    return jnp.cos(turned), jnp.where(first, -sine, sine)


def lane_swap(x):
    half = HEAD // 2
    lane = lax.broadcasted_iota(jnp.int32, x.shape, 1)
    first = lax.rem(lane, HEAD) < half
    return jnp.where(first, pltpu.roll(x, 2 * HEAD - half, 1), pltpu.roll(x, half, 1))


def keys_only(cosine, sine):
    lane = lax.broadcasted_iota(jnp.int32, cosine.shape, 1)
    return jnp.where(lane < HEAD, cosine, 1.0), jnp.where(lane < HEAD, sine, 0.0)


def attention_backward(
    branch_grad, output_weight, attention, q, kv, normed, q_weight, kv_weight, lengths, freq
):
    total, q_cols = q.shape
    width = normed.shape[1]
    block = 256

    def kernel(
        bg_ref, wo_ref, a_ref, q_ref, kv_ref, n_ref, qw_ref, kvw_ref, len_ref, freq_ref,
        dn_ref, dqkv_ref, dwo_ref, g_ref, dq_ref, dk_ref, dv_ref, pq_ref, pkv_ref,
    ):
        for i in range(total // block):
            rows = pl.ds(i * block, block)
            g_ref[rows, :] = mm_t(bg_ref[rows, :], wo_ref[...]).astype(BF16)
        attend_back(
            q_cols // HEAD, block, q_ref, kv_ref, g_ref, len_ref, dq_ref, dk_ref, dv_ref
        )
        for i in range(total // block):
            rows = pl.ds(i * block, block)
            cosine, sine = lane_rope(i * block, block, freq_ref[...], len_ref)
            for j in range(q_cols // (2 * HEAD)):
                lanes = slice(j * 2 * HEAD, (j + 1) * 2 * HEAD)
                x = dq_ref[rows, lanes]
                pq_ref[rows, lanes] = (x * cosine - lane_swap(x) * sine).astype(BF16)
            cosine, sine = keys_only(cosine, sine)
            x = jnp.concatenate([dk_ref[rows, :], dv_ref[rows, :]], axis=1)
            pkv_ref[rows, :] = (x * cosine - lane_swap(x) * sine).astype(BF16)
            dn_ref[rows, :] = (
                mm_t(pq_ref[rows, :], qw_ref[...]) + mm_t(pkv_ref[rows, :], kvw_ref[...])
            ).astype(BF16)
        for i in range(width // 512):
            cols = slice(i * 512, (i + 1) * 512)
            dqkv_ref[cols, :q_cols] = t_mm(n_ref[:, cols], pq_ref[...]).astype(BF16)
            dqkv_ref[cols, q_cols:] = t_mm(n_ref[:, cols], pkv_ref[...]).astype(BF16)
            dwo_ref[:, cols] = t_mm(a_ref[...], bg_ref[:, cols]).astype(BF16)

    return pl.pallas_call(
        kernel,
        out_shape=(
            jax.ShapeDtypeStruct((total, width), BF16),
            jax.ShapeDtypeStruct((width, q_cols + 2 * HEAD), BF16),
            jax.ShapeDtypeStruct((q_cols, width), BF16),
        ),
        in_specs=[VMEM] * 8 + [SMEM, VMEM],
        out_specs=[VMEM] * 3,
        scratch_shapes=[
            pltpu.VMEM((total, q_cols), BF16),
            pltpu.VMEM((total, q_cols), F32),
            pltpu.VMEM((total, HEAD), F32),
            pltpu.VMEM((total, HEAD), F32),
            pltpu.VMEM((total, q_cols), BF16),
            pltpu.VMEM((total, 2 * HEAD), BF16),
        ],
        compiler_params=pltpu.CompilerParams(vmem_limit_bytes=56 << 20),
        cost_estimate=pl.CostEstimate(flops=30_000_000_000, bytes_accessed=30 << 20, transcendentals=total * total),
        name="attention_backward",
    )(branch_grad, output_weight, attention, q, kv, normed, q_weight, kv_weight, lengths, freq)


def ffn_rows(nf, act_grad, wg, wu):
    gate, up = mm(nf, wg), mm(nf, wu)
    act_grad = act_grad.astype(F32)
    sigmoid = 1.0 / (1.0 + jnp.exp(-gate))
    silu = gate * sigmoid
    activated = (silu * up).astype(BF16)
    gate_grad = (act_grad * up * sigmoid * (1.0 + gate * (1.0 - sigmoid))).astype(BF16)
    return activated, gate_grad, (act_grad * silu).astype(BF16)


def ffn_own(group, nf, act_grads, wg, wu):
    groups, total, cols = act_grads.shape
    width = nf.shape[1]
    block = 256

    def kernel(g_ref, nf_ref, ag_ref, wg_ref, wu_ref, na_ref, act_ref, gg_ref, ug_ref, dn_ref):
        nf = nf_ref[...]
        act, gg, ug = ffn_rows(nf, ag_ref[0], wg_ref[...], wu_ref[...])
        na_ref[0], act_ref[0], gg_ref[0], ug_ref[0] = nf, act, gg, ug
        dn_ref[...] = (mm_t(gg, wg_ref[...]) + mm_t(ug, wu_ref[...])).astype(BF16)

    mine = pl.BlockSpec((1, block, width), lambda i, g: (g[0], i, 0))
    hid = pl.BlockSpec((1, block, cols), lambda i, g: (g[0], i, 0))
    plain = pl.BlockSpec((block, width), lambda i, g: (i, 0))
    whole = [
        pl.BlockSpec(w.shape, lambda i, g: (0, 0), pipeline_mode=pl.Buffered(1)) for w in (wg, wu)
    ]
    hidden = jax.ShapeDtypeStruct((groups, total, cols), BF16)
    return pl.pallas_call(
        kernel,
        grid_spec=pltpu.PrefetchScalarGridSpec(
            num_scalar_prefetch=1,
            grid=(total // block,),
            in_specs=[plain, hid] + whole,
            out_specs=[mine, hid, hid, hid, plain],
        ),
        out_shape=(
            jax.ShapeDtypeStruct((groups, total, width), BF16),
            hidden,
            hidden,
            hidden,
            jax.ShapeDtypeStruct((total, width), BF16),
        ),
        compiler_params=pltpu.CompilerParams(vmem_limit_bytes=48 << 20),
        cost_estimate=pl.CostEstimate(
            flops=12 * total * width * cols, bytes_accessed=40 << 20, transcendentals=total * cols
        ),
        name="ffn_own",
    )(group, nf, act_grads, wg, wu)


def ffn_other(where, held, fetched, act_grads, wg, wu, filled):
    groups, total, cols = act_grads.shape
    width = held.shape[1]
    block = 256
    per_half = total // 2 // block

    def kernel(w_ref, held_ref, fetched_ref, ag_ref, wg_ref, wu_ref, *rest):
        na_ref, act_ref, gg_ref, ug_ref, nf_ref = rest[4:]
        i = pl.program_id(0)

        @pl.when(i < per_half)
        def _():
            nf_ref[...] = held_ref[...]

        @pl.when(i >= per_half)
        def _():
            nf_ref[...] = fetched_ref[...]

        nf = nf_ref[...]
        act, gg, ug = ffn_rows(nf, ag_ref[0], wg_ref[...], wu_ref[...])
        na_ref[0], act_ref[0], gg_ref[0], ug_ref[0] = nf, act, gg, ug

    def row(i, w):
        half = jnp.where(i < per_half, w[1], 1 - w[1])
        return half * per_half + lax.rem(i, per_half)

    mine = pl.BlockSpec((1, block, width), lambda i, w: (w[0], row(i, w), 0))
    hid = pl.BlockSpec((1, block, cols), lambda i, w: (w[0], row(i, w), 0))
    first = pl.BlockSpec((block, width), lambda i, w: (jnp.minimum(i, per_half - 1), 0))
    last = pl.BlockSpec((block, width), lambda i, w: (jnp.maximum(i - per_half, 0), 0))
    whole = [
        pl.BlockSpec(w.shape, lambda i, g: (0, 0), pipeline_mode=pl.Buffered(1)) for w in (wg, wu)
    ]
    hidden = jax.ShapeDtypeStruct((groups, total, cols), BF16)
    return pl.pallas_call(
        kernel,
        grid_spec=pltpu.PrefetchScalarGridSpec(
            num_scalar_prefetch=1,
            grid=(2 * per_half,),
            in_specs=[first, last, hid] + whole + [pl.BlockSpec(memory_space=pl.ANY)] * 4,
            out_specs=[mine, hid, hid, hid],
            scratch_shapes=[pltpu.VMEM((block, width), BF16)],
        ),
        out_shape=(jax.ShapeDtypeStruct((groups, total, width), BF16), hidden, hidden, hidden),
        input_output_aliases={6: 0, 7: 1, 8: 2, 9: 3},
        compiler_params=pltpu.CompilerParams(vmem_limit_bytes=48 << 20),
        cost_estimate=pl.CostEstimate(
            flops=8 * total * width * cols, bytes_accessed=40 << 20, transcendentals=total * cols
        ),
        name="ffn_other",
    )(where, held, fetched, act_grads, wg, wu, *filled)


def output_rows(where, activated, down_weight, middle, deal, total):
    groups, total, cols = activated.shape
    local, width = middle.shape
    block = 256

    def kernel(w_ref, act_ref, wd_ref, mid_ref, deal_ref, o_ref, rows_ref):
        for i in range(total // block):
            rows = pl.ds(i * block, block)
            rows_ref[rows, :] = (RESIDUAL_SCALE * mm(act_ref[0, rows, :], wd_ref[...])).astype(BF16)
        own = pl.ds(pl.multiple_of(w_ref[1] * local, local), local)
        rows_ref[own, :] = (rows_ref[own, :].astype(F32) + mid_ref[...]).astype(BF16)
        for i in range(total // block):
            rows = pl.ds(i * block, block)
            packed = lax.broadcasted_iota(jnp.int32, (block, total), 1)
            chosen = (deal_ref[rows, :] == packed).astype(BF16)
            o_ref[rows, :] = mm(chosen, rows_ref[...]).astype(BF16)

    def full(shape):
        return pl.BlockSpec(shape, lambda i, w: (0,) * len(shape), pipeline_mode=pl.Buffered(1))

    return pl.pallas_call(
        kernel,
        grid_spec=pltpu.PrefetchScalarGridSpec(
            num_scalar_prefetch=1,
            grid=(1,),
            in_specs=[
                pl.BlockSpec((1, total, cols), lambda i, w: (w[0], 0, 0), pipeline_mode=pl.Buffered(1)),
                full(down_weight.shape),
                full(middle.shape),
                full(deal.shape),
            ],
            out_specs=full((total, width)),
            scratch_shapes=[pltpu.VMEM((total, width), BF16)],
        ),
        out_shape=jax.ShapeDtypeStruct((total, width), BF16),
        compiler_params=pltpu.CompilerParams(vmem_limit_bytes=48 << 20),
        cost_estimate=pl.CostEstimate(
            flops=2 * total * width * (cols + total) * 2, bytes_accessed=12 << 20, transcendentals=0
        ),
        name="output_rows",
    )(where, activated, down_weight, middle, deal)


def join_columns(blocks):
    n, rows, cols = blocks.shape

    def kernel(b_ref, o_ref):
        o_ref[...] = b_ref[0].astype(F32)

    return pl.pallas_call(
        kernel,
        grid=(n,),
        in_specs=[pl.BlockSpec((1, rows, cols), lambda i: (i, 0, 0))],
        out_specs=pl.BlockSpec((rows, cols), lambda i: (0, i)),
        out_shape=jax.ShapeDtypeStruct((rows, n * cols), F32),
        cost_estimate=pl.CostEstimate(
            flops=n * rows * cols, bytes_accessed=6 * n * rows * cols, transcendentals=0
        ),
        name="join_columns",
    )(blocks)


def join_heads(blocks, q_cols):
    n, rows, cols = blocks.shape

    def kernel(b_ref, q_ref, k_ref, v_ref):
        for i in range(n):
            q_ref[:, i * q_cols : (i + 1) * q_cols] = b_ref[i, :, :q_cols].astype(F32)
        kv = [b_ref[i, :, q_cols:].astype(F32) for i in range(n)]
        k_ref[...] = jnp.concatenate([x[:, :HEAD] for x in kv], axis=1)
        v_ref[...] = jnp.concatenate([x[:, HEAD:] for x in kv], axis=1)

    return pl.pallas_call(
        kernel,
        out_shape=(
            jax.ShapeDtypeStruct((rows, n * q_cols), F32),
            jax.ShapeDtypeStruct((rows, n * HEAD), F32),
            jax.ShapeDtypeStruct((rows, n * HEAD), F32),
        ),
        name="join_heads",
    )(blocks)


def weight_grad(left, right, dtype):
    groups, total, m = left.shape
    n = right.shape[2]
    block = 512
    steps = groups * total // block

    def kernel(l_ref, r_ref, o_ref, acc):
        k = pl.program_id(0)
        term = t_mm(l_ref[...], r_ref[...])

        @pl.when(k == 0)
        def _():
            acc[...] = term

        @pl.when(k > 0)
        def _():
            acc[...] += term

        @pl.when(k == steps - 1)
        def _():
            o_ref[...] = acc[...].astype(o_ref.dtype)

    return pl.pallas_call(
        kernel,
        grid=(steps,),
        in_specs=[
            pl.BlockSpec((block, m), lambda k: (k, 0)),
            pl.BlockSpec((block, n), lambda k: (k, 0)),
        ],
        out_specs=pl.BlockSpec((m, n), lambda k: (0, 0), pipeline_mode=pl.Buffered(1)),
        out_shape=jax.ShapeDtypeStruct((m, n), dtype),
        scratch_shapes=[pltpu.VMEM((m, n), F32)],
        compiler_params=pltpu.CompilerParams(vmem_limit_bytes=56 << 20),
        cost_estimate=pl.CostEstimate(
            flops=2 * groups * total * m * n, bytes_accessed=2 * groups * total * (m + n), transcendentals=0
        ),
        name="weight_grad",
    )(left.reshape(groups * total, m), right.reshape(groups * total, n))


def per_device_plane(
    tokens, attn_gain, query_weight, key_weight, value_weight, output_weight, ffn_gain,
    gate_weight, up_weight, down_weight, dealing, lengths, cotangent,
):
    n = 8
    here = lax.axis_index("shard")
    group = lax.axis_index("rep")
    replicas = lax.axis_size("rep")
    local, width = tokens.shape
    total = local * n
    rows = query_weight.shape[0]
    q_cols = query_weight.shape[1] // n
    ff_cols = gate_weight.shape[1] // n
    core = lax.rem(here, 2)
    half = HEAD // 2
    freq = ROPE_BASE ** (-(jnp.arange(half, dtype=F32) * 2.0) / (2.0 * half))
    freq = jnp.tile(freq, 4)[None, :]

    (
        normed, q, kv, attention, q_weight, kv_weight, gate_cols, up_cols,
        middle, normed_ffn, down_grads, act_grads, cot_own,
    ) = front(
        tokens, attn_gain, query_weight, key_weight, value_weight, output_weight, ffn_gain,
        gate_weight, up_weight, down_weight, dealing, lengths, cotangent, freq, replicas,
    )

    held = lax.dynamic_slice_in_dim(normed_ffn, core * (total // 2), total // 2)
    onward = [(i, (i + 1) % replicas) for i in range(replicas)]
    beside = [(i, i ^ 1) for i in range(n)]
    arrivals = []
    for hop in range(1, replicas):
        held = lax.ppermute(held, "rep", onward)
        where = jnp.stack([lax.rem(group + replicas - hop, replicas), core]).astype(jnp.int32)
        arrivals.append((where, held, lax.ppermute(held, "shard", beside)))

    *filled, normed_ffn_part = ffn_own(
        group.astype(jnp.int32)[None], normed_ffn, act_grads, gate_cols, up_cols
    )
    middle_grad, ffn_gain_part, branch_grad = pull_gather(
        normed_ffn_part, middle, ffn_gain, cot_own, 2
    )
    branch_grad = branch_grad.reshape(total, width)
    output_part = output_rows(
        jnp.stack([group, here]).astype(jnp.int32), filled[1], down_weight, middle,
        dealing.reshape(total, 1), total,
    )
    normed_part, qkv_grad, output_grad = attention_backward(
        branch_grad, output_weight, attention, q, kv, normed, q_weight, kv_weight, lengths, freq
    )
    tokens_grad, layer_output, gains = pull_tokens(
        normed_part, output_part, tokens, attn_gain, middle_grad, ffn_gain_part, replicas, 3
    )
    for where, from_ring, from_core in arrivals:
        filled = ffn_other(where, from_ring, from_core, act_grads, gate_cols, up_cols, filled)
    all_normed, all_activated, all_gate_grad, all_up_grad = filled

    gate_part = exchange(weight_grad(all_normed, all_gate_grad, BF16).reshape(n, rows, ff_cols))
    up_part = exchange(weight_grad(all_normed, all_up_grad, BF16).reshape(n, rows, ff_cols))
    down_grad = weight_grad(all_activated, down_grads, F32)
    output_grad = rep_sum(output_grad)
    qkv_part = rep_sum(exchange(qkv_grad.reshape(n, rows, q_cols + 2 * HEAD)))
    return (
        layer_output,
        tokens_grad,
        gains[0],
        *join_heads(qkv_part, q_cols),
        output_grad.astype(F32),
        gains[1],
        join_columns(gate_part),
        join_columns(up_part),
        down_grad,
    )


def per_device(
    tokens,
    attn_gain,
    query_weight,
    key_weight,
    value_weight,
    output_weight,
    ffn_gain,
    gate_weight,
    up_weight,
    down_weight,
    dealing,
    lengths,
    cotangent,
):
    n = lax.axis_size("shard")
    here = lax.axis_index("shard")
    local, width = tokens.shape
    total = local * n
    rows = query_weight.shape[0]
    ff_cols = gate_weight.shape[1] // n
    q_cols = query_weight.shape[1] // n
    copies = n // KV_HEADS
    own = here * local

    packed = jnp.arange(total, dtype=jnp.int32)
    segment, position = places(packed, lengths[0])
    cos_q, sin_q = rope_tables(position, q_cols)
    cos_k, sin_k = cos_q[:, :HEAD], sin_q[:, :HEAD]
    dealt = (dealing[0][:, None] == packed[None, :]).astype(BF16)

    def column_blocks(weight, cols):
        return weight.reshape(rows, n, cols).transpose(1, 0, 2)

    def head_blocks(weight):
        blocks = weight.reshape(rows, KV_HEADS, HEAD).transpose(1, 0, 2)
        return jnp.repeat(blocks, copies, axis=0)

    spread_cotangent = lax.all_gather(cotangent, ("rep", "shard"), axis=0, tiled=True)
    all_dealing = lax.all_gather(dealing, "rep", axis=0, tiled=True)
    qkv = exchange(
        jnp.concatenate(
            [column_blocks(query_weight, q_cols), head_blocks(key_weight), head_blocks(value_weight)],
            axis=2,
        )
    ).reshape(width, q_cols + 2 * HEAD)
    gate_cols = exchange(column_blocks(gate_weight, ff_cols)).reshape(width, ff_cols)
    up_cols = exchange(column_blocks(up_weight, ff_cols)).reshape(width, ff_cols)

    normed = gather_rows(rms_scale(tokens.astype(F32), attn_gain).astype(BF16))
    pre = mm(normed, qkv)
    queries = rotate(pre[:, :q_cols], cos_q, sin_q).astype(BF16)
    keys = rotate(pre[:, q_cols : q_cols + HEAD], cos_k, sin_k).astype(BF16)
    values = pre[:, q_cols + HEAD :].astype(BF16)
    attention = attention_forward(queries, jnp.concatenate([keys, values], axis=1), lengths)
    branch = scatter_rows(mm(attention, output_weight).astype(BF16))
    middle = tokens.astype(F32) + RESIDUAL_SCALE * branch.astype(F32)
    normed_ffn = gather_rows(rms_scale(middle, ffn_gain).astype(BF16))
    own_normed = lax.dynamic_slice_in_dim(normed_ffn, own, local)
    all_normed = lax.all_gather(own_normed, ("rep", "shard"), axis=0, tiled=True)

    reps = lax.axis_size("rep")
    group = lax.axis_index("rep")
    deals = (all_dealing[:, :, None] == packed[None, None, :]).astype(BF16)
    out_grad_all = lax.dot_general(
        deals,
        spread_cotangent.reshape(reps, total, width),
        (((1,), (1,)), ((0,), (0,))),
        preferred_element_type=F32,
    ).reshape(reps * total, width)
    down_grad_all = (RESIDUAL_SCALE * out_grad_all).astype(BF16)
    out_grad = lax.dynamic_slice_in_dim(out_grad_all, group * total + own, local)
    act_grad_all = mm_t(down_grad_all, down_weight)

    def ffn(rows_in, act_grad):
        gate = mm(rows_in, gate_cols)
        up = mm(rows_in, up_cols)
        sigmoid = jax.nn.sigmoid(gate)
        activated = (gate * sigmoid * up).astype(BF16)
        gate_grad = (act_grad * up * sigmoid * (1.0 + gate * (1.0 - sigmoid))).astype(BF16)
        up_grad = (act_grad * gate * sigmoid).astype(BF16)
        return activated, gate_grad, up_grad

    activated, gate_grad, up_grad = ffn(
        normed_ffn, lax.dynamic_slice_in_dim(act_grad_all, group * total, total)
    )
    normed_ffn_part = (mm_t(gate_grad, gate_cols) + mm_t(up_grad, up_cols)).astype(BF16)
    middle_part, ffn_gain_part = norm_pull(
        middle, ffn_gain, scatter_rows(normed_ffn_part).astype(F32)
    )
    middle_grad = out_grad + middle_part
    branch_grad = gather_rows((RESIDUAL_SCALE * middle_grad).astype(BF16))

    own_columns = lax.dynamic_slice_in_dim(dealt, own, local, axis=1)
    layer_output = scatter_rows(
        (
            RESIDUAL_SCALE * mm(mm(dealt, activated).astype(BF16), down_weight)
            + mm(own_columns, middle.astype(BF16))
        ).astype(BF16)
    )

    attention_grad = mm_t(branch_grad, output_weight).astype(BF16)
    dq, dk, dv = attention_gradients(
        queries, jnp.concatenate([keys, values], axis=1), attention_grad, lengths
    )
    pre_grad = jnp.concatenate(
        [
            unrotate(dq, cos_q, sin_q).astype(BF16),
            unrotate(dk, cos_k, sin_k).astype(BF16),
            dv.astype(BF16),
        ],
        axis=1,
    )
    normed_part = mm_t(pre_grad, qkv).astype(BF16)
    hidden_part, attn_gain_part = norm_pull(
        tokens.astype(F32), attn_gain, scatter_rows(normed_part).astype(F32)
    )
    tokens_grad = middle_grad + hidden_part

    activated, gate_grad, up_grad = ffn(all_normed, act_grad_all)
    gate_part = exchange(t_mm(all_normed, gate_grad).astype(BF16).reshape(n, rows, ff_cols))
    up_part = exchange(t_mm(all_normed, up_grad).astype(BF16).reshape(n, rows, ff_cols))
    down_part = t_mm(activated, down_grad_all)
    output_part = rep_sum(t_mm(attention, branch_grad).astype(BF16))
    qkv_part = rep_sum(exchange(t_mm(normed, pre_grad).astype(BF16).reshape(n, rows, q_cols + 2 * HEAD)))

    def join(blocks):
        return blocks.transpose(1, 0, 2).reshape(rows, -1).astype(F32)

    def join_heads(blocks):
        blocks = blocks.astype(F32).reshape(KV_HEADS, copies, rows, HEAD).sum(axis=1)
        return blocks.transpose(1, 0, 2).reshape(rows, KV_HEADS * HEAD)

    gain_grads = lax.psum(jnp.concatenate([attn_gain_part, ffn_gain_part]), ("rep", "shard"))
    return (
        layer_output,
        tokens_grad,
        gain_grads[0],
        join(qkv_part[:, :, :q_cols]),
        join_heads(qkv_part[:, :, q_cols : q_cols + HEAD]),
        join_heads(qkv_part[:, :, q_cols + HEAD :]),
        output_part.astype(F32),
        gain_grads[1],
        join(gate_part),
        join(up_part),
        down_part,
    )


def solution(mesh):
    both = P(("rep", "shard"), None)
    rowed = P("shard", None)
    return jax.shard_map(
        per_device_plane if mesh.shape["shard"] == 8 else per_device,
        mesh=mesh,
        in_specs=(
            both, P(), rowed, rowed, rowed, rowed, P(), rowed, rowed, rowed,
            P("rep", None), P("rep", None), both,
        ),
        out_specs=(both, both, P(), rowed, rowed, rowed, rowed, P(), rowed, rowed, rowed),
        check_vma=False,
    )
```

```python
import functools

import jax
import jax.numpy as jnp
from jax import lax
from jax.experimental import pallas as pl
from jax.experimental.pallas import tpu as pltpu
from jax.sharding import PartitionSpec as P

HEADS = 32
KV_HEADS = 8
HEAD = 64
EPSILON = 1e-05
RESIDUAL_SCALE = 0.22
SCORE_SCALE = 0.015625
ROPE_BASE = 10000000.0
MASKED = -1e30
BF16 = jnp.bfloat16
F32 = jnp.float32


def mm(a, b):
    return jnp.dot(a, b, preferred_element_type=F32)


def mm_t(a, b):
    return lax.dot_general(a, b, (((1,), (1,)), ((), ())), preferred_element_type=F32)


def t_mm(a, b):
    return lax.dot_general(a, b, (((0,), (0,)), ((), ())), preferred_element_type=F32)


def rms_scale(hidden, gain_vector):
    return (
        hidden
        * lax.rsqrt(jnp.mean(hidden * hidden, axis=-1, keepdims=True) + EPSILON)
        * gain_vector
    )


def places(packed_index, seq_lengths):
    seq_ends = jnp.cumsum(seq_lengths)
    starts = seq_ends - seq_lengths
    segment = jnp.sum((packed_index[:, None] >= seq_ends[None, :]).astype(jnp.int32), axis=1)
    chosen = segment[:, None] == jnp.arange(seq_lengths.shape[0], dtype=jnp.int32)[None, :]
    position = packed_index - jnp.sum(jnp.where(chosen, starts[None, :], 0), axis=1)
    return segment, position


def rope_tables(position, width):
    half = HEAD // 2
    frequency = ROPE_BASE ** (-(jnp.arange(half, dtype=F32) * 2.0) / (2.0 * half))
    turned = position.astype(F32)[:, None] * frequency[None, :]
    cosine, sine = jnp.cos(turned), jnp.sin(turned)
    cos_full = jnp.concatenate([cosine, cosine], axis=-1)
    sin_full = jnp.concatenate([-sine, sine], axis=-1)
    return jnp.tile(cos_full, (1, width // HEAD)), jnp.tile(sin_full, (1, width // HEAD))


def swap_halves(x):
    rows, width = x.shape
    half = HEAD // 2
    y = x.reshape(rows, width // HEAD, 2, half)
    return jnp.concatenate([y[:, :, 1:], y[:, :, :1]], axis=2).reshape(rows, width)


def rotate(x, cos_full, sin_full):
    return x * cos_full + swap_halves(x) * sin_full


def unrotate(x, cos_full, sin_full):
    return x * cos_full - swap_halves(x) * sin_full


def gather_rows(x):
    return lax.all_gather(x, "shard", axis=0, tiled=True)


def scatter_rows(x):
    return lax.psum_scatter(x, "shard", scatter_dimension=0, tiled=True)


def exchange(blocks):
    return lax.all_to_all(blocks, "shard", split_axis=0, concat_axis=0, tiled=True)


def rep_sum(x):
    count = lax.axis_size("rep")
    where = lax.axis_index("rep")
    half = count // 2
    for hop in range(half - 1):
        moved = lax.ppermute(
            x, "rep", [(hop, hop + 1), (count - 1 - hop, count - 2 - hop)]
        )
        x = (x.astype(F32) + moved.astype(F32)).astype(BF16)
    moved = lax.ppermute(x, "rep", [(half - 1, half), (half, half - 1)])
    x = (x.astype(F32) + moved.astype(F32)).astype(BF16)
    for hop in range(half - 1):
        near, far = half - 1 - hop, half + hop
        moved = lax.ppermute(x, "rep", [(near, near - 1), (far, far + 1)])
        x = jnp.where((where == near - 1) | (where == far + 1), moved, x)
    return x


def sum_over_replicas(arrays):
    count = lax.axis_size("rep")
    where = lax.axis_index("rep")
    half = count // 2
    for hop in range(half):
        inward = [(hop, hop + 1), (count - 1 - hop, count - 2 - hop)]
        moved = [lax.ppermute(x, "rep", inward) for x in arrays]
        yield moved
        arrays = [(x.astype(F32) + y.astype(F32)).astype(BF16) for x, y in zip(arrays, moved)]
    for hop in range(half - 1):
        near, far = half - 1 - hop, half + hop
        moved = [lax.ppermute(x, "rep", [(near, near - 1), (far, far + 1)]) for x in arrays]
        outside = (where == near - 1) | (where == far + 1)
        arrays = [jnp.where(outside, y, x) for x, y in zip(arrays, moved)]
    yield arrays


MESH = pl.DeviceIdType.MESH


def flip(index, bits):
    for weight in (1, 2, 4):
        if bits & weight:
            index = index + weight - 2 * weight * lax.rem(lax.div(index, weight), 2)
    return index


def send(src, dst, sems, k, target):
    return pltpu.make_async_remote_copy(
        src_ref=src,
        dst_ref=dst,
        send_sem=sems.at[0, k],
        recv_sem=sems.at[1, k],
        device_id={"shard": target},
        device_id_type=MESH,
    )


def greet(me, masks):
    barrier = pltpu.get_barrier_semaphore()
    for mask in masks:
        pl.semaphore_signal(
            barrier, inc=1, device_id={"shard": flip(me, mask)}, device_id_type=MESH
        )
    pl.semaphore_wait(barrier, len(masks))


GATHER_SEMS = 13
BULK = (12, 2, 2)


def gather_steps(me, out, sems):
    core, px, py, diag = (flip(me, mask) for mask in (1, 2, 4, 6))
    half = out.shape[1] // 2
    low, high, whole = pl.ds(0, half), pl.ds(half, half), pl.ds(0, 2 * half)

    def move(k, block, rows, target):
        ref = out.at[block, rows]
        copy = send(ref, ref, sems, k, target)
        copy.start()
        return copy

    x_low, y_high = move(0, me, low, px), move(1, me, high, py)
    own = move(2, me, whole, core)
    x_high, y_low = move(3, me, high, px), move(4, me, low, py)
    yield
    x_low.wait_recv()
    diag_low = move(5, px, low, py)
    pieces = [own, move(6, px, low, core)]
    yield
    y_high.wait_recv()
    diag_high = move(7, py, high, px)
    pieces.append(move(8, py, high, core))
    yield
    x_high.wait_recv()
    pieces.append(move(9, px, high, core))
    yield
    y_low.wait_recv()
    pieces.append(move(10, py, low, core))
    yield
    diag_low.wait_recv()
    pieces.append(move(11, diag, low, core))
    diag_high.wait_recv()
    pieces.append(move(12, diag, high, core))
    yield
    for copy in pieces:
        copy.wait_recv()
    for copy in [x_low, y_high, x_high, y_low, diag_low, diag_high] + pieces:
        copy.wait_send()


def gather_blocks(me, out, sems):
    for unused_step in gather_steps(me, out, sems):
        pass


SCATTER_SEMS = 10


def scatter_steps(me, partial, sib_out, sib_in, acc, x_out, x_in, y_out, y_in, sems):
    core, px, py = (flip(me, mask) for mask in (1, 2, 4))
    half = acc.shape[1] // 2
    masks = (6, 2, 4, 0)
    low, high = pl.ds(0, half), pl.ds(half, half)
    copies = []

    def move(src, dst, k, target):
        copy = send(src, dst, sems, k, target)
        copy.start()
        copies.append(copy)
        return copy

    inside = []
    for i, mask in enumerate(masks):
        sib_out[i] = partial(flip(core, mask)).astype(BF16)
        inside.append(move(sib_out.at[i], sib_in.at[i], i, core))
    yield
    for i, mask in enumerate(masks):
        term = partial(flip(me, mask))
        inside[i].wait_recv()
        acc[i] = term + sib_in[i].astype(F32)
        if mask == 6:
            x_out[0] = acc[i, low].astype(BF16)
            x_diag = move(x_out.at[0], x_in.at[0], 4, px)
            y_out[0] = acc[i, high].astype(BF16)
            y_diag = move(y_out.at[0], y_in.at[0], 5, py)
        if mask == 2:
            x_out[1] = acc[i, low].astype(BF16)
            x_near = move(x_out.at[1], x_in.at[1], 6, px)
        if mask == 4:
            y_out[1] = acc[i, high].astype(BF16)
            y_near = move(y_out.at[1], y_in.at[1], 7, py)
    yield
    x_diag.wait_recv()
    y_out[2] = (acc[2, low] + x_in[0].astype(F32)).astype(BF16)
    y_last = move(y_out.at[2], y_in.at[2], 8, py)
    y_diag.wait_recv()
    x_out[2] = (acc[1, high] + y_in[0].astype(F32)).astype(BF16)
    x_last = move(x_out.at[2], x_in.at[2], 9, px)
    yield
    x_near.wait_recv()
    y_near.wait_recv()
    y_last.wait_recv()
    acc[3, low] = acc[3, low] + x_in[1].astype(F32) + y_in[2].astype(F32)
    x_last.wait_recv()
    acc[3, high] = acc[3, high] + y_in[1].astype(F32) + x_in[2].astype(F32)
    yield
    for copy in copies:
        copy.wait_send()


def scatter_blocks(me, partial, *buffers):
    for unused_step in scatter_steps(me, partial, *buffers):
        pass
    return buffers[2][3]


def scatter_scratch(rows, width):
    half = rows // 2
    return [
        pltpu.VMEM((4, rows, width), BF16),
        pltpu.VMEM((4, rows, width), BF16),
        pltpu.VMEM((4, rows, width), F32),
        pltpu.VMEM((3, half, width), BF16),
        pltpu.VMEM((3, half, width), BF16),
        pltpu.VMEM((3, half, width), BF16),
        pltpu.VMEM((3, half, width), BF16),
        pltpu.SemaphoreType.DMA((2, SCATTER_SEMS)),
    ]


VMEM = pl.BlockSpec(memory_space=pltpu.VMEM)
SMEM = pl.BlockSpec(memory_space=pltpu.SMEM)
ANY = pl.BlockSpec(memory_space=pl.ANY)


def comm_params(collective_id, mebibytes):
    return pltpu.CompilerParams(
        collective_id=collective_id, has_side_effects=True, vmem_limit_bytes=mebibytes << 20
    )


def front(
    tokens, attn_gain, query_weight, key_weight, value_weight, output_weight, ffn_gain,
    gate_weight, up_weight, down_weight, dealing, lengths, cotangent, freq, replicas,
):
    local, width = tokens.shape
    total = 8 * local
    shard_rows = query_weight.shape[0]
    q_cols = query_weight.shape[1] // 8
    ff_cols = gate_weight.shape[1] // 8
    block = 256
    others = (1, 2, 3, 4, 5, 6, 7)

    def kernel(
        tok_ref, gain_ref, wq_hbm, wk_ref, wv_ref, wo_ref, fgain_ref, wg_hbm, wu_hbm,
        wd_ref, deal_ref, len_ref, cot_ref, freq_ref,
        n_ref, q_ref, kv_ref, att_ref, qw_ref, kvw_ref, wg_out, wu_out, mid_ref, nf_ref, dg_out, ag_out, cot_out,
        kv_stage, c_all, dg_own, ag_stage,
        sib_out, sib_in, acc, x_out, x_in, y_out, y_in, scatter_sems,
        n_sems, c_sems, nf_sems, qkv_sems, bulk_sems, ring_sems, pair_sems, local_sems,
    ):
        me = lax.axis_index("shard")
        group = lax.axis_index("rep")
        core = lax.rem(me, 2)
        after = lax.rem(group + 1, replicas)
        before = lax.rem(group + replicas - 1, replicas)

        barrier = pltpu.get_barrier_semaphore()
        for mask in others:
            pl.semaphore_signal(
                barrier, inc=1, device_id={"shard": flip(me, mask)}, device_id_type=MESH
            )
        for neighbour in (after, before):
            pl.semaphore_signal(
                barrier, inc=1, device_id={"rep": neighbour}, device_id_type=MESH
            )
        n_ref[me] = rms_scale(tok_ref[...].astype(F32), gain_ref[...]).astype(BF16)
        c_all[me] = cot_ref[...]
        for d in range(8):
            lanes = slice(d * HEAD, (d + 1) * HEAD)
            kv_stage[d] = jnp.concatenate([wk_ref[:, lanes], wv_ref[:, lanes]], axis=1)
        pl.semaphore_wait(barrier, len(others) + 2)

        gather_c = gather_steps(me, c_all, c_sems)
        next(gather_c)
        gather_n = gather_steps(me, n_ref, n_sems)
        next(gather_n)
        weights = []
        for mask in others:
            peer = flip(me, mask)
            columns = pl.ds(pl.multiple_of(peer * q_cols, q_cols), q_cols)
            weights.append(send(wq_hbm.at[:, columns], qw_ref.at[me], qkv_sems, 2 * mask - 2, peer))
            weights.append(send(kv_stage.at[peer], kvw_ref.at[me], qkv_sems, 2 * mask - 1, peer))
        for copy in weights:
            copy.start()
        own_columns = pl.ds(pl.multiple_of(me * ff_cols, ff_cols), ff_cols)
        own_q = pl.ds(pl.multiple_of(me * q_cols, q_cols), q_cols)
        gate_slot, up_slot = ag_stage.at[:shard_rows], ag_stage.at[pl.ds(shard_rows, shard_rows)]
        kept = [
            pltpu.make_async_copy(wg_hbm.at[:, own_columns], gate_slot, local_sems.at[0]),
            pltpu.make_async_copy(wu_hbm.at[:, own_columns], up_slot, local_sems.at[1]),
            pltpu.make_async_copy(wq_hbm.at[:, own_q], qw_ref.at[me], local_sems.at[2]),
        ]
        for copy in kept:
            copy.start()
        kvw_ref[me] = kv_stage[me]

        bulk, waiting = [], []
        for source, target in ((wg_hbm, wg_out), (wu_hbm, wu_out)):
            for part in range(2):
                rows = pl.ds(part * (shard_rows // 2), shard_rows // 2)
                for mask in (2, 4, 6, 3, 5, 7, 1):
                    waiting.append((source, target, rows, mask))

        def more(count):
            for unused in range(min(count, len(waiting))):
                source, target, rows, mask = waiting.pop(0)
                peer = flip(me, mask)
                columns = pl.ds(pl.multiple_of(peer * ff_cols, ff_cols), ff_cols)
                copy = send(
                    source.at[rows, columns], target.at[me, rows], bulk_sems, len(bulk), peer
                )
                copy.start()
                bulk.append(copy)

        for unused in gather_c:
            pass

        def permute(first):
            for i in range(total // 2 // block):
                row0 = pl.multiple_of(first + i * block, block)
                packed = row0 + lax.broadcasted_iota(jnp.int32, (block, total), 0)
                chosen = (deal_ref[...] == packed).astype(BF16)
                dealt = mm(chosen, c_all[...].reshape(total, width))
                dg_own[pl.ds(row0, block), :] = (RESIDUAL_SCALE * dealt).astype(BF16)

        near = pl.multiple_of(core * (total // 2), total // 2)
        far = pl.multiple_of((1 - core) * (total // 2), total // 2)
        half = pl.ds(near, total // 2)

        def ring(hop):
            held = lax.rem(group + replicas - hop, replicas)
            ref = dg_out.at[held, half]
            copy = pltpu.make_async_remote_copy(
                src_ref=dg_own.at[half] if hop == 0 else ref,
                dst_ref=ref,
                send_sem=ring_sems.at[0, hop],
                recv_sem=ring_sems.at[1, hop],
                device_id={"rep": after},
                device_id_type=MESH,
            )
            copy.start()
            return copy

        def share(hop):
            held = lax.rem(group + replicas - hop, replicas)
            ref = dg_out.at[held, half]
            copy = send(ref, ref, pair_sems, hop - 1, flip(me, 1))
            copy.start()
            return copy

        permute(near)
        hops, shares = [ring(0)], []
        for unused in range(4):
            next(gather_n)
        permute(far)
        packed = me * local + lax.broadcasted_iota(jnp.int32, (local, total), 0)
        chosen = (deal_ref[...] == packed).astype(BF16)
        cot_out[...] = mm(chosen, c_all[...].reshape(total, width)).astype(BF16)
        store = pltpu.make_async_copy(dg_own, dg_out.at[group], local_sems.at[3])
        store.start()
        for unused in gather_n:
            pass
        for copy in kept:
            copy.wait()
        kept = [
            pltpu.make_async_copy(gate_slot, wg_out.at[me], local_sems.at[0]),
            pltpu.make_async_copy(up_slot, wu_out.at[me], local_sems.at[1]),
        ]
        for copy in kept:
            copy.start()
        for copy in weights:
            copy.wait_recv()
        more(BULK[0])
        for i in range(total // block):
            rows = pl.ds(i * block, block)
            x = n_ref[pl.ds(i * block // local, block // local)].reshape(block, width)
            cosine, sine = lane_rope(i * block, block, freq_ref[...], len_ref)
            pre = mm(x, qw_ref[...].reshape(width, q_cols))
            for j in range(q_cols // (2 * HEAD)):
                lanes = slice(j * 2 * HEAD, (j + 1) * 2 * HEAD)
                y = pre[:, lanes]
                q_ref[rows, lanes] = (y * cosine + lane_swap(y) * sine).astype(BF16)
            cosine, sine = keys_only(cosine, sine)
            y = mm(x, kvw_ref[...].reshape(width, 2 * HEAD))
            kv_ref[rows, :] = (y * cosine + lane_swap(y) * sine).astype(BF16)
        attend(q_cols // HEAD, block, q_ref, kv_ref, len_ref, att_ref)

        def partial(d):
            return mm(att_ref[pl.ds(pl.multiple_of(d * local, local), local), :], wo_ref[...])

        def next_hop():
            hop = len(hops)
            hops[-1].wait_recv()
            if hop < replicas - 1:
                hops.append(ring(hop))
            shares.append(share(hop))

        def act_grad(held, source):
            for i in range(total // block):
                rows = pl.ds(i * block, block)
                ag_stage[rows, :] = mm_t(source[rows, :], wd_ref[...]).astype(BF16)
            copy = pltpu.make_async_copy(ag_stage, ag_out.at[held], local_sems.at[3])
            copy.start()
            copy.wait()

        next_hop()
        scatter = scatter_steps(
            me, partial, sib_out, sib_in, acc, x_out, x_in, y_out, y_in, scatter_sems
        )
        next(scatter)
        more(BULK[1])
        for unused in scatter:
            pass
        branch = acc[3]
        middle = tok_ref[...].astype(F32) + RESIDUAL_SCALE * branch
        mid_ref[...] = middle
        nf_ref[me] = rms_scale(middle, fgain_ref[...]).astype(BF16)
        gather_nf = gather_steps(me, nf_ref, nf_sems)
        next(gather_nf)
        more(BULK[2])
        for unused in gather_nf:
            pass
        more(len(waiting))
        store.wait()
        for copy in kept:
            copy.wait()
        act_grad(group, dg_own)
        hops[0].wait_send()
        if len(shares) < replicas - 1:
            next_hop()
        for done in range(replicas - 1):
            if len(shares) < done + 1:
                next_hop()
            held = lax.rem(group + replicas - 1 - done, replicas)
            shares[done].wait_recv()
            load = pltpu.make_async_copy(dg_out.at[held], dg_own, local_sems.at[3])
            load.start()
            load.wait()
            act_grad(held, dg_own)
        for copy in bulk:
            copy.wait_recv()
        for copy in weights + bulk + hops[1:] + shares:
            copy.wait_send()

    rows8 = jax.ShapeDtypeStruct((8, local, width), BF16)
    half_sems = pltpu.SemaphoreType.DMA
    outs = pl.pallas_call(
        kernel,
        out_shape=(
            rows8,
            jax.ShapeDtypeStruct((total, q_cols), BF16),
            jax.ShapeDtypeStruct((total, 2 * HEAD), BF16),
            jax.ShapeDtypeStruct((total, q_cols), BF16),
            jax.ShapeDtypeStruct((8, shard_rows, q_cols), BF16),
            jax.ShapeDtypeStruct((8, shard_rows, 2 * HEAD), BF16),
            jax.ShapeDtypeStruct((8, shard_rows, ff_cols), BF16),
            jax.ShapeDtypeStruct((8, shard_rows, ff_cols), BF16),
            jax.ShapeDtypeStruct((local, width), F32),
            rows8,
            jax.ShapeDtypeStruct((replicas, total, width), BF16),
            jax.ShapeDtypeStruct((replicas, total, ff_cols), BF16),
            jax.ShapeDtypeStruct((local, width), BF16),
        ),
        in_specs=[VMEM, VMEM, ANY, VMEM, VMEM, VMEM, VMEM, ANY, ANY, VMEM, VMEM, SMEM, VMEM, VMEM],
        out_specs=[VMEM] * 6 + [ANY, ANY, VMEM, VMEM, ANY, ANY, VMEM],
        scratch_shapes=[
            pltpu.VMEM((8, shard_rows, 2 * HEAD), BF16),
            pltpu.VMEM((8, local, width), BF16),
            pltpu.VMEM((total, width), BF16),
            pltpu.VMEM((total, ff_cols), BF16),
        ]
        + scatter_scratch(local, width)
        + [
            half_sems((2, GATHER_SEMS)),
            half_sems((2, GATHER_SEMS)),
            half_sems((2, GATHER_SEMS)),
            half_sems((2, 14)),
            half_sems((2, 28)),
            half_sems((2, replicas)),
            half_sems((2, replicas)),
            half_sems((4,)),
        ],
        compiler_params=comm_params(0, 56),
        cost_estimate=pl.CostEstimate(
            flops=200_000_000_000, bytes_accessed=50 << 20, transcendentals=total * total
        ),
        name="front",
    )(
        tokens, attn_gain[None, :], query_weight, key_weight, value_weight, output_weight,
        ffn_gain[None, :], gate_weight, up_weight, down_weight, dealing, lengths, cotangent, freq,
    )
    normed, q, kv, attention, qw, kvw, wg, wu, middle, nf, dg, ag, cot = outs
    return (
        normed.reshape(total, width), q, kv, attention,
        qw.reshape(width, q_cols), kvw.reshape(width, 2 * HEAD),
        wg.reshape(width, ff_cols), wu.reshape(width, ff_cols),
        middle, nf.reshape(total, width), dg, ag, cot,
    )


def norm_pull(x, gain, grad):
    scale = lax.rsqrt(jnp.mean(x * x, axis=-1, keepdims=True) + EPSILON)
    pulled = gain * grad
    rows_part = scale * pulled - x * (
        scale * scale * scale * jnp.mean(pulled * x, axis=-1, keepdims=True)
    )
    return rows_part, jnp.sum(grad * x * scale, axis=0, keepdims=True)


def pull_gather(part, middle, gain, out_grad, collective_id):
    rows, width = middle.shape

    def kernel(p_ref, m_ref, gain_ref, g_ref, mg_ref, gain_part, out, *scratch):
        me = lax.axis_index("shard")
        *buffers, scatter_sems, sems = scratch
        greet(me, (1, 2, 4))
        grad = scatter_blocks(
            me,
            lambda d: p_ref[pl.ds(pl.multiple_of(d * rows, rows), rows), :].astype(F32),
            *buffers,
            scatter_sems,
        )
        rows_part, gain_row = norm_pull(m_ref[...], gain_ref[...], grad)
        gain_part[...] = gain_row
        middle_grad = g_ref[...].astype(F32) + rows_part
        mg_ref[...] = middle_grad
        out[me] = (RESIDUAL_SCALE * middle_grad).astype(BF16)
        gather_blocks(me, out, sems)

    return pl.pallas_call(
        kernel,
        out_shape=(
            jax.ShapeDtypeStruct((rows, width), F32),
            jax.ShapeDtypeStruct((1, width), F32),
            jax.ShapeDtypeStruct((8, rows, width), BF16),
        ),
        in_specs=[VMEM] * 4,
        out_specs=[VMEM] * 3,
        scratch_shapes=scatter_scratch(rows, width)
        + [pltpu.SemaphoreType.DMA((2, GATHER_SEMS))],
        compiler_params=comm_params(collective_id, 44),
        cost_estimate=pl.CostEstimate(
            flops=50_000_000_000, bytes_accessed=50 * rows * width, transcendentals=rows
        ),
        name="pull_gather",
    )(part, middle, gain[None, :], out_grad)


def pull_tokens(part, out_part, hidden, gain, middle_grad, other_gain, replicas, collective_id):
    rows, width = middle_grad.shape
    levels = [("shard", 1), ("shard", 2), ("shard", 4)]
    level = 1
    while level < replicas:
        levels.append(("rep", level))
        level *= 2

    def kernel(
        p_ref, o_ref, h_ref, gain_ref, mg_ref, og_ref, out, lay, gains, gain_in, gain_out, gain_sems, *scratch
    ):
        me = lax.axis_index("shard")
        group = lax.axis_index("rep")
        first, second = scratch[:8], scratch[8:]
        barrier = pltpu.get_barrier_semaphore()
        peers = []
        for axis, weight in levels:
            index = me if axis == "shard" else group
            peers.append({axis: index + weight - 2 * weight * lax.rem(lax.div(index, weight), 2)})
        for peer in peers:
            pl.semaphore_signal(barrier, inc=1, device_id=peer, device_id_type=MESH)
        pl.semaphore_wait(barrier, len(peers))

        def blocks_of(ref):
            return lambda d: ref[pl.ds(pl.multiple_of(d * rows, rows), rows), :].astype(F32)

        grads = scatter_steps(me, blocks_of(p_ref), *first)
        outputs = scatter_steps(me, blocks_of(o_ref), *second)
        next(grads)
        next(grads)
        next(outputs)
        next(grads)
        next(outputs)
        next(grads)
        rows_part, gain_row = norm_pull(h_ref[...].astype(F32), gain_ref[...], first[2][3])
        out[...] = mg_ref[...] + rows_part
        total = jnp.concatenate([gain_row, og_ref[...]], axis=0)
        for i, peer in enumerate(peers):
            gain_out[i] = total
            copy = pltpu.make_async_remote_copy(
                src_ref=gain_out.at[i],
                dst_ref=gain_in.at[i],
                send_sem=gain_sems.at[0, i],
                recv_sem=gain_sems.at[1, i],
                device_id=peer,
                device_id_type=MESH,
            )
            copy.start()
            if i == 1:
                next(outputs)
            copy.wait()
            total = total + gain_in[i]
        gains[...] = total
        next(outputs)
        lay[...] = second[2][3].astype(BF16)
        for steps in (grads, outputs):
            for unused in steps:
                pass

    return pl.pallas_call(
        kernel,
        out_shape=(
            jax.ShapeDtypeStruct((rows, width), F32),
            jax.ShapeDtypeStruct((rows, width), BF16),
            jax.ShapeDtypeStruct((2, width), F32),
        ),
        in_specs=[VMEM] * 6,
        out_specs=[VMEM] * 3,
        scratch_shapes=[
            pltpu.VMEM((len(levels), 2, width), F32),
            pltpu.VMEM((len(levels), 2, width), F32),
            pltpu.SemaphoreType.DMA((2, len(levels))),
        ]
        + scatter_scratch(rows, width)
        + scatter_scratch(rows, width),
        compiler_params=comm_params(collective_id, 52),
        cost_estimate=pl.CostEstimate(
            flops=50_000_000_000, bytes_accessed=50 * rows * width, transcendentals=rows
        ),
        name="pull_tokens",
    )(part, out_part, hidden, gain[None, :], middle_grad, other_gain)


def softmax_block(q, k, allowed):
    scores = SCORE_SCALE * mm_t(q, k)
    scores = jnp.where(allowed, scores, MASKED)
    top = jnp.max(scores, axis=-1, keepdims=True)
    weight = jnp.exp(scores - top)
    return weight * (1.0 / jnp.sum(weight, axis=-1, keepdims=True))


def allowed_block(row0, cols, start):
    shape = (start.shape[0], cols)
    query = row0 + lax.broadcasted_iota(jnp.int32, shape, 0)
    key = lax.broadcasted_iota(jnp.int32, shape, 1)
    return (key >= start) & (key <= query)


def sequence_starts(row0, shape, lengths_ref):
    row = row0 + lax.broadcasted_iota(jnp.int32, shape, 0)
    start = jnp.zeros(shape, jnp.int32)
    end = 0
    for i in range(lengths_ref.shape[1]):
        length = lengths_ref[0, i]
        end = end + length
        start = start + jnp.where(row >= end, length, 0)
    return start


def attend(heads, block, q_ref, kv_ref, lengths_ref, o_ref):
    total = kv_ref.shape[0]
    for i in range(total // block):
        cols = (i + 1) * block
        rows = pl.ds(i * block, block)
        allowed = allowed_block(
            i * block, cols, sequence_starts(i * block, (block, 1), lengths_ref)
        )
        kv = kv_ref[:cols, :]
        k, v = kv[:, :HEAD], kv[:, HEAD:]
        for h in range(heads):
            lanes = slice(h * HEAD, (h + 1) * HEAD)
            probs = softmax_block(q_ref[rows, lanes], k, allowed)
            o_ref[rows, lanes] = mm(probs.astype(BF16), v).astype(BF16)


def attend_back(heads, block, q_ref, kv_ref, g_ref, lengths_ref, dq_ref, dk_ref, dv_ref):
    total = kv_ref.shape[0]
    dk_ref[...] = jnp.zeros_like(dk_ref)
    dv_ref[...] = jnp.zeros_like(dv_ref)
    for i in range(total // block):
        cols = (i + 1) * block
        rows = pl.ds(i * block, block)
        allowed = allowed_block(
            i * block, cols, sequence_starts(i * block, (block, 1), lengths_ref)
        )
        kv = kv_ref[:cols, :]
        k, v = kv[:, :HEAD], kv[:, HEAD:]
        for h in range(heads):
            lanes = slice(h * HEAD, (h + 1) * HEAD)
            q, g = q_ref[rows, lanes], g_ref[rows, lanes]
            probs = softmax_block(q, k, allowed)
            probs_grad = mm_t(g, v)
            delta = jnp.sum(probs * probs_grad, axis=-1, keepdims=True)
            score_grad = (probs * (probs_grad - delta)).astype(BF16)
            dq_ref[rows, lanes] = SCORE_SCALE * mm(score_grad, k)
            dk_ref[:cols, :] += SCORE_SCALE * t_mm(score_grad, q)
            dv_ref[:cols, :] += t_mm(probs.astype(BF16), g)


def attention_forward(q, kv, lengths):
    total, width = q.shape

    def kernel(q_ref, kv_ref, lengths_ref, o_ref):
        attend(width // HEAD, 256, q_ref, kv_ref, lengths_ref, o_ref)

    return pl.pallas_call(
        kernel,
        out_shape=jax.ShapeDtypeStruct((total, width), BF16),
        in_specs=[VMEM, VMEM, SMEM],
        out_specs=VMEM,
        compiler_params=pltpu.CompilerParams(vmem_limit_bytes=40 << 20),
        name="attention_forward",
    )(q, kv, lengths)


def attention_gradients(q, kv, grad, lengths):
    total, width = q.shape

    def kernel(q_ref, kv_ref, g_ref, lengths_ref, dq_ref, dk_ref, dv_ref):
        attend_back(width // HEAD, 256, q_ref, kv_ref, g_ref, lengths_ref, dq_ref, dk_ref, dv_ref)

    return pl.pallas_call(
        kernel,
        out_shape=(
            jax.ShapeDtypeStruct((total, width), F32),
            jax.ShapeDtypeStruct((total, HEAD), F32),
            jax.ShapeDtypeStruct((total, HEAD), F32),
        ),
        in_specs=[VMEM, VMEM, VMEM, SMEM],
        out_specs=[VMEM] * 3,
        compiler_params=pltpu.CompilerParams(vmem_limit_bytes=40 << 20),
        name="attention_gradients",
    )(q, kv, grad, lengths)


def lane_rope(row0, rows, freq, lengths_ref):
    shape = (rows, 2 * HEAD)
    row = row0 + lax.broadcasted_iota(jnp.int32, shape, 0)
    position = row - sequence_starts(row0, shape, lengths_ref)
    turned = position.astype(F32) * freq
    lane = lax.broadcasted_iota(jnp.int32, shape, 1)
    first = lax.rem(lane, HEAD) < HEAD // 2
    sine = jnp.sin(turned)
    return jnp.cos(turned), jnp.where(first, -sine, sine)


def lane_swap(x):
    half = HEAD // 2
    lane = lax.broadcasted_iota(jnp.int32, x.shape, 1)
    first = lax.rem(lane, HEAD) < half
    return jnp.where(first, pltpu.roll(x, 2 * HEAD - half, 1), pltpu.roll(x, half, 1))


def keys_only(cosine, sine):
    lane = lax.broadcasted_iota(jnp.int32, cosine.shape, 1)
    return jnp.where(lane < HEAD, cosine, 1.0), jnp.where(lane < HEAD, sine, 0.0)


def attention_backward(
    branch_grad, output_weight, attention, q, kv, normed, q_weight, kv_weight, lengths, freq
):
    total, q_cols = q.shape
    width = normed.shape[1]
    block = 256

    def kernel(
        bg_ref, wo_ref, a_ref, q_ref, kv_ref, n_ref, qw_ref, kvw_ref, len_ref, freq_ref,
        dn_ref, dqkv_ref, dwo_ref, g_ref, dq_ref, dk_ref, dv_ref, pq_ref, pkv_ref,
    ):
        for i in range(total // block):
            rows = pl.ds(i * block, block)
            g_ref[rows, :] = mm_t(bg_ref[rows, :], wo_ref[...]).astype(BF16)
        attend_back(
            q_cols // HEAD, block, q_ref, kv_ref, g_ref, len_ref, dq_ref, dk_ref, dv_ref
        )
        for i in range(total // block):
            rows = pl.ds(i * block, block)
            cosine, sine = lane_rope(i * block, block, freq_ref[...], len_ref)
            for j in range(q_cols // (2 * HEAD)):
                lanes = slice(j * 2 * HEAD, (j + 1) * 2 * HEAD)
                x = dq_ref[rows, lanes]
                pq_ref[rows, lanes] = (x * cosine - lane_swap(x) * sine).astype(BF16)
            cosine, sine = keys_only(cosine, sine)
            x = jnp.concatenate([dk_ref[rows, :], dv_ref[rows, :]], axis=1)
            pkv_ref[rows, :] = (x * cosine - lane_swap(x) * sine).astype(BF16)
            dn_ref[rows, :] = (
                mm_t(pq_ref[rows, :], qw_ref[...]) + mm_t(pkv_ref[rows, :], kvw_ref[...])
            ).astype(BF16)
        for i in range(width // 512):
            cols = slice(i * 512, (i + 1) * 512)
            dqkv_ref[cols, :q_cols] = t_mm(n_ref[:, cols], pq_ref[...]).astype(BF16)
            dqkv_ref[cols, q_cols:] = t_mm(n_ref[:, cols], pkv_ref[...]).astype(BF16)
            dwo_ref[:, cols] = t_mm(a_ref[...], bg_ref[:, cols]).astype(BF16)

    return pl.pallas_call(
        kernel,
        out_shape=(
            jax.ShapeDtypeStruct((total, width), BF16),
            jax.ShapeDtypeStruct((width, q_cols + 2 * HEAD), BF16),
            jax.ShapeDtypeStruct((q_cols, width), BF16),
        ),
        in_specs=[VMEM] * 8 + [SMEM, VMEM],
        out_specs=[VMEM] * 3,
        scratch_shapes=[
            pltpu.VMEM((total, q_cols), BF16),
            pltpu.VMEM((total, q_cols), F32),
            pltpu.VMEM((total, HEAD), F32),
            pltpu.VMEM((total, HEAD), F32),
            pltpu.VMEM((total, q_cols), BF16),
            pltpu.VMEM((total, 2 * HEAD), BF16),
        ],
        compiler_params=pltpu.CompilerParams(vmem_limit_bytes=56 << 20),
        cost_estimate=pl.CostEstimate(flops=30_000_000_000, bytes_accessed=30 << 20, transcendentals=total * total),
        name="attention_backward",
    )(branch_grad, output_weight, attention, q, kv, normed, q_weight, kv_weight, lengths, freq)


def ffn_rows(nf, act_grad, wg, wu):
    gate, up = mm(nf, wg), mm(nf, wu)
    act_grad = act_grad.astype(F32)
    sigmoid = 1.0 / (1.0 + jnp.exp(-gate))
    silu = gate * sigmoid
    activated = (silu * up).astype(BF16)
    gate_grad = (act_grad * up * sigmoid * (1.0 + gate * (1.0 - sigmoid))).astype(BF16)
    return activated, gate_grad, (act_grad * silu).astype(BF16)


def ffn_own(group, nf, act_grads, wg, wu):
    groups, total, cols = act_grads.shape
    width = nf.shape[1]
    block = 256

    def kernel(g_ref, nf_ref, ag_ref, wg_ref, wu_ref, na_ref, act_ref, gg_ref, ug_ref, dn_ref):
        nf = nf_ref[...]
        act, gg, ug = ffn_rows(nf, ag_ref[0], wg_ref[...], wu_ref[...])
        na_ref[0], act_ref[0], gg_ref[0], ug_ref[0] = nf, act, gg, ug
        dn_ref[...] = (mm_t(gg, wg_ref[...]) + mm_t(ug, wu_ref[...])).astype(BF16)

    mine = pl.BlockSpec((1, block, width), lambda i, g: (g[0], i, 0))
    hid = pl.BlockSpec((1, block, cols), lambda i, g: (g[0], i, 0))
    plain = pl.BlockSpec((block, width), lambda i, g: (i, 0))
    whole = [
        pl.BlockSpec(w.shape, lambda i, g: (0, 0), pipeline_mode=pl.Buffered(1)) for w in (wg, wu)
    ]
    hidden = jax.ShapeDtypeStruct((groups, total, cols), BF16)
    return pl.pallas_call(
        kernel,
        grid_spec=pltpu.PrefetchScalarGridSpec(
            num_scalar_prefetch=1,
            grid=(total // block,),
            in_specs=[plain, hid] + whole,
            out_specs=[mine, hid, hid, hid, plain],
        ),
        out_shape=(
            jax.ShapeDtypeStruct((groups, total, width), BF16),
            hidden,
            hidden,
            hidden,
            jax.ShapeDtypeStruct((total, width), BF16),
        ),
        compiler_params=pltpu.CompilerParams(vmem_limit_bytes=48 << 20),
        cost_estimate=pl.CostEstimate(
            flops=12 * total * width * cols, bytes_accessed=40 << 20, transcendentals=total * cols
        ),
        name="ffn_own",
    )(group, nf, act_grads, wg, wu)


def ffn_other(where, held, fetched, act_grads, wg, wu, filled):
    groups, total, cols = act_grads.shape
    width = held.shape[1]
    block = 256
    per_half = total // 2 // block

    def kernel(w_ref, held_ref, fetched_ref, ag_ref, wg_ref, wu_ref, *rest):
        na_ref, act_ref, gg_ref, ug_ref, nf_ref = rest[4:]
        i = pl.program_id(0)

        @pl.when(i < per_half)
        def _():
            nf_ref[...] = held_ref[...]

        @pl.when(i >= per_half)
        def _():
            nf_ref[...] = fetched_ref[...]

        nf = nf_ref[...]
        act, gg, ug = ffn_rows(nf, ag_ref[0], wg_ref[...], wu_ref[...])
        na_ref[0], act_ref[0], gg_ref[0], ug_ref[0] = nf, act, gg, ug

    def row(i, w):
        half = jnp.where(i < per_half, w[1], 1 - w[1])
        return half * per_half + lax.rem(i, per_half)

    mine = pl.BlockSpec((1, block, width), lambda i, w: (w[0], row(i, w), 0))
    hid = pl.BlockSpec((1, block, cols), lambda i, w: (w[0], row(i, w), 0))
    first = pl.BlockSpec((block, width), lambda i, w: (jnp.minimum(i, per_half - 1), 0))
    last = pl.BlockSpec((block, width), lambda i, w: (jnp.maximum(i - per_half, 0), 0))
    whole = [
        pl.BlockSpec(w.shape, lambda i, g: (0, 0), pipeline_mode=pl.Buffered(1)) for w in (wg, wu)
    ]
    hidden = jax.ShapeDtypeStruct((groups, total, cols), BF16)
    return pl.pallas_call(
        kernel,
        grid_spec=pltpu.PrefetchScalarGridSpec(
            num_scalar_prefetch=1,
            grid=(2 * per_half,),
            in_specs=[first, last, hid] + whole + [pl.BlockSpec(memory_space=pl.ANY)] * 4,
            out_specs=[mine, hid, hid, hid],
            scratch_shapes=[pltpu.VMEM((block, width), BF16)],
        ),
        out_shape=(jax.ShapeDtypeStruct((groups, total, width), BF16), hidden, hidden, hidden),
        input_output_aliases={6: 0, 7: 1, 8: 2, 9: 3},
        compiler_params=pltpu.CompilerParams(vmem_limit_bytes=48 << 20),
        cost_estimate=pl.CostEstimate(
            flops=8 * total * width * cols, bytes_accessed=40 << 20, transcendentals=total * cols
        ),
        name="ffn_other",
    )(where, held, fetched, act_grads, wg, wu, *filled)


def output_rows(where, activated, down_weight, middle, deal, total):
    groups, total, cols = activated.shape
    local, width = middle.shape
    block = 256

    def kernel(w_ref, act_ref, wd_ref, mid_ref, deal_ref, o_ref, rows_ref):
        for i in range(total // block):
            rows = pl.ds(i * block, block)
            rows_ref[rows, :] = (RESIDUAL_SCALE * mm(act_ref[0, rows, :], wd_ref[...])).astype(BF16)
        own = pl.ds(pl.multiple_of(w_ref[1] * local, local), local)
        rows_ref[own, :] = (rows_ref[own, :].astype(F32) + mid_ref[...]).astype(BF16)
        for i in range(total // block):
            rows = pl.ds(i * block, block)
            packed = lax.broadcasted_iota(jnp.int32, (block, total), 1)
            chosen = (deal_ref[rows, :] == packed).astype(BF16)
            o_ref[rows, :] = mm(chosen, rows_ref[...]).astype(BF16)

    def full(shape):
        return pl.BlockSpec(shape, lambda i, w: (0,) * len(shape), pipeline_mode=pl.Buffered(1))

    return pl.pallas_call(
        kernel,
        grid_spec=pltpu.PrefetchScalarGridSpec(
            num_scalar_prefetch=1,
            grid=(1,),
            in_specs=[
                pl.BlockSpec((1, total, cols), lambda i, w: (w[0], 0, 0), pipeline_mode=pl.Buffered(1)),
                full(down_weight.shape),
                full(middle.shape),
                full(deal.shape),
            ],
            out_specs=full((total, width)),
            scratch_shapes=[pltpu.VMEM((total, width), BF16)],
        ),
        out_shape=jax.ShapeDtypeStruct((total, width), BF16),
        compiler_params=pltpu.CompilerParams(vmem_limit_bytes=48 << 20),
        cost_estimate=pl.CostEstimate(
            flops=2 * total * width * (cols + total) * 2, bytes_accessed=12 << 20, transcendentals=0
        ),
        name="output_rows",
    )(where, activated, down_weight, middle, deal)


def join_columns(blocks):
    n, rows, cols = blocks.shape

    def kernel(b_ref, o_ref):
        o_ref[...] = b_ref[0].astype(F32)

    return pl.pallas_call(
        kernel,
        grid=(n,),
        in_specs=[pl.BlockSpec((1, rows, cols), lambda i: (i, 0, 0))],
        out_specs=pl.BlockSpec((rows, cols), lambda i: (0, i)),
        out_shape=jax.ShapeDtypeStruct((rows, n * cols), F32),
        cost_estimate=pl.CostEstimate(
            flops=n * rows * cols, bytes_accessed=6 * n * rows * cols, transcendentals=0
        ),
        name="join_columns",
    )(blocks)


def join_heads(blocks, q_cols):
    n, rows, cols = blocks.shape

    def kernel(b_ref, q_ref, k_ref, v_ref):
        for i in range(n):
            q_ref[:, i * q_cols : (i + 1) * q_cols] = b_ref[i, :, :q_cols].astype(F32)
        kv = [b_ref[i, :, q_cols:].astype(F32) for i in range(n)]
        k_ref[...] = jnp.concatenate([x[:, :HEAD] for x in kv], axis=1)
        v_ref[...] = jnp.concatenate([x[:, HEAD:] for x in kv], axis=1)

    return pl.pallas_call(
        kernel,
        out_shape=(
            jax.ShapeDtypeStruct((rows, n * q_cols), F32),
            jax.ShapeDtypeStruct((rows, n * HEAD), F32),
            jax.ShapeDtypeStruct((rows, n * HEAD), F32),
        ),
        name="join_heads",
    )(blocks)


def weight_grad(left, right, dtype):
    groups, total, m = left.shape
    n = right.shape[2]
    block = 512
    steps = groups * total // block

    def kernel(l_ref, r_ref, o_ref, acc):
        k = pl.program_id(0)
        term = t_mm(l_ref[...], r_ref[...])

        @pl.when(k == 0)
        def _():
            acc[...] = term

        @pl.when(k > 0)
        def _():
            acc[...] += term

        @pl.when(k == steps - 1)
        def _():
            o_ref[...] = acc[...].astype(o_ref.dtype)

    return pl.pallas_call(
        kernel,
        grid=(steps,),
        in_specs=[
            pl.BlockSpec((block, m), lambda k: (k, 0)),
            pl.BlockSpec((block, n), lambda k: (k, 0)),
        ],
        out_specs=pl.BlockSpec((m, n), lambda k: (0, 0), pipeline_mode=pl.Buffered(1)),
        out_shape=jax.ShapeDtypeStruct((m, n), dtype),
        scratch_shapes=[pltpu.VMEM((m, n), F32)],
        compiler_params=pltpu.CompilerParams(vmem_limit_bytes=56 << 20),
        cost_estimate=pl.CostEstimate(
            flops=2 * groups * total * m * n, bytes_accessed=2 * groups * total * (m + n), transcendentals=0
        ),
        name="weight_grad",
    )(left.reshape(groups * total, m), right.reshape(groups * total, n))


def per_device_plane(
    tokens, attn_gain, query_weight, key_weight, value_weight, output_weight, ffn_gain,
    gate_weight, up_weight, down_weight, dealing, lengths, cotangent,
):
    n = 8
    here = lax.axis_index("shard")
    group = lax.axis_index("rep")
    replicas = lax.axis_size("rep")
    local, width = tokens.shape
    total = local * n
    rows = query_weight.shape[0]
    q_cols = query_weight.shape[1] // n
    ff_cols = gate_weight.shape[1] // n
    core = lax.rem(here, 2)
    half = HEAD // 2
    freq = ROPE_BASE ** (-(jnp.arange(half, dtype=F32) * 2.0) / (2.0 * half))
    freq = jnp.tile(freq, 4)[None, :]

    (
        normed, q, kv, attention, q_weight, kv_weight, gate_cols, up_cols,
        middle, normed_ffn, down_grads, act_grads, cot_own,
    ) = front(
        tokens, attn_gain, query_weight, key_weight, value_weight, output_weight, ffn_gain,
        gate_weight, up_weight, down_weight, dealing, lengths, cotangent, freq, replicas,
    )

    held = lax.dynamic_slice_in_dim(normed_ffn, core * (total // 2), total // 2)
    onward = [(i, (i + 1) % replicas) for i in range(replicas)]
    beside = [(i, i ^ 1) for i in range(n)]
    arrivals = []
    for hop in range(1, replicas):
        held = lax.ppermute(held, "rep", onward)
        where = jnp.stack([lax.rem(group + replicas - hop, replicas), core]).astype(jnp.int32)
        arrivals.append((where, held, lax.ppermute(held, "shard", beside)))

    *filled, normed_ffn_part = ffn_own(
        group.astype(jnp.int32)[None], normed_ffn, act_grads, gate_cols, up_cols
    )
    middle_grad, ffn_gain_part, branch_grad = pull_gather(
        normed_ffn_part, middle, ffn_gain, cot_own, 2
    )
    branch_grad, unused_hop = lax.optimization_barrier(
        (branch_grad.reshape(total, width), arrivals[0][1])
    )
    output_part = output_rows(
        jnp.stack([group, here]).astype(jnp.int32), filled[1], down_weight, middle,
        dealing.reshape(total, 1), total,
    )
    normed_part, qkv_grad, output_grad = attention_backward(
        branch_grad, output_weight, attention, q, kv, normed, q_weight, kv_weight, lengths, freq
    )
    normed_part, unused_hop = lax.optimization_barrier((normed_part, arrivals[1][1]))
    tokens_grad, layer_output, gains = pull_tokens(
        normed_part, output_part, tokens, attn_gain, middle_grad, ffn_gain_part, replicas, 3
    )
    act_grads, tokens_grad = lax.optimization_barrier((act_grads, tokens_grad))
    qkv_part = exchange(qkv_grad.reshape(n, rows, q_cols + 2 * HEAD))
    for hop, (where, from_ring, from_core) in enumerate(arrivals):
        if hop == len(arrivals) - 1:
            act_grads, qkv_part = lax.optimization_barrier((act_grads, qkv_part))
        filled = ffn_other(where, from_ring, from_core, act_grads, gate_cols, up_cols, filled)
    all_normed, all_activated, all_gate_grad, all_up_grad = filled

    output_grad, qkv_part, unused_hop = lax.optimization_barrier(
        (output_grad, qkv_part, arrivals[-1][1])
    )
    summed = sum_over_replicas([output_grad, qkv_part])
    output_moved = next(summed)
    gate_part = exchange(weight_grad(all_normed, all_gate_grad, BF16).reshape(n, rows, ff_cols))
    all_up_grad, unused_move = lax.optimization_barrier((all_up_grad, output_moved))
    output_moved = next(summed)
    up_part = exchange(weight_grad(all_normed, all_up_grad, BF16).reshape(n, rows, ff_cols))
    all_activated, unused_move = lax.optimization_barrier((all_activated, output_moved))
    down_grad = weight_grad(all_activated, down_grads, F32)
    for output_grad, qkv_part in summed:
        pass
    return (
        layer_output,
        tokens_grad,
        gains[0],
        *join_heads(qkv_part, q_cols),
        output_grad.astype(F32),
        gains[1],
        join_columns(gate_part),
        join_columns(up_part),
        down_grad,
    )


def per_device(
    tokens,
    attn_gain,
    query_weight,
    key_weight,
    value_weight,
    output_weight,
    ffn_gain,
    gate_weight,
    up_weight,
    down_weight,
    dealing,
    lengths,
    cotangent,
):
    n = lax.axis_size("shard")
    here = lax.axis_index("shard")
    local, width = tokens.shape
    total = local * n
    rows = query_weight.shape[0]
    ff_cols = gate_weight.shape[1] // n
    q_cols = query_weight.shape[1] // n
    copies = n // KV_HEADS
    own = here * local

    packed = jnp.arange(total, dtype=jnp.int32)
    segment, position = places(packed, lengths[0])
    cos_q, sin_q = rope_tables(position, q_cols)
    cos_k, sin_k = cos_q[:, :HEAD], sin_q[:, :HEAD]
    dealt = (dealing[0][:, None] == packed[None, :]).astype(BF16)

    def column_blocks(weight, cols):
        return weight.reshape(rows, n, cols).transpose(1, 0, 2)

    def head_blocks(weight):
        blocks = weight.reshape(rows, KV_HEADS, HEAD).transpose(1, 0, 2)
        return jnp.repeat(blocks, copies, axis=0)

    spread_cotangent = lax.all_gather(cotangent, ("rep", "shard"), axis=0, tiled=True)
    all_dealing = lax.all_gather(dealing, "rep", axis=0, tiled=True)
    qkv = exchange(
        jnp.concatenate(
            [column_blocks(query_weight, q_cols), head_blocks(key_weight), head_blocks(value_weight)],
            axis=2,
        )
    ).reshape(width, q_cols + 2 * HEAD)
    gate_cols = exchange(column_blocks(gate_weight, ff_cols)).reshape(width, ff_cols)
    up_cols = exchange(column_blocks(up_weight, ff_cols)).reshape(width, ff_cols)

    normed = gather_rows(rms_scale(tokens.astype(F32), attn_gain).astype(BF16))
    pre = mm(normed, qkv)
    queries = rotate(pre[:, :q_cols], cos_q, sin_q).astype(BF16)
    keys = rotate(pre[:, q_cols : q_cols + HEAD], cos_k, sin_k).astype(BF16)
    values = pre[:, q_cols + HEAD :].astype(BF16)
    attention = attention_forward(queries, jnp.concatenate([keys, values], axis=1), lengths)
    branch = scatter_rows(mm(attention, output_weight).astype(BF16))
    middle = tokens.astype(F32) + RESIDUAL_SCALE * branch.astype(F32)
    normed_ffn = gather_rows(rms_scale(middle, ffn_gain).astype(BF16))
    own_normed = lax.dynamic_slice_in_dim(normed_ffn, own, local)
    all_normed = lax.all_gather(own_normed, ("rep", "shard"), axis=0, tiled=True)

    reps = lax.axis_size("rep")
    group = lax.axis_index("rep")
    deals = (all_dealing[:, :, None] == packed[None, None, :]).astype(BF16)
    out_grad_all = lax.dot_general(
        deals,
        spread_cotangent.reshape(reps, total, width),
        (((1,), (1,)), ((0,), (0,))),
        preferred_element_type=F32,
    ).reshape(reps * total, width)
    down_grad_all = (RESIDUAL_SCALE * out_grad_all).astype(BF16)
    out_grad = lax.dynamic_slice_in_dim(out_grad_all, group * total + own, local)
    act_grad_all = mm_t(down_grad_all, down_weight)

    def ffn(rows_in, act_grad):
        gate = mm(rows_in, gate_cols)
        up = mm(rows_in, up_cols)
        sigmoid = jax.nn.sigmoid(gate)
        activated = (gate * sigmoid * up).astype(BF16)
        gate_grad = (act_grad * up * sigmoid * (1.0 + gate * (1.0 - sigmoid))).astype(BF16)
        up_grad = (act_grad * gate * sigmoid).astype(BF16)
        return activated, gate_grad, up_grad

    activated, gate_grad, up_grad = ffn(
        normed_ffn, lax.dynamic_slice_in_dim(act_grad_all, group * total, total)
    )
    normed_ffn_part = (mm_t(gate_grad, gate_cols) + mm_t(up_grad, up_cols)).astype(BF16)
    middle_part, ffn_gain_part = norm_pull(
        middle, ffn_gain, scatter_rows(normed_ffn_part).astype(F32)
    )
    middle_grad = out_grad + middle_part
    branch_grad = gather_rows((RESIDUAL_SCALE * middle_grad).astype(BF16))

    own_columns = lax.dynamic_slice_in_dim(dealt, own, local, axis=1)
    layer_output = scatter_rows(
        (
            RESIDUAL_SCALE * mm(mm(dealt, activated).astype(BF16), down_weight)
            + mm(own_columns, middle.astype(BF16))
        ).astype(BF16)
    )

    attention_grad = mm_t(branch_grad, output_weight).astype(BF16)
    dq, dk, dv = attention_gradients(
        queries, jnp.concatenate([keys, values], axis=1), attention_grad, lengths
    )
    pre_grad = jnp.concatenate(
        [
            unrotate(dq, cos_q, sin_q).astype(BF16),
            unrotate(dk, cos_k, sin_k).astype(BF16),
            dv.astype(BF16),
        ],
        axis=1,
    )
    normed_part = mm_t(pre_grad, qkv).astype(BF16)
    hidden_part, attn_gain_part = norm_pull(
        tokens.astype(F32), attn_gain, scatter_rows(normed_part).astype(F32)
    )
    tokens_grad = middle_grad + hidden_part

    activated, gate_grad, up_grad = ffn(all_normed, act_grad_all)
    gate_part = exchange(t_mm(all_normed, gate_grad).astype(BF16).reshape(n, rows, ff_cols))
    up_part = exchange(t_mm(all_normed, up_grad).astype(BF16).reshape(n, rows, ff_cols))
    down_part = t_mm(activated, down_grad_all)
    output_part = rep_sum(t_mm(attention, branch_grad).astype(BF16))
    qkv_part = rep_sum(exchange(t_mm(normed, pre_grad).astype(BF16).reshape(n, rows, q_cols + 2 * HEAD)))

    def join(blocks):
        return blocks.transpose(1, 0, 2).reshape(rows, -1).astype(F32)

    def join_heads(blocks):
        blocks = blocks.astype(F32).reshape(KV_HEADS, copies, rows, HEAD).sum(axis=1)
        return blocks.transpose(1, 0, 2).reshape(rows, KV_HEADS * HEAD)

    gain_grads = lax.psum(jnp.concatenate([attn_gain_part, ffn_gain_part]), ("rep", "shard"))
    return (
        layer_output,
        tokens_grad,
        gain_grads[0],
        join(qkv_part[:, :, :q_cols]),
        join_heads(qkv_part[:, :, q_cols : q_cols + HEAD]),
        join_heads(qkv_part[:, :, q_cols + HEAD :]),
        output_part.astype(F32),
        gain_grads[1],
        join(gate_part),
        join(up_part),
        down_part,
    )


def solution(mesh):
    both = P(("rep", "shard"), None)
    rowed = P("shard", None)
    return jax.shard_map(
        per_device_plane if mesh.shape["shard"] == 8 else per_device,
        mesh=mesh,
        in_specs=(
            both, P(), rowed, rowed, rowed, rowed, P(), rowed, rowed, rowed,
            P("rep", None), P("rep", None), both,
        ),
        out_specs=(both, both, P(), rowed, rowed, rowed, rowed, P(), rowed, rowed, rowed),
        check_vma=False,
    )
```

```python
import functools

import jax
import jax.numpy as jnp
from jax import lax
from jax.experimental import pallas as pl
from jax.experimental.pallas import tpu as pltpu
from jax.sharding import PartitionSpec as P

HEADS = 32
KV_HEADS = 8
HEAD = 64
EPSILON = 1e-05
RESIDUAL_SCALE = 0.22
SCORE_SCALE = 0.015625
ROPE_BASE = 10000000.0
MASKED = -1e30
BF16 = jnp.bfloat16
F32 = jnp.float32


def mm(a, b):
    return jnp.dot(a, b, preferred_element_type=F32)


def mm_t(a, b):
    return lax.dot_general(a, b, (((1,), (1,)), ((), ())), preferred_element_type=F32)


def t_mm(a, b):
    return lax.dot_general(a, b, (((0,), (0,)), ((), ())), preferred_element_type=F32)


def rms_scale(hidden, gain_vector):
    return (
        hidden
        * lax.rsqrt(jnp.mean(hidden * hidden, axis=-1, keepdims=True) + EPSILON)
        * gain_vector
    )


def places(packed_index, seq_lengths):
    seq_ends = jnp.cumsum(seq_lengths)
    starts = seq_ends - seq_lengths
    segment = jnp.sum((packed_index[:, None] >= seq_ends[None, :]).astype(jnp.int32), axis=1)
    chosen = segment[:, None] == jnp.arange(seq_lengths.shape[0], dtype=jnp.int32)[None, :]
    position = packed_index - jnp.sum(jnp.where(chosen, starts[None, :], 0), axis=1)
    return segment, position


def rope_tables(position, width):
    half = HEAD // 2
    frequency = ROPE_BASE ** (-(jnp.arange(half, dtype=F32) * 2.0) / (2.0 * half))
    turned = position.astype(F32)[:, None] * frequency[None, :]
    cosine, sine = jnp.cos(turned), jnp.sin(turned)
    cos_full = jnp.concatenate([cosine, cosine], axis=-1)
    sin_full = jnp.concatenate([-sine, sine], axis=-1)
    return jnp.tile(cos_full, (1, width // HEAD)), jnp.tile(sin_full, (1, width // HEAD))


def swap_halves(x):
    rows, width = x.shape
    half = HEAD // 2
    y = x.reshape(rows, width // HEAD, 2, half)
    return jnp.concatenate([y[:, :, 1:], y[:, :, :1]], axis=2).reshape(rows, width)


def rotate(x, cos_full, sin_full):
    return x * cos_full + swap_halves(x) * sin_full


def unrotate(x, cos_full, sin_full):
    return x * cos_full - swap_halves(x) * sin_full


def gather_rows(x):
    return lax.all_gather(x, "shard", axis=0, tiled=True)


def scatter_rows(x):
    return lax.psum_scatter(x, "shard", scatter_dimension=0, tiled=True)


def exchange(blocks):
    return lax.all_to_all(blocks, "shard", split_axis=0, concat_axis=0, tiled=True)


def rep_sum(x):
    count = lax.axis_size("rep")
    where = lax.axis_index("rep")
    half = count // 2
    for hop in range(half - 1):
        moved = lax.ppermute(
            x, "rep", [(hop, hop + 1), (count - 1 - hop, count - 2 - hop)]
        )
        x = (x.astype(F32) + moved.astype(F32)).astype(BF16)
    moved = lax.ppermute(x, "rep", [(half - 1, half), (half, half - 1)])
    x = (x.astype(F32) + moved.astype(F32)).astype(BF16)
    for hop in range(half - 1):
        near, far = half - 1 - hop, half + hop
        moved = lax.ppermute(x, "rep", [(near, near - 1), (far, far + 1)])
        x = jnp.where((where == near - 1) | (where == far + 1), moved, x)
    return x


MESH = pl.DeviceIdType.MESH


def flip(index, bits):
    for weight in (1, 2, 4):
        if bits & weight:
            index = index + weight - 2 * weight * lax.rem(lax.div(index, weight), 2)
    return index


def send(src, dst, sems, k, target):
    return pltpu.make_async_remote_copy(
        src_ref=src,
        dst_ref=dst,
        send_sem=sems.at[0, k],
        recv_sem=sems.at[1, k],
        device_id={"shard": target},
        device_id_type=MESH,
    )


def greet(me, masks):
    barrier = pltpu.get_barrier_semaphore()
    for mask in masks:
        pl.semaphore_signal(
            barrier, inc=1, device_id={"shard": flip(me, mask)}, device_id_type=MESH
        )
    pl.semaphore_wait(barrier, len(masks))


GATHER_SEMS = 13
BULK = (12, 2, 2)


def gather_steps(me, out, sems):
    core, px, py, diag = (flip(me, mask) for mask in (1, 2, 4, 6))
    half = out.shape[1] // 2
    low, high, whole = pl.ds(0, half), pl.ds(half, half), pl.ds(0, 2 * half)

    def move(k, block, rows, target):
        ref = out.at[block, rows]
        copy = send(ref, ref, sems, k, target)
        copy.start()
        return copy

    x_low, y_high = move(0, me, low, px), move(1, me, high, py)
    own = move(2, me, whole, core)
    x_high, y_low = move(3, me, high, px), move(4, me, low, py)
    yield
    x_low.wait_recv()
    diag_low = move(5, px, low, py)
    pieces = [own, move(6, px, low, core)]
    yield
    y_high.wait_recv()
    diag_high = move(7, py, high, px)
    pieces.append(move(8, py, high, core))
    yield
    x_high.wait_recv()
    pieces.append(move(9, px, high, core))
    yield
    y_low.wait_recv()
    pieces.append(move(10, py, low, core))
    yield
    diag_low.wait_recv()
    pieces.append(move(11, diag, low, core))
    diag_high.wait_recv()
    pieces.append(move(12, diag, high, core))
    yield
    for copy in pieces:
        copy.wait_recv()
    for copy in [x_low, y_high, x_high, y_low, diag_low, diag_high] + pieces:
        copy.wait_send()


def gather_blocks(me, out, sems):
    for unused_step in gather_steps(me, out, sems):
        pass


SCATTER_SEMS = 10


def scatter_steps(me, partial, sib_out, sib_in, acc, x_out, x_in, y_out, y_in, sems):
    core, px, py = (flip(me, mask) for mask in (1, 2, 4))
    half = acc.shape[1] // 2
    masks = (6, 2, 4, 0)
    low, high = pl.ds(0, half), pl.ds(half, half)
    copies = []

    def move(src, dst, k, target):
        copy = send(src, dst, sems, k, target)
        copy.start()
        copies.append(copy)
        return copy

    inside = []
    for i, mask in enumerate(masks):
        sib_out[i] = partial(flip(core, mask)).astype(BF16)
        inside.append(move(sib_out.at[i], sib_in.at[i], i, core))
    yield
    for i, mask in enumerate(masks):
        term = partial(flip(me, mask))
        inside[i].wait_recv()
        acc[i] = term + sib_in[i].astype(F32)
        if mask == 6:
            x_out[0] = acc[i, low].astype(BF16)
            x_diag = move(x_out.at[0], x_in.at[0], 4, px)
            y_out[0] = acc[i, high].astype(BF16)
            y_diag = move(y_out.at[0], y_in.at[0], 5, py)
        if mask == 2:
            x_out[1] = acc[i, low].astype(BF16)
            x_near = move(x_out.at[1], x_in.at[1], 6, px)
        if mask == 4:
            y_out[1] = acc[i, high].astype(BF16)
            y_near = move(y_out.at[1], y_in.at[1], 7, py)
    yield
    x_diag.wait_recv()
    y_out[2] = (acc[2, low] + x_in[0].astype(F32)).astype(BF16)
    y_last = move(y_out.at[2], y_in.at[2], 8, py)
    y_diag.wait_recv()
    x_out[2] = (acc[1, high] + y_in[0].astype(F32)).astype(BF16)
    x_last = move(x_out.at[2], x_in.at[2], 9, px)
    yield
    x_near.wait_recv()
    y_near.wait_recv()
    y_last.wait_recv()
    acc[3, low] = acc[3, low] + x_in[1].astype(F32) + y_in[2].astype(F32)
    x_last.wait_recv()
    acc[3, high] = acc[3, high] + y_in[1].astype(F32) + x_in[2].astype(F32)
    yield
    for copy in copies:
        copy.wait_send()


def scatter_blocks(me, partial, *buffers):
    for unused_step in scatter_steps(me, partial, *buffers):
        pass
    return buffers[2][3]


def scatter_scratch(rows, width):
    half = rows // 2
    return [
        pltpu.VMEM((4, rows, width), BF16),
        pltpu.VMEM((4, rows, width), BF16),
        pltpu.VMEM((4, rows, width), F32),
        pltpu.VMEM((3, half, width), BF16),
        pltpu.VMEM((3, half, width), BF16),
        pltpu.VMEM((3, half, width), BF16),
        pltpu.VMEM((3, half, width), BF16),
        pltpu.SemaphoreType.DMA((2, SCATTER_SEMS)),
    ]


VMEM = pl.BlockSpec(memory_space=pltpu.VMEM)
SMEM = pl.BlockSpec(memory_space=pltpu.SMEM)
ANY = pl.BlockSpec(memory_space=pl.ANY)


def comm_params(collective_id, mebibytes):
    return pltpu.CompilerParams(
        collective_id=collective_id, has_side_effects=True, vmem_limit_bytes=mebibytes << 20
    )


def front(
    tokens, attn_gain, query_weight, key_weight, value_weight, output_weight, ffn_gain,
    gate_weight, up_weight, down_weight, dealing, lengths, cotangent, freq, replicas,
):
    local, width = tokens.shape
    total = 8 * local
    shard_rows = query_weight.shape[0]
    q_cols = query_weight.shape[1] // 8
    ff_cols = gate_weight.shape[1] // 8
    block = 256
    others = (1, 2, 3, 4, 5, 6, 7)

    def kernel(
        tok_ref, gain_ref, wq_hbm, wk_ref, wv_ref, wo_ref, fgain_ref, wg_hbm, wu_hbm,
        wd_ref, deal_ref, len_ref, cot_ref, freq_ref,
        n_ref, q_ref, kv_ref, att_ref, qw_ref, kvw_ref, wg_out, wu_out, mid_ref, nf_ref, dg_out, ag_out, cot_out,
        kv_stage, c_all, dg_own, ag_stage,
        sib_out, sib_in, acc, x_out, x_in, y_out, y_in, scatter_sems,
        n_sems, c_sems, nf_sems, qkv_sems, bulk_sems, ring_sems, pair_sems, local_sems,
    ):
        me = lax.axis_index("shard")
        group = lax.axis_index("rep")
        core = lax.rem(me, 2)
        after = lax.rem(group + 1, replicas)
        before = lax.rem(group + replicas - 1, replicas)

        barrier = pltpu.get_barrier_semaphore()
        for mask in others:
            pl.semaphore_signal(
                barrier, inc=1, device_id={"shard": flip(me, mask)}, device_id_type=MESH
            )
        for neighbour in (after, before):
            pl.semaphore_signal(
                barrier, inc=1, device_id={"rep": neighbour}, device_id_type=MESH
            )
        n_ref[me] = rms_scale(tok_ref[...].astype(F32), gain_ref[...]).astype(BF16)
        c_all[me] = cot_ref[...]
        for d in range(8):
            lanes = slice(d * HEAD, (d + 1) * HEAD)
            kv_stage[d] = jnp.concatenate([wk_ref[:, lanes], wv_ref[:, lanes]], axis=1)
        pl.semaphore_wait(barrier, len(others) + 2)

        gather_c = gather_steps(me, c_all, c_sems)
        next(gather_c)
        gather_n = gather_steps(me, n_ref, n_sems)
        next(gather_n)
        weights = []
        for mask in others:
            peer = flip(me, mask)
            columns = pl.ds(pl.multiple_of(peer * q_cols, q_cols), q_cols)
            weights.append(send(wq_hbm.at[:, columns], qw_ref.at[me], qkv_sems, 2 * mask - 2, peer))
            weights.append(send(kv_stage.at[peer], kvw_ref.at[me], qkv_sems, 2 * mask - 1, peer))
        for copy in weights:
            copy.start()
        own_columns = pl.ds(pl.multiple_of(me * ff_cols, ff_cols), ff_cols)
        own_q = pl.ds(pl.multiple_of(me * q_cols, q_cols), q_cols)
        gate_slot, up_slot = ag_stage.at[:shard_rows], ag_stage.at[pl.ds(shard_rows, shard_rows)]
        kept = [
            pltpu.make_async_copy(wg_hbm.at[:, own_columns], gate_slot, local_sems.at[0]),
            pltpu.make_async_copy(wu_hbm.at[:, own_columns], up_slot, local_sems.at[1]),
            pltpu.make_async_copy(wq_hbm.at[:, own_q], qw_ref.at[me], local_sems.at[2]),
        ]
        for copy in kept:
            copy.start()
        kvw_ref[me] = kv_stage[me]

        bulk, waiting = [], []
        for source, target in ((wg_hbm, wg_out), (wu_hbm, wu_out)):
            for part in range(2):
                rows = pl.ds(part * (shard_rows // 2), shard_rows // 2)
                for mask in (2, 4, 6, 3, 5, 7, 1):
                    waiting.append((source, target, rows, mask))

        def more(count):
            for unused in range(min(count, len(waiting))):
                source, target, rows, mask = waiting.pop(0)
                peer = flip(me, mask)
                columns = pl.ds(pl.multiple_of(peer * ff_cols, ff_cols), ff_cols)
                copy = send(
                    source.at[rows, columns], target.at[me, rows], bulk_sems, len(bulk), peer
                )
                copy.start()
                bulk.append(copy)

        for unused in gather_c:
            pass

        def permute(first):
            for i in range(total // 2 // block):
                row0 = pl.multiple_of(first + i * block, block)
                packed = row0 + lax.broadcasted_iota(jnp.int32, (block, total), 0)
                chosen = (deal_ref[...] == packed).astype(BF16)
                dealt = mm(chosen, c_all[...].reshape(total, width))
                dg_own[pl.ds(row0, block), :] = (RESIDUAL_SCALE * dealt).astype(BF16)

        near = pl.multiple_of(core * (total // 2), total // 2)
        far = pl.multiple_of((1 - core) * (total // 2), total // 2)
        half = pl.ds(near, total // 2)

        def ring(hop):
            held = lax.rem(group + replicas - hop, replicas)
            ref = dg_out.at[held, half]
            copy = pltpu.make_async_remote_copy(
                src_ref=dg_own.at[half] if hop == 0 else ref,
                dst_ref=ref,
                send_sem=ring_sems.at[0, hop],
                recv_sem=ring_sems.at[1, hop],
                device_id={"rep": after},
                device_id_type=MESH,
            )
            copy.start()
            return copy

        def share(hop):
            held = lax.rem(group + replicas - hop, replicas)
            ref = dg_out.at[held, half]
            copy = send(ref, ref, pair_sems, hop - 1, flip(me, 1))
            copy.start()
            return copy

        permute(near)
        hops, shares = [ring(0)], []
        for unused in range(4):
            next(gather_n)
        permute(far)
        packed = me * local + lax.broadcasted_iota(jnp.int32, (local, total), 0)
        chosen = (deal_ref[...] == packed).astype(BF16)
        cot_out[...] = mm(chosen, c_all[...].reshape(total, width)).astype(BF16)
        store = pltpu.make_async_copy(dg_own, dg_out.at[group], local_sems.at[3])
        store.start()
        for unused in gather_n:
            pass
        for copy in kept:
            copy.wait()
        kept = [
            pltpu.make_async_copy(gate_slot, wg_out.at[me], local_sems.at[0]),
            pltpu.make_async_copy(up_slot, wu_out.at[me], local_sems.at[1]),
        ]
        for copy in kept:
            copy.start()
        for copy in weights:
            copy.wait_recv()
        more(BULK[0])
        for i in range(total // block):
            rows = pl.ds(i * block, block)
            x = n_ref[pl.ds(i * block // local, block // local)].reshape(block, width)
            cosine, sine = lane_rope(i * block, block, freq_ref[...], len_ref)
            pre = mm(x, qw_ref[...].reshape(width, q_cols))
            for j in range(q_cols // (2 * HEAD)):
                lanes = slice(j * 2 * HEAD, (j + 1) * 2 * HEAD)
                y = pre[:, lanes]
                q_ref[rows, lanes] = (y * cosine + lane_swap(y) * sine).astype(BF16)
            cosine, sine = keys_only(cosine, sine)
            y = mm(x, kvw_ref[...].reshape(width, 2 * HEAD))
            kv_ref[rows, :] = (y * cosine + lane_swap(y) * sine).astype(BF16)
        attend(q_cols // HEAD, block, q_ref, kv_ref, len_ref, att_ref)

        def partial(d):
            return mm(att_ref[pl.ds(pl.multiple_of(d * local, local), local), :], wo_ref[...])

        def next_hop():
            hop = len(hops)
            hops[-1].wait_recv()
            if hop < replicas - 1:
                hops.append(ring(hop))
            shares.append(share(hop))

        def act_grad(held, source):
            for i in range(total // block):
                rows = pl.ds(i * block, block)
                ag_stage[rows, :] = mm_t(source[rows, :], wd_ref[...]).astype(BF16)
            copy = pltpu.make_async_copy(ag_stage, ag_out.at[held], local_sems.at[3])
            copy.start()
            copy.wait()

        next_hop()
        scatter = scatter_steps(
            me, partial, sib_out, sib_in, acc, x_out, x_in, y_out, y_in, scatter_sems
        )
        next(scatter)
        more(BULK[1])
        for unused in scatter:
            pass
        branch = acc[3]
        middle = tok_ref[...].astype(F32) + RESIDUAL_SCALE * branch
        mid_ref[...] = middle
        nf_ref[me] = rms_scale(middle, fgain_ref[...]).astype(BF16)
        gather_nf = gather_steps(me, nf_ref, nf_sems)
        next(gather_nf)
        more(BULK[2])
        for unused in gather_nf:
            pass
        more(len(waiting))
        store.wait()
        for copy in kept:
            copy.wait()
        act_grad(group, dg_own)
        hops[0].wait_send()
        if len(shares) < replicas - 1:
            next_hop()
        for done in range(replicas - 1):
            if len(shares) < done + 1:
                next_hop()
            held = lax.rem(group + replicas - 1 - done, replicas)
            shares[done].wait_recv()
            load = pltpu.make_async_copy(dg_out.at[held], dg_own, local_sems.at[3])
            load.start()
            load.wait()
            act_grad(held, dg_own)
        for copy in bulk:
            copy.wait_recv()
        for copy in weights + bulk + hops[1:] + shares:
            copy.wait_send()

    rows8 = jax.ShapeDtypeStruct((8, local, width), BF16)
    half_sems = pltpu.SemaphoreType.DMA
    outs = pl.pallas_call(
        kernel,
        out_shape=(
            rows8,
            jax.ShapeDtypeStruct((total, q_cols), BF16),
            jax.ShapeDtypeStruct((total, 2 * HEAD), BF16),
            jax.ShapeDtypeStruct((total, q_cols), BF16),
            jax.ShapeDtypeStruct((8, shard_rows, q_cols), BF16),
            jax.ShapeDtypeStruct((8, shard_rows, 2 * HEAD), BF16),
            jax.ShapeDtypeStruct((8, shard_rows, ff_cols), BF16),
            jax.ShapeDtypeStruct((8, shard_rows, ff_cols), BF16),
            jax.ShapeDtypeStruct((local, width), F32),
            rows8,
            jax.ShapeDtypeStruct((replicas, total, width), BF16),
            jax.ShapeDtypeStruct((replicas, total, ff_cols), BF16),
            jax.ShapeDtypeStruct((local, width), BF16),
        ),
        in_specs=[VMEM, VMEM, ANY, VMEM, VMEM, VMEM, VMEM, ANY, ANY, VMEM, VMEM, SMEM, VMEM, VMEM],
        out_specs=[VMEM] * 6 + [ANY, ANY, VMEM, VMEM, ANY, ANY, VMEM],
        scratch_shapes=[
            pltpu.VMEM((8, shard_rows, 2 * HEAD), BF16),
            pltpu.VMEM((8, local, width), BF16),
            pltpu.VMEM((total, width), BF16),
            pltpu.VMEM((total, ff_cols), BF16),
        ]
        + scatter_scratch(local, width)
        + [
            half_sems((2, GATHER_SEMS)),
            half_sems((2, GATHER_SEMS)),
            half_sems((2, GATHER_SEMS)),
            half_sems((2, 14)),
            half_sems((2, 28)),
            half_sems((2, replicas)),
            half_sems((2, replicas)),
            half_sems((4,)),
        ],
        compiler_params=comm_params(0, 56),
        cost_estimate=pl.CostEstimate(
            flops=200_000_000_000, bytes_accessed=50 << 20, transcendentals=total * total
        ),
        name="front",
    )(
        tokens, attn_gain[None, :], query_weight, key_weight, value_weight, output_weight,
        ffn_gain[None, :], gate_weight, up_weight, down_weight, dealing, lengths, cotangent, freq,
    )
    normed, q, kv, attention, qw, kvw, wg, wu, middle, nf, dg, ag, cot = outs
    return (
        normed.reshape(total, width), q, kv, attention,
        qw.reshape(width, q_cols), kvw.reshape(width, 2 * HEAD),
        wg.reshape(width, ff_cols), wu.reshape(width, ff_cols),
        middle, nf.reshape(total, width), dg, ag, cot,
    )


def norm_pull(x, gain, grad):
    scale = lax.rsqrt(jnp.mean(x * x, axis=-1, keepdims=True) + EPSILON)
    pulled = gain * grad
    rows_part = scale * pulled - x * (
        scale * scale * scale * jnp.mean(pulled * x, axis=-1, keepdims=True)
    )
    return rows_part, jnp.sum(grad * x * scale, axis=0, keepdims=True)


def pull_gather(part, middle, gain, out_grad, collective_id):
    rows, width = middle.shape

    def kernel(p_ref, m_ref, gain_ref, g_ref, mg_ref, gain_part, out, *scratch):
        me = lax.axis_index("shard")
        *buffers, scatter_sems, sems = scratch
        greet(me, (1, 2, 4))
        grad = scatter_blocks(
            me,
            lambda d: p_ref[pl.ds(pl.multiple_of(d * rows, rows), rows), :].astype(F32),
            *buffers,
            scatter_sems,
        )
        rows_part, gain_row = norm_pull(m_ref[...], gain_ref[...], grad)
        gain_part[...] = gain_row
        middle_grad = g_ref[...].astype(F32) + rows_part
        mg_ref[...] = middle_grad
        out[me] = (RESIDUAL_SCALE * middle_grad).astype(BF16)
        gather_blocks(me, out, sems)

    return pl.pallas_call(
        kernel,
        out_shape=(
            jax.ShapeDtypeStruct((rows, width), F32),
            jax.ShapeDtypeStruct((1, width), F32),
            jax.ShapeDtypeStruct((8, rows, width), BF16),
        ),
        in_specs=[VMEM] * 4,
        out_specs=[VMEM] * 3,
        scratch_shapes=scatter_scratch(rows, width)
        + [pltpu.SemaphoreType.DMA((2, GATHER_SEMS))],
        compiler_params=comm_params(collective_id, 44),
        cost_estimate=pl.CostEstimate(
            flops=50_000_000_000, bytes_accessed=50 * rows * width, transcendentals=rows
        ),
        name="pull_gather",
    )(part, middle, gain[None, :], out_grad)


def pull_tokens(part, out_part, hidden, gain, middle_grad, other_gain, replicas, collective_id):
    rows, width = middle_grad.shape
    levels = [("shard", 1), ("shard", 2), ("shard", 4)]
    level = 1
    while level < replicas:
        levels.append(("rep", level))
        level *= 2

    def kernel(
        p_ref, o_ref, h_ref, gain_ref, mg_ref, og_ref, out, lay, gains, gain_in, gain_out, gain_sems, *scratch
    ):
        me = lax.axis_index("shard")
        group = lax.axis_index("rep")
        first, second = scratch[:8], scratch[8:]
        barrier = pltpu.get_barrier_semaphore()
        peers = []
        for axis, weight in levels:
            index = me if axis == "shard" else group
            peers.append({axis: index + weight - 2 * weight * lax.rem(lax.div(index, weight), 2)})
        for peer in peers:
            pl.semaphore_signal(barrier, inc=1, device_id=peer, device_id_type=MESH)
        pl.semaphore_wait(barrier, len(peers))

        def blocks_of(ref):
            return lambda d: ref[pl.ds(pl.multiple_of(d * rows, rows), rows), :].astype(F32)

        grads = scatter_steps(me, blocks_of(p_ref), *first)
        outputs = scatter_steps(me, blocks_of(o_ref), *second)
        next(grads)
        next(grads)
        next(outputs)
        next(grads)
        next(outputs)
        next(grads)
        rows_part, gain_row = norm_pull(h_ref[...].astype(F32), gain_ref[...], first[2][3])
        out[...] = mg_ref[...] + rows_part
        total = jnp.concatenate([gain_row, og_ref[...]], axis=0)
        for i, peer in enumerate(peers):
            gain_out[i] = total
            copy = pltpu.make_async_remote_copy(
                src_ref=gain_out.at[i],
                dst_ref=gain_in.at[i],
                send_sem=gain_sems.at[0, i],
                recv_sem=gain_sems.at[1, i],
                device_id=peer,
                device_id_type=MESH,
            )
            copy.start()
            if i == 1:
                next(outputs)
            copy.wait()
            total = total + gain_in[i]
        gains[...] = total
        next(outputs)
        lay[...] = second[2][3].astype(BF16)
        for steps in (grads, outputs):
            for unused in steps:
                pass

    return pl.pallas_call(
        kernel,
        out_shape=(
            jax.ShapeDtypeStruct((rows, width), F32),
            jax.ShapeDtypeStruct((rows, width), BF16),
            jax.ShapeDtypeStruct((2, width), F32),
        ),
        in_specs=[VMEM] * 6,
        out_specs=[VMEM] * 3,
        scratch_shapes=[
            pltpu.VMEM((len(levels), 2, width), F32),
            pltpu.VMEM((len(levels), 2, width), F32),
            pltpu.SemaphoreType.DMA((2, len(levels))),
        ]
        + scatter_scratch(rows, width)
        + scatter_scratch(rows, width),
        compiler_params=comm_params(collective_id, 52),
        cost_estimate=pl.CostEstimate(
            flops=50_000_000_000, bytes_accessed=50 * rows * width, transcendentals=rows
        ),
        name="pull_tokens",
    )(part, out_part, hidden, gain[None, :], middle_grad, other_gain)


def softmax_block(q, k, allowed):
    scores = SCORE_SCALE * mm_t(q, k)
    scores = jnp.where(allowed, scores, MASKED)
    top = jnp.max(scores, axis=-1, keepdims=True)
    weight = jnp.exp(scores - top)
    return weight * (1.0 / jnp.sum(weight, axis=-1, keepdims=True))


def allowed_block(row0, cols, start):
    shape = (start.shape[0], cols)
    query = row0 + lax.broadcasted_iota(jnp.int32, shape, 0)
    key = lax.broadcasted_iota(jnp.int32, shape, 1)
    return (key >= start) & (key <= query)


def sequence_starts(row0, shape, lengths_ref):
    row = row0 + lax.broadcasted_iota(jnp.int32, shape, 0)
    start = jnp.zeros(shape, jnp.int32)
    end = 0
    for i in range(lengths_ref.shape[1]):
        length = lengths_ref[0, i]
        end = end + length
        start = start + jnp.where(row >= end, length, 0)
    return start


def attend(heads, block, q_ref, kv_ref, lengths_ref, o_ref):
    total = kv_ref.shape[0]
    for i in range(total // block):
        cols = (i + 1) * block
        rows = pl.ds(i * block, block)
        allowed = allowed_block(
            i * block, cols, sequence_starts(i * block, (block, 1), lengths_ref)
        )
        kv = kv_ref[:cols, :]
        k, v = kv[:, :HEAD], kv[:, HEAD:]
        for h in range(heads):
            lanes = slice(h * HEAD, (h + 1) * HEAD)
            probs = softmax_block(q_ref[rows, lanes], k, allowed)
            o_ref[rows, lanes] = mm(probs.astype(BF16), v).astype(BF16)


def attend_back(heads, block, q_ref, kv_ref, g_ref, lengths_ref, dq_ref, dk_ref, dv_ref):
    total = kv_ref.shape[0]
    dk_ref[...] = jnp.zeros_like(dk_ref)
    dv_ref[...] = jnp.zeros_like(dv_ref)
    for i in range(total // block):
        cols = (i + 1) * block
        rows = pl.ds(i * block, block)
        allowed = allowed_block(
            i * block, cols, sequence_starts(i * block, (block, 1), lengths_ref)
        )
        kv = kv_ref[:cols, :]
        k, v = kv[:, :HEAD], kv[:, HEAD:]
        for h in range(heads):
            lanes = slice(h * HEAD, (h + 1) * HEAD)
            q, g = q_ref[rows, lanes], g_ref[rows, lanes]
            probs = softmax_block(q, k, allowed)
            probs_grad = mm_t(g, v)
            delta = jnp.sum(probs * probs_grad, axis=-1, keepdims=True)
            score_grad = (probs * (probs_grad - delta)).astype(BF16)
            dq_ref[rows, lanes] = SCORE_SCALE * mm(score_grad, k)
            dk_ref[:cols, :] += SCORE_SCALE * t_mm(score_grad, q)
            dv_ref[:cols, :] += t_mm(probs.astype(BF16), g)


def attention_forward(q, kv, lengths):
    total, width = q.shape

    def kernel(q_ref, kv_ref, lengths_ref, o_ref):
        attend(width // HEAD, 256, q_ref, kv_ref, lengths_ref, o_ref)

    return pl.pallas_call(
        kernel,
        out_shape=jax.ShapeDtypeStruct((total, width), BF16),
        in_specs=[VMEM, VMEM, SMEM],
        out_specs=VMEM,
        compiler_params=pltpu.CompilerParams(vmem_limit_bytes=40 << 20),
        name="attention_forward",
    )(q, kv, lengths)


def attention_gradients(q, kv, grad, lengths):
    total, width = q.shape

    def kernel(q_ref, kv_ref, g_ref, lengths_ref, dq_ref, dk_ref, dv_ref):
        attend_back(width // HEAD, 256, q_ref, kv_ref, g_ref, lengths_ref, dq_ref, dk_ref, dv_ref)

    return pl.pallas_call(
        kernel,
        out_shape=(
            jax.ShapeDtypeStruct((total, width), F32),
            jax.ShapeDtypeStruct((total, HEAD), F32),
            jax.ShapeDtypeStruct((total, HEAD), F32),
        ),
        in_specs=[VMEM, VMEM, VMEM, SMEM],
        out_specs=[VMEM] * 3,
        compiler_params=pltpu.CompilerParams(vmem_limit_bytes=40 << 20),
        name="attention_gradients",
    )(q, kv, grad, lengths)


def lane_rope(row0, rows, freq, lengths_ref):
    shape = (rows, 2 * HEAD)
    row = row0 + lax.broadcasted_iota(jnp.int32, shape, 0)
    position = row - sequence_starts(row0, shape, lengths_ref)
    turned = position.astype(F32) * freq
    lane = lax.broadcasted_iota(jnp.int32, shape, 1)
    first = lax.rem(lane, HEAD) < HEAD // 2
    sine = jnp.sin(turned)
    return jnp.cos(turned), jnp.where(first, -sine, sine)


def lane_swap(x):
    half = HEAD // 2
    lane = lax.broadcasted_iota(jnp.int32, x.shape, 1)
    first = lax.rem(lane, HEAD) < half
    return jnp.where(first, pltpu.roll(x, 2 * HEAD - half, 1), pltpu.roll(x, half, 1))


def keys_only(cosine, sine):
    lane = lax.broadcasted_iota(jnp.int32, cosine.shape, 1)
    return jnp.where(lane < HEAD, cosine, 1.0), jnp.where(lane < HEAD, sine, 0.0)


def attention_backward(
    branch_grad, output_weight, attention, q, kv, normed, q_weight, kv_weight, lengths, freq
):
    total, q_cols = q.shape
    width = normed.shape[1]
    block = 256

    def kernel(
        bg_ref, wo_ref, a_ref, q_ref, kv_ref, n_ref, qw_ref, kvw_ref, len_ref, freq_ref,
        dn_ref, dqkv_ref, dwo_ref, g_ref, dq_ref, dk_ref, dv_ref, pq_ref, pkv_ref,
    ):
        for i in range(total // block):
            rows = pl.ds(i * block, block)
            g_ref[rows, :] = mm_t(bg_ref[rows, :], wo_ref[...]).astype(BF16)
        attend_back(
            q_cols // HEAD, block, q_ref, kv_ref, g_ref, len_ref, dq_ref, dk_ref, dv_ref
        )
        for i in range(total // block):
            rows = pl.ds(i * block, block)
            cosine, sine = lane_rope(i * block, block, freq_ref[...], len_ref)
            for j in range(q_cols // (2 * HEAD)):
                lanes = slice(j * 2 * HEAD, (j + 1) * 2 * HEAD)
                x = dq_ref[rows, lanes]
                pq_ref[rows, lanes] = (x * cosine - lane_swap(x) * sine).astype(BF16)
            cosine, sine = keys_only(cosine, sine)
            x = jnp.concatenate([dk_ref[rows, :], dv_ref[rows, :]], axis=1)
            pkv_ref[rows, :] = (x * cosine - lane_swap(x) * sine).astype(BF16)
            dn_ref[rows, :] = (
                mm_t(pq_ref[rows, :], qw_ref[...]) + mm_t(pkv_ref[rows, :], kvw_ref[...])
            ).astype(BF16)
        for i in range(width // 512):
            cols = slice(i * 512, (i + 1) * 512)
            dqkv_ref[cols, :q_cols] = t_mm(n_ref[:, cols], pq_ref[...]).astype(BF16)
            dqkv_ref[cols, q_cols:] = t_mm(n_ref[:, cols], pkv_ref[...]).astype(BF16)
            dwo_ref[:, cols] = t_mm(a_ref[...], bg_ref[:, cols]).astype(BF16)

    return pl.pallas_call(
        kernel,
        out_shape=(
            jax.ShapeDtypeStruct((total, width), BF16),
            jax.ShapeDtypeStruct((width, q_cols + 2 * HEAD), BF16),
            jax.ShapeDtypeStruct((q_cols, width), BF16),
        ),
        in_specs=[VMEM] * 8 + [SMEM, VMEM],
        out_specs=[VMEM] * 3,
        scratch_shapes=[
            pltpu.VMEM((total, q_cols), BF16),
            pltpu.VMEM((total, q_cols), F32),
            pltpu.VMEM((total, HEAD), F32),
            pltpu.VMEM((total, HEAD), F32),
            pltpu.VMEM((total, q_cols), BF16),
            pltpu.VMEM((total, 2 * HEAD), BF16),
        ],
        compiler_params=pltpu.CompilerParams(vmem_limit_bytes=56 << 20),
        cost_estimate=pl.CostEstimate(flops=30_000_000_000, bytes_accessed=30 << 20, transcendentals=total * total),
        name="attention_backward",
    )(branch_grad, output_weight, attention, q, kv, normed, q_weight, kv_weight, lengths, freq)


def ffn_rows(nf, act_grad, wg, wu):
    gate, up = mm(nf, wg), mm(nf, wu)
    act_grad = act_grad.astype(F32)
    sigmoid = 1.0 / (1.0 + jnp.exp(-gate))
    silu = gate * sigmoid
    activated = (silu * up).astype(BF16)
    gate_grad = (act_grad * up * sigmoid * (1.0 + gate * (1.0 - sigmoid))).astype(BF16)
    return activated, gate_grad, (act_grad * silu).astype(BF16)


def ffn_own(group, nf, act_grads, wg, wu):
    groups, total, cols = act_grads.shape
    width = nf.shape[1]
    block = 256

    def kernel(g_ref, nf_ref, ag_ref, wg_ref, wu_ref, na_ref, act_ref, gg_ref, ug_ref, dn_ref):
        nf = nf_ref[...]
        act, gg, ug = ffn_rows(nf, ag_ref[0], wg_ref[...], wu_ref[...])
        na_ref[0], act_ref[0], gg_ref[0], ug_ref[0] = nf, act, gg, ug
        dn_ref[...] = (mm_t(gg, wg_ref[...]) + mm_t(ug, wu_ref[...])).astype(BF16)

    mine = pl.BlockSpec((1, block, width), lambda i, g: (g[0], i, 0))
    hid = pl.BlockSpec((1, block, cols), lambda i, g: (g[0], i, 0))
    plain = pl.BlockSpec((block, width), lambda i, g: (i, 0))
    whole = [
        pl.BlockSpec(w.shape, lambda i, g: (0, 0), pipeline_mode=pl.Buffered(1)) for w in (wg, wu)
    ]
    hidden = jax.ShapeDtypeStruct((groups, total, cols), BF16)
    return pl.pallas_call(
        kernel,
        grid_spec=pltpu.PrefetchScalarGridSpec(
            num_scalar_prefetch=1,
            grid=(total // block,),
            in_specs=[plain, hid] + whole,
            out_specs=[mine, hid, hid, hid, plain],
        ),
        out_shape=(
            jax.ShapeDtypeStruct((groups, total, width), BF16),
            hidden,
            hidden,
            hidden,
            jax.ShapeDtypeStruct((total, width), BF16),
        ),
        compiler_params=pltpu.CompilerParams(vmem_limit_bytes=48 << 20),
        cost_estimate=pl.CostEstimate(
            flops=12 * total * width * cols, bytes_accessed=40 << 20, transcendentals=total * cols
        ),
        name="ffn_own",
    )(group, nf, act_grads, wg, wu)


def ffn_other(where, held, fetched, act_grads, wg, wu, filled):
    groups, total, cols = act_grads.shape
    width = held.shape[1]
    block = 256
    per_half = total // 2 // block

    def kernel(w_ref, held_ref, fetched_ref, ag_ref, wg_ref, wu_ref, *rest):
        na_ref, act_ref, gg_ref, ug_ref, nf_ref = rest[4:]
        i = pl.program_id(0)

        @pl.when(i < per_half)
        def _():
            nf_ref[...] = held_ref[...]

        @pl.when(i >= per_half)
        def _():
            nf_ref[...] = fetched_ref[...]

        nf = nf_ref[...]
        act, gg, ug = ffn_rows(nf, ag_ref[0], wg_ref[...], wu_ref[...])
        na_ref[0], act_ref[0], gg_ref[0], ug_ref[0] = nf, act, gg, ug

    def row(i, w):
        half = jnp.where(i < per_half, w[1], 1 - w[1])
        return half * per_half + lax.rem(i, per_half)

    mine = pl.BlockSpec((1, block, width), lambda i, w: (w[0], row(i, w), 0))
    hid = pl.BlockSpec((1, block, cols), lambda i, w: (w[0], row(i, w), 0))
    first = pl.BlockSpec((block, width), lambda i, w: (jnp.minimum(i, per_half - 1), 0))
    last = pl.BlockSpec((block, width), lambda i, w: (jnp.maximum(i - per_half, 0), 0))
    whole = [
        pl.BlockSpec(w.shape, lambda i, g: (0, 0), pipeline_mode=pl.Buffered(1)) for w in (wg, wu)
    ]
    hidden = jax.ShapeDtypeStruct((groups, total, cols), BF16)
    return pl.pallas_call(
        kernel,
        grid_spec=pltpu.PrefetchScalarGridSpec(
            num_scalar_prefetch=1,
            grid=(2 * per_half,),
            in_specs=[first, last, hid] + whole + [pl.BlockSpec(memory_space=pl.ANY)] * 4,
            out_specs=[mine, hid, hid, hid],
            scratch_shapes=[pltpu.VMEM((block, width), BF16)],
        ),
        out_shape=(jax.ShapeDtypeStruct((groups, total, width), BF16), hidden, hidden, hidden),
        input_output_aliases={6: 0, 7: 1, 8: 2, 9: 3},
        compiler_params=pltpu.CompilerParams(vmem_limit_bytes=48 << 20),
        cost_estimate=pl.CostEstimate(
            flops=8 * total * width * cols, bytes_accessed=40 << 20, transcendentals=total * cols
        ),
        name="ffn_other",
    )(where, held, fetched, act_grads, wg, wu, *filled)


def output_rows(where, activated, down_weight, middle, deal, total):
    groups, total, cols = activated.shape
    local, width = middle.shape
    block = 256

    def kernel(w_ref, act_ref, wd_ref, mid_ref, deal_ref, o_ref, rows_ref):
        for i in range(total // block):
            rows = pl.ds(i * block, block)
            rows_ref[rows, :] = (RESIDUAL_SCALE * mm(act_ref[0, rows, :], wd_ref[...])).astype(BF16)
        own = pl.ds(pl.multiple_of(w_ref[1] * local, local), local)
        rows_ref[own, :] = (rows_ref[own, :].astype(F32) + mid_ref[...]).astype(BF16)
        for i in range(total // block):
            rows = pl.ds(i * block, block)
            packed = lax.broadcasted_iota(jnp.int32, (block, total), 1)
            chosen = (deal_ref[rows, :] == packed).astype(BF16)
            o_ref[rows, :] = mm(chosen, rows_ref[...]).astype(BF16)

    def full(shape):
        return pl.BlockSpec(shape, lambda i, w: (0,) * len(shape), pipeline_mode=pl.Buffered(1))

    return pl.pallas_call(
        kernel,
        grid_spec=pltpu.PrefetchScalarGridSpec(
            num_scalar_prefetch=1,
            grid=(1,),
            in_specs=[
                pl.BlockSpec((1, total, cols), lambda i, w: (w[0], 0, 0), pipeline_mode=pl.Buffered(1)),
                full(down_weight.shape),
                full(middle.shape),
                full(deal.shape),
            ],
            out_specs=full((total, width)),
            scratch_shapes=[pltpu.VMEM((total, width), BF16)],
        ),
        out_shape=jax.ShapeDtypeStruct((total, width), BF16),
        compiler_params=pltpu.CompilerParams(vmem_limit_bytes=48 << 20),
        cost_estimate=pl.CostEstimate(
            flops=2 * total * width * (cols + total) * 2, bytes_accessed=12 << 20, transcendentals=0
        ),
        name="output_rows",
    )(where, activated, down_weight, middle, deal)


def join_heads(blocks, q_cols):
    n, rows, cols = blocks.shape

    def kernel(b_ref, q_ref, k_ref, v_ref):
        for i in range(n):
            q_ref[:, i * q_cols : (i + 1) * q_cols] = b_ref[i, :, :q_cols].astype(F32)
        kv = [b_ref[i, :, q_cols:].astype(F32) for i in range(n)]
        k_ref[...] = jnp.concatenate([x[:, :HEAD] for x in kv], axis=1)
        v_ref[...] = jnp.concatenate([x[:, HEAD:] for x in kv], axis=1)

    return pl.pallas_call(
        kernel,
        out_shape=(
            jax.ShapeDtypeStruct((rows, n * q_cols), F32),
            jax.ShapeDtypeStruct((rows, n * HEAD), F32),
            jax.ShapeDtypeStruct((rows, n * HEAD), F32),
        ),
        name="join_heads",
    )(blocks)


def finish(normed, gate_grad, up_grad, activated, down_grad, output_part, qkv_part, collective_id):
    depth, width = normed.shape
    cols = gate_grad.shape[1]
    rows = width // 8
    tall = cols // rows
    steps = 8 + tall
    chunks = 4
    sums = (output_part, qkv_part)

    def kernel(
        nf_hbm, gg_hbm, ug_hbm, act_hbm, dg_hbm, o_in, qkv_in,
        gate_out, up_out, down_out, o_out, qkv_out,
        gg, ug, dg, left, stage, tall_stage, o_mid, qkv_mid, o_last, qkv_last,
        load_sems, left_sems, own_sems, tall_sems, push_sems, relay_sems,
    ):
        me = lax.axis_index("shard")
        group = lax.axis_index("rep")
        inner = (group == 1) | (group == 2)
        outer = (group == 0) | (group == 3)
        beside = group + 1 - 2 * lax.rem(group, 2)
        across = 3 - group

        def peer_of(i):
            mask = 7 - i
            index = 0
            for weight in (1, 2, 4):
                bits = lax.rem(lax.div(me, weight), 2) + lax.rem(lax.div(mask, weight), 2)
                index = index + weight * lax.rem(bits, 2)
            return index

        def start_left(i, slot):
            @pl.when(i < 8)
            def _():
                first = pl.multiple_of(peer_of(i) * rows, rows)
                pltpu.make_async_copy(
                    nf_hbm.at[:, pl.ds(first, rows)], left.at[slot], left_sems.at[slot]
                ).start()

            @pl.when((i >= 8) & (i < steps))
            def _():
                first = pl.multiple_of((i - 8) * rows, rows)
                pltpu.make_async_copy(
                    act_hbm.at[:, pl.ds(first, rows)], left.at[slot], left_sems.at[slot]
                ).start()

        def wait_left(slot):
            pltpu.make_async_copy(
                nf_hbm.at[:, pl.ds(0, rows)], left.at[slot], left_sems.at[slot]
            ).wait()

        loads = [
            pltpu.make_async_copy(source, target, load_sems.at[k])
            for k, (source, target) in enumerate(((gg_hbm, gg), (ug_hbm, ug), (dg_hbm, dg)))
        ]
        start_left(0, 0)
        for load in loads:
            load.start()
        barrier = pltpu.get_barrier_semaphore()
        for mask in range(1, 8):
            pl.semaphore_signal(
                barrier, inc=1, device_id={"shard": flip(me, mask)}, device_id_type=MESH
            )
        for neighbour in (beside, across):
            pl.semaphore_signal(
                barrier, inc=1, device_id={"rep": neighbour}, device_id_type=MESH
            )
        pl.semaphore_wait(barrier, 9)

        arrays = ((o_in, o_mid, o_last, o_out), (qkv_in, qkv_mid, qkv_last, qkv_out))

        def relay_copy(stage_index, k, c, target):
            start, mid, last, out = arrays[k]
            size = start.shape[0] // chunks
            part = pl.ds(pl.multiple_of(c * size, size), size)
            source, arrived = ((start, mid), (mid, last), (out, out))[stage_index]
            return pltpu.make_async_remote_copy(
                src_ref=source.at[part],
                dst_ref=arrived.at[part],
                send_sem=relay_sems.at[0, stage_index, k * chunks + c],
                recv_sem=relay_sems.at[1, stage_index, k * chunks + c],
                device_id={"rep": target},
                device_id_type=MESH,
            )

        @pl.when(outer)
        def _():
            for c in range(chunks):
                for k in range(2):
                    relay_copy(0, k, c, beside).start()

        def relay(t):
            def part_of(k, c):
                size = arrays[k][0].shape[0] // chunks
                return pl.ds(pl.multiple_of(c * size, size), size)

            @pl.when(inner & (t < chunks))
            def _():
                for k in range(2):
                    start, mid, last, out = arrays[k]
                    part = part_of(k, t)
                    relay_copy(0, k, t, beside).wait_recv()
                    mid[part, :] = (start[part, :].astype(F32) + mid[part, :].astype(F32)).astype(BF16)
                    relay_copy(1, k, t, across).start()

            @pl.when(inner & (t >= 1) & (t <= chunks))
            def _():
                for k in range(2):
                    start, mid, last, out = arrays[k]
                    part = part_of(k, t - 1)
                    relay_copy(1, k, t - 1, across).wait_recv()
                    out[part, :] = (mid[part, :].astype(F32) + last[part, :].astype(F32)).astype(BF16)
                    relay_copy(2, k, t - 1, beside).start()

            @pl.when(outer & (t >= 2) & (t <= chunks + 1))
            def _():
                for k in range(2):
                    relay_copy(2, k, t - 2, beside).wait_recv()

        outputs = (gate_out, up_out)
        own_columns = pl.ds(pl.multiple_of(me * cols, cols), cols)

        def push(i, j, target):
            return send(
                stage.at[i, j], outputs[j].at[:, own_columns], push_sems, 2 * i + j, target
            )

        def wide(i, carry):
            slot = lax.rem(i, 2)
            start_left(i + 1, 1 - slot)
            wait_left(slot)
            for j, right in enumerate((gg, ug)):

                @pl.when(i == 0)
                def _():
                    loads[j].wait()

                stage[i, j] = t_mm(left[slot], right[...]).astype(BF16)

                @pl.when(i < 7)
                def _():
                    push(i, j, peer_of(i)).start()

                @pl.when(i == 7)
                def _():
                    pltpu.make_async_copy(
                        stage.at[7, j], outputs[j].at[:, own_columns], own_sems.at[j]
                    ).start()

            @pl.when(lax.rem(i, 2) == 1)
            def _():
                relay(lax.div(i, 2))

            return carry

        lax.fori_loop(0, 8, wide, 0)
        loads[2].wait()

        def tall_copy(i):
            slot = lax.rem(i, 2)
            first = pl.multiple_of((i - 8) * rows, rows)
            return pltpu.make_async_copy(
                tall_stage.at[slot], down_out.at[pl.ds(first, rows), :], tall_sems.at[slot]
            )

        def high(i, carry):
            slot = lax.rem(i, 2)
            start_left(i + 1, 1 - slot)
            wait_left(slot)

            @pl.when(i >= 10)
            def _():
                tall_copy(i - 2).wait()

            tall_stage[slot] = t_mm(left[slot], dg[...]).astype(BF16)
            tall_copy(i).start()

            @pl.when(lax.rem(i, 2) == 1)
            def _():
                relay(lax.div(i, 2))

            return carry

        lax.fori_loop(8, steps, high, 0)
        for i in (steps - 2, steps - 1):
            tall_copy(i).wait()
        for j in range(2):
            pltpu.make_async_copy(
                stage.at[7, j], outputs[j].at[:, own_columns], own_sems.at[j]
            ).wait()
        for t in range(steps // 2, chunks + 2):
            relay(t)

        def drain(i, carry):
            for j in range(2):
                push(i, j, peer_of(i)).wait()
            return carry

        lax.fori_loop(0, 7, drain, 0)

        @pl.when(outer)
        def _():
            for c in range(chunks):
                for k in range(2):
                    relay_copy(0, k, c, beside).wait_send()

        @pl.when(inner)
        def _():
            for c in range(chunks):
                for k in range(2):
                    relay_copy(1, k, c, across).wait_send()
                    relay_copy(2, k, c, beside).wait_send()

    exchanged = jax.ShapeDtypeStruct((rows, 8 * cols), BF16)
    return pl.pallas_call(
        kernel,
        out_shape=(
            exchanged,
            exchanged,
            jax.ShapeDtypeStruct((cols, width), BF16),
            jax.ShapeDtypeStruct(output_part.shape, BF16),
            jax.ShapeDtypeStruct(qkv_part.shape, BF16),
        ),
        in_specs=[ANY] * 5 + [VMEM] * 2,
        out_specs=[ANY] * 3 + [VMEM] * 2,
        scratch_shapes=[
            pltpu.VMEM((depth, cols), BF16),
            pltpu.VMEM((depth, cols), BF16),
            pltpu.VMEM((depth, width), BF16),
            pltpu.VMEM((2, depth, rows), BF16),
            pltpu.VMEM((8, 2, rows, cols), BF16),
            pltpu.VMEM((2, rows, width), BF16),
        ]
        + [pltpu.VMEM(x.shape, BF16) for unused in range(2) for x in sums]
        + [
            pltpu.SemaphoreType.DMA((3,)),
            pltpu.SemaphoreType.DMA((2,)),
            pltpu.SemaphoreType.DMA((2,)),
            pltpu.SemaphoreType.DMA((2,)),
            pltpu.SemaphoreType.DMA((2, 14)),
            pltpu.SemaphoreType.DMA((2, 3, 2 * chunks)),
        ],
        compiler_params=comm_params(collective_id, 62),
        cost_estimate=pl.CostEstimate(
            flops=120_000_000_000, bytes_accessed=80 << 20, transcendentals=0
        ),
        name="finish",
    )(normed, gate_grad, up_grad, activated, down_grad, output_part, qkv_part)


def output_rows(where, activated, down_weight, middle, deal, total):
    groups, total, cols = activated.shape
    local, width = middle.shape
    block = 256

    def kernel(w_ref, act_ref, wd_ref, mid_ref, deal_ref, o_ref, rows_ref):
        for i in range(total // block):
            rows = pl.ds(i * block, block)
            rows_ref[rows, :] = (RESIDUAL_SCALE * mm(act_ref[0, rows, :], wd_ref[...])).astype(BF16)
        own = pl.ds(pl.multiple_of(w_ref[1] * local, local), local)
        rows_ref[own, :] = (rows_ref[own, :].astype(F32) + mid_ref[...]).astype(BF16)
        for i in range(total // block):
            rows = pl.ds(i * block, block)
            packed = lax.broadcasted_iota(jnp.int32, (block, total), 1)
            chosen = (deal_ref[rows, :] == packed).astype(BF16)
            o_ref[rows, :] = mm(chosen, rows_ref[...]).astype(BF16)

    def full(shape):
        return pl.BlockSpec(shape, lambda i, w: (0,) * len(shape), pipeline_mode=pl.Buffered(1))

    return pl.pallas_call(
        kernel,
        grid_spec=pltpu.PrefetchScalarGridSpec(
            num_scalar_prefetch=1,
            grid=(1,),
            in_specs=[
                pl.BlockSpec((1, total, cols), lambda i, w: (w[0], 0, 0), pipeline_mode=pl.Buffered(1)),
                full(down_weight.shape),
                full(middle.shape),
                full(deal.shape),
            ],
            out_specs=full((total, width)),
            scratch_shapes=[pltpu.VMEM((total, width), BF16)],
        ),
        out_shape=jax.ShapeDtypeStruct((total, width), BF16),
        compiler_params=pltpu.CompilerParams(vmem_limit_bytes=48 << 20),
        cost_estimate=pl.CostEstimate(
            flops=2 * total * width * (cols + total) * 2, bytes_accessed=12 << 20, transcendentals=0
        ),
        name="output_rows",
    )(where, activated, down_weight, middle, deal)


def join_heads(blocks, q_cols):
    n, rows, cols = blocks.shape

    def kernel(b_ref, q_ref, k_ref, v_ref):
        for i in range(n):
            q_ref[:, i * q_cols : (i + 1) * q_cols] = b_ref[i, :, :q_cols].astype(F32)
        kv = [b_ref[i, :, q_cols:].astype(F32) for i in range(n)]
        k_ref[...] = jnp.concatenate([x[:, :HEAD] for x in kv], axis=1)
        v_ref[...] = jnp.concatenate([x[:, HEAD:] for x in kv], axis=1)

    return pl.pallas_call(
        kernel,
        out_shape=(
            jax.ShapeDtypeStruct((rows, n * q_cols), F32),
            jax.ShapeDtypeStruct((rows, n * HEAD), F32),
            jax.ShapeDtypeStruct((rows, n * HEAD), F32),
        ),
        name="join_heads",
    )(blocks)


def weight_grad(left, right, dtype):
    groups, total, m = left.shape
    n = right.shape[2]
    block = 512
    steps = groups * total // block

    def kernel(l_ref, r_ref, o_ref, acc):
        k = pl.program_id(0)
        term = t_mm(l_ref[...], r_ref[...])

        @pl.when(k == 0)
        def _():
            acc[...] = term

        @pl.when(k > 0)
        def _():
            acc[...] += term

        @pl.when(k == steps - 1)
        def _():
            o_ref[...] = acc[...].astype(o_ref.dtype)

    return pl.pallas_call(
        kernel,
        grid=(steps,),
        in_specs=[
            pl.BlockSpec((block, m), lambda k: (k, 0)),
            pl.BlockSpec((block, n), lambda k: (k, 0)),
        ],
        out_specs=pl.BlockSpec((m, n), lambda k: (0, 0), pipeline_mode=pl.Buffered(1)),
        out_shape=jax.ShapeDtypeStruct((m, n), dtype),
        scratch_shapes=[pltpu.VMEM((m, n), F32)],
        compiler_params=pltpu.CompilerParams(vmem_limit_bytes=56 << 20),
        cost_estimate=pl.CostEstimate(
            flops=2 * groups * total * m * n, bytes_accessed=2 * groups * total * (m + n), transcendentals=0
        ),
        name="weight_grad",
    )(left.reshape(groups * total, m), right.reshape(groups * total, n))


def per_device_plane(
    tokens, attn_gain, query_weight, key_weight, value_weight, output_weight, ffn_gain,
    gate_weight, up_weight, down_weight, dealing, lengths, cotangent,
):
    n = 8
    here = lax.axis_index("shard")
    group = lax.axis_index("rep")
    replicas = lax.axis_size("rep")
    local, width = tokens.shape
    total = local * n
    rows = query_weight.shape[0]
    q_cols = query_weight.shape[1] // n
    ff_cols = gate_weight.shape[1] // n
    core = lax.rem(here, 2)
    half = HEAD // 2
    freq = ROPE_BASE ** (-(jnp.arange(half, dtype=F32) * 2.0) / (2.0 * half))
    freq = jnp.tile(freq, 4)[None, :]

    (
        normed, q, kv, attention, q_weight, kv_weight, gate_cols, up_cols,
        middle, normed_ffn, down_grads, act_grads, cot_own,
    ) = front(
        tokens, attn_gain, query_weight, key_weight, value_weight, output_weight, ffn_gain,
        gate_weight, up_weight, down_weight, dealing, lengths, cotangent, freq, replicas,
    )

    held = lax.dynamic_slice_in_dim(normed_ffn, core * (total // 2), total // 2)
    onward = [(i, (i + 1) % replicas) for i in range(replicas)]
    beside = [(i, i ^ 1) for i in range(n)]
    arrivals = []
    for hop in range(1, replicas):
        held = lax.ppermute(held, "rep", onward)
        where = jnp.stack([lax.rem(group + replicas - hop, replicas), core]).astype(jnp.int32)
        arrivals.append((where, held, lax.ppermute(held, "shard", beside)))

    *filled, normed_ffn_part = ffn_own(
        group.astype(jnp.int32)[None], normed_ffn, act_grads, gate_cols, up_cols
    )
    middle_grad, ffn_gain_part, branch_grad = pull_gather(
        normed_ffn_part, middle, ffn_gain, cot_own, 2
    )
    branch_grad, unused_hop = lax.optimization_barrier(
        (branch_grad.reshape(total, width), arrivals[0][1])
    )
    output_part = output_rows(
        jnp.stack([group, here]).astype(jnp.int32), filled[1], down_weight, middle,
        dealing.reshape(total, 1), total,
    )
    normed_part, qkv_grad, output_grad = attention_backward(
        branch_grad, output_weight, attention, q, kv, normed, q_weight, kv_weight, lengths, freq
    )
    normed_part, unused_hop = lax.optimization_barrier((normed_part, arrivals[1][1]))
    tokens_grad, layer_output, gains = pull_tokens(
        normed_part, output_part, tokens, attn_gain, middle_grad, ffn_gain_part, replicas, 3
    )
    act_grads, tokens_grad = lax.optimization_barrier((act_grads, tokens_grad))
    qkv_part = exchange(qkv_grad.reshape(n, rows, q_cols + 2 * HEAD))
    for where, from_ring, from_core in arrivals:
        filled = ffn_other(where, from_ring, from_core, act_grads, gate_cols, up_cols, filled)
    left, *rights = [x.reshape(replicas * total, -1) for x in (filled[0], filled[2], filled[3])]
    gate_grad, up_grad, down_grad, output_grad, qkv_grad = finish(
        left, *rights, filled[1].reshape(replicas * total, -1), down_grads.reshape(replicas * total, -1),
        output_grad, qkv_part.reshape(width, -1), 4,
    )
    return (
        layer_output,
        tokens_grad,
        gains[0],
        *join_heads(qkv_grad.reshape(n, rows, -1), q_cols),
        output_grad.astype(F32),
        gains[1],
        gate_grad.astype(F32),
        up_grad.astype(F32),
        down_grad.astype(F32),
    )


def per_device(
    tokens,
    attn_gain,
    query_weight,
    key_weight,
    value_weight,
    output_weight,
    ffn_gain,
    gate_weight,
    up_weight,
    down_weight,
    dealing,
    lengths,
    cotangent,
):
    n = lax.axis_size("shard")
    here = lax.axis_index("shard")
    local, width = tokens.shape
    total = local * n
    rows = query_weight.shape[0]
    ff_cols = gate_weight.shape[1] // n
    q_cols = query_weight.shape[1] // n
    copies = n // KV_HEADS
    own = here * local

    packed = jnp.arange(total, dtype=jnp.int32)
    segment, position = places(packed, lengths[0])
    cos_q, sin_q = rope_tables(position, q_cols)
    cos_k, sin_k = cos_q[:, :HEAD], sin_q[:, :HEAD]
    dealt = (dealing[0][:, None] == packed[None, :]).astype(BF16)

    def column_blocks(weight, cols):
        return weight.reshape(rows, n, cols).transpose(1, 0, 2)

    def head_blocks(weight):
        blocks = weight.reshape(rows, KV_HEADS, HEAD).transpose(1, 0, 2)
        return jnp.repeat(blocks, copies, axis=0)

    spread_cotangent = lax.all_gather(cotangent, ("rep", "shard"), axis=0, tiled=True)
    all_dealing = lax.all_gather(dealing, "rep", axis=0, tiled=True)
    qkv = exchange(
        jnp.concatenate(
            [column_blocks(query_weight, q_cols), head_blocks(key_weight), head_blocks(value_weight)],
            axis=2,
        )
    ).reshape(width, q_cols + 2 * HEAD)
    gate_cols = exchange(column_blocks(gate_weight, ff_cols)).reshape(width, ff_cols)
    up_cols = exchange(column_blocks(up_weight, ff_cols)).reshape(width, ff_cols)

    normed = gather_rows(rms_scale(tokens.astype(F32), attn_gain).astype(BF16))
    pre = mm(normed, qkv)
    queries = rotate(pre[:, :q_cols], cos_q, sin_q).astype(BF16)
    keys = rotate(pre[:, q_cols : q_cols + HEAD], cos_k, sin_k).astype(BF16)
    values = pre[:, q_cols + HEAD :].astype(BF16)
    attention = attention_forward(queries, jnp.concatenate([keys, values], axis=1), lengths)
    branch = scatter_rows(mm(attention, output_weight).astype(BF16))
    middle = tokens.astype(F32) + RESIDUAL_SCALE * branch.astype(F32)
    normed_ffn = gather_rows(rms_scale(middle, ffn_gain).astype(BF16))
    own_normed = lax.dynamic_slice_in_dim(normed_ffn, own, local)
    all_normed = lax.all_gather(own_normed, ("rep", "shard"), axis=0, tiled=True)

    reps = lax.axis_size("rep")
    group = lax.axis_index("rep")
    deals = (all_dealing[:, :, None] == packed[None, None, :]).astype(BF16)
    out_grad_all = lax.dot_general(
        deals,
        spread_cotangent.reshape(reps, total, width),
        (((1,), (1,)), ((0,), (0,))),
        preferred_element_type=F32,
    ).reshape(reps * total, width)
    down_grad_all = (RESIDUAL_SCALE * out_grad_all).astype(BF16)
    out_grad = lax.dynamic_slice_in_dim(out_grad_all, group * total + own, local)
    act_grad_all = mm_t(down_grad_all, down_weight)

    def ffn(rows_in, act_grad):
        gate = mm(rows_in, gate_cols)
        up = mm(rows_in, up_cols)
        sigmoid = jax.nn.sigmoid(gate)
        activated = (gate * sigmoid * up).astype(BF16)
        gate_grad = (act_grad * up * sigmoid * (1.0 + gate * (1.0 - sigmoid))).astype(BF16)
        up_grad = (act_grad * gate * sigmoid).astype(BF16)
        return activated, gate_grad, up_grad

    activated, gate_grad, up_grad = ffn(
        normed_ffn, lax.dynamic_slice_in_dim(act_grad_all, group * total, total)
    )
    normed_ffn_part = (mm_t(gate_grad, gate_cols) + mm_t(up_grad, up_cols)).astype(BF16)
    middle_part, ffn_gain_part = norm_pull(
        middle, ffn_gain, scatter_rows(normed_ffn_part).astype(F32)
    )
    middle_grad = out_grad + middle_part
    branch_grad = gather_rows((RESIDUAL_SCALE * middle_grad).astype(BF16))

    own_columns = lax.dynamic_slice_in_dim(dealt, own, local, axis=1)
    layer_output = scatter_rows(
        (
            RESIDUAL_SCALE * mm(mm(dealt, activated).astype(BF16), down_weight)
            + mm(own_columns, middle.astype(BF16))
        ).astype(BF16)
    )

    attention_grad = mm_t(branch_grad, output_weight).astype(BF16)
    dq, dk, dv = attention_gradients(
        queries, jnp.concatenate([keys, values], axis=1), attention_grad, lengths
    )
    pre_grad = jnp.concatenate(
        [
            unrotate(dq, cos_q, sin_q).astype(BF16),
            unrotate(dk, cos_k, sin_k).astype(BF16),
            dv.astype(BF16),
        ],
        axis=1,
    )
    normed_part = mm_t(pre_grad, qkv).astype(BF16)
    hidden_part, attn_gain_part = norm_pull(
        tokens.astype(F32), attn_gain, scatter_rows(normed_part).astype(F32)
    )
    tokens_grad = middle_grad + hidden_part

    activated, gate_grad, up_grad = ffn(all_normed, act_grad_all)
    gate_part = exchange(t_mm(all_normed, gate_grad).astype(BF16).reshape(n, rows, ff_cols))
    up_part = exchange(t_mm(all_normed, up_grad).astype(BF16).reshape(n, rows, ff_cols))
    down_part = t_mm(activated, down_grad_all)
    output_part = rep_sum(t_mm(attention, branch_grad).astype(BF16))
    qkv_part = rep_sum(exchange(t_mm(normed, pre_grad).astype(BF16).reshape(n, rows, q_cols + 2 * HEAD)))

    def join(blocks):
        return blocks.transpose(1, 0, 2).reshape(rows, -1).astype(F32)

    def join_heads(blocks):
        blocks = blocks.astype(F32).reshape(KV_HEADS, copies, rows, HEAD).sum(axis=1)
        return blocks.transpose(1, 0, 2).reshape(rows, KV_HEADS * HEAD)

    gain_grads = lax.psum(jnp.concatenate([attn_gain_part, ffn_gain_part]), ("rep", "shard"))
    return (
        layer_output,
        tokens_grad,
        gain_grads[0],
        join(qkv_part[:, :, :q_cols]),
        join_heads(qkv_part[:, :, q_cols : q_cols + HEAD]),
        join_heads(qkv_part[:, :, q_cols + HEAD :]),
        output_part.astype(F32),
        gain_grads[1],
        join(gate_part),
        join(up_part),
        down_part,
    )


def solution(mesh):
    both = P(("rep", "shard"), None)
    rowed = P("shard", None)
    return jax.shard_map(
        per_device_plane if (mesh.shape["rep"], mesh.shape["shard"]) == (4, 8) else per_device,
        mesh=mesh,
        in_specs=(
            both, P(), rowed, rowed, rowed, rowed, P(), rowed, rowed, rowed,
            P("rep", None), P("rep", None), both,
        ),
        out_specs=(both, both, P(), rowed, rowed, rowed, rowed, P(), rowed, rowed, rowed),
        check_vma=False,
    )
```

```python
import functools

import jax
import jax.numpy as jnp
from jax import lax
from jax.experimental import pallas as pl
from jax.experimental.pallas import tpu as pltpu
from jax.sharding import PartitionSpec as P

HEADS = 32
KV_HEADS = 8
HEAD = 64
EPSILON = 1e-05
RESIDUAL_SCALE = 0.22
SCORE_SCALE = 0.015625
ROPE_BASE = 10000000.0
MASKED = -1e30
BF16 = jnp.bfloat16
F32 = jnp.float32


def mm(a, b):
    return jnp.dot(a, b, preferred_element_type=F32)


def mm_t(a, b):
    return lax.dot_general(a, b, (((1,), (1,)), ((), ())), preferred_element_type=F32)


def t_mm(a, b):
    return lax.dot_general(a, b, (((0,), (0,)), ((), ())), preferred_element_type=F32)


def rms_scale(hidden, gain_vector):
    return (
        hidden
        * lax.rsqrt(jnp.mean(hidden * hidden, axis=-1, keepdims=True) + EPSILON)
        * gain_vector
    )


def places(packed_index, seq_lengths):
    seq_ends = jnp.cumsum(seq_lengths)
    starts = seq_ends - seq_lengths
    segment = jnp.sum((packed_index[:, None] >= seq_ends[None, :]).astype(jnp.int32), axis=1)
    chosen = segment[:, None] == jnp.arange(seq_lengths.shape[0], dtype=jnp.int32)[None, :]
    position = packed_index - jnp.sum(jnp.where(chosen, starts[None, :], 0), axis=1)
    return segment, position


def rope_tables(position, width):
    half = HEAD // 2
    frequency = ROPE_BASE ** (-(jnp.arange(half, dtype=F32) * 2.0) / (2.0 * half))
    turned = position.astype(F32)[:, None] * frequency[None, :]
    cosine, sine = jnp.cos(turned), jnp.sin(turned)
    cos_full = jnp.concatenate([cosine, cosine], axis=-1)
    sin_full = jnp.concatenate([-sine, sine], axis=-1)
    return jnp.tile(cos_full, (1, width // HEAD)), jnp.tile(sin_full, (1, width // HEAD))


def swap_halves(x):
    rows, width = x.shape
    half = HEAD // 2
    y = x.reshape(rows, width // HEAD, 2, half)
    return jnp.concatenate([y[:, :, 1:], y[:, :, :1]], axis=2).reshape(rows, width)


def rotate(x, cos_full, sin_full):
    return x * cos_full + swap_halves(x) * sin_full


def unrotate(x, cos_full, sin_full):
    return x * cos_full - swap_halves(x) * sin_full


def gather_rows(x):
    return lax.all_gather(x, "shard", axis=0, tiled=True)


def scatter_rows(x):
    return lax.psum_scatter(x, "shard", scatter_dimension=0, tiled=True)


def exchange(blocks):
    return lax.all_to_all(blocks, "shard", split_axis=0, concat_axis=0, tiled=True)


def rep_sum(x):
    count = lax.axis_size("rep")
    where = lax.axis_index("rep")
    half = count // 2
    for hop in range(half - 1):
        moved = lax.ppermute(
            x, "rep", [(hop, hop + 1), (count - 1 - hop, count - 2 - hop)]
        )
        x = (x.astype(F32) + moved.astype(F32)).astype(BF16)
    moved = lax.ppermute(x, "rep", [(half - 1, half), (half, half - 1)])
    x = (x.astype(F32) + moved.astype(F32)).astype(BF16)
    for hop in range(half - 1):
        near, far = half - 1 - hop, half + hop
        moved = lax.ppermute(x, "rep", [(near, near - 1), (far, far + 1)])
        x = jnp.where((where == near - 1) | (where == far + 1), moved, x)
    return x


MESH = pl.DeviceIdType.MESH


def flip(index, bits):
    for weight in (1, 2, 4):
        if bits & weight:
            index = index + weight - 2 * weight * lax.rem(lax.div(index, weight), 2)
    return index


def send(src, dst, sems, k, target):
    return pltpu.make_async_remote_copy(
        src_ref=src,
        dst_ref=dst,
        send_sem=sems.at[0, k],
        recv_sem=sems.at[1, k],
        device_id={"shard": target},
        device_id_type=MESH,
    )


def greet(me, masks):
    barrier = pltpu.get_barrier_semaphore()
    for mask in masks:
        pl.semaphore_signal(
            barrier, inc=1, device_id={"shard": flip(me, mask)}, device_id_type=MESH
        )
    pl.semaphore_wait(barrier, len(masks))


GATHER_SEMS = 13
BULK = (12, 2, 2)


def gather_steps(me, out, sems):
    core, px, py, diag = (flip(me, mask) for mask in (1, 2, 4, 6))
    half = out.shape[1] // 2
    low, high, whole = pl.ds(0, half), pl.ds(half, half), pl.ds(0, 2 * half)

    def move(k, block, rows, target):
        ref = out.at[block, rows]
        copy = send(ref, ref, sems, k, target)
        copy.start()
        return copy

    x_low, y_high = move(0, me, low, px), move(1, me, high, py)
    own = move(2, me, whole, core)
    x_high, y_low = move(3, me, high, px), move(4, me, low, py)
    yield
    x_low.wait_recv()
    diag_low = move(5, px, low, py)
    pieces = [own, move(6, px, low, core)]
    yield
    y_high.wait_recv()
    diag_high = move(7, py, high, px)
    pieces.append(move(8, py, high, core))
    yield
    x_high.wait_recv()
    pieces.append(move(9, px, high, core))
    yield
    y_low.wait_recv()
    pieces.append(move(10, py, low, core))
    yield
    diag_low.wait_recv()
    pieces.append(move(11, diag, low, core))
    diag_high.wait_recv()
    pieces.append(move(12, diag, high, core))
    yield
    for copy in pieces:
        copy.wait_recv()
    for copy in [x_low, y_high, x_high, y_low, diag_low, diag_high] + pieces:
        copy.wait_send()


def gather_blocks(me, out, sems):
    for unused_step in gather_steps(me, out, sems):
        pass


SCATTER_SEMS = 10


def scatter_steps(me, partial, sib_out, sib_in, acc, x_out, x_in, y_out, y_in, sems):
    core, px, py = (flip(me, mask) for mask in (1, 2, 4))
    half = acc.shape[1] // 2
    masks = (6, 2, 4, 0)
    low, high = pl.ds(0, half), pl.ds(half, half)
    copies = []

    def move(src, dst, k, target):
        copy = send(src, dst, sems, k, target)
        copy.start()
        copies.append(copy)
        return copy

    inside = []
    for i, mask in enumerate(masks):
        sib_out[i] = partial(flip(core, mask)).astype(BF16)
        inside.append(move(sib_out.at[i], sib_in.at[i], i, core))
    yield
    for i, mask in enumerate(masks):
        term = partial(flip(me, mask))
        inside[i].wait_recv()
        acc[i] = term + sib_in[i].astype(F32)
        if mask == 6:
            x_out[0] = acc[i, low].astype(BF16)
            x_diag = move(x_out.at[0], x_in.at[0], 4, px)
            y_out[0] = acc[i, high].astype(BF16)
            y_diag = move(y_out.at[0], y_in.at[0], 5, py)
        if mask == 2:
            x_out[1] = acc[i, low].astype(BF16)
            x_near = move(x_out.at[1], x_in.at[1], 6, px)
        if mask == 4:
            y_out[1] = acc[i, high].astype(BF16)
            y_near = move(y_out.at[1], y_in.at[1], 7, py)
    yield
    x_diag.wait_recv()
    y_out[2] = (acc[2, low] + x_in[0].astype(F32)).astype(BF16)
    y_last = move(y_out.at[2], y_in.at[2], 8, py)
    y_diag.wait_recv()
    x_out[2] = (acc[1, high] + y_in[0].astype(F32)).astype(BF16)
    x_last = move(x_out.at[2], x_in.at[2], 9, px)
    yield
    x_near.wait_recv()
    y_near.wait_recv()
    y_last.wait_recv()
    acc[3, low] = acc[3, low] + x_in[1].astype(F32) + y_in[2].astype(F32)
    x_last.wait_recv()
    acc[3, high] = acc[3, high] + y_in[1].astype(F32) + x_in[2].astype(F32)
    yield
    for copy in copies:
        copy.wait_send()


def scatter_blocks(me, partial, *buffers):
    for unused_step in scatter_steps(me, partial, *buffers):
        pass
    return buffers[2][3]


def scatter_scratch(rows, width):
    half = rows // 2
    return [
        pltpu.VMEM((4, rows, width), BF16),
        pltpu.VMEM((4, rows, width), BF16),
        pltpu.VMEM((4, rows, width), F32),
        pltpu.VMEM((3, half, width), BF16),
        pltpu.VMEM((3, half, width), BF16),
        pltpu.VMEM((3, half, width), BF16),
        pltpu.VMEM((3, half, width), BF16),
        pltpu.SemaphoreType.DMA((2, SCATTER_SEMS)),
    ]


VMEM = pl.BlockSpec(memory_space=pltpu.VMEM)
SMEM = pl.BlockSpec(memory_space=pltpu.SMEM)
ANY = pl.BlockSpec(memory_space=pl.ANY)


def comm_params(collective_id, mebibytes):
    return pltpu.CompilerParams(
        collective_id=collective_id, has_side_effects=True, vmem_limit_bytes=mebibytes << 20
    )


def front(
    tokens, attn_gain, query_weight, key_weight, value_weight, output_weight, ffn_gain,
    gate_weight, up_weight, down_weight, dealing, lengths, cotangent, freq, replicas,
):
    local, width = tokens.shape
    total = 8 * local
    shard_rows = query_weight.shape[0]
    q_cols = query_weight.shape[1] // 8
    ff_cols = gate_weight.shape[1] // 8
    block = 256
    others = (1, 2, 3, 4, 5, 6, 7)

    def kernel(
        tok_ref, gain_ref, wq_hbm, wk_ref, wv_ref, wo_ref, fgain_ref, wg_hbm, wu_hbm,
        wd_ref, deal_ref, len_ref, cot_ref, freq_ref,
        n_ref, q_ref, kv_ref, att_ref, qw_ref, kvw_ref, wg_out, wu_out, mid_ref, nf_ref, dg_out, ag_out, cot_out, half_out,
        kv_stage, c_all, dg_own, ag_stage,
        sib_out, sib_in, acc, x_out, x_in, y_out, y_in, scatter_sems,
        n_sems, c_sems, nf_sems, qkv_sems, bulk_sems, ring_sems, pair_sems, local_sems,
    ):
        me = lax.axis_index("shard")
        group = lax.axis_index("rep")
        core = lax.rem(me, 2)
        after = lax.rem(group + 1, replicas)
        before = lax.rem(group + replicas - 1, replicas)

        barrier = pltpu.get_barrier_semaphore()
        for mask in others:
            pl.semaphore_signal(
                barrier, inc=1, device_id={"shard": flip(me, mask)}, device_id_type=MESH
            )
        for neighbour in (after, before):
            pl.semaphore_signal(
                barrier, inc=1, device_id={"rep": neighbour}, device_id_type=MESH
            )
        n_ref[me] = rms_scale(tok_ref[...].astype(F32), gain_ref[...]).astype(BF16)
        c_all[me] = cot_ref[...]
        for d in range(8):
            lanes = slice(d * HEAD, (d + 1) * HEAD)
            kv_stage[d] = jnp.concatenate([wk_ref[:, lanes], wv_ref[:, lanes]], axis=1)
        pl.semaphore_wait(barrier, len(others) + 2)

        gather_c = gather_steps(me, c_all, c_sems)
        next(gather_c)
        gather_n = gather_steps(me, n_ref, n_sems)
        next(gather_n)
        weights = []
        for mask in others:
            peer = flip(me, mask)
            columns = pl.ds(pl.multiple_of(peer * q_cols, q_cols), q_cols)
            weights.append(send(wq_hbm.at[:, columns], qw_ref.at[me], qkv_sems, 2 * mask - 2, peer))
            weights.append(send(kv_stage.at[peer], kvw_ref.at[me], qkv_sems, 2 * mask - 1, peer))
        for copy in weights:
            copy.start()
        own_columns = pl.ds(pl.multiple_of(me * ff_cols, ff_cols), ff_cols)
        own_q = pl.ds(pl.multiple_of(me * q_cols, q_cols), q_cols)
        gate_slot, up_slot = ag_stage.at[:shard_rows], ag_stage.at[pl.ds(shard_rows, shard_rows)]
        kept = [
            pltpu.make_async_copy(wg_hbm.at[:, own_columns], gate_slot, local_sems.at[0]),
            pltpu.make_async_copy(wu_hbm.at[:, own_columns], up_slot, local_sems.at[1]),
            pltpu.make_async_copy(wq_hbm.at[:, own_q], qw_ref.at[me], local_sems.at[2]),
        ]
        for copy in kept:
            copy.start()
        kvw_ref[me] = kv_stage[me]

        bulk, waiting = [], []
        for source, target in ((wg_hbm, wg_out), (wu_hbm, wu_out)):
            for part in range(2):
                rows = pl.ds(part * (shard_rows // 2), shard_rows // 2)
                for mask in (2, 4, 6, 3, 5, 7, 1):
                    waiting.append((source, target, rows, mask))

        def more(count):
            for unused in range(min(count, len(waiting))):
                source, target, rows, mask = waiting.pop(0)
                peer = flip(me, mask)
                columns = pl.ds(pl.multiple_of(peer * ff_cols, ff_cols), ff_cols)
                copy = send(
                    source.at[rows, columns], target.at[me, rows], bulk_sems, len(bulk), peer
                )
                copy.start()
                bulk.append(copy)

        for unused in gather_c:
            pass

        def permute(first):
            for i in range(total // 2 // block):
                row0 = pl.multiple_of(first + i * block, block)
                packed = row0 + lax.broadcasted_iota(jnp.int32, (block, total), 0)
                chosen = (deal_ref[...] == packed).astype(BF16)
                dealt = mm(chosen, c_all[...].reshape(total, width))
                dg_own[pl.ds(row0, block), :] = (RESIDUAL_SCALE * dealt).astype(BF16)

        near = pl.multiple_of(core * (total // 2), total // 2)
        far = pl.multiple_of((1 - core) * (total // 2), total // 2)
        half = pl.ds(near, total // 2)

        def ring(hop):
            held = lax.rem(group + replicas - hop, replicas)
            ref = dg_out.at[held, half]
            copy = pltpu.make_async_remote_copy(
                src_ref=dg_own.at[half] if hop == 0 else ref,
                dst_ref=ref,
                send_sem=ring_sems.at[0, hop],
                recv_sem=ring_sems.at[1, hop],
                device_id={"rep": after},
                device_id_type=MESH,
            )
            copy.start()
            return copy

        def share(hop):
            held = lax.rem(group + replicas - hop, replicas)
            ref = dg_out.at[held, half]
            copy = send(ref, ref, pair_sems, hop - 1, flip(me, 1))
            copy.start()
            return copy

        permute(near)
        hops, shares = [ring(0)], []
        for unused in range(4):
            next(gather_n)
        permute(far)
        packed = me * local + lax.broadcasted_iota(jnp.int32, (local, total), 0)
        chosen = (deal_ref[...] == packed).astype(BF16)
        cot_out[...] = mm(chosen, c_all[...].reshape(total, width)).astype(BF16)
        store = pltpu.make_async_copy(dg_own, dg_out.at[group], local_sems.at[3])
        store.start()
        for unused in gather_n:
            pass
        for copy in kept:
            copy.wait()
        kept = [
            pltpu.make_async_copy(gate_slot, wg_out.at[me], local_sems.at[0]),
            pltpu.make_async_copy(up_slot, wu_out.at[me], local_sems.at[1]),
        ]
        for copy in kept:
            copy.start()
        for copy in weights:
            copy.wait_recv()
        more(BULK[0])
        for i in range(total // block):
            rows = pl.ds(i * block, block)
            x = n_ref[pl.ds(i * block // local, block // local)].reshape(block, width)
            cosine, sine = lane_rope(i * block, block, freq_ref[...], len_ref)
            pre = mm(x, qw_ref[...].reshape(width, q_cols))
            for j in range(q_cols // (2 * HEAD)):
                lanes = slice(j * 2 * HEAD, (j + 1) * 2 * HEAD)
                y = pre[:, lanes]
                q_ref[rows, lanes] = (y * cosine + lane_swap(y) * sine).astype(BF16)
            cosine, sine = keys_only(cosine, sine)
            y = mm(x, kvw_ref[...].reshape(width, 2 * HEAD))
            kv_ref[rows, :] = (y * cosine + lane_swap(y) * sine).astype(BF16)
        attend(q_cols // HEAD, block, q_ref, kv_ref, len_ref, att_ref)

        def partial(d):
            return mm(att_ref[pl.ds(pl.multiple_of(d * local, local), local), :], wo_ref[...])

        def next_hop():
            hop = len(hops)
            hops[-1].wait_recv()
            if hop < replicas - 1:
                hops.append(ring(hop))
            shares.append(share(hop))

        def act_grad(held, source):
            for i in range(total // block):
                rows = pl.ds(i * block, block)
                ag_stage[rows, :] = mm_t(source[rows, :], wd_ref[...]).astype(BF16)
            copy = pltpu.make_async_copy(ag_stage, ag_out.at[held], local_sems.at[3])
            copy.start()
            copy.wait()

        next_hop()
        scatter = scatter_steps(
            me, partial, sib_out, sib_in, acc, x_out, x_in, y_out, y_in, scatter_sems
        )
        next(scatter)
        more(BULK[1])
        for unused in scatter:
            pass
        branch = acc[3]
        middle = tok_ref[...].astype(F32) + RESIDUAL_SCALE * branch
        mid_ref[...] = middle
        nf_ref[me] = rms_scale(middle, fgain_ref[...]).astype(BF16)
        gather_nf = gather_steps(me, nf_ref, nf_sems)
        next(gather_nf)
        more(BULK[2])
        for unused in gather_nf:
            pass
        more(len(waiting))
        give = pltpu.make_async_copy(nf_ref.at[pl.ds(4 * core, 4)], half_out, local_sems.at[4])
        give.start()
        store.wait()
        for copy in kept:
            copy.wait()
        act_grad(group, dg_own)
        hops[0].wait_send()
        if len(shares) < replicas - 1:
            next_hop()
        for done in range(replicas - 1):
            if len(shares) < done + 1:
                next_hop()
            held = lax.rem(group + replicas - 1 - done, replicas)
            shares[done].wait_recv()
            load = pltpu.make_async_copy(dg_out.at[held], dg_own, local_sems.at[3])
            load.start()
            load.wait()
            act_grad(held, dg_own)
        give.wait()
        for copy in bulk:
            copy.wait_recv()
        for copy in weights + bulk + hops[1:] + shares:
            copy.wait_send()

    rows8 = jax.ShapeDtypeStruct((8, local, width), BF16)
    half_sems = pltpu.SemaphoreType.DMA
    outs = pl.pallas_call(
        kernel,
        out_shape=(
            rows8,
            jax.ShapeDtypeStruct((total, q_cols), BF16),
            jax.ShapeDtypeStruct((total, 2 * HEAD), BF16),
            jax.ShapeDtypeStruct((total, q_cols), BF16),
            jax.ShapeDtypeStruct((8, shard_rows, q_cols), BF16),
            jax.ShapeDtypeStruct((8, shard_rows, 2 * HEAD), BF16),
            jax.ShapeDtypeStruct((8, shard_rows, ff_cols), BF16),
            jax.ShapeDtypeStruct((8, shard_rows, ff_cols), BF16),
            jax.ShapeDtypeStruct((local, width), F32),
            rows8,
            jax.ShapeDtypeStruct((replicas, total, width), BF16),
            jax.ShapeDtypeStruct((replicas, total, ff_cols), BF16),
            jax.ShapeDtypeStruct((local, width), BF16),
            jax.ShapeDtypeStruct((4, local, width), BF16),
        ),
        in_specs=[VMEM, VMEM, ANY, VMEM, VMEM, VMEM, VMEM, ANY, ANY, VMEM, VMEM, SMEM, VMEM, VMEM],
        out_specs=[VMEM] * 6 + [ANY, ANY, VMEM, VMEM, ANY, ANY, VMEM, ANY],
        scratch_shapes=[
            pltpu.VMEM((8, shard_rows, 2 * HEAD), BF16),
            pltpu.VMEM((8, local, width), BF16),
            pltpu.VMEM((total, width), BF16),
            pltpu.VMEM((total, ff_cols), BF16),
        ]
        + scatter_scratch(local, width)
        + [
            half_sems((2, GATHER_SEMS)),
            half_sems((2, GATHER_SEMS)),
            half_sems((2, GATHER_SEMS)),
            half_sems((2, 14)),
            half_sems((2, 28)),
            half_sems((2, replicas)),
            half_sems((2, replicas)),
            half_sems((5,)),
        ],
        compiler_params=comm_params(0, 56),
        cost_estimate=pl.CostEstimate(
            flops=200_000_000_000, bytes_accessed=50 << 20, transcendentals=total * total
        ),
        name="front",
    )(
        tokens, attn_gain[None, :], query_weight, key_weight, value_weight, output_weight,
        ffn_gain[None, :], gate_weight, up_weight, down_weight, dealing, lengths, cotangent, freq,
    )
    normed, q, kv, attention, qw, kvw, wg, wu, middle, nf, dg, ag, cot, held = outs
    return (
        normed.reshape(total, width), q, kv, attention,
        qw.reshape(width, q_cols), kvw.reshape(width, 2 * HEAD),
        wg.reshape(width, ff_cols), wu.reshape(width, ff_cols),
        middle, nf.reshape(total, width), dg, ag, cot,
        held.reshape(total // 2, width),
    )


def norm_pull(x, gain, grad):
    scale = lax.rsqrt(jnp.mean(x * x, axis=-1, keepdims=True) + EPSILON)
    pulled = gain * grad
    rows_part = scale * pulled - x * (
        scale * scale * scale * jnp.mean(pulled * x, axis=-1, keepdims=True)
    )
    return rows_part, jnp.sum(grad * x * scale, axis=0, keepdims=True)


def pull_gather(part, middle, gain, out_grad, activated, down_weight, deal, collective_id):
    rows, width = middle.shape
    groups, total, cols = activated.shape
    block = 256

    def kernel(
        p_ref, m_ref, gain_ref, g_ref, act_hbm, wd_ref, deal_ref,
        mg_ref, gain_part, out, dealt_ref, act_ref, packed_ref, act_sem, *scratch,
    ):
        me = lax.axis_index("shard")
        *buffers, scatter_sems, sems = scratch
        load = pltpu.make_async_copy(act_hbm.at[lax.axis_index("rep")], act_ref, act_sem.at[0])
        load.start()
        greet(me, (1, 2, 4))

        def down(i, carry):
            chunk = pl.ds(pl.multiple_of(i * block, block), block)
            packed_ref[chunk, :] = (RESIDUAL_SCALE * mm(act_ref[chunk, :], wd_ref[...])).astype(BF16)
            return carry

        def deal_out(i, carry):
            chunk = pl.ds(pl.multiple_of(i * block, block), block)
            packed = lax.broadcasted_iota(jnp.int32, (block, total), 1)
            chosen = (deal_ref[chunk, :] == packed).astype(BF16)
            dealt_ref[chunk, :] = mm(chosen, packed_ref[...]).astype(BF16)
            return carry

        half = total // block // 2
        scatter = scatter_steps(
            me,
            lambda d: p_ref[pl.ds(pl.multiple_of(d * rows, rows), rows), :].astype(F32),
            *buffers,
            scatter_sems,
        )
        next(scatter)
        load.wait()
        lax.fori_loop(0, half, down, 0)
        next(scatter)
        lax.fori_loop(half, 2 * half, down, 0)
        own = pl.ds(pl.multiple_of(me * rows, rows), rows)
        packed_ref[own, :] = (packed_ref[own, :].astype(F32) + m_ref[...]).astype(BF16)
        next(scatter)
        for unused in scatter:
            pass
        rows_part, gain_row = norm_pull(m_ref[...], gain_ref[...], buffers[2][3])
        gain_part[...] = gain_row
        middle_grad = g_ref[...].astype(F32) + rows_part
        mg_ref[...] = middle_grad
        out[me] = (RESIDUAL_SCALE * middle_grad).astype(BF16)
        gather = gather_steps(me, out, sems)
        next(gather)
        lax.fori_loop(0, half, deal_out, 0)
        for unused in range(2):
            next(gather)
        lax.fori_loop(half, 2 * half, deal_out, 0)
        for unused in gather:
            pass

    return pl.pallas_call(
        kernel,
        out_shape=(
            jax.ShapeDtypeStruct((rows, width), F32),
            jax.ShapeDtypeStruct((1, width), F32),
            jax.ShapeDtypeStruct((8, rows, width), BF16),
            jax.ShapeDtypeStruct((total, width), BF16),
        ),
        in_specs=[VMEM] * 4 + [ANY] + [VMEM] * 2,
        out_specs=[VMEM] * 4,
        scratch_shapes=[
            pltpu.VMEM((total, cols), BF16),
            pltpu.VMEM((total, width), BF16),
            pltpu.SemaphoreType.DMA((1,)),
        ]
        + scatter_scratch(rows, width)
        + [pltpu.SemaphoreType.DMA((2, GATHER_SEMS))],
        compiler_params=comm_params(collective_id, 56),
        cost_estimate=pl.CostEstimate(
            flops=60_000_000_000, bytes_accessed=50 * rows * width, transcendentals=rows
        ),
        name="pull_gather",
    )(part, middle, gain[None, :], out_grad, activated, down_weight, deal)


def pull_tokens(
    part, out_part, hidden, gain, middle_grad, other_gain, near, act_grads, wg, wu, filled, replicas, collective_id
):
    rows, width = middle_grad.shape
    groups, total, cols = act_grads.shape
    block = 256
    levels = [("shard", 1), ("shard", 2), ("shard", 4)]
    level = 1
    while level < replicas:
        levels.append(("rep", level))
        level *= 2
    per_half = total // 2 // block

    def kernel(
        p_ref, o_ref, h_ref, gain_ref, mg_ref, og_ref, wg_ref, wu_ref, ag_hbm,
        before_held, before_fetched, after_held, after_fetched, unused_na, unused_act, unused_gg, unused_ug,
        out, lay, gains, na_hbm, act_hbm, gg_hbm, ug_hbm,
        nf_buf, ag_buf, done_buf, in_sems, out_sems, gain_in, gain_out, gain_sems, *scratch,
    ):
        me = lax.axis_index("shard")
        group = lax.axis_index("rep")
        core = lax.rem(me, 2)
        before = lax.rem(group + replicas - 1, replicas)
        after = lax.rem(group + 1, replicas)
        first, second = scratch[:8], scratch[8:]
        parts = (
            (before, before_held, core),
            (before, before_fetched, 1 - core),
            (after, after_held, core),
            (after, after_fetched, 1 - core),
        )

        def rows_of(p, r):
            return pl.ds(pl.multiple_of((parts[p][2] * per_half + r) * block, block), block)

        def loads(p, r):
            held, source, unused = parts[p]
            slot = (p % 2) * per_half + r
            return [
                pltpu.make_async_copy(
                    source.at[pl.ds(pl.multiple_of(r * block, block), block)],
                    nf_buf.at[slot],
                    in_sems.at[0, slot],
                ),
                pltpu.make_async_copy(ag_hbm.at[held, rows_of(p, r)], ag_buf.at[slot], in_sems.at[1, slot]),
            ]

        def stores(p, r):
            held = parts[p][0]
            slot = (p % 2) * per_half + r
            where = rows_of(p, r)
            return [
                pltpu.make_async_copy(nf_buf.at[slot], na_hbm.at[held, where], out_sems.at[0, slot])
            ] + [
                pltpu.make_async_copy(done_buf.at[k, slot], target.at[held, where], out_sems.at[k + 1, slot])
                for k, target in enumerate((act_hbm, gg_hbm, ug_hbm))
            ]

        def start_loads(p):
            for r in range(per_half):
                for copy in loads(p, r):
                    copy.start()

        def wait_stores(p):
            for r in range(per_half):
                for copy in stores(p, r):
                    copy.wait()

        def fill(p):
            if p > 0:
                wait_stores(p - 1)
            if p + 1 < len(parts):
                start_loads(p + 1)

            def step(r, carry):
                slot = (p % 2) * per_half + r
                for copy in loads(p, r):
                    copy.wait()
                results = ffn_rows(nf_buf[slot], ag_buf[slot], wg_ref[...], wu_ref[...])
                for k, result in enumerate(results):
                    done_buf[k, slot] = result
                for copy in stores(p, r):
                    copy.start()
                return carry

            lax.fori_loop(0, per_half, step, 0)

        start_loads(0)
        barrier = pltpu.get_barrier_semaphore()
        peers = []
        for axis, weight in levels:
            index = me if axis == "shard" else group
            peers.append({axis: index + weight - 2 * weight * lax.rem(lax.div(index, weight), 2)})
        for peer in peers:
            pl.semaphore_signal(barrier, inc=1, device_id=peer, device_id_type=MESH)
        pl.semaphore_wait(barrier, len(peers))

        def blocks_of(ref):
            return lambda d: ref[pl.ds(pl.multiple_of(d * rows, rows), rows), :].astype(F32)

        grads = scatter_steps(me, blocks_of(p_ref), *first)
        outputs = scatter_steps(me, blocks_of(o_ref), *second)
        next(grads)
        next(outputs)
        fill(0)
        next(grads)
        fill(1)
        next(grads)
        next(outputs)
        fill(2)
        next(grads)
        next(outputs)
        rows_part, gain_row = norm_pull(h_ref[...].astype(F32), gain_ref[...], first[2][3])
        out[...] = mg_ref[...] + rows_part
        sums = jnp.concatenate([gain_row, og_ref[...]], axis=0)
        for i, peer in enumerate(peers):
            gain_out[i] = sums
            copy = pltpu.make_async_remote_copy(
                src_ref=gain_out.at[i],
                dst_ref=gain_in.at[i],
                send_sem=gain_sems.at[0, i],
                recv_sem=gain_sems.at[1, i],
                device_id=peer,
                device_id_type=MESH,
            )
            copy.start()
            if i == 0:
                fill(3)
            copy.wait()
            sums = sums + gain_in[i]
        gains[...] = sums
        next(outputs)
        lay[...] = second[2][3].astype(BF16)
        for steps in (grads, outputs):
            for unused in steps:
                pass
        wait_stores(3)

    hidden_shape = jax.ShapeDtypeStruct((groups, total, cols), BF16)
    return pl.pallas_call(
        kernel,
        out_shape=(
            jax.ShapeDtypeStruct((rows, width), F32),
            jax.ShapeDtypeStruct((rows, width), BF16),
            jax.ShapeDtypeStruct((2, width), F32),
            jax.ShapeDtypeStruct((groups, total, width), BF16),
            hidden_shape,
            hidden_shape,
            hidden_shape,
        ),
        in_specs=[VMEM] * 8 + [ANY] * 9,
        out_specs=[VMEM] * 3 + [ANY] * 4,
        input_output_aliases={13: 3, 14: 4, 15: 5, 16: 6},
        scratch_shapes=[
            pltpu.VMEM((2 * per_half, block, width), BF16),
            pltpu.VMEM((2 * per_half, block, cols), BF16),
            pltpu.VMEM((3, 2 * per_half, block, cols), BF16),
            pltpu.SemaphoreType.DMA((2, 2 * per_half)),
            pltpu.SemaphoreType.DMA((4, 2 * per_half)),
            pltpu.VMEM((len(levels), 2, width), F32),
            pltpu.VMEM((len(levels), 2, width), F32),
            pltpu.SemaphoreType.DMA((2, len(levels))),
        ]
        + scatter_scratch(rows, width)
        + scatter_scratch(rows, width),
        compiler_params=comm_params(collective_id, 62),
        cost_estimate=pl.CostEstimate(
            flops=60_000_000_000, bytes_accessed=50 * rows * width, transcendentals=rows
        ),
        name="pull_tokens",
    )(
        part, out_part, hidden, gain[None, :], middle_grad, other_gain, wg, wu, act_grads, *near, *filled
    )


def softmax_block(q, k, allowed):
    scores = SCORE_SCALE * mm_t(q, k)
    scores = jnp.where(allowed, scores, MASKED)
    top = jnp.max(scores, axis=-1, keepdims=True)
    weight = jnp.exp(scores - top)
    return weight * (1.0 / jnp.sum(weight, axis=-1, keepdims=True))


def allowed_block(row0, cols, start):
    shape = (start.shape[0], cols)
    query = row0 + lax.broadcasted_iota(jnp.int32, shape, 0)
    key = lax.broadcasted_iota(jnp.int32, shape, 1)
    return (key >= start) & (key <= query)


def sequence_starts(row0, shape, lengths_ref):
    row = row0 + lax.broadcasted_iota(jnp.int32, shape, 0)
    start = jnp.zeros(shape, jnp.int32)
    end = 0
    for i in range(lengths_ref.shape[1]):
        length = lengths_ref[0, i]
        end = end + length
        start = start + jnp.where(row >= end, length, 0)
    return start


def attend(heads, block, q_ref, kv_ref, lengths_ref, o_ref):
    total = kv_ref.shape[0]
    for i in range(total // block):
        cols = (i + 1) * block
        rows = pl.ds(i * block, block)
        allowed = allowed_block(
            i * block, cols, sequence_starts(i * block, (block, 1), lengths_ref)
        )
        kv = kv_ref[:cols, :]
        k, v = kv[:, :HEAD], kv[:, HEAD:]
        for h in range(heads):
            lanes = slice(h * HEAD, (h + 1) * HEAD)
            probs = softmax_block(q_ref[rows, lanes], k, allowed)
            o_ref[rows, lanes] = mm(probs.astype(BF16), v).astype(BF16)


def attend_back(heads, block, q_ref, kv_ref, g_ref, lengths_ref, dq_ref, dk_ref, dv_ref):
    total = kv_ref.shape[0]
    dk_ref[...] = jnp.zeros_like(dk_ref)
    dv_ref[...] = jnp.zeros_like(dv_ref)
    for i in range(total // block):
        cols = (i + 1) * block
        rows = pl.ds(i * block, block)
        allowed = allowed_block(
            i * block, cols, sequence_starts(i * block, (block, 1), lengths_ref)
        )
        kv = kv_ref[:cols, :]
        k, v = kv[:, :HEAD], kv[:, HEAD:]
        for h in range(heads):
            lanes = slice(h * HEAD, (h + 1) * HEAD)
            q, g = q_ref[rows, lanes], g_ref[rows, lanes]
            probs = softmax_block(q, k, allowed)
            probs_grad = mm_t(g, v)
            delta = jnp.sum(probs * probs_grad, axis=-1, keepdims=True)
            score_grad = (probs * (probs_grad - delta)).astype(BF16)
            dq_ref[rows, lanes] = SCORE_SCALE * mm(score_grad, k)
            dk_ref[:cols, :] += SCORE_SCALE * t_mm(score_grad, q)
            dv_ref[:cols, :] += t_mm(probs.astype(BF16), g)


def attention_forward(q, kv, lengths):
    total, width = q.shape

    def kernel(q_ref, kv_ref, lengths_ref, o_ref):
        attend(width // HEAD, 256, q_ref, kv_ref, lengths_ref, o_ref)

    return pl.pallas_call(
        kernel,
        out_shape=jax.ShapeDtypeStruct((total, width), BF16),
        in_specs=[VMEM, VMEM, SMEM],
        out_specs=VMEM,
        compiler_params=pltpu.CompilerParams(vmem_limit_bytes=40 << 20),
        name="attention_forward",
    )(q, kv, lengths)


def attention_gradients(q, kv, grad, lengths):
    total, width = q.shape

    def kernel(q_ref, kv_ref, g_ref, lengths_ref, dq_ref, dk_ref, dv_ref):
        attend_back(width // HEAD, 256, q_ref, kv_ref, g_ref, lengths_ref, dq_ref, dk_ref, dv_ref)

    return pl.pallas_call(
        kernel,
        out_shape=(
            jax.ShapeDtypeStruct((total, width), F32),
            jax.ShapeDtypeStruct((total, HEAD), F32),
            jax.ShapeDtypeStruct((total, HEAD), F32),
        ),
        in_specs=[VMEM, VMEM, VMEM, SMEM],
        out_specs=[VMEM] * 3,
        compiler_params=pltpu.CompilerParams(vmem_limit_bytes=40 << 20),
        name="attention_gradients",
    )(q, kv, grad, lengths)


def lane_rope(row0, rows, freq, lengths_ref):
    shape = (rows, 2 * HEAD)
    row = row0 + lax.broadcasted_iota(jnp.int32, shape, 0)
    position = row - sequence_starts(row0, shape, lengths_ref)
    turned = position.astype(F32) * freq
    lane = lax.broadcasted_iota(jnp.int32, shape, 1)
    first = lax.rem(lane, HEAD) < HEAD // 2
    sine = jnp.sin(turned)
    return jnp.cos(turned), jnp.where(first, -sine, sine)


def lane_swap(x):
    half = HEAD // 2
    lane = lax.broadcasted_iota(jnp.int32, x.shape, 1)
    first = lax.rem(lane, HEAD) < half
    return jnp.where(first, pltpu.roll(x, 2 * HEAD - half, 1), pltpu.roll(x, half, 1))


def keys_only(cosine, sine):
    lane = lax.broadcasted_iota(jnp.int32, cosine.shape, 1)
    return jnp.where(lane < HEAD, cosine, 1.0), jnp.where(lane < HEAD, sine, 0.0)


def attention_backward(
    branch_grad, output_weight, attention, q, kv, normed, q_weight, kv_weight, lengths, freq
):
    total, q_cols = q.shape
    width = normed.shape[1]
    block = 256

    def kernel(
        bg_ref, wo_ref, a_ref, q_ref, kv_ref, n_ref, qw_ref, kvw_ref, len_ref, freq_ref,
        dn_ref, dqkv_ref, dwo_ref, g_ref, dq_ref, dk_ref, dv_ref, pq_ref, pkv_ref,
    ):
        for i in range(total // block):
            rows = pl.ds(i * block, block)
            g_ref[rows, :] = mm_t(bg_ref[rows, :], wo_ref[...]).astype(BF16)
        attend_back(
            q_cols // HEAD, block, q_ref, kv_ref, g_ref, len_ref, dq_ref, dk_ref, dv_ref
        )
        for i in range(total // block):
            rows = pl.ds(i * block, block)
            cosine, sine = lane_rope(i * block, block, freq_ref[...], len_ref)
            for j in range(q_cols // (2 * HEAD)):
                lanes = slice(j * 2 * HEAD, (j + 1) * 2 * HEAD)
                x = dq_ref[rows, lanes]
                pq_ref[rows, lanes] = (x * cosine - lane_swap(x) * sine).astype(BF16)
            cosine, sine = keys_only(cosine, sine)
            x = jnp.concatenate([dk_ref[rows, :], dv_ref[rows, :]], axis=1)
            pkv_ref[rows, :] = (x * cosine - lane_swap(x) * sine).astype(BF16)
            dn_ref[rows, :] = (
                mm_t(pq_ref[rows, :], qw_ref[...]) + mm_t(pkv_ref[rows, :], kvw_ref[...])
            ).astype(BF16)
        for i in range(width // 512):
            cols = slice(i * 512, (i + 1) * 512)
            dqkv_ref[cols, :q_cols] = t_mm(n_ref[:, cols], pq_ref[...]).astype(BF16)
            dqkv_ref[cols, q_cols:] = t_mm(n_ref[:, cols], pkv_ref[...]).astype(BF16)
            dwo_ref[:, cols] = t_mm(a_ref[...], bg_ref[:, cols]).astype(BF16)

    return pl.pallas_call(
        kernel,
        out_shape=(
            jax.ShapeDtypeStruct((total, width), BF16),
            jax.ShapeDtypeStruct((width, q_cols + 2 * HEAD), BF16),
            jax.ShapeDtypeStruct((q_cols, width), BF16),
        ),
        in_specs=[VMEM] * 8 + [SMEM, VMEM],
        out_specs=[VMEM] * 3,
        scratch_shapes=[
            pltpu.VMEM((total, q_cols), BF16),
            pltpu.VMEM((total, q_cols), F32),
            pltpu.VMEM((total, HEAD), F32),
            pltpu.VMEM((total, HEAD), F32),
            pltpu.VMEM((total, q_cols), BF16),
            pltpu.VMEM((total, 2 * HEAD), BF16),
        ],
        compiler_params=pltpu.CompilerParams(vmem_limit_bytes=56 << 20),
        cost_estimate=pl.CostEstimate(flops=30_000_000_000, bytes_accessed=30 << 20, transcendentals=total * total),
        name="attention_backward",
    )(branch_grad, output_weight, attention, q, kv, normed, q_weight, kv_weight, lengths, freq)


def ffn_rows(nf, act_grad, wg, wu):
    gate, up = mm(nf, wg), mm(nf, wu)
    act_grad = act_grad.astype(F32)
    sigmoid = 1.0 / (1.0 + jnp.exp(-gate))
    silu = gate * sigmoid
    activated = (silu * up).astype(BF16)
    gate_grad = (act_grad * up * sigmoid * (1.0 + gate * (1.0 - sigmoid))).astype(BF16)
    return activated, gate_grad, (act_grad * silu).astype(BF16)


def ffn_own(group, nf, act_grads, wg, wu):
    groups, total, cols = act_grads.shape
    width = nf.shape[1]
    block = 256

    def kernel(g_ref, nf_ref, ag_ref, wg_ref, wu_ref, na_ref, act_ref, gg_ref, ug_ref, dn_ref):
        nf = nf_ref[...]
        act, gg, ug = ffn_rows(nf, ag_ref[0], wg_ref[...], wu_ref[...])
        na_ref[0], act_ref[0], gg_ref[0], ug_ref[0] = nf, act, gg, ug
        dn_ref[...] = (mm_t(gg, wg_ref[...]) + mm_t(ug, wu_ref[...])).astype(BF16)

    mine = pl.BlockSpec((1, block, width), lambda i, g: (g[0], i, 0))
    hid = pl.BlockSpec((1, block, cols), lambda i, g: (g[0], i, 0))
    plain = pl.BlockSpec((block, width), lambda i, g: (i, 0))
    whole = [
        pl.BlockSpec(w.shape, lambda i, g: (0, 0), pipeline_mode=pl.Buffered(1)) for w in (wg, wu)
    ]
    hidden = jax.ShapeDtypeStruct((groups, total, cols), BF16)
    return pl.pallas_call(
        kernel,
        grid_spec=pltpu.PrefetchScalarGridSpec(
            num_scalar_prefetch=1,
            grid=(total // block,),
            in_specs=[plain, hid] + whole,
            out_specs=[mine, hid, hid, hid, plain],
        ),
        out_shape=(
            jax.ShapeDtypeStruct((groups, total, width), BF16),
            hidden,
            hidden,
            hidden,
            jax.ShapeDtypeStruct((total, width), BF16),
        ),
        compiler_params=pltpu.CompilerParams(vmem_limit_bytes=48 << 20),
        cost_estimate=pl.CostEstimate(
            flops=12 * total * width * cols, bytes_accessed=40 << 20, transcendentals=total * cols
        ),
        name="ffn_own",
    )(group, nf, act_grads, wg, wu)


def ffn_other(where, held, fetched, act_grads, wg, wu, filled):
    groups, total, cols = act_grads.shape
    width = held.shape[1]
    block = 256
    per_half = total // 2 // block

    def kernel(w_ref, held_ref, fetched_ref, ag_ref, wg_ref, wu_ref, *rest):
        na_ref, act_ref, gg_ref, ug_ref, nf_ref = rest[4:]
        i = pl.program_id(0)

        @pl.when(i < per_half)
        def _():
            nf_ref[...] = held_ref[...]

        @pl.when(i >= per_half)
        def _():
            nf_ref[...] = fetched_ref[...]

        nf = nf_ref[...]
        act, gg, ug = ffn_rows(nf, ag_ref[0], wg_ref[...], wu_ref[...])
        na_ref[0], act_ref[0], gg_ref[0], ug_ref[0] = nf, act, gg, ug

    def row(i, w):
        half = jnp.where(i < per_half, w[1], 1 - w[1])
        return half * per_half + lax.rem(i, per_half)

    mine = pl.BlockSpec((1, block, width), lambda i, w: (w[0], row(i, w), 0))
    hid = pl.BlockSpec((1, block, cols), lambda i, w: (w[0], row(i, w), 0))
    first = pl.BlockSpec((block, width), lambda i, w: (jnp.minimum(i, per_half - 1), 0))
    last = pl.BlockSpec((block, width), lambda i, w: (jnp.maximum(i - per_half, 0), 0))
    whole = [
        pl.BlockSpec(w.shape, lambda i, g: (0, 0), pipeline_mode=pl.Buffered(1)) for w in (wg, wu)
    ]
    hidden = jax.ShapeDtypeStruct((groups, total, cols), BF16)
    return pl.pallas_call(
        kernel,
        grid_spec=pltpu.PrefetchScalarGridSpec(
            num_scalar_prefetch=1,
            grid=(2 * per_half,),
            in_specs=[first, last, hid] + whole + [pl.BlockSpec(memory_space=pl.ANY)] * 4,
            out_specs=[mine, hid, hid, hid],
            scratch_shapes=[pltpu.VMEM((block, width), BF16)],
        ),
        out_shape=(jax.ShapeDtypeStruct((groups, total, width), BF16), hidden, hidden, hidden),
        input_output_aliases={6: 0, 7: 1, 8: 2, 9: 3},
        compiler_params=pltpu.CompilerParams(vmem_limit_bytes=48 << 20),
        cost_estimate=pl.CostEstimate(
            flops=8 * total * width * cols, bytes_accessed=40 << 20, transcendentals=total * cols
        ),
        name="ffn_other",
    )(where, held, fetched, act_grads, wg, wu, *filled)


def join_heads(blocks, q_cols):
    n, rows, cols = blocks.shape

    def kernel(b_ref, q_ref, k_ref, v_ref):
        for i in range(n):
            q_ref[:, i * q_cols : (i + 1) * q_cols] = b_ref[i, :, :q_cols].astype(F32)
        kv = [b_ref[i, :, q_cols:].astype(F32) for i in range(n)]
        k_ref[...] = jnp.concatenate([x[:, :HEAD] for x in kv], axis=1)
        v_ref[...] = jnp.concatenate([x[:, HEAD:] for x in kv], axis=1)

    return pl.pallas_call(
        kernel,
        out_shape=(
            jax.ShapeDtypeStruct((rows, n * q_cols), F32),
            jax.ShapeDtypeStruct((rows, n * HEAD), F32),
            jax.ShapeDtypeStruct((rows, n * HEAD), F32),
        ),
        name="join_heads",
    )(blocks)


def finish(normed, gate_grad, up_grad, activated, down_grad, output_part, qkv_part, collective_id):
    depth, width = normed.shape
    cols = gate_grad.shape[1]
    rows = width // 8
    tall = cols // rows
    steps = 8 + tall
    chunks = 4
    sums = (output_part, qkv_part)

    def kernel(
        nf_hbm, gg_hbm, ug_hbm, act_hbm, dg_hbm, o_in, qkv_in,
        gate_out, up_out, down_out, o_out, qkv_out,
        gg, ug, dg, left, stage, tall_stage, o_mid, qkv_mid, o_last, qkv_last,
        load_sems, left_sems, own_sems, tall_sems, push_sems, relay_sems,
    ):
        me = lax.axis_index("shard")
        group = lax.axis_index("rep")
        inner = (group == 1) | (group == 2)
        outer = (group == 0) | (group == 3)
        beside = group + 1 - 2 * lax.rem(group, 2)
        across = 3 - group

        def peer_of(i):
            mask = 7 - i
            index = 0
            for weight in (1, 2, 4):
                bits = lax.rem(lax.div(me, weight), 2) + lax.rem(lax.div(mask, weight), 2)
                index = index + weight * lax.rem(bits, 2)
            return index

        def start_left(i, slot):
            @pl.when(i < 8)
            def _():
                first = pl.multiple_of(peer_of(i) * rows, rows)
                pltpu.make_async_copy(
                    nf_hbm.at[:, pl.ds(first, rows)], left.at[slot], left_sems.at[slot]
                ).start()

            @pl.when((i >= 8) & (i < steps))
            def _():
                first = pl.multiple_of((i - 8) * rows, rows)
                pltpu.make_async_copy(
                    act_hbm.at[:, pl.ds(first, rows)], left.at[slot], left_sems.at[slot]
                ).start()

        def wait_left(slot):
            pltpu.make_async_copy(
                nf_hbm.at[:, pl.ds(0, rows)], left.at[slot], left_sems.at[slot]
            ).wait()

        loads = [
            pltpu.make_async_copy(source, target, load_sems.at[k])
            for k, (source, target) in enumerate(((gg_hbm, gg), (ug_hbm, ug), (dg_hbm, dg)))
        ]
        start_left(0, 0)
        for load in loads:
            load.start()
        barrier = pltpu.get_barrier_semaphore()
        for mask in range(1, 8):
            pl.semaphore_signal(
                barrier, inc=1, device_id={"shard": flip(me, mask)}, device_id_type=MESH
            )
        for neighbour in (beside, across):
            pl.semaphore_signal(
                barrier, inc=1, device_id={"rep": neighbour}, device_id_type=MESH
            )
        pl.semaphore_wait(barrier, 9)

        arrays = ((o_in, o_mid, o_last, o_out), (qkv_in, qkv_mid, qkv_last, qkv_out))

        def relay_copy(stage_index, k, c, target):
            start, mid, last, out = arrays[k]
            size = start.shape[0] // chunks
            part = pl.ds(pl.multiple_of(c * size, size), size)
            source, arrived = ((start, mid), (mid, last), (out, out))[stage_index]
            return pltpu.make_async_remote_copy(
                src_ref=source.at[part],
                dst_ref=arrived.at[part],
                send_sem=relay_sems.at[0, stage_index, k * chunks + c],
                recv_sem=relay_sems.at[1, stage_index, k * chunks + c],
                device_id={"rep": target},
                device_id_type=MESH,
            )

        @pl.when(outer)
        def _():
            for c in range(chunks):
                for k in range(2):
                    relay_copy(0, k, c, beside).start()

        def relay(t):
            def part_of(k, c):
                size = arrays[k][0].shape[0] // chunks
                return pl.ds(pl.multiple_of(c * size, size), size)

            @pl.when(inner & (t < chunks))
            def _():
                for k in range(2):
                    start, mid, last, out = arrays[k]
                    part = part_of(k, t)
                    relay_copy(0, k, t, beside).wait_recv()
                    mid[part, :] = (start[part, :].astype(F32) + mid[part, :].astype(F32)).astype(BF16)
                    relay_copy(1, k, t, across).start()

            @pl.when(inner & (t >= 1) & (t <= chunks))
            def _():
                for k in range(2):
                    start, mid, last, out = arrays[k]
                    part = part_of(k, t - 1)
                    relay_copy(1, k, t - 1, across).wait_recv()
                    out[part, :] = (mid[part, :].astype(F32) + last[part, :].astype(F32)).astype(BF16)
                    relay_copy(2, k, t - 1, beside).start()

            @pl.when(outer & (t >= 2) & (t <= chunks + 1))
            def _():
                for k in range(2):
                    relay_copy(2, k, t - 2, beside).wait_recv()

        outputs = (gate_out, up_out)
        own_columns = pl.ds(pl.multiple_of(me * cols, cols), cols)

        def push(i, j, target):
            return send(
                stage.at[i, j], outputs[j].at[:, own_columns], push_sems, 2 * i + j, target
            )

        def wide(i, carry):
            slot = lax.rem(i, 2)
            start_left(i + 1, 1 - slot)
            wait_left(slot)
            for j, right in enumerate((gg, ug)):

                @pl.when(i == 0)
                def _():
                    loads[j].wait()

                stage[i, j] = t_mm(left[slot], right[...]).astype(BF16)

                @pl.when(i < 7)
                def _():
                    push(i, j, peer_of(i)).start()

                @pl.when(i == 7)
                def _():
                    pltpu.make_async_copy(
                        stage.at[7, j], outputs[j].at[:, own_columns], own_sems.at[j]
                    ).start()

            @pl.when(lax.rem(i, 2) == 1)
            def _():
                relay(lax.div(i, 2))

            return carry

        lax.fori_loop(0, 8, wide, 0)
        loads[2].wait()

        def tall_copy(i):
            slot = lax.rem(i, 2)
            first = pl.multiple_of((i - 8) * rows, rows)
            return pltpu.make_async_copy(
                tall_stage.at[slot], down_out.at[pl.ds(first, rows), :], tall_sems.at[slot]
            )

        def high(i, carry):
            slot = lax.rem(i, 2)
            start_left(i + 1, 1 - slot)
            wait_left(slot)

            @pl.when(i >= 10)
            def _():
                tall_copy(i - 2).wait()

            tall_stage[slot] = t_mm(left[slot], dg[...]).astype(BF16)
            tall_copy(i).start()

            @pl.when(lax.rem(i, 2) == 1)
            def _():
                relay(lax.div(i, 2))

            return carry

        lax.fori_loop(8, steps, high, 0)
        for i in (steps - 2, steps - 1):
            tall_copy(i).wait()
        for j in range(2):
            pltpu.make_async_copy(
                stage.at[7, j], outputs[j].at[:, own_columns], own_sems.at[j]
            ).wait()
        for t in range(steps // 2, chunks + 2):
            relay(t)

        def drain(i, carry):
            for j in range(2):
                push(i, j, peer_of(i)).wait()
            return carry

        lax.fori_loop(0, 7, drain, 0)

        @pl.when(outer)
        def _():
            for c in range(chunks):
                for k in range(2):
                    relay_copy(0, k, c, beside).wait_send()

        @pl.when(inner)
        def _():
            for c in range(chunks):
                for k in range(2):
                    relay_copy(1, k, c, across).wait_send()
                    relay_copy(2, k, c, beside).wait_send()

    exchanged = jax.ShapeDtypeStruct((rows, 8 * cols), BF16)
    return pl.pallas_call(
        kernel,
        out_shape=(
            exchanged,
            exchanged,
            jax.ShapeDtypeStruct((cols, width), BF16),
            jax.ShapeDtypeStruct(output_part.shape, BF16),
            jax.ShapeDtypeStruct(qkv_part.shape, BF16),
        ),
        in_specs=[ANY] * 5 + [VMEM] * 2,
        out_specs=[ANY] * 3 + [VMEM] * 2,
        scratch_shapes=[
            pltpu.VMEM((depth, cols), BF16),
            pltpu.VMEM((depth, cols), BF16),
            pltpu.VMEM((depth, width), BF16),
            pltpu.VMEM((2, depth, rows), BF16),
            pltpu.VMEM((8, 2, rows, cols), BF16),
            pltpu.VMEM((2, rows, width), BF16),
        ]
        + [pltpu.VMEM(x.shape, BF16) for unused in range(2) for x in sums]
        + [
            pltpu.SemaphoreType.DMA((3,)),
            pltpu.SemaphoreType.DMA((2,)),
            pltpu.SemaphoreType.DMA((2,)),
            pltpu.SemaphoreType.DMA((2,)),
            pltpu.SemaphoreType.DMA((2, 14)),
            pltpu.SemaphoreType.DMA((2, 3, 2 * chunks)),
        ],
        compiler_params=comm_params(collective_id, 62),
        cost_estimate=pl.CostEstimate(
            flops=120_000_000_000, bytes_accessed=80 << 20, transcendentals=0
        ),
        name="finish",
    )(normed, gate_grad, up_grad, activated, down_grad, output_part, qkv_part)


def output_rows(where, activated, down_weight, middle, deal, total):
    groups, total, cols = activated.shape
    local, width = middle.shape
    block = 256

    def kernel(w_ref, act_ref, wd_ref, mid_ref, deal_ref, o_ref, rows_ref):
        for i in range(total // block):
            rows = pl.ds(i * block, block)
            rows_ref[rows, :] = (RESIDUAL_SCALE * mm(act_ref[0, rows, :], wd_ref[...])).astype(BF16)
        own = pl.ds(pl.multiple_of(w_ref[1] * local, local), local)
        rows_ref[own, :] = (rows_ref[own, :].astype(F32) + mid_ref[...]).astype(BF16)
        for i in range(total // block):
            rows = pl.ds(i * block, block)
            packed = lax.broadcasted_iota(jnp.int32, (block, total), 1)
            chosen = (deal_ref[rows, :] == packed).astype(BF16)
            o_ref[rows, :] = mm(chosen, rows_ref[...]).astype(BF16)

    def full(shape):
        return pl.BlockSpec(shape, lambda i, w: (0,) * len(shape), pipeline_mode=pl.Buffered(1))

    return pl.pallas_call(
        kernel,
        grid_spec=pltpu.PrefetchScalarGridSpec(
            num_scalar_prefetch=1,
            grid=(1,),
            in_specs=[
                pl.BlockSpec((1, total, cols), lambda i, w: (w[0], 0, 0), pipeline_mode=pl.Buffered(1)),
                full(down_weight.shape),
                full(middle.shape),
                full(deal.shape),
            ],
            out_specs=full((total, width)),
            scratch_shapes=[pltpu.VMEM((total, width), BF16)],
        ),
        out_shape=jax.ShapeDtypeStruct((total, width), BF16),
        compiler_params=pltpu.CompilerParams(vmem_limit_bytes=48 << 20),
        cost_estimate=pl.CostEstimate(
            flops=2 * total * width * (cols + total) * 2, bytes_accessed=12 << 20, transcendentals=0
        ),
        name="output_rows",
    )(where, activated, down_weight, middle, deal)


def join_heads(blocks, q_cols):
    n, rows, cols = blocks.shape

    def kernel(b_ref, q_ref, k_ref, v_ref):
        for i in range(n):
            q_ref[:, i * q_cols : (i + 1) * q_cols] = b_ref[i, :, :q_cols].astype(F32)
        kv = [b_ref[i, :, q_cols:].astype(F32) for i in range(n)]
        k_ref[...] = jnp.concatenate([x[:, :HEAD] for x in kv], axis=1)
        v_ref[...] = jnp.concatenate([x[:, HEAD:] for x in kv], axis=1)

    return pl.pallas_call(
        kernel,
        out_shape=(
            jax.ShapeDtypeStruct((rows, n * q_cols), F32),
            jax.ShapeDtypeStruct((rows, n * HEAD), F32),
            jax.ShapeDtypeStruct((rows, n * HEAD), F32),
        ),
        name="join_heads",
    )(blocks)


def weight_grad(left, right, dtype):
    groups, total, m = left.shape
    n = right.shape[2]
    block = 512
    steps = groups * total // block

    def kernel(l_ref, r_ref, o_ref, acc):
        k = pl.program_id(0)
        term = t_mm(l_ref[...], r_ref[...])

        @pl.when(k == 0)
        def _():
            acc[...] = term

        @pl.when(k > 0)
        def _():
            acc[...] += term

        @pl.when(k == steps - 1)
        def _():
            o_ref[...] = acc[...].astype(o_ref.dtype)

    return pl.pallas_call(
        kernel,
        grid=(steps,),
        in_specs=[
            pl.BlockSpec((block, m), lambda k: (k, 0)),
            pl.BlockSpec((block, n), lambda k: (k, 0)),
        ],
        out_specs=pl.BlockSpec((m, n), lambda k: (0, 0), pipeline_mode=pl.Buffered(1)),
        out_shape=jax.ShapeDtypeStruct((m, n), dtype),
        scratch_shapes=[pltpu.VMEM((m, n), F32)],
        compiler_params=pltpu.CompilerParams(vmem_limit_bytes=56 << 20),
        cost_estimate=pl.CostEstimate(
            flops=2 * groups * total * m * n, bytes_accessed=2 * groups * total * (m + n), transcendentals=0
        ),
        name="weight_grad",
    )(left.reshape(groups * total, m), right.reshape(groups * total, n))


def per_device_plane(
    tokens, attn_gain, query_weight, key_weight, value_weight, output_weight, ffn_gain,
    gate_weight, up_weight, down_weight, dealing, lengths, cotangent,
):
    n = 8
    here = lax.axis_index("shard")
    group = lax.axis_index("rep")
    replicas = lax.axis_size("rep")
    local, width = tokens.shape
    total = local * n
    rows = query_weight.shape[0]
    q_cols = query_weight.shape[1] // n
    ff_cols = gate_weight.shape[1] // n
    core = lax.rem(here, 2)
    half = HEAD // 2
    freq = ROPE_BASE ** (-(jnp.arange(half, dtype=F32) * 2.0) / (2.0 * half))
    freq = jnp.tile(freq, 4)[None, :]

    (
        normed, q, kv, attention, q_weight, kv_weight, gate_cols, up_cols,
        middle, normed_ffn, down_grads, act_grads, cot_own, held,
    ) = front(
        tokens, attn_gain, query_weight, key_weight, value_weight, output_weight, ffn_gain,
        gate_weight, up_weight, down_weight, dealing, lengths, cotangent, freq, replicas,
    )

    def shift(x, by):
        return lax.ppermute(x, "rep", [(i, (i + by) % replicas) for i in range(replicas)])

    def fetch(x):
        return lax.ppermute(x, "shard", [(i, i ^ 1) for i in range(n)])

    before, after = shift(held, 1), shift(held, replicas - 1)
    *filled, normed_ffn_part = ffn_own(
        group.astype(jnp.int32)[None], normed_ffn, act_grads, gate_cols, up_cols
    )
    middle_grad, ffn_gain_part, branch_grad, output_part = pull_gather(
        normed_ffn_part, middle, ffn_gain, cot_own, filled[1], down_weight, dealing.reshape(total, 1), 2
    )
    normed_part, qkv_grad, output_grad = attention_backward(
        branch_grad.reshape(total, width), output_weight, attention, q, kv, normed, q_weight, kv_weight,
        lengths, freq,
    )
    before, after, unused_part = lax.optimization_barrier((before, after, normed_part))
    opposite = shift(before, 1)
    qkv_part = exchange(qkv_grad.reshape(n, rows, q_cols + 2 * HEAD))
    tokens_grad, layer_output, gains, *filled = pull_tokens(
        normed_part, output_part, tokens, attn_gain, middle_grad, ffn_gain_part,
        (before, fetch(before), after, fetch(after)), act_grads, gate_cols, up_cols, filled, replicas, 3,
    )
    opposite, unused_rows = lax.optimization_barrier((opposite, tokens_grad))
    where = jnp.stack([lax.rem(group + replicas - 2, replicas), core]).astype(jnp.int32)
    filled = ffn_other(where, opposite, fetch(opposite), act_grads, gate_cols, up_cols, filled)
    left, *rights = [x.reshape(replicas * total, -1) for x in (filled[0], filled[2], filled[3])]
    gate_grad, up_grad, down_grad, output_grad, qkv_grad = finish(
        left, *rights, filled[1].reshape(replicas * total, -1), down_grads.reshape(replicas * total, -1),
        output_grad, qkv_part.reshape(width, -1), 4,
    )
    return (
        layer_output,
        tokens_grad,
        gains[0],
        *join_heads(qkv_grad.reshape(n, rows, -1), q_cols),
        output_grad.astype(F32),
        gains[1],
        gate_grad.astype(F32),
        up_grad.astype(F32),
        down_grad.astype(F32),
    )


def per_device(
    tokens,
    attn_gain,
    query_weight,
    key_weight,
    value_weight,
    output_weight,
    ffn_gain,
    gate_weight,
    up_weight,
    down_weight,
    dealing,
    lengths,
    cotangent,
):
    n = lax.axis_size("shard")
    here = lax.axis_index("shard")
    local, width = tokens.shape
    total = local * n
    rows = query_weight.shape[0]
    ff_cols = gate_weight.shape[1] // n
    q_cols = query_weight.shape[1] // n
    copies = n // KV_HEADS
    own = here * local

    packed = jnp.arange(total, dtype=jnp.int32)
    segment, position = places(packed, lengths[0])
    cos_q, sin_q = rope_tables(position, q_cols)
    cos_k, sin_k = cos_q[:, :HEAD], sin_q[:, :HEAD]
    dealt = (dealing[0][:, None] == packed[None, :]).astype(BF16)

    def column_blocks(weight, cols):
        return weight.reshape(rows, n, cols).transpose(1, 0, 2)

    def head_blocks(weight):
        blocks = weight.reshape(rows, KV_HEADS, HEAD).transpose(1, 0, 2)
        return jnp.repeat(blocks, copies, axis=0)

    spread_cotangent = lax.all_gather(cotangent, ("rep", "shard"), axis=0, tiled=True)
    all_dealing = lax.all_gather(dealing, "rep", axis=0, tiled=True)
    qkv = exchange(
        jnp.concatenate(
            [column_blocks(query_weight, q_cols), head_blocks(key_weight), head_blocks(value_weight)],
            axis=2,
        )
    ).reshape(width, q_cols + 2 * HEAD)
    gate_cols = exchange(column_blocks(gate_weight, ff_cols)).reshape(width, ff_cols)
    up_cols = exchange(column_blocks(up_weight, ff_cols)).reshape(width, ff_cols)

    normed = gather_rows(rms_scale(tokens.astype(F32), attn_gain).astype(BF16))
    pre = mm(normed, qkv)
    queries = rotate(pre[:, :q_cols], cos_q, sin_q).astype(BF16)
    keys = rotate(pre[:, q_cols : q_cols + HEAD], cos_k, sin_k).astype(BF16)
    values = pre[:, q_cols + HEAD :].astype(BF16)
    attention = attention_forward(queries, jnp.concatenate([keys, values], axis=1), lengths)
    branch = scatter_rows(mm(attention, output_weight).astype(BF16))
    middle = tokens.astype(F32) + RESIDUAL_SCALE * branch.astype(F32)
    normed_ffn = gather_rows(rms_scale(middle, ffn_gain).astype(BF16))
    own_normed = lax.dynamic_slice_in_dim(normed_ffn, own, local)
    all_normed = lax.all_gather(own_normed, ("rep", "shard"), axis=0, tiled=True)

    reps = lax.axis_size("rep")
    group = lax.axis_index("rep")
    deals = (all_dealing[:, :, None] == packed[None, None, :]).astype(BF16)
    out_grad_all = lax.dot_general(
        deals,
        spread_cotangent.reshape(reps, total, width),
        (((1,), (1,)), ((0,), (0,))),
        preferred_element_type=F32,
    ).reshape(reps * total, width)
    down_grad_all = (RESIDUAL_SCALE * out_grad_all).astype(BF16)
    out_grad = lax.dynamic_slice_in_dim(out_grad_all, group * total + own, local)
    act_grad_all = mm_t(down_grad_all, down_weight)

    def ffn(rows_in, act_grad):
        gate = mm(rows_in, gate_cols)
        up = mm(rows_in, up_cols)
        sigmoid = jax.nn.sigmoid(gate)
        activated = (gate * sigmoid * up).astype(BF16)
        gate_grad = (act_grad * up * sigmoid * (1.0 + gate * (1.0 - sigmoid))).astype(BF16)
        up_grad = (act_grad * gate * sigmoid).astype(BF16)
        return activated, gate_grad, up_grad

    activated, gate_grad, up_grad = ffn(
        normed_ffn, lax.dynamic_slice_in_dim(act_grad_all, group * total, total)
    )
    normed_ffn_part = (mm_t(gate_grad, gate_cols) + mm_t(up_grad, up_cols)).astype(BF16)
    middle_part, ffn_gain_part = norm_pull(
        middle, ffn_gain, scatter_rows(normed_ffn_part).astype(F32)
    )
    middle_grad = out_grad + middle_part
    branch_grad = gather_rows((RESIDUAL_SCALE * middle_grad).astype(BF16))

    own_columns = lax.dynamic_slice_in_dim(dealt, own, local, axis=1)
    layer_output = scatter_rows(
        (
            RESIDUAL_SCALE * mm(mm(dealt, activated).astype(BF16), down_weight)
            + mm(own_columns, middle.astype(BF16))
        ).astype(BF16)
    )

    attention_grad = mm_t(branch_grad, output_weight).astype(BF16)
    dq, dk, dv = attention_gradients(
        queries, jnp.concatenate([keys, values], axis=1), attention_grad, lengths
    )
    pre_grad = jnp.concatenate(
        [
            unrotate(dq, cos_q, sin_q).astype(BF16),
            unrotate(dk, cos_k, sin_k).astype(BF16),
            dv.astype(BF16),
        ],
        axis=1,
    )
    normed_part = mm_t(pre_grad, qkv).astype(BF16)
    hidden_part, attn_gain_part = norm_pull(
        tokens.astype(F32), attn_gain, scatter_rows(normed_part).astype(F32)
    )
    tokens_grad = middle_grad + hidden_part

    activated, gate_grad, up_grad = ffn(all_normed, act_grad_all)
    gate_part = exchange(t_mm(all_normed, gate_grad).astype(BF16).reshape(n, rows, ff_cols))
    up_part = exchange(t_mm(all_normed, up_grad).astype(BF16).reshape(n, rows, ff_cols))
    down_part = t_mm(activated, down_grad_all)
    output_part = rep_sum(t_mm(attention, branch_grad).astype(BF16))
    qkv_part = rep_sum(exchange(t_mm(normed, pre_grad).astype(BF16).reshape(n, rows, q_cols + 2 * HEAD)))

    def join(blocks):
        return blocks.transpose(1, 0, 2).reshape(rows, -1).astype(F32)

    def join_heads(blocks):
        blocks = blocks.astype(F32).reshape(KV_HEADS, copies, rows, HEAD).sum(axis=1)
        return blocks.transpose(1, 0, 2).reshape(rows, KV_HEADS * HEAD)

    gain_grads = lax.psum(jnp.concatenate([attn_gain_part, ffn_gain_part]), ("rep", "shard"))
    return (
        layer_output,
        tokens_grad,
        gain_grads[0],
        join(qkv_part[:, :, :q_cols]),
        join_heads(qkv_part[:, :, q_cols : q_cols + HEAD]),
        join_heads(qkv_part[:, :, q_cols + HEAD :]),
        output_part.astype(F32),
        gain_grads[1],
        join(gate_part),
        join(up_part),
        down_part,
    )


def solution(mesh):
    both = P(("rep", "shard"), None)
    rowed = P("shard", None)
    return jax.shard_map(
        per_device_plane if (mesh.shape["rep"], mesh.shape["shard"]) == (4, 8) else per_device,
        mesh=mesh,
        in_specs=(
            both, P(), rowed, rowed, rowed, rowed, P(), rowed, rowed, rowed,
            P("rep", None), P("rep", None), both,
        ),
        out_specs=(both, both, P(), rowed, rowed, rowed, rowed, P(), rowed, rowed, rowed),
        check_vma=False,
    )
```

```python
import functools

import jax
import jax.numpy as jnp
from jax import lax
from jax.experimental import pallas as pl
from jax.experimental.pallas import tpu as pltpu
from jax.sharding import PartitionSpec as P

HEADS = 32
KV_HEADS = 8
HEAD = 64
EPSILON = 1e-05
RESIDUAL_SCALE = 0.22
SCORE_SCALE = 0.015625
ROPE_BASE = 10000000.0
MASKED = -1e30
BF16 = jnp.bfloat16
F32 = jnp.float32


def mm(a, b):
    return jnp.dot(a, b, preferred_element_type=F32)


def mm_t(a, b):
    return lax.dot_general(a, b, (((1,), (1,)), ((), ())), preferred_element_type=F32)


def t_mm(a, b):
    return lax.dot_general(a, b, (((0,), (0,)), ((), ())), preferred_element_type=F32)


def rms_scale(hidden, gain_vector):
    return (
        hidden
        * lax.rsqrt(jnp.mean(hidden * hidden, axis=-1, keepdims=True) + EPSILON)
        * gain_vector
    )


def places(packed_index, seq_lengths):
    seq_ends = jnp.cumsum(seq_lengths)
    starts = seq_ends - seq_lengths
    segment = jnp.sum((packed_index[:, None] >= seq_ends[None, :]).astype(jnp.int32), axis=1)
    chosen = segment[:, None] == jnp.arange(seq_lengths.shape[0], dtype=jnp.int32)[None, :]
    position = packed_index - jnp.sum(jnp.where(chosen, starts[None, :], 0), axis=1)
    return segment, position


def rope_tables(position, width):
    half = HEAD // 2
    frequency = ROPE_BASE ** (-(jnp.arange(half, dtype=F32) * 2.0) / (2.0 * half))
    turned = position.astype(F32)[:, None] * frequency[None, :]
    cosine, sine = jnp.cos(turned), jnp.sin(turned)
    cos_full = jnp.concatenate([cosine, cosine], axis=-1)
    sin_full = jnp.concatenate([-sine, sine], axis=-1)
    return jnp.tile(cos_full, (1, width // HEAD)), jnp.tile(sin_full, (1, width // HEAD))


def swap_halves(x):
    rows, width = x.shape
    half = HEAD // 2
    y = x.reshape(rows, width // HEAD, 2, half)
    return jnp.concatenate([y[:, :, 1:], y[:, :, :1]], axis=2).reshape(rows, width)


def rotate(x, cos_full, sin_full):
    return x * cos_full + swap_halves(x) * sin_full


def unrotate(x, cos_full, sin_full):
    return x * cos_full - swap_halves(x) * sin_full


def gather_rows(x):
    return lax.all_gather(x, "shard", axis=0, tiled=True)


def scatter_rows(x):
    return lax.psum_scatter(x, "shard", scatter_dimension=0, tiled=True)


def exchange(blocks):
    return lax.all_to_all(blocks, "shard", split_axis=0, concat_axis=0, tiled=True)


def rep_sum(x):
    count = lax.axis_size("rep")
    where = lax.axis_index("rep")
    half = count // 2
    for hop in range(half - 1):
        moved = lax.ppermute(
            x, "rep", [(hop, hop + 1), (count - 1 - hop, count - 2 - hop)]
        )
        x = (x.astype(F32) + moved.astype(F32)).astype(BF16)
    moved = lax.ppermute(x, "rep", [(half - 1, half), (half, half - 1)])
    x = (x.astype(F32) + moved.astype(F32)).astype(BF16)
    for hop in range(half - 1):
        near, far = half - 1 - hop, half + hop
        moved = lax.ppermute(x, "rep", [(near, near - 1), (far, far + 1)])
        x = jnp.where((where == near - 1) | (where == far + 1), moved, x)
    return x


MESH = pl.DeviceIdType.MESH


def flip(index, bits):
    for weight in (1, 2, 4):
        if bits & weight:
            index = index + weight - 2 * weight * lax.rem(lax.div(index, weight), 2)
    return index


def send(src, dst, sems, k, target):
    return pltpu.make_async_remote_copy(
        src_ref=src,
        dst_ref=dst,
        send_sem=sems.at[0, k],
        recv_sem=sems.at[1, k],
        device_id={"shard": target},
        device_id_type=MESH,
    )


def greet(me, masks):
    barrier = pltpu.get_barrier_semaphore()
    for mask in masks:
        pl.semaphore_signal(
            barrier, inc=1, device_id={"shard": flip(me, mask)}, device_id_type=MESH
        )
    pl.semaphore_wait(barrier, len(masks))


GATHER_SEMS = 13
BULK = (12, 2, 2)


def gather_steps(me, out, sems):
    core, px, py, diag = (flip(me, mask) for mask in (1, 2, 4, 6))
    half = out.shape[1] // 2
    low, high, whole = pl.ds(0, half), pl.ds(half, half), pl.ds(0, 2 * half)

    def move(k, block, rows, target):
        ref = out.at[block, rows]
        copy = send(ref, ref, sems, k, target)
        copy.start()
        return copy

    x_low, y_high = move(0, me, low, px), move(1, me, high, py)
    own = move(2, me, whole, core)
    x_high, y_low = move(3, me, high, px), move(4, me, low, py)
    yield
    x_low.wait_recv()
    diag_low = move(5, px, low, py)
    pieces = [own, move(6, px, low, core)]
    yield
    y_high.wait_recv()
    diag_high = move(7, py, high, px)
    pieces.append(move(8, py, high, core))
    yield
    x_high.wait_recv()
    pieces.append(move(9, px, high, core))
    yield
    y_low.wait_recv()
    pieces.append(move(10, py, low, core))
    yield
    diag_low.wait_recv()
    pieces.append(move(11, diag, low, core))
    diag_high.wait_recv()
    pieces.append(move(12, diag, high, core))
    yield
    for copy in pieces:
        copy.wait_recv()
    for copy in [x_low, y_high, x_high, y_low, diag_low, diag_high] + pieces:
        copy.wait_send()


def gather_blocks(me, out, sems):
    for unused_step in gather_steps(me, out, sems):
        pass


SCATTER_SEMS = 10


def scatter_steps(me, partial, sib_out, sib_in, acc, x_out, x_in, y_out, y_in, sems):
    core, px, py = (flip(me, mask) for mask in (1, 2, 4))
    half = acc.shape[1] // 2
    masks = (6, 2, 4, 0)
    low, high = pl.ds(0, half), pl.ds(half, half)
    copies = []

    def move(src, dst, k, target):
        copy = send(src, dst, sems, k, target)
        copy.start()
        copies.append(copy)
        return copy

    inside = []
    for i, mask in enumerate(masks):
        sib_out[i] = partial(flip(core, mask)).astype(BF16)
        inside.append(move(sib_out.at[i], sib_in.at[i], i, core))
    yield
    for i, mask in enumerate(masks):
        term = partial(flip(me, mask))
        inside[i].wait_recv()
        acc[i] = term + sib_in[i].astype(F32)
        if mask == 6:
            x_out[0] = acc[i, low].astype(BF16)
            x_diag = move(x_out.at[0], x_in.at[0], 4, px)
            y_out[0] = acc[i, high].astype(BF16)
            y_diag = move(y_out.at[0], y_in.at[0], 5, py)
        if mask == 2:
            x_out[1] = acc[i, low].astype(BF16)
            x_near = move(x_out.at[1], x_in.at[1], 6, px)
        if mask == 4:
            y_out[1] = acc[i, high].astype(BF16)
            y_near = move(y_out.at[1], y_in.at[1], 7, py)
    yield
    x_diag.wait_recv()
    y_out[2] = (acc[2, low] + x_in[0].astype(F32)).astype(BF16)
    y_last = move(y_out.at[2], y_in.at[2], 8, py)
    y_diag.wait_recv()
    x_out[2] = (acc[1, high] + y_in[0].astype(F32)).astype(BF16)
    x_last = move(x_out.at[2], x_in.at[2], 9, px)
    yield
    x_near.wait_recv()
    y_near.wait_recv()
    y_last.wait_recv()
    acc[3, low] = acc[3, low] + x_in[1].astype(F32) + y_in[2].astype(F32)
    x_last.wait_recv()
    acc[3, high] = acc[3, high] + y_in[1].astype(F32) + x_in[2].astype(F32)
    yield
    for copy in copies:
        copy.wait_send()


def scatter_blocks(me, partial, *buffers):
    for unused_step in scatter_steps(me, partial, *buffers):
        pass
    return buffers[2][3]


def scatter_scratch(rows, width):
    half = rows // 2
    return [
        pltpu.VMEM((4, rows, width), BF16),
        pltpu.VMEM((4, rows, width), BF16),
        pltpu.VMEM((4, rows, width), F32),
        pltpu.VMEM((3, half, width), BF16),
        pltpu.VMEM((3, half, width), BF16),
        pltpu.VMEM((3, half, width), BF16),
        pltpu.VMEM((3, half, width), BF16),
        pltpu.SemaphoreType.DMA((2, SCATTER_SEMS)),
    ]


VMEM = pl.BlockSpec(memory_space=pltpu.VMEM)
SMEM = pl.BlockSpec(memory_space=pltpu.SMEM)
ANY = pl.BlockSpec(memory_space=pl.ANY)


def comm_params(collective_id, mebibytes):
    return pltpu.CompilerParams(
        collective_id=collective_id, has_side_effects=True, vmem_limit_bytes=mebibytes << 20
    )


def front(
    tokens, attn_gain, query_weight, key_weight, value_weight, output_weight, ffn_gain,
    gate_weight, up_weight, down_weight, dealing, lengths, cotangent, freq, replicas,
):
    local, width = tokens.shape
    total = 8 * local
    shard_rows = query_weight.shape[0]
    q_cols = query_weight.shape[1] // 8
    ff_cols = gate_weight.shape[1] // 8
    block = 256
    others = (1, 2, 3, 4, 5, 6, 7)

    def kernel(
        tok_ref, gain_ref, wq_hbm, wk_ref, wv_ref, wo_ref, fgain_ref, wg_hbm, wu_hbm,
        wd_ref, deal_ref, len_ref, cot_ref, freq_ref,
        n_ref, q_ref, kv_ref, att_ref, qw_ref, kvw_ref, wg_out, wu_out, mid_ref, nf_ref, dg_out, ag_out, cot_out, half_out,
        kv_stage, c_all, dg_own, ag_stage,
        sib_out, sib_in, acc, x_out, x_in, y_out, y_in, scatter_sems,
        n_sems, c_sems, nf_sems, qkv_sems, bulk_sems, ring_sems, pair_sems, local_sems,
    ):
        me = lax.axis_index("shard")
        group = lax.axis_index("rep")
        core = lax.rem(me, 2)
        after = lax.rem(group + 1, replicas)
        before = lax.rem(group + replicas - 1, replicas)

        barrier = pltpu.get_barrier_semaphore()
        for mask in others:
            pl.semaphore_signal(
                barrier, inc=1, device_id={"shard": flip(me, mask)}, device_id_type=MESH
            )
        for neighbour in (after, before):
            pl.semaphore_signal(
                barrier, inc=1, device_id={"rep": neighbour}, device_id_type=MESH
            )
        c_all[me] = cot_ref[...]
        for d in range(8):
            lanes = slice(d * HEAD, (d + 1) * HEAD)
            kv_stage[d] = jnp.concatenate([wk_ref[:, lanes], wv_ref[:, lanes]], axis=1)
        pl.semaphore_wait(barrier, len(others) + 2)

        gather_c = gather_steps(me, c_all, c_sems)
        next(gather_c)
        n_ref[me] = rms_scale(tok_ref[...].astype(F32), gain_ref[...]).astype(BF16)
        weights = []
        for mask in others:
            peer = flip(me, mask)
            columns = pl.ds(pl.multiple_of(peer * q_cols, q_cols), q_cols)
            weights.append(send(wq_hbm.at[:, columns], qw_ref.at[me], qkv_sems, 2 * mask - 2, peer))
            weights.append(send(kv_stage.at[peer], kvw_ref.at[me], qkv_sems, 2 * mask - 1, peer))
        own_columns = pl.ds(pl.multiple_of(me * ff_cols, ff_cols), ff_cols)
        own_q = pl.ds(pl.multiple_of(me * q_cols, q_cols), q_cols)
        gate_slot, up_slot = ag_stage.at[:shard_rows], ag_stage.at[pl.ds(shard_rows, shard_rows)]
        kept = [
            pltpu.make_async_copy(wg_hbm.at[:, own_columns], gate_slot, local_sems.at[0]),
            pltpu.make_async_copy(wu_hbm.at[:, own_columns], up_slot, local_sems.at[1]),
            pltpu.make_async_copy(wq_hbm.at[:, own_q], qw_ref.at[me], local_sems.at[2]),
        ]
        for copy in kept:
            copy.start()
        kvw_ref[me] = kv_stage[me]

        bulk, waiting = [], []
        for source, target in ((wg_hbm, wg_out), (wu_hbm, wu_out)):
            for part in range(2):
                rows = pl.ds(part * (shard_rows // 2), shard_rows // 2)
                for mask in (2, 4, 6, 3, 5, 7, 1):
                    waiting.append((source, target, rows, mask))

        def more(count):
            for unused in range(min(count, len(waiting))):
                source, target, rows, mask = waiting.pop(0)
                peer = flip(me, mask)
                columns = pl.ds(pl.multiple_of(peer * ff_cols, ff_cols), ff_cols)
                copy = send(
                    source.at[rows, columns], target.at[me, rows], bulk_sems, len(bulk), peer
                )
                copy.start()
                bulk.append(copy)

        for unused in gather_c:
            pass
        gather_n = gather_steps(me, n_ref, n_sems)
        next(gather_n)
        for copy in weights:
            copy.start()

        def permute(first):
            for i in range(total // 2 // block):
                row0 = pl.multiple_of(first + i * block, block)
                packed = row0 + lax.broadcasted_iota(jnp.int32, (block, total), 0)
                chosen = (deal_ref[...] == packed).astype(BF16)
                dealt = mm(chosen, c_all[...].reshape(total, width))
                dg_own[pl.ds(row0, block), :] = (RESIDUAL_SCALE * dealt).astype(BF16)

        near = pl.multiple_of(core * (total // 2), total // 2)
        far = pl.multiple_of((1 - core) * (total // 2), total // 2)
        half = pl.ds(near, total // 2)

        opposite = lax.rem(group + 2, replicas)
        held_groups = (before, after, opposite)

        def pass_on(k):
            ref = dg_out.at[before if k == 2 else group, half]
            copy = pltpu.make_async_remote_copy(
                src_ref=ref if k == 2 else dg_own.at[half],
                dst_ref=ref,
                send_sem=ring_sems.at[0, k],
                recv_sem=ring_sems.at[1, k],
                device_id={"rep": before if k == 1 else after},
                device_id_type=MESH,
            )
            copy.start()
            return copy

        def share(k):
            ref = dg_out.at[held_groups[k], half]
            copy = send(ref, ref, pair_sems, k, flip(me, 1))
            copy.start()
            return copy

        permute(near)
        hops = [pass_on(0)]
        for unused in range(4):
            next(gather_n)
        permute(far)
        packed = me * local + lax.broadcasted_iota(jnp.int32, (local, total), 0)
        chosen = (deal_ref[...] == packed).astype(BF16)
        cot_out[...] = mm(chosen, c_all[...].reshape(total, width)).astype(BF16)
        store = pltpu.make_async_copy(dg_own, dg_out.at[group], local_sems.at[3])
        store.start()
        for unused in gather_n:
            pass
        for copy in kept:
            copy.wait()
        kept = [
            pltpu.make_async_copy(gate_slot, wg_out.at[me], local_sems.at[0]),
            pltpu.make_async_copy(up_slot, wu_out.at[me], local_sems.at[1]),
        ]
        for copy in kept:
            copy.start()
        for copy in weights:
            copy.wait_recv()
        more(BULK[0])
        for i in range(total // block):
            rows = pl.ds(i * block, block)
            x = n_ref[pl.ds(i * block // local, block // local)].reshape(block, width)
            cosine, sine = lane_rope(i * block, block, freq_ref[...], len_ref)
            pre = mm(x, qw_ref[...].reshape(width, q_cols))
            for j in range(q_cols // (2 * HEAD)):
                lanes = slice(j * 2 * HEAD, (j + 1) * 2 * HEAD)
                y = pre[:, lanes]
                q_ref[rows, lanes] = (y * cosine + lane_swap(y) * sine).astype(BF16)
            cosine, sine = keys_only(cosine, sine)
            y = mm(x, kvw_ref[...].reshape(width, 2 * HEAD))
            kv_ref[rows, :] = (y * cosine + lane_swap(y) * sine).astype(BF16)
        hops.append(pass_on(1))
        attend(q_cols // HEAD, block, q_ref, kv_ref, len_ref, att_ref)

        def partial(d):
            return mm(att_ref[pl.ds(pl.multiple_of(d * local, local), local), :], wo_ref[...])

        pending = {}

        def act_grad(held, first, loaded):
            rows = pl.ds(first, total // 2)
            if not loaded:
                load = pltpu.make_async_copy(
                    dg_out.at[held, rows], dg_own.at[rows], local_sems.at[3]
                )
                load.start()
                load.wait()
            slot = 0 if first is near else 1
            if slot in pending:
                pending[slot].wait()
            for i in range(total // 2 // block):
                part = pl.ds(pl.multiple_of(first + i * block, block), block)
                ag_stage[part, :] = mm_t(dg_own[part, :], wd_ref[...]).astype(BF16)
            pending[slot] = pltpu.make_async_copy(
                ag_stage.at[rows], ag_out.at[held, rows], local_sems.at[5 + slot]
            )
            pending[slot].start()

        hops[0].wait_recv()
        hops.append(pass_on(2))
        shares = [share(0)]
        scatter = scatter_steps(
            me, partial, sib_out, sib_in, acc, x_out, x_in, y_out, y_in, scatter_sems
        )
        next(scatter)
        more(BULK[1])
        for unused in scatter:
            pass
        branch = acc[3]
        middle = tok_ref[...].astype(F32) + RESIDUAL_SCALE * branch
        mid_ref[...] = middle
        nf_ref[me] = rms_scale(middle, fgain_ref[...]).astype(BF16)
        gather_nf = gather_steps(me, nf_ref, nf_sems)
        next(gather_nf)
        more(BULK[2])
        for unused in gather_nf:
            pass
        more(len(waiting))
        give = pltpu.make_async_copy(nf_ref.at[pl.ds(4 * core, 4)], half_out, local_sems.at[4])
        give.start()
        store.wait()
        for copy in kept:
            copy.wait()
        act_grad(group, near, True)
        act_grad(group, far, True)
        hops[0].wait_send()
        hops[1].wait_send()
        for k in range(3):
            if k > 0:
                hops[k].wait_recv()
                shares.append(share(k))
            act_grad(held_groups[k], near, False)
            shares[k].wait_recv()
            act_grad(held_groups[k], far, False)
        for copy in pending.values():
            copy.wait()
        give.wait()
        for copy in bulk:
            copy.wait_recv()
        for copy in weights + bulk + hops[2:] + shares:
            copy.wait_send()

    rows8 = jax.ShapeDtypeStruct((8, local, width), BF16)
    half_sems = pltpu.SemaphoreType.DMA
    outs = pl.pallas_call(
        kernel,
        out_shape=(
            rows8,
            jax.ShapeDtypeStruct((total, q_cols), BF16),
            jax.ShapeDtypeStruct((total, 2 * HEAD), BF16),
            jax.ShapeDtypeStruct((total, q_cols), BF16),
            jax.ShapeDtypeStruct((8, shard_rows, q_cols), BF16),
            jax.ShapeDtypeStruct((8, shard_rows, 2 * HEAD), BF16),
            jax.ShapeDtypeStruct((8, shard_rows, ff_cols), BF16),
            jax.ShapeDtypeStruct((8, shard_rows, ff_cols), BF16),
            jax.ShapeDtypeStruct((local, width), F32),
            rows8,
            jax.ShapeDtypeStruct((replicas, total, width), BF16),
            jax.ShapeDtypeStruct((replicas, total, ff_cols), BF16),
            jax.ShapeDtypeStruct((local, width), BF16),
            jax.ShapeDtypeStruct((4, local, width), BF16),
        ),
        in_specs=[VMEM, VMEM, ANY, VMEM, VMEM, VMEM, VMEM, ANY, ANY, VMEM, VMEM, SMEM, VMEM, VMEM],
        out_specs=[VMEM] * 6 + [ANY, ANY, VMEM, VMEM, ANY, ANY, VMEM, ANY],
        scratch_shapes=[
            pltpu.VMEM((8, shard_rows, 2 * HEAD), BF16),
            pltpu.VMEM((8, local, width), BF16),
            pltpu.VMEM((total, width), BF16),
            pltpu.VMEM((total, ff_cols), BF16),
        ]
        + scatter_scratch(local, width)
        + [
            half_sems((2, GATHER_SEMS)),
            half_sems((2, GATHER_SEMS)),
            half_sems((2, GATHER_SEMS)),
            half_sems((2, 14)),
            half_sems((2, 28)),
            half_sems((2, replicas)),
            half_sems((2, replicas)),
            half_sems((7,)),
        ],
        compiler_params=comm_params(0, 56),
        cost_estimate=pl.CostEstimate(
            flops=200_000_000_000, bytes_accessed=50 << 20, transcendentals=total * total
        ),
        name="front",
    )(
        tokens, attn_gain[None, :], query_weight, key_weight, value_weight, output_weight,
        ffn_gain[None, :], gate_weight, up_weight, down_weight, dealing, lengths, cotangent, freq,
    )
    normed, q, kv, attention, qw, kvw, wg, wu, middle, nf, dg, ag, cot, held = outs
    return (
        normed.reshape(total, width), q, kv, attention,
        qw.reshape(width, q_cols), kvw.reshape(width, 2 * HEAD),
        wg.reshape(width, ff_cols), wu.reshape(width, ff_cols),
        middle, nf.reshape(total, width), dg, ag, cot,
        held.reshape(total // 2, width),
    )


def norm_pull(x, gain, grad):
    scale = lax.rsqrt(jnp.mean(x * x, axis=-1, keepdims=True) + EPSILON)
    pulled = gain * grad
    rows_part = scale * pulled - x * (
        scale * scale * scale * jnp.mean(pulled * x, axis=-1, keepdims=True)
    )
    return rows_part, jnp.sum(grad * x * scale, axis=0, keepdims=True)


def pull_gather(part, middle, gain, out_grad, activated, down_weight, deal, collective_id):
    rows, width = middle.shape
    groups, total, cols = activated.shape
    block = 256

    def kernel(
        p_ref, m_ref, gain_ref, g_ref, act_hbm, wd_ref, deal_ref,
        mg_ref, gain_part, out, dealt_ref, act_ref, packed_ref, act_sem, *scratch,
    ):
        me = lax.axis_index("shard")
        *buffers, scatter_sems, sems = scratch
        load = pltpu.make_async_copy(act_hbm.at[lax.axis_index("rep")], act_ref, act_sem.at[0])
        load.start()
        greet(me, (1, 2, 4))

        def down(i, carry):
            chunk = pl.ds(pl.multiple_of(i * block, block), block)
            packed_ref[chunk, :] = (RESIDUAL_SCALE * mm(act_ref[chunk, :], wd_ref[...])).astype(BF16)
            return carry

        def deal_out(i, carry):
            chunk = pl.ds(pl.multiple_of(i * block, block), block)
            packed = lax.broadcasted_iota(jnp.int32, (block, total), 1)
            chosen = (deal_ref[chunk, :] == packed).astype(BF16)
            dealt_ref[chunk, :] = mm(chosen, packed_ref[...]).astype(BF16)
            return carry

        half = total // block // 2
        scatter = scatter_steps(
            me,
            lambda d: p_ref[pl.ds(pl.multiple_of(d * rows, rows), rows), :].astype(F32),
            *buffers,
            scatter_sems,
        )
        next(scatter)
        load.wait()
        lax.fori_loop(0, half, down, 0)
        next(scatter)
        lax.fori_loop(half, 2 * half, down, 0)
        own = pl.ds(pl.multiple_of(me * rows, rows), rows)
        packed_ref[own, :] = (packed_ref[own, :].astype(F32) + m_ref[...]).astype(BF16)
        next(scatter)
        for unused in scatter:
            pass
        rows_part, gain_row = norm_pull(m_ref[...], gain_ref[...], buffers[2][3])
        gain_part[...] = gain_row
        middle_grad = g_ref[...].astype(F32) + rows_part
        mg_ref[...] = middle_grad
        out[me] = (RESIDUAL_SCALE * middle_grad).astype(BF16)
        gather = gather_steps(me, out, sems)
        next(gather)
        lax.fori_loop(0, half, deal_out, 0)
        for unused in range(2):
            next(gather)
        lax.fori_loop(half, 2 * half, deal_out, 0)
        for unused in gather:
            pass

    return pl.pallas_call(
        kernel,
        out_shape=(
            jax.ShapeDtypeStruct((rows, width), F32),
            jax.ShapeDtypeStruct((1, width), F32),
            jax.ShapeDtypeStruct((8, rows, width), BF16),
            jax.ShapeDtypeStruct((total, width), BF16),
        ),
        in_specs=[VMEM] * 4 + [ANY] + [VMEM] * 2,
        out_specs=[VMEM] * 4,
        scratch_shapes=[
            pltpu.VMEM((total, cols), BF16),
            pltpu.VMEM((total, width), BF16),
            pltpu.SemaphoreType.DMA((1,)),
        ]
        + scatter_scratch(rows, width)
        + [pltpu.SemaphoreType.DMA((2, GATHER_SEMS))],
        compiler_params=comm_params(collective_id, 56),
        cost_estimate=pl.CostEstimate(
            flops=60_000_000_000, bytes_accessed=50 * rows * width, transcendentals=rows
        ),
        name="pull_gather",
    )(part, middle, gain[None, :], out_grad, activated, down_weight, deal)


def pull_tokens(
    part, out_part, hidden, gain, middle_grad, other_gain, near, act_grads, wg, wu, filled, replicas, collective_id
):
    rows, width = middle_grad.shape
    groups, total, cols = act_grads.shape
    block = 256
    levels = [("shard", 1), ("shard", 2), ("shard", 4)]
    level = 1
    while level < replicas:
        levels.append(("rep", level))
        level *= 2
    per_half = total // 2 // block

    def kernel(
        p_ref, o_ref, h_ref, gain_ref, mg_ref, og_ref, wg_ref, wu_ref, ag_hbm,
        before_held, before_fetched, after_held, after_fetched, unused_na, unused_act, unused_gg, unused_ug,
        out, lay, gains, na_hbm, act_hbm, gg_hbm, ug_hbm,
        nf_buf, ag_buf, done_buf, in_sems, out_sems, gain_in, gain_out, gain_sems, *scratch,
    ):
        me = lax.axis_index("shard")
        group = lax.axis_index("rep")
        core = lax.rem(me, 2)
        before = lax.rem(group + replicas - 1, replicas)
        after = lax.rem(group + 1, replicas)
        first, second = scratch[:8], scratch[8:]
        parts = (
            (before, before_held, core),
            (before, before_fetched, 1 - core),
            (after, after_held, core),
            (after, after_fetched, 1 - core),
        )

        def rows_of(p, r):
            return pl.ds(pl.multiple_of((parts[p][2] * per_half + r) * block, block), block)

        def loads(p, r):
            held, source, unused = parts[p]
            slot = (p % 2) * per_half + r
            return [
                pltpu.make_async_copy(
                    source.at[pl.ds(pl.multiple_of(r * block, block), block)],
                    nf_buf.at[slot],
                    in_sems.at[0, slot],
                ),
                pltpu.make_async_copy(ag_hbm.at[held, rows_of(p, r)], ag_buf.at[slot], in_sems.at[1, slot]),
            ]

        def stores(p, r):
            held = parts[p][0]
            slot = (p % 2) * per_half + r
            where = rows_of(p, r)
            return [
                pltpu.make_async_copy(nf_buf.at[slot], na_hbm.at[held, where], out_sems.at[0, slot])
            ] + [
                pltpu.make_async_copy(done_buf.at[k, slot], target.at[held, where], out_sems.at[k + 1, slot])
                for k, target in enumerate((act_hbm, gg_hbm, ug_hbm))
            ]

        def start_loads(p):
            for r in range(per_half):
                for copy in loads(p, r):
                    copy.start()

        def wait_stores(p):
            for r in range(per_half):
                for copy in stores(p, r):
                    copy.wait()

        def fill(p):
            if p > 0:
                wait_stores(p - 1)
            if p + 1 < len(parts):
                start_loads(p + 1)

            def step(r, carry):
                slot = (p % 2) * per_half + r
                for copy in loads(p, r):
                    copy.wait()
                results = ffn_rows(nf_buf[slot], ag_buf[slot], wg_ref[...], wu_ref[...])
                for k, result in enumerate(results):
                    done_buf[k, slot] = result
                for copy in stores(p, r):
                    copy.start()
                return carry

            lax.fori_loop(0, per_half, step, 0)

        start_loads(0)
        barrier = pltpu.get_barrier_semaphore()
        peers = []
        for axis, weight in levels:
            index = me if axis == "shard" else group
            peers.append({axis: index + weight - 2 * weight * lax.rem(lax.div(index, weight), 2)})
        for peer in peers:
            pl.semaphore_signal(barrier, inc=1, device_id=peer, device_id_type=MESH)
        pl.semaphore_wait(barrier, len(peers))

        def blocks_of(ref):
            return lambda d: ref[pl.ds(pl.multiple_of(d * rows, rows), rows), :].astype(F32)

        grads = scatter_steps(me, blocks_of(p_ref), *first)
        outputs = scatter_steps(me, blocks_of(o_ref), *second)
        next(grads)
        next(outputs)
        fill(0)
        next(grads)
        fill(1)
        next(grads)
        next(outputs)
        fill(2)
        next(grads)
        next(outputs)
        rows_part, gain_row = norm_pull(h_ref[...].astype(F32), gain_ref[...], first[2][3])
        out[...] = mg_ref[...] + rows_part
        sums = jnp.concatenate([gain_row, og_ref[...]], axis=0)
        for i, peer in enumerate(peers):
            gain_out[i] = sums
            copy = pltpu.make_async_remote_copy(
                src_ref=gain_out.at[i],
                dst_ref=gain_in.at[i],
                send_sem=gain_sems.at[0, i],
                recv_sem=gain_sems.at[1, i],
                device_id=peer,
                device_id_type=MESH,
            )
            copy.start()
            if i == 0:
                fill(3)
            copy.wait()
            sums = sums + gain_in[i]
        gains[...] = sums
        next(outputs)
        lay[...] = second[2][3].astype(BF16)
        for steps in (grads, outputs):
            for unused in steps:
                pass
        wait_stores(3)

    hidden_shape = jax.ShapeDtypeStruct((groups, total, cols), BF16)
    return pl.pallas_call(
        kernel,
        out_shape=(
            jax.ShapeDtypeStruct((rows, width), F32),
            jax.ShapeDtypeStruct((rows, width), BF16),
            jax.ShapeDtypeStruct((2, width), F32),
            jax.ShapeDtypeStruct((groups, total, width), BF16),
            hidden_shape,
            hidden_shape,
            hidden_shape,
        ),
        in_specs=[VMEM] * 8 + [ANY] * 9,
        out_specs=[VMEM] * 3 + [ANY] * 4,
        input_output_aliases={13: 3, 14: 4, 15: 5, 16: 6},
        scratch_shapes=[
            pltpu.VMEM((2 * per_half, block, width), BF16),
            pltpu.VMEM((2 * per_half, block, cols), BF16),
            pltpu.VMEM((3, 2 * per_half, block, cols), BF16),
            pltpu.SemaphoreType.DMA((2, 2 * per_half)),
            pltpu.SemaphoreType.DMA((4, 2 * per_half)),
            pltpu.VMEM((len(levels), 2, width), F32),
            pltpu.VMEM((len(levels), 2, width), F32),
            pltpu.SemaphoreType.DMA((2, len(levels))),
        ]
        + scatter_scratch(rows, width)
        + scatter_scratch(rows, width),
        compiler_params=comm_params(collective_id, 62),
        cost_estimate=pl.CostEstimate(
            flops=60_000_000_000, bytes_accessed=50 * rows * width, transcendentals=rows
        ),
        name="pull_tokens",
    )(
        part, out_part, hidden, gain[None, :], middle_grad, other_gain, wg, wu, act_grads, *near, *filled
    )


def softmax_block(q, k, allowed):
    scores = SCORE_SCALE * mm_t(q, k)
    scores = jnp.where(allowed, scores, MASKED)
    top = jnp.max(scores, axis=-1, keepdims=True)
    weight = jnp.exp(scores - top)
    return weight * (1.0 / jnp.sum(weight, axis=-1, keepdims=True))


def allowed_block(row0, cols, start):
    shape = (start.shape[0], cols)
    query = row0 + lax.broadcasted_iota(jnp.int32, shape, 0)
    key = lax.broadcasted_iota(jnp.int32, shape, 1)
    return (key >= start) & (key <= query)


def sequence_starts(row0, shape, lengths_ref):
    row = row0 + lax.broadcasted_iota(jnp.int32, shape, 0)
    start = jnp.zeros(shape, jnp.int32)
    end = 0
    for i in range(lengths_ref.shape[1]):
        length = lengths_ref[0, i]
        end = end + length
        start = start + jnp.where(row >= end, length, 0)
    return start


def attend(heads, block, q_ref, kv_ref, lengths_ref, o_ref):
    total = kv_ref.shape[0]
    for i in range(total // block):
        cols = (i + 1) * block
        rows = pl.ds(i * block, block)
        allowed = allowed_block(
            i * block, cols, sequence_starts(i * block, (block, 1), lengths_ref)
        )
        kv = kv_ref[:cols, :]
        k, v = kv[:, :HEAD], kv[:, HEAD:]
        for h in range(heads):
            lanes = slice(h * HEAD, (h + 1) * HEAD)
            probs = softmax_block(q_ref[rows, lanes], k, allowed)
            o_ref[rows, lanes] = mm(probs.astype(BF16), v).astype(BF16)


def attend_back(heads, block, q_ref, kv_ref, g_ref, lengths_ref, dq_ref, dk_ref, dv_ref):
    total = kv_ref.shape[0]
    dk_ref[...] = jnp.zeros_like(dk_ref)
    dv_ref[...] = jnp.zeros_like(dv_ref)
    for i in range(total // block):
        cols = (i + 1) * block
        rows = pl.ds(i * block, block)
        allowed = allowed_block(
            i * block, cols, sequence_starts(i * block, (block, 1), lengths_ref)
        )
        kv = kv_ref[:cols, :]
        k, v = kv[:, :HEAD], kv[:, HEAD:]
        for h in range(heads):
            lanes = slice(h * HEAD, (h + 1) * HEAD)
            q, g = q_ref[rows, lanes], g_ref[rows, lanes]
            probs = softmax_block(q, k, allowed)
            probs_grad = mm_t(g, v)
            delta = jnp.sum(probs * probs_grad, axis=-1, keepdims=True)
            score_grad = (probs * (probs_grad - delta)).astype(BF16)
            dq_ref[rows, lanes] = SCORE_SCALE * mm(score_grad, k)
            dk_ref[:cols, :] += SCORE_SCALE * t_mm(score_grad, q)
            dv_ref[:cols, :] += t_mm(probs.astype(BF16), g)


def attention_forward(q, kv, lengths):
    total, width = q.shape

    def kernel(q_ref, kv_ref, lengths_ref, o_ref):
        attend(width // HEAD, 256, q_ref, kv_ref, lengths_ref, o_ref)

    return pl.pallas_call(
        kernel,
        out_shape=jax.ShapeDtypeStruct((total, width), BF16),
        in_specs=[VMEM, VMEM, SMEM],
        out_specs=VMEM,
        compiler_params=pltpu.CompilerParams(vmem_limit_bytes=40 << 20),
        name="attention_forward",
    )(q, kv, lengths)


def attention_gradients(q, kv, grad, lengths):
    total, width = q.shape

    def kernel(q_ref, kv_ref, g_ref, lengths_ref, dq_ref, dk_ref, dv_ref):
        attend_back(width // HEAD, 256, q_ref, kv_ref, g_ref, lengths_ref, dq_ref, dk_ref, dv_ref)

    return pl.pallas_call(
        kernel,
        out_shape=(
            jax.ShapeDtypeStruct((total, width), F32),
            jax.ShapeDtypeStruct((total, HEAD), F32),
            jax.ShapeDtypeStruct((total, HEAD), F32),
        ),
        in_specs=[VMEM, VMEM, VMEM, SMEM],
        out_specs=[VMEM] * 3,
        compiler_params=pltpu.CompilerParams(vmem_limit_bytes=40 << 20),
        name="attention_gradients",
    )(q, kv, grad, lengths)


def lane_rope(row0, rows, freq, lengths_ref):
    shape = (rows, 2 * HEAD)
    row = row0 + lax.broadcasted_iota(jnp.int32, shape, 0)
    position = row - sequence_starts(row0, shape, lengths_ref)
    turned = position.astype(F32) * freq
    lane = lax.broadcasted_iota(jnp.int32, shape, 1)
    first = lax.rem(lane, HEAD) < HEAD // 2
    sine = jnp.sin(turned)
    return jnp.cos(turned), jnp.where(first, -sine, sine)


def lane_swap(x):
    half = HEAD // 2
    lane = lax.broadcasted_iota(jnp.int32, x.shape, 1)
    first = lax.rem(lane, HEAD) < half
    return jnp.where(first, pltpu.roll(x, 2 * HEAD - half, 1), pltpu.roll(x, half, 1))


def keys_only(cosine, sine):
    lane = lax.broadcasted_iota(jnp.int32, cosine.shape, 1)
    return jnp.where(lane < HEAD, cosine, 1.0), jnp.where(lane < HEAD, sine, 0.0)


def attention_backward(
    branch_grad, output_weight, attention, q, kv, normed, q_weight, kv_weight, lengths, freq
):
    total, q_cols = q.shape
    width = normed.shape[1]
    block = 256

    def kernel(
        bg_ref, wo_ref, a_ref, q_ref, kv_ref, n_ref, qw_ref, kvw_ref, len_ref, freq_ref,
        dn_ref, dqkv_ref, dwo_ref, g_ref, dq_ref, dk_ref, dv_ref, pq_ref, pkv_ref,
    ):
        for i in range(total // block):
            rows = pl.ds(i * block, block)
            g_ref[rows, :] = mm_t(bg_ref[rows, :], wo_ref[...]).astype(BF16)
        attend_back(
            q_cols // HEAD, block, q_ref, kv_ref, g_ref, len_ref, dq_ref, dk_ref, dv_ref
        )
        for i in range(total // block):
            rows = pl.ds(i * block, block)
            cosine, sine = lane_rope(i * block, block, freq_ref[...], len_ref)
            for j in range(q_cols // (2 * HEAD)):
                lanes = slice(j * 2 * HEAD, (j + 1) * 2 * HEAD)
                x = dq_ref[rows, lanes]
                pq_ref[rows, lanes] = (x * cosine - lane_swap(x) * sine).astype(BF16)
            cosine, sine = keys_only(cosine, sine)
            x = jnp.concatenate([dk_ref[rows, :], dv_ref[rows, :]], axis=1)
            pkv_ref[rows, :] = (x * cosine - lane_swap(x) * sine).astype(BF16)
            dn_ref[rows, :] = (
                mm_t(pq_ref[rows, :], qw_ref[...]) + mm_t(pkv_ref[rows, :], kvw_ref[...])
            ).astype(BF16)
        for i in range(width // 512):
            cols = slice(i * 512, (i + 1) * 512)
            dqkv_ref[cols, :q_cols] = t_mm(n_ref[:, cols], pq_ref[...]).astype(BF16)
            dqkv_ref[cols, q_cols:] = t_mm(n_ref[:, cols], pkv_ref[...]).astype(BF16)
            dwo_ref[:, cols] = t_mm(a_ref[...], bg_ref[:, cols]).astype(BF16)

    return pl.pallas_call(
        kernel,
        out_shape=(
            jax.ShapeDtypeStruct((total, width), BF16),
            jax.ShapeDtypeStruct((width, q_cols + 2 * HEAD), BF16),
            jax.ShapeDtypeStruct((q_cols, width), BF16),
        ),
        in_specs=[VMEM] * 8 + [SMEM, VMEM],
        out_specs=[VMEM] * 3,
        scratch_shapes=[
            pltpu.VMEM((total, q_cols), BF16),
            pltpu.VMEM((total, q_cols), F32),
            pltpu.VMEM((total, HEAD), F32),
            pltpu.VMEM((total, HEAD), F32),
            pltpu.VMEM((total, q_cols), BF16),
            pltpu.VMEM((total, 2 * HEAD), BF16),
        ],
        compiler_params=pltpu.CompilerParams(vmem_limit_bytes=56 << 20),
        cost_estimate=pl.CostEstimate(flops=30_000_000_000, bytes_accessed=30 << 20, transcendentals=total * total),
        name="attention_backward",
    )(branch_grad, output_weight, attention, q, kv, normed, q_weight, kv_weight, lengths, freq)


def ffn_rows(nf, act_grad, wg, wu):
    gate, up = mm(nf, wg), mm(nf, wu)
    act_grad = act_grad.astype(F32)
    sigmoid = 1.0 / (1.0 + jnp.exp(-gate))
    silu = gate * sigmoid
    activated = (silu * up).astype(BF16)
    gate_grad = (act_grad * up * sigmoid * (1.0 + gate * (1.0 - sigmoid))).astype(BF16)
    return activated, gate_grad, (act_grad * silu).astype(BF16)


def ffn_own(group, nf, act_grads, wg, wu):
    groups, total, cols = act_grads.shape
    width = nf.shape[1]
    block = 256

    def kernel(g_ref, nf_ref, ag_ref, wg_ref, wu_ref, na_ref, act_ref, gg_ref, ug_ref, dn_ref):
        nf = nf_ref[...]
        act, gg, ug = ffn_rows(nf, ag_ref[0], wg_ref[...], wu_ref[...])
        na_ref[0], act_ref[0], gg_ref[0], ug_ref[0] = nf, act, gg, ug
        dn_ref[...] = (mm_t(gg, wg_ref[...]) + mm_t(ug, wu_ref[...])).astype(BF16)

    mine = pl.BlockSpec((1, block, width), lambda i, g: (g[0], i, 0))
    hid = pl.BlockSpec((1, block, cols), lambda i, g: (g[0], i, 0))
    plain = pl.BlockSpec((block, width), lambda i, g: (i, 0))
    whole = [
        pl.BlockSpec(w.shape, lambda i, g: (0, 0), pipeline_mode=pl.Buffered(1)) for w in (wg, wu)
    ]
    hidden = jax.ShapeDtypeStruct((groups, total, cols), BF16)
    return pl.pallas_call(
        kernel,
        grid_spec=pltpu.PrefetchScalarGridSpec(
            num_scalar_prefetch=1,
            grid=(total // block,),
            in_specs=[plain, hid] + whole,
            out_specs=[mine, hid, hid, hid, plain],
        ),
        out_shape=(
            jax.ShapeDtypeStruct((groups, total, width), BF16),
            hidden,
            hidden,
            hidden,
            jax.ShapeDtypeStruct((total, width), BF16),
        ),
        compiler_params=pltpu.CompilerParams(vmem_limit_bytes=48 << 20),
        cost_estimate=pl.CostEstimate(
            flops=12 * total * width * cols, bytes_accessed=40 << 20, transcendentals=total * cols
        ),
        name="ffn_own",
    )(group, nf, act_grads, wg, wu)


def ffn_other(where, held, fetched, act_grads, wg, wu, filled):
    groups, total, cols = act_grads.shape
    width = held.shape[1]
    block = 256
    per_half = total // 2 // block

    def kernel(w_ref, held_ref, fetched_ref, ag_ref, wg_ref, wu_ref, *rest):
        na_ref, act_ref, gg_ref, ug_ref, nf_ref = rest[4:]
        i = pl.program_id(0)

        @pl.when(i < per_half)
        def _():
            nf_ref[...] = held_ref[...]

        @pl.when(i >= per_half)
        def _():
            nf_ref[...] = fetched_ref[...]

        nf = nf_ref[...]
        act, gg, ug = ffn_rows(nf, ag_ref[0], wg_ref[...], wu_ref[...])
        na_ref[0], act_ref[0], gg_ref[0], ug_ref[0] = nf, act, gg, ug

    def row(i, w):
        half = jnp.where(i < per_half, w[1], 1 - w[1])
        return half * per_half + lax.rem(i, per_half)

    mine = pl.BlockSpec((1, block, width), lambda i, w: (w[0], row(i, w), 0))
    hid = pl.BlockSpec((1, block, cols), lambda i, w: (w[0], row(i, w), 0))
    first = pl.BlockSpec((block, width), lambda i, w: (jnp.minimum(i, per_half - 1), 0))
    last = pl.BlockSpec((block, width), lambda i, w: (jnp.maximum(i - per_half, 0), 0))
    whole = [
        pl.BlockSpec(w.shape, lambda i, g: (0, 0), pipeline_mode=pl.Buffered(1)) for w in (wg, wu)
    ]
    hidden = jax.ShapeDtypeStruct((groups, total, cols), BF16)
    return pl.pallas_call(
        kernel,
        grid_spec=pltpu.PrefetchScalarGridSpec(
            num_scalar_prefetch=1,
            grid=(2 * per_half,),
            in_specs=[first, last, hid] + whole + [pl.BlockSpec(memory_space=pl.ANY)] * 4,
            out_specs=[mine, hid, hid, hid],
            scratch_shapes=[pltpu.VMEM((block, width), BF16)],
        ),
        out_shape=(jax.ShapeDtypeStruct((groups, total, width), BF16), hidden, hidden, hidden),
        input_output_aliases={6: 0, 7: 1, 8: 2, 9: 3},
        compiler_params=pltpu.CompilerParams(vmem_limit_bytes=48 << 20),
        cost_estimate=pl.CostEstimate(
            flops=8 * total * width * cols, bytes_accessed=40 << 20, transcendentals=total * cols
        ),
        name="ffn_other",
    )(where, held, fetched, act_grads, wg, wu, *filled)


def join_heads(blocks, q_cols):
    n, rows, cols = blocks.shape

    def kernel(b_ref, q_ref, k_ref, v_ref):
        for i in range(n):
            q_ref[:, i * q_cols : (i + 1) * q_cols] = b_ref[i, :, :q_cols].astype(F32)
        kv = [b_ref[i, :, q_cols:].astype(F32) for i in range(n)]
        k_ref[...] = jnp.concatenate([x[:, :HEAD] for x in kv], axis=1)
        v_ref[...] = jnp.concatenate([x[:, HEAD:] for x in kv], axis=1)

    return pl.pallas_call(
        kernel,
        out_shape=(
            jax.ShapeDtypeStruct((rows, n * q_cols), F32),
            jax.ShapeDtypeStruct((rows, n * HEAD), F32),
            jax.ShapeDtypeStruct((rows, n * HEAD), F32),
        ),
        name="join_heads",
    )(blocks)


def finish(normed, gate_grad, up_grad, activated, down_grad, output_part, qkv_part, collective_id):
    depth, width = normed.shape
    cols = gate_grad.shape[1]
    rows = width // 8
    tall = cols // rows
    steps = 8 + tall
    chunks = 4
    sums = (output_part, qkv_part)

    def kernel(
        nf_hbm, gg_hbm, ug_hbm, act_hbm, dg_hbm, o_in, qkv_in,
        gate_out, up_out, down_out, o_out, qkv_out,
        gg, ug, dg, left, stage, tall_stage, o_mid, qkv_mid, o_last, qkv_last,
        load_sems, left_sems, own_sems, tall_sems, push_sems, relay_sems,
    ):
        me = lax.axis_index("shard")
        group = lax.axis_index("rep")
        inner = (group == 1) | (group == 2)
        outer = (group == 0) | (group == 3)
        beside = group + 1 - 2 * lax.rem(group, 2)
        across = 3 - group

        def peer_of(i):
            mask = 7 - i
            index = 0
            for weight in (1, 2, 4):
                bits = lax.rem(lax.div(me, weight), 2) + lax.rem(lax.div(mask, weight), 2)
                index = index + weight * lax.rem(bits, 2)
            return index

        def start_left(i, slot):
            @pl.when(i < 8)
            def _():
                first = pl.multiple_of(peer_of(i) * rows, rows)
                pltpu.make_async_copy(
                    nf_hbm.at[:, pl.ds(first, rows)], left.at[slot], left_sems.at[slot]
                ).start()

            @pl.when((i >= 8) & (i < steps))
            def _():
                first = pl.multiple_of((i - 8) * rows, rows)
                pltpu.make_async_copy(
                    act_hbm.at[:, pl.ds(first, rows)], left.at[slot], left_sems.at[slot]
                ).start()

        def wait_left(slot):
            pltpu.make_async_copy(
                nf_hbm.at[:, pl.ds(0, rows)], left.at[slot], left_sems.at[slot]
            ).wait()

        loads = [
            pltpu.make_async_copy(source, target, load_sems.at[k])
            for k, (source, target) in enumerate(((gg_hbm, gg), (ug_hbm, ug), (dg_hbm, dg)))
        ]
        start_left(0, 0)
        for load in loads:
            load.start()
        barrier = pltpu.get_barrier_semaphore()
        for mask in range(1, 8):
            pl.semaphore_signal(
                barrier, inc=1, device_id={"shard": flip(me, mask)}, device_id_type=MESH
            )
        for neighbour in (beside, across):
            pl.semaphore_signal(
                barrier, inc=1, device_id={"rep": neighbour}, device_id_type=MESH
            )
        pl.semaphore_wait(barrier, 9)

        arrays = ((o_in, o_mid, o_last, o_out), (qkv_in, qkv_mid, qkv_last, qkv_out))

        def relay_copy(stage_index, k, c, target):
            start, mid, last, out = arrays[k]
            size = start.shape[0] // chunks
            part = pl.ds(pl.multiple_of(c * size, size), size)
            source, arrived = ((start, mid), (mid, last), (out, out))[stage_index]
            return pltpu.make_async_remote_copy(
                src_ref=source.at[part],
                dst_ref=arrived.at[part],
                send_sem=relay_sems.at[0, stage_index, k * chunks + c],
                recv_sem=relay_sems.at[1, stage_index, k * chunks + c],
                device_id={"rep": target},
                device_id_type=MESH,
            )

        @pl.when(outer)
        def _():
            for c in range(chunks):
                for k in range(2):
                    relay_copy(0, k, c, beside).start()

        def relay(t):
            def part_of(k, c):
                size = arrays[k][0].shape[0] // chunks
                return pl.ds(pl.multiple_of(c * size, size), size)

            @pl.when(inner & (t < chunks))
            def _():
                for k in range(2):
                    start, mid, last, out = arrays[k]
                    part = part_of(k, t)
                    relay_copy(0, k, t, beside).wait_recv()
                    mid[part, :] = (start[part, :].astype(F32) + mid[part, :].astype(F32)).astype(BF16)
                    relay_copy(1, k, t, across).start()

            @pl.when(inner & (t >= 1) & (t <= chunks))
            def _():
                for k in range(2):
                    start, mid, last, out = arrays[k]
                    part = part_of(k, t - 1)
                    relay_copy(1, k, t - 1, across).wait_recv()
                    out[part, :] = (mid[part, :].astype(F32) + last[part, :].astype(F32)).astype(BF16)
                    relay_copy(2, k, t - 1, beside).start()

            @pl.when(outer & (t >= 2) & (t <= chunks + 1))
            def _():
                for k in range(2):
                    relay_copy(2, k, t - 2, beside).wait_recv()

        outputs = (gate_out, up_out)
        own_columns = pl.ds(pl.multiple_of(me * cols, cols), cols)

        def push(i, j, target):
            return send(
                stage.at[i, j], outputs[j].at[:, own_columns], push_sems, 2 * i + j, target
            )

        def wide(i, carry):
            slot = lax.rem(i, 2)
            start_left(i + 1, 1 - slot)
            wait_left(slot)
            for j, right in enumerate((gg, ug)):

                @pl.when(i == 0)
                def _():
                    loads[j].wait()

                stage[i, j] = t_mm(left[slot], right[...]).astype(BF16)

                @pl.when(i < 7)
                def _():
                    push(i, j, peer_of(i)).start()

                @pl.when(i == 7)
                def _():
                    pltpu.make_async_copy(
                        stage.at[7, j], outputs[j].at[:, own_columns], own_sems.at[j]
                    ).start()

            @pl.when(lax.rem(i, 2) == 1)
            def _():
                relay(lax.div(i, 2))

            return carry

        lax.fori_loop(0, 8, wide, 0)
        loads[2].wait()

        def tall_copy(i):
            slot = lax.rem(i, 2)
            first = pl.multiple_of((i - 8) * rows, rows)
            return pltpu.make_async_copy(
                tall_stage.at[slot], down_out.at[pl.ds(first, rows), :], tall_sems.at[slot]
            )

        def high(i, carry):
            slot = lax.rem(i, 2)
            start_left(i + 1, 1 - slot)
            wait_left(slot)

            @pl.when(i >= 10)
            def _():
                tall_copy(i - 2).wait()

            tall_stage[slot] = t_mm(left[slot], dg[...]).astype(BF16)
            tall_copy(i).start()

            @pl.when(lax.rem(i, 2) == 1)
            def _():
                relay(lax.div(i, 2))

            return carry

        lax.fori_loop(8, steps, high, 0)
        for i in (steps - 2, steps - 1):
            tall_copy(i).wait()
        for j in range(2):
            pltpu.make_async_copy(
                stage.at[7, j], outputs[j].at[:, own_columns], own_sems.at[j]
            ).wait()
        for t in range(steps // 2, chunks + 2):
            relay(t)

        def drain(i, carry):
            for j in range(2):
                push(i, j, peer_of(i)).wait()
            return carry

        lax.fori_loop(0, 7, drain, 0)

        @pl.when(outer)
        def _():
            for c in range(chunks):
                for k in range(2):
                    relay_copy(0, k, c, beside).wait_send()

        @pl.when(inner)
        def _():
            for c in range(chunks):
                for k in range(2):
                    relay_copy(1, k, c, across).wait_send()
                    relay_copy(2, k, c, beside).wait_send()

    exchanged = jax.ShapeDtypeStruct((rows, 8 * cols), BF16)
    return pl.pallas_call(
        kernel,
        out_shape=(
            exchanged,
            exchanged,
            jax.ShapeDtypeStruct((cols, width), BF16),
            jax.ShapeDtypeStruct(output_part.shape, BF16),
            jax.ShapeDtypeStruct(qkv_part.shape, BF16),
        ),
        in_specs=[ANY] * 5 + [VMEM] * 2,
        out_specs=[ANY] * 3 + [VMEM] * 2,
        scratch_shapes=[
            pltpu.VMEM((depth, cols), BF16),
            pltpu.VMEM((depth, cols), BF16),
            pltpu.VMEM((depth, width), BF16),
            pltpu.VMEM((2, depth, rows), BF16),
            pltpu.VMEM((8, 2, rows, cols), BF16),
            pltpu.VMEM((2, rows, width), BF16),
        ]
        + [pltpu.VMEM(x.shape, BF16) for unused in range(2) for x in sums]
        + [
            pltpu.SemaphoreType.DMA((3,)),
            pltpu.SemaphoreType.DMA((2,)),
            pltpu.SemaphoreType.DMA((2,)),
            pltpu.SemaphoreType.DMA((2,)),
            pltpu.SemaphoreType.DMA((2, 14)),
            pltpu.SemaphoreType.DMA((2, 3, 2 * chunks)),
        ],
        compiler_params=comm_params(collective_id, 62),
        cost_estimate=pl.CostEstimate(
            flops=120_000_000_000, bytes_accessed=80 << 20, transcendentals=0
        ),
        name="finish",
    )(normed, gate_grad, up_grad, activated, down_grad, output_part, qkv_part)


def output_rows(where, activated, down_weight, middle, deal, total):
    groups, total, cols = activated.shape
    local, width = middle.shape
    block = 256

    def kernel(w_ref, act_ref, wd_ref, mid_ref, deal_ref, o_ref, rows_ref):
        for i in range(total // block):
            rows = pl.ds(i * block, block)
            rows_ref[rows, :] = (RESIDUAL_SCALE * mm(act_ref[0, rows, :], wd_ref[...])).astype(BF16)
        own = pl.ds(pl.multiple_of(w_ref[1] * local, local), local)
        rows_ref[own, :] = (rows_ref[own, :].astype(F32) + mid_ref[...]).astype(BF16)
        for i in range(total // block):
            rows = pl.ds(i * block, block)
            packed = lax.broadcasted_iota(jnp.int32, (block, total), 1)
            chosen = (deal_ref[rows, :] == packed).astype(BF16)
            o_ref[rows, :] = mm(chosen, rows_ref[...]).astype(BF16)

    def full(shape):
        return pl.BlockSpec(shape, lambda i, w: (0,) * len(shape), pipeline_mode=pl.Buffered(1))

    return pl.pallas_call(
        kernel,
        grid_spec=pltpu.PrefetchScalarGridSpec(
            num_scalar_prefetch=1,
            grid=(1,),
            in_specs=[
                pl.BlockSpec((1, total, cols), lambda i, w: (w[0], 0, 0), pipeline_mode=pl.Buffered(1)),
                full(down_weight.shape),
                full(middle.shape),
                full(deal.shape),
            ],
            out_specs=full((total, width)),
            scratch_shapes=[pltpu.VMEM((total, width), BF16)],
        ),
        out_shape=jax.ShapeDtypeStruct((total, width), BF16),
        compiler_params=pltpu.CompilerParams(vmem_limit_bytes=48 << 20),
        cost_estimate=pl.CostEstimate(
            flops=2 * total * width * (cols + total) * 2, bytes_accessed=12 << 20, transcendentals=0
        ),
        name="output_rows",
    )(where, activated, down_weight, middle, deal)


def join_heads(blocks, q_cols):
    n, rows, cols = blocks.shape

    def kernel(b_ref, q_ref, k_ref, v_ref):
        for i in range(n):
            q_ref[:, i * q_cols : (i + 1) * q_cols] = b_ref[i, :, :q_cols].astype(F32)
        kv = [b_ref[i, :, q_cols:].astype(F32) for i in range(n)]
        k_ref[...] = jnp.concatenate([x[:, :HEAD] for x in kv], axis=1)
        v_ref[...] = jnp.concatenate([x[:, HEAD:] for x in kv], axis=1)

    return pl.pallas_call(
        kernel,
        out_shape=(
            jax.ShapeDtypeStruct((rows, n * q_cols), F32),
            jax.ShapeDtypeStruct((rows, n * HEAD), F32),
            jax.ShapeDtypeStruct((rows, n * HEAD), F32),
        ),
        name="join_heads",
    )(blocks)


def weight_grad(left, right, dtype):
    groups, total, m = left.shape
    n = right.shape[2]
    block = 512
    steps = groups * total // block

    def kernel(l_ref, r_ref, o_ref, acc):
        k = pl.program_id(0)
        term = t_mm(l_ref[...], r_ref[...])

        @pl.when(k == 0)
        def _():
            acc[...] = term

        @pl.when(k > 0)
        def _():
            acc[...] += term

        @pl.when(k == steps - 1)
        def _():
            o_ref[...] = acc[...].astype(o_ref.dtype)

    return pl.pallas_call(
        kernel,
        grid=(steps,),
        in_specs=[
            pl.BlockSpec((block, m), lambda k: (k, 0)),
            pl.BlockSpec((block, n), lambda k: (k, 0)),
        ],
        out_specs=pl.BlockSpec((m, n), lambda k: (0, 0), pipeline_mode=pl.Buffered(1)),
        out_shape=jax.ShapeDtypeStruct((m, n), dtype),
        scratch_shapes=[pltpu.VMEM((m, n), F32)],
        compiler_params=pltpu.CompilerParams(vmem_limit_bytes=56 << 20),
        cost_estimate=pl.CostEstimate(
            flops=2 * groups * total * m * n, bytes_accessed=2 * groups * total * (m + n), transcendentals=0
        ),
        name="weight_grad",
    )(left.reshape(groups * total, m), right.reshape(groups * total, n))


def per_device_plane(
    tokens, attn_gain, query_weight, key_weight, value_weight, output_weight, ffn_gain,
    gate_weight, up_weight, down_weight, dealing, lengths, cotangent,
):
    n = 8
    here = lax.axis_index("shard")
    group = lax.axis_index("rep")
    replicas = lax.axis_size("rep")
    local, width = tokens.shape
    total = local * n
    rows = query_weight.shape[0]
    q_cols = query_weight.shape[1] // n
    ff_cols = gate_weight.shape[1] // n
    core = lax.rem(here, 2)
    half = HEAD // 2
    freq = ROPE_BASE ** (-(jnp.arange(half, dtype=F32) * 2.0) / (2.0 * half))
    freq = jnp.tile(freq, 4)[None, :]

    (
        normed, q, kv, attention, q_weight, kv_weight, gate_cols, up_cols,
        middle, normed_ffn, down_grads, act_grads, cot_own, held,
    ) = front(
        tokens, attn_gain, query_weight, key_weight, value_weight, output_weight, ffn_gain,
        gate_weight, up_weight, down_weight, dealing, lengths, cotangent, freq, replicas,
    )

    def shift(x, by):
        return lax.ppermute(x, "rep", [(i, (i + by) % replicas) for i in range(replicas)])

    def fetch(x):
        return lax.ppermute(x, "shard", [(i, i ^ 1) for i in range(n)])

    before, after = shift(held, 1), shift(held, replicas - 1)
    *filled, normed_ffn_part = ffn_own(
        group.astype(jnp.int32)[None], normed_ffn, act_grads, gate_cols, up_cols
    )
    middle_grad, ffn_gain_part, branch_grad, output_part = pull_gather(
        normed_ffn_part, middle, ffn_gain, cot_own, filled[1], down_weight, dealing.reshape(total, 1), 2
    )
    normed_part, qkv_grad, output_grad = attention_backward(
        branch_grad.reshape(total, width), output_weight, attention, q, kv, normed, q_weight, kv_weight,
        lengths, freq,
    )
    before, after, unused_part = lax.optimization_barrier((before, after, normed_part))
    opposite = shift(before, 1)
    qkv_part = exchange(qkv_grad.reshape(n, rows, q_cols + 2 * HEAD))
    tokens_grad, layer_output, gains, *filled = pull_tokens(
        normed_part, output_part, tokens, attn_gain, middle_grad, ffn_gain_part,
        (before, fetch(before), after, fetch(after)), act_grads, gate_cols, up_cols, filled, replicas, 3,
    )
    opposite, unused_rows = lax.optimization_barrier((opposite, tokens_grad))
    where = jnp.stack([lax.rem(group + replicas - 2, replicas), core]).astype(jnp.int32)
    filled = ffn_other(where, opposite, fetch(opposite), act_grads, gate_cols, up_cols, filled)
    left, *rights = [x.reshape(replicas * total, -1) for x in (filled[0], filled[2], filled[3])]
    gate_grad, up_grad, down_grad, output_grad, qkv_grad = finish(
        left, *rights, filled[1].reshape(replicas * total, -1), down_grads.reshape(replicas * total, -1),
        output_grad, qkv_part.reshape(width, -1), 4,
    )
    return (
        layer_output,
        tokens_grad,
        gains[0],
        *join_heads(qkv_grad.reshape(n, rows, -1), q_cols),
        output_grad.astype(F32),
        gains[1],
        gate_grad.astype(F32),
        up_grad.astype(F32),
        down_grad.astype(F32),
    )


def per_device(
    tokens,
    attn_gain,
    query_weight,
    key_weight,
    value_weight,
    output_weight,
    ffn_gain,
    gate_weight,
    up_weight,
    down_weight,
    dealing,
    lengths,
    cotangent,
):
    n = lax.axis_size("shard")
    here = lax.axis_index("shard")
    local, width = tokens.shape
    total = local * n
    rows = query_weight.shape[0]
    ff_cols = gate_weight.shape[1] // n
    q_cols = query_weight.shape[1] // n
    copies = n // KV_HEADS
    own = here * local

    packed = jnp.arange(total, dtype=jnp.int32)
    segment, position = places(packed, lengths[0])
    cos_q, sin_q = rope_tables(position, q_cols)
    cos_k, sin_k = cos_q[:, :HEAD], sin_q[:, :HEAD]
    dealt = (dealing[0][:, None] == packed[None, :]).astype(BF16)

    def column_blocks(weight, cols):
        return weight.reshape(rows, n, cols).transpose(1, 0, 2)

    def head_blocks(weight):
        blocks = weight.reshape(rows, KV_HEADS, HEAD).transpose(1, 0, 2)
        return jnp.repeat(blocks, copies, axis=0)

    spread_cotangent = lax.all_gather(cotangent, ("rep", "shard"), axis=0, tiled=True)
    all_dealing = lax.all_gather(dealing, "rep", axis=0, tiled=True)
    qkv = exchange(
        jnp.concatenate(
            [column_blocks(query_weight, q_cols), head_blocks(key_weight), head_blocks(value_weight)],
            axis=2,
        )
    ).reshape(width, q_cols + 2 * HEAD)
    gate_cols = exchange(column_blocks(gate_weight, ff_cols)).reshape(width, ff_cols)
    up_cols = exchange(column_blocks(up_weight, ff_cols)).reshape(width, ff_cols)

    normed = gather_rows(rms_scale(tokens.astype(F32), attn_gain).astype(BF16))
    pre = mm(normed, qkv)
    queries = rotate(pre[:, :q_cols], cos_q, sin_q).astype(BF16)
    keys = rotate(pre[:, q_cols : q_cols + HEAD], cos_k, sin_k).astype(BF16)
    values = pre[:, q_cols + HEAD :].astype(BF16)
    attention = attention_forward(queries, jnp.concatenate([keys, values], axis=1), lengths)
    branch = scatter_rows(mm(attention, output_weight).astype(BF16))
    middle = tokens.astype(F32) + RESIDUAL_SCALE * branch.astype(F32)
    normed_ffn = gather_rows(rms_scale(middle, ffn_gain).astype(BF16))
    own_normed = lax.dynamic_slice_in_dim(normed_ffn, own, local)
    all_normed = lax.all_gather(own_normed, ("rep", "shard"), axis=0, tiled=True)

    reps = lax.axis_size("rep")
    group = lax.axis_index("rep")
    deals = (all_dealing[:, :, None] == packed[None, None, :]).astype(BF16)
    out_grad_all = lax.dot_general(
        deals,
        spread_cotangent.reshape(reps, total, width),
        (((1,), (1,)), ((0,), (0,))),
        preferred_element_type=F32,
    ).reshape(reps * total, width)
    down_grad_all = (RESIDUAL_SCALE * out_grad_all).astype(BF16)
    out_grad = lax.dynamic_slice_in_dim(out_grad_all, group * total + own, local)
    act_grad_all = mm_t(down_grad_all, down_weight)

    def ffn(rows_in, act_grad):
        gate = mm(rows_in, gate_cols)
        up = mm(rows_in, up_cols)
        sigmoid = jax.nn.sigmoid(gate)
        activated = (gate * sigmoid * up).astype(BF16)
        gate_grad = (act_grad * up * sigmoid * (1.0 + gate * (1.0 - sigmoid))).astype(BF16)
        up_grad = (act_grad * gate * sigmoid).astype(BF16)
        return activated, gate_grad, up_grad

    activated, gate_grad, up_grad = ffn(
        normed_ffn, lax.dynamic_slice_in_dim(act_grad_all, group * total, total)
    )
    normed_ffn_part = (mm_t(gate_grad, gate_cols) + mm_t(up_grad, up_cols)).astype(BF16)
    middle_part, ffn_gain_part = norm_pull(
        middle, ffn_gain, scatter_rows(normed_ffn_part).astype(F32)
    )
    middle_grad = out_grad + middle_part
    branch_grad = gather_rows((RESIDUAL_SCALE * middle_grad).astype(BF16))

    own_columns = lax.dynamic_slice_in_dim(dealt, own, local, axis=1)
    layer_output = scatter_rows(
        (
            RESIDUAL_SCALE * mm(mm(dealt, activated).astype(BF16), down_weight)
            + mm(own_columns, middle.astype(BF16))
        ).astype(BF16)
    )

    attention_grad = mm_t(branch_grad, output_weight).astype(BF16)
    dq, dk, dv = attention_gradients(
        queries, jnp.concatenate([keys, values], axis=1), attention_grad, lengths
    )
    pre_grad = jnp.concatenate(
        [
            unrotate(dq, cos_q, sin_q).astype(BF16),
            unrotate(dk, cos_k, sin_k).astype(BF16),
            dv.astype(BF16),
        ],
        axis=1,
    )
    normed_part = mm_t(pre_grad, qkv).astype(BF16)
    hidden_part, attn_gain_part = norm_pull(
        tokens.astype(F32), attn_gain, scatter_rows(normed_part).astype(F32)
    )
    tokens_grad = middle_grad + hidden_part

    activated, gate_grad, up_grad = ffn(all_normed, act_grad_all)
    gate_part = exchange(t_mm(all_normed, gate_grad).astype(BF16).reshape(n, rows, ff_cols))
    up_part = exchange(t_mm(all_normed, up_grad).astype(BF16).reshape(n, rows, ff_cols))
    down_part = t_mm(activated, down_grad_all)
    output_part = rep_sum(t_mm(attention, branch_grad).astype(BF16))
    qkv_part = rep_sum(exchange(t_mm(normed, pre_grad).astype(BF16).reshape(n, rows, q_cols + 2 * HEAD)))

    def join(blocks):
        return blocks.transpose(1, 0, 2).reshape(rows, -1).astype(F32)

    def join_heads(blocks):
        blocks = blocks.astype(F32).reshape(KV_HEADS, copies, rows, HEAD).sum(axis=1)
        return blocks.transpose(1, 0, 2).reshape(rows, KV_HEADS * HEAD)

    gain_grads = lax.psum(jnp.concatenate([attn_gain_part, ffn_gain_part]), ("rep", "shard"))
    return (
        layer_output,
        tokens_grad,
        gain_grads[0],
        join(qkv_part[:, :, :q_cols]),
        join_heads(qkv_part[:, :, q_cols : q_cols + HEAD]),
        join_heads(qkv_part[:, :, q_cols + HEAD :]),
        output_part.astype(F32),
        gain_grads[1],
        join(gate_part),
        join(up_part),
        down_part,
    )


def solution(mesh):
    both = P(("rep", "shard"), None)
    rowed = P("shard", None)
    return jax.shard_map(
        per_device_plane if (mesh.shape["rep"], mesh.shape["shard"]) == (4, 8) else per_device,
        mesh=mesh,
        in_specs=(
            both, P(), rowed, rowed, rowed, rowed, P(), rowed, rowed, rowed,
            P("rep", None), P("rep", None), both,
        ),
        out_specs=(both, both, P(), rowed, rowed, rowed, rowed, P(), rowed, rowed, rowed),
        check_vma=False,
    )
```

```python
import functools

import jax
import jax.numpy as jnp
from jax import lax
from jax.experimental import pallas as pl
from jax.experimental.pallas import tpu as pltpu
from jax.sharding import PartitionSpec as P

HEADS = 32
KV_HEADS = 8
HEAD = 64
EPSILON = 1e-05
RESIDUAL_SCALE = 0.22
SCORE_SCALE = 0.015625
ROPE_BASE = 10000000.0
MASKED = -1e30
BF16 = jnp.bfloat16
F32 = jnp.float32


def mm(a, b):
    return jnp.dot(a, b, preferred_element_type=F32)


def mm_t(a, b):
    return lax.dot_general(a, b, (((1,), (1,)), ((), ())), preferred_element_type=F32)


def t_mm(a, b):
    return lax.dot_general(a, b, (((0,), (0,)), ((), ())), preferred_element_type=F32)


def rms_scale(hidden, gain_vector):
    return (
        hidden
        * lax.rsqrt(jnp.mean(hidden * hidden, axis=-1, keepdims=True) + EPSILON)
        * gain_vector
    )


def places(packed_index, seq_lengths):
    seq_ends = jnp.cumsum(seq_lengths)
    starts = seq_ends - seq_lengths
    segment = jnp.sum((packed_index[:, None] >= seq_ends[None, :]).astype(jnp.int32), axis=1)
    chosen = segment[:, None] == jnp.arange(seq_lengths.shape[0], dtype=jnp.int32)[None, :]
    position = packed_index - jnp.sum(jnp.where(chosen, starts[None, :], 0), axis=1)
    return segment, position


def rope_tables(position, width):
    half = HEAD // 2
    frequency = ROPE_BASE ** (-(jnp.arange(half, dtype=F32) * 2.0) / (2.0 * half))
    turned = position.astype(F32)[:, None] * frequency[None, :]
    cosine, sine = jnp.cos(turned), jnp.sin(turned)
    cos_full = jnp.concatenate([cosine, cosine], axis=-1)
    sin_full = jnp.concatenate([-sine, sine], axis=-1)
    return jnp.tile(cos_full, (1, width // HEAD)), jnp.tile(sin_full, (1, width // HEAD))


def swap_halves(x):
    rows, width = x.shape
    half = HEAD // 2
    y = x.reshape(rows, width // HEAD, 2, half)
    return jnp.concatenate([y[:, :, 1:], y[:, :, :1]], axis=2).reshape(rows, width)


def rotate(x, cos_full, sin_full):
    return x * cos_full + swap_halves(x) * sin_full


def unrotate(x, cos_full, sin_full):
    return x * cos_full - swap_halves(x) * sin_full


def gather_rows(x):
    return lax.all_gather(x, "shard", axis=0, tiled=True)


def scatter_rows(x):
    return lax.psum_scatter(x, "shard", scatter_dimension=0, tiled=True)


def exchange(blocks):
    return lax.all_to_all(blocks, "shard", split_axis=0, concat_axis=0, tiled=True)


def rep_sum(x):
    count = lax.axis_size("rep")
    where = lax.axis_index("rep")
    half = count // 2
    for hop in range(half - 1):
        moved = lax.ppermute(
            x, "rep", [(hop, hop + 1), (count - 1 - hop, count - 2 - hop)]
        )
        x = (x.astype(F32) + moved.astype(F32)).astype(BF16)
    moved = lax.ppermute(x, "rep", [(half - 1, half), (half, half - 1)])
    x = (x.astype(F32) + moved.astype(F32)).astype(BF16)
    for hop in range(half - 1):
        near, far = half - 1 - hop, half + hop
        moved = lax.ppermute(x, "rep", [(near, near - 1), (far, far + 1)])
        x = jnp.where((where == near - 1) | (where == far + 1), moved, x)
    return x


MESH = pl.DeviceIdType.MESH


def flip(index, bits):
    for weight in (1, 2, 4):
        if bits & weight:
            index = index + weight - 2 * weight * lax.rem(lax.div(index, weight), 2)
    return index


def send(src, dst, sems, k, target):
    return pltpu.make_async_remote_copy(
        src_ref=src,
        dst_ref=dst,
        send_sem=sems.at[0, k],
        recv_sem=sems.at[1, k],
        device_id={"shard": target},
        device_id_type=MESH,
    )


def greet(me, masks):
    barrier = pltpu.get_barrier_semaphore()
    for mask in masks:
        pl.semaphore_signal(
            barrier, inc=1, device_id={"shard": flip(me, mask)}, device_id_type=MESH
        )
    pl.semaphore_wait(barrier, len(masks))


GATHER_SEMS = 13
BULK = (12, 2, 2)


def gather_steps(me, out, sems):
    core, px, py, diag = (flip(me, mask) for mask in (1, 2, 4, 6))
    half = out.shape[1] // 2
    low, high, whole = pl.ds(0, half), pl.ds(half, half), pl.ds(0, 2 * half)

    def move(k, block, rows, target):
        ref = out.at[block, rows]
        copy = send(ref, ref, sems, k, target)
        copy.start()
        return copy

    x_low, y_high = move(0, me, low, px), move(1, me, high, py)
    own = move(2, me, whole, core)
    x_high, y_low = move(3, me, high, px), move(4, me, low, py)
    yield
    x_low.wait_recv()
    diag_low = move(5, px, low, py)
    pieces = [own, move(6, px, low, core)]
    yield
    y_high.wait_recv()
    diag_high = move(7, py, high, px)
    pieces.append(move(8, py, high, core))
    yield
    x_high.wait_recv()
    pieces.append(move(9, px, high, core))
    yield
    y_low.wait_recv()
    pieces.append(move(10, py, low, core))
    yield
    diag_low.wait_recv()
    pieces.append(move(11, diag, low, core))
    diag_high.wait_recv()
    pieces.append(move(12, diag, high, core))
    yield
    for copy in pieces:
        copy.wait_recv()
    for copy in [x_low, y_high, x_high, y_low, diag_low, diag_high] + pieces:
        copy.wait_send()


def gather_blocks(me, out, sems):
    for unused_step in gather_steps(me, out, sems):
        pass


SCATTER_SEMS = 10


def scatter_steps(me, partial, sib_out, sib_in, acc, x_out, x_in, y_out, y_in, sems):
    core, px, py = (flip(me, mask) for mask in (1, 2, 4))
    half = acc.shape[1] // 2
    masks = (6, 2, 4, 0)
    low, high = pl.ds(0, half), pl.ds(half, half)
    copies = []

    def move(src, dst, k, target):
        copy = send(src, dst, sems, k, target)
        copy.start()
        copies.append(copy)
        return copy

    inside = []
    for i, mask in enumerate(masks):
        sib_out[i] = partial(flip(core, mask)).astype(BF16)
        inside.append(move(sib_out.at[i], sib_in.at[i], i, core))
    yield
    for i, mask in enumerate(masks):
        term = partial(flip(me, mask))
        inside[i].wait_recv()
        acc[i] = term + sib_in[i].astype(F32)
        if mask == 6:
            x_out[0] = acc[i, low].astype(BF16)
            x_diag = move(x_out.at[0], x_in.at[0], 4, px)
            y_out[0] = acc[i, high].astype(BF16)
            y_diag = move(y_out.at[0], y_in.at[0], 5, py)
        if mask == 2:
            x_out[1] = acc[i, low].astype(BF16)
            x_near = move(x_out.at[1], x_in.at[1], 6, px)
        if mask == 4:
            y_out[1] = acc[i, high].astype(BF16)
            y_near = move(y_out.at[1], y_in.at[1], 7, py)
    yield
    x_diag.wait_recv()
    y_out[2] = (acc[2, low] + x_in[0].astype(F32)).astype(BF16)
    y_last = move(y_out.at[2], y_in.at[2], 8, py)
    y_diag.wait_recv()
    x_out[2] = (acc[1, high] + y_in[0].astype(F32)).astype(BF16)
    x_last = move(x_out.at[2], x_in.at[2], 9, px)
    yield
    x_near.wait_recv()
    y_near.wait_recv()
    y_last.wait_recv()
    acc[3, low] = acc[3, low] + x_in[1].astype(F32) + y_in[2].astype(F32)
    x_last.wait_recv()
    acc[3, high] = acc[3, high] + y_in[1].astype(F32) + x_in[2].astype(F32)
    yield
    for copy in copies:
        copy.wait_send()


def scatter_blocks(me, partial, *buffers):
    for unused_step in scatter_steps(me, partial, *buffers):
        pass
    return buffers[2][3]


def scatter_scratch(rows, width):
    half = rows // 2
    return [
        pltpu.VMEM((4, rows, width), BF16),
        pltpu.VMEM((4, rows, width), BF16),
        pltpu.VMEM((4, rows, width), F32),
        pltpu.VMEM((3, half, width), BF16),
        pltpu.VMEM((3, half, width), BF16),
        pltpu.VMEM((3, half, width), BF16),
        pltpu.VMEM((3, half, width), BF16),
        pltpu.SemaphoreType.DMA((2, SCATTER_SEMS)),
    ]


VMEM = pl.BlockSpec(memory_space=pltpu.VMEM)
SMEM = pl.BlockSpec(memory_space=pltpu.SMEM)
ANY = pl.BlockSpec(memory_space=pl.ANY)


def comm_params(collective_id, mebibytes):
    return pltpu.CompilerParams(
        collective_id=collective_id, has_side_effects=True, vmem_limit_bytes=mebibytes << 20
    )


def front(
    tokens, attn_gain, query_weight, key_weight, value_weight, output_weight, ffn_gain,
    gate_weight, up_weight, down_weight, dealing, lengths, cotangent, freq, replicas,
):
    local, width = tokens.shape
    total = 8 * local
    shard_rows = query_weight.shape[0]
    q_cols = query_weight.shape[1] // 8
    ff_cols = gate_weight.shape[1] // 8
    block = 256
    others = (1, 2, 3, 4, 5, 6, 7)

    def kernel(
        tok_ref, gain_ref, wq_hbm, wk_ref, wv_ref, wo_ref, fgain_ref, wg_hbm, wu_hbm,
        wd_ref, deal_ref, len_ref, cot_ref, freq_ref,
        n_ref, q_ref, kv_ref, att_ref, qw_ref, kvw_ref, wg_out, wu_out, mid_ref, nf_ref, dg_out, ag_out, cot_out, half_out,
        kv_stage, c_all, dg_own, ag_stage,
        sib_out, sib_in, acc, x_out, x_in, y_out, y_in, scatter_sems,
        n_sems, c_sems, nf_sems, qkv_sems, bulk_sems, ring_sems, pair_sems, local_sems,
    ):
        me = lax.axis_index("shard")
        group = lax.axis_index("rep")
        core = lax.rem(me, 2)
        after = lax.rem(group + 1, replicas)
        before = lax.rem(group + replicas - 1, replicas)

        barrier = pltpu.get_barrier_semaphore()
        for mask in others:
            pl.semaphore_signal(
                barrier, inc=1, device_id={"shard": flip(me, mask)}, device_id_type=MESH
            )
        for neighbour in (after, before):
            pl.semaphore_signal(
                barrier, inc=1, device_id={"rep": neighbour}, device_id_type=MESH
            )
        c_all[me] = cot_ref[...]
        for d in range(8):
            lanes = slice(d * HEAD, (d + 1) * HEAD)
            kv_stage[d] = jnp.concatenate([wk_ref[:, lanes], wv_ref[:, lanes]], axis=1)
        pl.semaphore_wait(barrier, len(others) + 2)

        gather_c = gather_steps(me, c_all, c_sems)
        next(gather_c)
        n_ref[me] = rms_scale(tok_ref[...].astype(F32), gain_ref[...]).astype(BF16)
        weights = []
        for mask in others:
            peer = flip(me, mask)
            columns = pl.ds(pl.multiple_of(peer * q_cols, q_cols), q_cols)
            weights.append(send(wq_hbm.at[:, columns], qw_ref.at[me], qkv_sems, 2 * mask - 2, peer))
            weights.append(send(kv_stage.at[peer], kvw_ref.at[me], qkv_sems, 2 * mask - 1, peer))
        own_columns = pl.ds(pl.multiple_of(me * ff_cols, ff_cols), ff_cols)
        own_q = pl.ds(pl.multiple_of(me * q_cols, q_cols), q_cols)
        gate_slot, up_slot = ag_stage.at[:shard_rows], ag_stage.at[pl.ds(shard_rows, shard_rows)]
        kept = [
            pltpu.make_async_copy(wg_hbm.at[:, own_columns], gate_slot, local_sems.at[0]),
            pltpu.make_async_copy(wu_hbm.at[:, own_columns], up_slot, local_sems.at[1]),
            pltpu.make_async_copy(wq_hbm.at[:, own_q], qw_ref.at[me], local_sems.at[2]),
        ]
        for copy in kept:
            copy.start()
        kvw_ref[me] = kv_stage[me]

        bulk, waiting = [], []
        for source, target in ((wg_hbm, wg_out), (wu_hbm, wu_out)):
            for part in range(2):
                rows = pl.ds(part * (shard_rows // 2), shard_rows // 2)
                for mask in (2, 4, 6, 3, 5, 7, 1):
                    waiting.append((source, target, rows, mask))

        def more(count):
            for unused in range(min(count, len(waiting))):
                source, target, rows, mask = waiting.pop(0)
                peer = flip(me, mask)
                columns = pl.ds(pl.multiple_of(peer * ff_cols, ff_cols), ff_cols)
                copy = send(
                    source.at[rows, columns], target.at[me, rows], bulk_sems, len(bulk), peer
                )
                copy.start()
                bulk.append(copy)

        for unused in gather_c:
            pass
        gather_n = gather_steps(me, n_ref, n_sems)
        next(gather_n)
        for copy in weights:
            copy.start()

        def permute(first):
            def step(i, carry):
                row0 = pl.multiple_of(first + i * block, block)
                packed = row0 + lax.broadcasted_iota(jnp.int32, (block, total), 0)
                chosen = (deal_ref[...] == packed).astype(BF16)
                dealt = mm(chosen, c_all[...].reshape(total, width))
                dg_own[pl.ds(row0, block), :] = (RESIDUAL_SCALE * dealt).astype(BF16)
                return carry

            lax.fori_loop(0, total // 2 // block, step, 0)

        near = pl.multiple_of(core * (total // 2), total // 2)
        far = pl.multiple_of((1 - core) * (total // 2), total // 2)
        half = pl.ds(near, total // 2)

        opposite = lax.rem(group + 2, replicas)
        held_groups = (before, after, opposite)

        def pass_on(k):
            ref = dg_out.at[before if k == 2 else group, half]
            copy = pltpu.make_async_remote_copy(
                src_ref=ref if k == 2 else dg_own.at[half],
                dst_ref=ref,
                send_sem=ring_sems.at[0, k],
                recv_sem=ring_sems.at[1, k],
                device_id={"rep": before if k == 1 else after},
                device_id_type=MESH,
            )
            copy.start()
            return copy

        def share(k):
            ref = dg_out.at[held_groups[k], half]
            copy = send(ref, ref, pair_sems, k, flip(me, 1))
            copy.start()
            return copy

        permute(near)
        hops = [pass_on(0)]
        for unused in range(4):
            next(gather_n)
        permute(far)
        packed = me * local + lax.broadcasted_iota(jnp.int32, (local, total), 0)
        chosen = (deal_ref[...] == packed).astype(BF16)
        cot_out[...] = mm(chosen, c_all[...].reshape(total, width)).astype(BF16)
        store = pltpu.make_async_copy(dg_own, dg_out.at[group], local_sems.at[3])
        store.start()
        for unused in gather_n:
            pass
        for copy in kept:
            copy.wait()
        kept = [
            pltpu.make_async_copy(gate_slot, wg_out.at[me], local_sems.at[0]),
            pltpu.make_async_copy(up_slot, wu_out.at[me], local_sems.at[1]),
        ]
        for copy in kept:
            copy.start()
        for copy in weights:
            copy.wait_recv()
        more(BULK[0])
        def project(i, carry):
            row0 = pl.multiple_of(i * block, block)
            rows = pl.ds(row0, block)
            x = n_ref[pl.ds(i * (block // local), block // local)].reshape(block, width)
            cosine, sine = lane_rope(row0, block, freq_ref[...], len_ref)
            pre = mm(x, qw_ref[...].reshape(width, q_cols))
            for j in range(q_cols // (2 * HEAD)):
                lanes = slice(j * 2 * HEAD, (j + 1) * 2 * HEAD)
                y = pre[:, lanes]
                q_ref[rows, lanes] = (y * cosine + lane_swap(y) * sine).astype(BF16)
            cosine, sine = keys_only(cosine, sine)
            y = mm(x, kvw_ref[...].reshape(width, 2 * HEAD))
            kv_ref[rows, :] = (y * cosine + lane_swap(y) * sine).astype(BF16)
            return carry

        lax.fori_loop(0, total // block, project, 0)
        hops.append(pass_on(1))
        attend(q_cols // HEAD, block, q_ref, kv_ref, len_ref, att_ref)

        def partial(d):
            return mm(att_ref[pl.ds(pl.multiple_of(d * local, local), local), :], wo_ref[...])

        pending = {}

        def act_grad(held, first, loaded):
            rows = pl.ds(first, total // 2)
            if not loaded:
                load = pltpu.make_async_copy(
                    dg_out.at[held, rows], dg_own.at[rows], local_sems.at[3]
                )
                load.start()
                load.wait()
            slot = 0 if first is near else 1
            if slot in pending:
                pending[slot].wait()

            def step(i, carry):
                part = pl.ds(pl.multiple_of(first + i * block, block), block)
                ag_stage[part, :] = mm_t(dg_own[part, :], wd_ref[...]).astype(BF16)
                return carry

            lax.fori_loop(0, total // 2 // block, step, 0)
            pending[slot] = pltpu.make_async_copy(
                ag_stage.at[rows], ag_out.at[held, rows], local_sems.at[5 + slot]
            )
            pending[slot].start()

        hops[0].wait_recv()
        hops.append(pass_on(2))
        shares = [share(0)]
        scatter = scatter_steps(
            me, partial, sib_out, sib_in, acc, x_out, x_in, y_out, y_in, scatter_sems
        )
        next(scatter)
        more(BULK[1])
        for unused in scatter:
            pass
        branch = acc[3]
        middle = tok_ref[...].astype(F32) + RESIDUAL_SCALE * branch
        mid_ref[...] = middle
        nf_ref[me] = rms_scale(middle, fgain_ref[...]).astype(BF16)
        gather_nf = gather_steps(me, nf_ref, nf_sems)
        next(gather_nf)
        more(BULK[2])
        for unused in gather_nf:
            pass
        more(len(waiting))
        give = pltpu.make_async_copy(nf_ref.at[pl.ds(4 * core, 4)], half_out, local_sems.at[4])
        give.start()
        store.wait()
        for copy in kept:
            copy.wait()
        act_grad(group, near, True)
        act_grad(group, far, True)
        hops[0].wait_send()
        hops[1].wait_send()
        for k in range(3):
            if k > 0:
                hops[k].wait_recv()
                shares.append(share(k))
            act_grad(held_groups[k], near, False)
            shares[k].wait_recv()
            act_grad(held_groups[k], far, False)
        for copy in pending.values():
            copy.wait()
        give.wait()
        for copy in bulk:
            copy.wait_recv()
        for copy in weights + bulk + hops[2:] + shares:
            copy.wait_send()

    rows8 = jax.ShapeDtypeStruct((8, local, width), BF16)
    half_sems = pltpu.SemaphoreType.DMA
    outs = pl.pallas_call(
        kernel,
        out_shape=(
            rows8,
            jax.ShapeDtypeStruct((total, q_cols), BF16),
            jax.ShapeDtypeStruct((total, 2 * HEAD), BF16),
            jax.ShapeDtypeStruct((total, q_cols), BF16),
            jax.ShapeDtypeStruct((8, shard_rows, q_cols), BF16),
            jax.ShapeDtypeStruct((8, shard_rows, 2 * HEAD), BF16),
            jax.ShapeDtypeStruct((8, shard_rows, ff_cols), BF16),
            jax.ShapeDtypeStruct((8, shard_rows, ff_cols), BF16),
            jax.ShapeDtypeStruct((local, width), F32),
            rows8,
            jax.ShapeDtypeStruct((replicas, total, width), BF16),
            jax.ShapeDtypeStruct((replicas, total, ff_cols), BF16),
            jax.ShapeDtypeStruct((local, width), BF16),
            jax.ShapeDtypeStruct((4, local, width), BF16),
        ),
        in_specs=[VMEM, VMEM, ANY, VMEM, VMEM, VMEM, VMEM, ANY, ANY, VMEM, VMEM, SMEM, VMEM, VMEM],
        out_specs=[VMEM] * 6 + [ANY, ANY, VMEM, VMEM, ANY, ANY, VMEM, ANY],
        scratch_shapes=[
            pltpu.VMEM((8, shard_rows, 2 * HEAD), BF16),
            pltpu.VMEM((8, local, width), BF16),
            pltpu.VMEM((total, width), BF16),
            pltpu.VMEM((total, ff_cols), BF16),
        ]
        + scatter_scratch(local, width)
        + [
            half_sems((2, GATHER_SEMS)),
            half_sems((2, GATHER_SEMS)),
            half_sems((2, GATHER_SEMS)),
            half_sems((2, 14)),
            half_sems((2, 28)),
            half_sems((2, replicas)),
            half_sems((2, replicas)),
            half_sems((7,)),
        ],
        compiler_params=comm_params(0, 56),
        cost_estimate=pl.CostEstimate(
            flops=200_000_000_000, bytes_accessed=50 << 20, transcendentals=total * total
        ),
        name="front",
    )(
        tokens, attn_gain[None, :], query_weight, key_weight, value_weight, output_weight,
        ffn_gain[None, :], gate_weight, up_weight, down_weight, dealing, lengths, cotangent, freq,
    )
    normed, q, kv, attention, qw, kvw, wg, wu, middle, nf, dg, ag, cot, held = outs
    return (
        normed.reshape(total, width), q, kv, attention,
        qw.reshape(width, q_cols), kvw.reshape(width, 2 * HEAD),
        wg.reshape(width, ff_cols), wu.reshape(width, ff_cols),
        middle, nf.reshape(total, width), dg, ag, cot,
        held.reshape(total // 2, width),
    )


def norm_pull(x, gain, grad):
    scale = lax.rsqrt(jnp.mean(x * x, axis=-1, keepdims=True) + EPSILON)
    pulled = gain * grad
    rows_part = scale * pulled - x * (
        scale * scale * scale * jnp.mean(pulled * x, axis=-1, keepdims=True)
    )
    return rows_part, jnp.sum(grad * x * scale, axis=0, keepdims=True)


def pull_gather(part, middle, gain, out_grad, activated, down_weight, deal, collective_id):
    rows, width = middle.shape
    groups, total, cols = activated.shape
    block = 256

    def kernel(
        p_ref, m_ref, gain_ref, g_ref, act_hbm, wd_ref, deal_ref,
        mg_ref, gain_part, out, dealt_ref, act_ref, packed_ref, act_sem, *scratch,
    ):
        me = lax.axis_index("shard")
        *buffers, scatter_sems, sems = scratch
        load = pltpu.make_async_copy(act_hbm.at[lax.axis_index("rep")], act_ref, act_sem.at[0])
        load.start()
        greet(me, (1, 2, 4))

        def down(i, carry):
            chunk = pl.ds(pl.multiple_of(i * block, block), block)
            packed_ref[chunk, :] = (RESIDUAL_SCALE * mm(act_ref[chunk, :], wd_ref[...])).astype(BF16)
            return carry

        def deal_out(i, carry):
            chunk = pl.ds(pl.multiple_of(i * block, block), block)
            packed = lax.broadcasted_iota(jnp.int32, (block, total), 1)
            chosen = (deal_ref[chunk, :] == packed).astype(BF16)
            dealt_ref[chunk, :] = mm(chosen, packed_ref[...]).astype(BF16)
            return carry

        half = total // block // 2
        scatter = scatter_steps(
            me,
            lambda d: p_ref[pl.ds(pl.multiple_of(d * rows, rows), rows), :].astype(F32),
            *buffers,
            scatter_sems,
        )
        next(scatter)
        load.wait()
        lax.fori_loop(0, half, down, 0)
        next(scatter)
        lax.fori_loop(half, 2 * half, down, 0)
        own = pl.ds(pl.multiple_of(me * rows, rows), rows)
        packed_ref[own, :] = (packed_ref[own, :].astype(F32) + m_ref[...]).astype(BF16)
        next(scatter)
        for unused in scatter:
            pass
        rows_part, gain_row = norm_pull(m_ref[...], gain_ref[...], buffers[2][3])
        gain_part[...] = gain_row
        middle_grad = g_ref[...].astype(F32) + rows_part
        mg_ref[...] = middle_grad
        out[me] = (RESIDUAL_SCALE * middle_grad).astype(BF16)
        gather = gather_steps(me, out, sems)
        next(gather)
        lax.fori_loop(0, half, deal_out, 0)
        for unused in range(2):
            next(gather)
        lax.fori_loop(half, 2 * half, deal_out, 0)
        for unused in gather:
            pass

    return pl.pallas_call(
        kernel,
        out_shape=(
            jax.ShapeDtypeStruct((rows, width), F32),
            jax.ShapeDtypeStruct((1, width), F32),
            jax.ShapeDtypeStruct((8, rows, width), BF16),
            jax.ShapeDtypeStruct((total, width), BF16),
        ),
        in_specs=[VMEM] * 4 + [ANY] + [VMEM] * 2,
        out_specs=[VMEM] * 4,
        scratch_shapes=[
            pltpu.VMEM((total, cols), BF16),
            pltpu.VMEM((total, width), BF16),
            pltpu.SemaphoreType.DMA((1,)),
        ]
        + scatter_scratch(rows, width)
        + [pltpu.SemaphoreType.DMA((2, GATHER_SEMS))],
        compiler_params=comm_params(collective_id, 56),
        cost_estimate=pl.CostEstimate(
            flops=60_000_000_000, bytes_accessed=50 * rows * width, transcendentals=rows
        ),
        name="pull_gather",
    )(part, middle, gain[None, :], out_grad, activated, down_weight, deal)


def pull_tokens(
    part, out_part, hidden, gain, middle_grad, other_gain, near, act_grads, wg, wu, filled, replicas, collective_id
):
    rows, width = middle_grad.shape
    groups, total, cols = act_grads.shape
    block = 256
    levels = [("shard", 1), ("shard", 2), ("shard", 4)]
    level = 1
    while level < replicas:
        levels.append(("rep", level))
        level *= 2
    per_half = total // 2 // block

    def kernel(
        p_ref, o_ref, h_ref, gain_ref, mg_ref, og_ref, wg_ref, wu_ref, ag_hbm,
        before_held, after_held, unused_na, unused_act, unused_gg, unused_ug,
        out, lay, gains, na_hbm, act_hbm, gg_hbm, ug_hbm, fetched, share_sems,
        nf_buf, ag_buf, done_buf, in_sems, out_sems, gain_in, gain_out, gain_sems, *scratch,
    ):
        me = lax.axis_index("shard")
        group = lax.axis_index("rep")
        core = lax.rem(me, 2)
        before = lax.rem(group + replicas - 1, replicas)
        after = lax.rem(group + 1, replicas)
        first, second = scratch[:8], scratch[8:]
        parts = (
            (before, before_held, core),
            (after, after_held, core),
            (before, fetched.at[0], 1 - core),
            (after, fetched.at[1], 1 - core),
        )

        def rows_of(p, r):
            return pl.ds(pl.multiple_of((parts[p][2] * per_half + r) * block, block), block)

        def loads(p, r):
            held, source, unused = parts[p]
            slot = (p % 2) * per_half + r
            return [
                pltpu.make_async_copy(
                    source.at[pl.ds(pl.multiple_of(r * block, block), block)],
                    nf_buf.at[slot],
                    in_sems.at[0, slot],
                ),
                pltpu.make_async_copy(ag_hbm.at[held, rows_of(p, r)], ag_buf.at[slot], in_sems.at[1, slot]),
            ]

        def stores(p, r):
            held = parts[p][0]
            slot = (p % 2) * per_half + r
            where = rows_of(p, r)
            return [
                pltpu.make_async_copy(nf_buf.at[slot], na_hbm.at[held, where], out_sems.at[0, slot])
            ] + [
                pltpu.make_async_copy(done_buf.at[k, slot], target.at[held, where], out_sems.at[k + 1, slot])
                for k, target in enumerate((act_hbm, gg_hbm, ug_hbm))
            ]

        def start_loads(p):
            for r in range(per_half):
                for copy in loads(p, r):
                    copy.start()

        def wait_stores(p):
            for r in range(per_half):
                for copy in stores(p, r):
                    copy.wait()

        def fill(p):
            if p > 0:
                wait_stores(p - 1)
            if p in (1, 2):
                shares[p - 1].wait_recv()
            if p + 1 < len(parts):
                start_loads(p + 1)

            def step(r, carry):
                slot = (p % 2) * per_half + r
                for copy in loads(p, r):
                    copy.wait()
                results = ffn_rows(nf_buf[slot], ag_buf[slot], wg_ref[...], wu_ref[...])
                for k, result in enumerate(results):
                    done_buf[k, slot] = result
                for copy in stores(p, r):
                    copy.start()
                return carry

            lax.fori_loop(0, per_half, step, 0)

        start_loads(0)
        barrier = pltpu.get_barrier_semaphore()
        peers = []
        for axis, weight in levels:
            index = me if axis == "shard" else group
            peers.append({axis: index + weight - 2 * weight * lax.rem(lax.div(index, weight), 2)})
        for peer in peers:
            pl.semaphore_signal(barrier, inc=1, device_id=peer, device_id_type=MESH)
        pl.semaphore_wait(barrier, len(peers))

        def blocks_of(ref):
            return lambda d: ref[pl.ds(pl.multiple_of(d * rows, rows), rows), :].astype(F32)

        grads = scatter_steps(me, blocks_of(p_ref), *first)
        outputs = scatter_steps(me, blocks_of(o_ref), *second)
        next(grads)
        next(outputs)
        shares = [
            send(source, fetched.at[k], share_sems, k, flip(me, 1))
            for k, source in enumerate((before_held, after_held))
        ]
        for copy in shares:
            copy.start()
        fill(0)
        next(grads)
        fill(1)
        next(grads)
        next(outputs)
        fill(2)
        next(grads)
        next(outputs)
        rows_part, gain_row = norm_pull(h_ref[...].astype(F32), gain_ref[...], first[2][3])
        out[...] = mg_ref[...] + rows_part
        sums = jnp.concatenate([gain_row, og_ref[...]], axis=0)
        for i, peer in enumerate(peers):
            gain_out[i] = sums
            copy = pltpu.make_async_remote_copy(
                src_ref=gain_out.at[i],
                dst_ref=gain_in.at[i],
                send_sem=gain_sems.at[0, i],
                recv_sem=gain_sems.at[1, i],
                device_id=peer,
                device_id_type=MESH,
            )
            copy.start()
            if i == 0:
                fill(3)
            copy.wait()
            sums = sums + gain_in[i]
        gains[...] = sums
        next(outputs)
        lay[...] = second[2][3].astype(BF16)
        for steps in (grads, outputs):
            for unused in steps:
                pass
        wait_stores(3)
        for copy in shares:
            copy.wait_send()

    hidden_shape = jax.ShapeDtypeStruct((groups, total, cols), BF16)
    return pl.pallas_call(
        kernel,
        out_shape=(
            jax.ShapeDtypeStruct((rows, width), F32),
            jax.ShapeDtypeStruct((rows, width), BF16),
            jax.ShapeDtypeStruct((2, width), F32),
            jax.ShapeDtypeStruct((groups, total, width), BF16),
            hidden_shape,
            hidden_shape,
            hidden_shape,
            jax.ShapeDtypeStruct((2, total // 2, width), BF16),
        ),
        in_specs=[VMEM] * 8 + [ANY] * 7,
        out_specs=[VMEM] * 3 + [ANY] * 5,
        input_output_aliases={11: 3, 12: 4, 13: 5, 14: 6},
        scratch_shapes=[
            pltpu.SemaphoreType.DMA((2, 2)),
            pltpu.VMEM((2 * per_half, block, width), BF16),
            pltpu.VMEM((2 * per_half, block, cols), BF16),
            pltpu.VMEM((3, 2 * per_half, block, cols), BF16),
            pltpu.SemaphoreType.DMA((2, 2 * per_half)),
            pltpu.SemaphoreType.DMA((4, 2 * per_half)),
            pltpu.VMEM((len(levels), 2, width), F32),
            pltpu.VMEM((len(levels), 2, width), F32),
            pltpu.SemaphoreType.DMA((2, len(levels))),
        ]
        + scatter_scratch(rows, width)
        + scatter_scratch(rows, width),
        compiler_params=comm_params(collective_id, 62),
        cost_estimate=pl.CostEstimate(
            flops=60_000_000_000, bytes_accessed=50 * rows * width, transcendentals=rows
        ),
        name="pull_tokens",
    )(
        part, out_part, hidden, gain[None, :], middle_grad, other_gain, wg, wu, act_grads, *near, *filled
    )


def softmax_block(q, k, allowed):
    scores = SCORE_SCALE * mm_t(q, k)
    scores = jnp.where(allowed, scores, MASKED)
    top = jnp.max(scores, axis=-1, keepdims=True)
    weight = jnp.exp(scores - top)
    return weight * (1.0 / jnp.sum(weight, axis=-1, keepdims=True))


def allowed_block(row0, cols, start):
    shape = (start.shape[0], cols)
    query = row0 + lax.broadcasted_iota(jnp.int32, shape, 0)
    key = lax.broadcasted_iota(jnp.int32, shape, 1)
    return (key >= start) & (key <= query)


def sequence_starts(row0, shape, lengths_ref):
    row = row0 + lax.broadcasted_iota(jnp.int32, shape, 0)
    start = jnp.zeros(shape, jnp.int32)
    end = 0
    for i in range(lengths_ref.shape[1]):
        length = lengths_ref[0, i]
        end = end + length
        start = start + jnp.where(row >= end, length, 0)
    return start


def attend(heads, block, q_ref, kv_ref, lengths_ref, o_ref):
    total = kv_ref.shape[0]
    for i in range(total // block):
        cols = (i + 1) * block
        rows = pl.ds(i * block, block)
        allowed = allowed_block(
            i * block, cols, sequence_starts(i * block, (block, 1), lengths_ref)
        )
        kv = kv_ref[:cols, :]
        k, v = kv[:, :HEAD], kv[:, HEAD:]
        for h in range(heads):
            lanes = slice(h * HEAD, (h + 1) * HEAD)
            probs = softmax_block(q_ref[rows, lanes], k, allowed)
            o_ref[rows, lanes] = mm(probs.astype(BF16), v).astype(BF16)


def attend_back(heads, block, q_ref, kv_ref, g_ref, lengths_ref, dq_ref, dk_ref, dv_ref):
    total = kv_ref.shape[0]
    dk_ref[...] = jnp.zeros_like(dk_ref)
    dv_ref[...] = jnp.zeros_like(dv_ref)
    for i in range(total // block):
        cols = (i + 1) * block
        rows = pl.ds(i * block, block)
        allowed = allowed_block(
            i * block, cols, sequence_starts(i * block, (block, 1), lengths_ref)
        )
        kv = kv_ref[:cols, :]
        k, v = kv[:, :HEAD], kv[:, HEAD:]
        for h in range(heads):
            lanes = slice(h * HEAD, (h + 1) * HEAD)
            q, g = q_ref[rows, lanes], g_ref[rows, lanes]
            probs = softmax_block(q, k, allowed)
            probs_grad = mm_t(g, v)
            delta = jnp.sum(probs * probs_grad, axis=-1, keepdims=True)
            score_grad = (probs * (probs_grad - delta)).astype(BF16)
            dq_ref[rows, lanes] = SCORE_SCALE * mm(score_grad, k)
            dk_ref[:cols, :] += SCORE_SCALE * t_mm(score_grad, q)
            dv_ref[:cols, :] += t_mm(probs.astype(BF16), g)


def attention_forward(q, kv, lengths):
    total, width = q.shape

    def kernel(q_ref, kv_ref, lengths_ref, o_ref):
        attend(width // HEAD, 256, q_ref, kv_ref, lengths_ref, o_ref)

    return pl.pallas_call(
        kernel,
        out_shape=jax.ShapeDtypeStruct((total, width), BF16),
        in_specs=[VMEM, VMEM, SMEM],
        out_specs=VMEM,
        compiler_params=pltpu.CompilerParams(vmem_limit_bytes=40 << 20),
        name="attention_forward",
    )(q, kv, lengths)


def attention_gradients(q, kv, grad, lengths):
    total, width = q.shape

    def kernel(q_ref, kv_ref, g_ref, lengths_ref, dq_ref, dk_ref, dv_ref):
        attend_back(width // HEAD, 256, q_ref, kv_ref, g_ref, lengths_ref, dq_ref, dk_ref, dv_ref)

    return pl.pallas_call(
        kernel,
        out_shape=(
            jax.ShapeDtypeStruct((total, width), F32),
            jax.ShapeDtypeStruct((total, HEAD), F32),
            jax.ShapeDtypeStruct((total, HEAD), F32),
        ),
        in_specs=[VMEM, VMEM, VMEM, SMEM],
        out_specs=[VMEM] * 3,
        compiler_params=pltpu.CompilerParams(vmem_limit_bytes=40 << 20),
        name="attention_gradients",
    )(q, kv, grad, lengths)


def lane_rope(row0, rows, freq, lengths_ref):
    shape = (rows, 2 * HEAD)
    row = row0 + lax.broadcasted_iota(jnp.int32, shape, 0)
    position = row - sequence_starts(row0, shape, lengths_ref)
    turned = position.astype(F32) * freq
    lane = lax.broadcasted_iota(jnp.int32, shape, 1)
    first = lax.rem(lane, HEAD) < HEAD // 2
    sine = jnp.sin(turned)
    return jnp.cos(turned), jnp.where(first, -sine, sine)


def lane_swap(x):
    half = HEAD // 2
    lane = lax.broadcasted_iota(jnp.int32, x.shape, 1)
    first = lax.rem(lane, HEAD) < half
    return jnp.where(first, pltpu.roll(x, 2 * HEAD - half, 1), pltpu.roll(x, half, 1))


def keys_only(cosine, sine):
    lane = lax.broadcasted_iota(jnp.int32, cosine.shape, 1)
    return jnp.where(lane < HEAD, cosine, 1.0), jnp.where(lane < HEAD, sine, 0.0)


def attention_backward(
    branch_grad, output_weight, attention, q, kv, normed, q_weight, kv_weight, lengths, freq
):
    total, q_cols = q.shape
    width = normed.shape[1]
    block = 256

    def kernel(
        bg_ref, wo_ref, a_ref, q_ref, kv_ref, n_ref, qw_ref, kvw_ref, len_ref, freq_ref,
        dn_ref, dqkv_ref, dwo_ref, g_ref, dq_ref, dk_ref, dv_ref, pq_ref, pkv_ref,
    ):
        def open_up(i, carry):
            rows = pl.ds(pl.multiple_of(i * block, block), block)
            g_ref[rows, :] = mm_t(bg_ref[rows, :], wo_ref[...]).astype(BF16)
            return carry

        lax.fori_loop(0, total // block, open_up, 0)
        attend_back(
            q_cols // HEAD, block, q_ref, kv_ref, g_ref, len_ref, dq_ref, dk_ref, dv_ref
        )
        def close_up(i, carry):
            row0 = pl.multiple_of(i * block, block)
            rows = pl.ds(row0, block)
            cosine, sine = lane_rope(row0, block, freq_ref[...], len_ref)
            for j in range(q_cols // (2 * HEAD)):
                lanes = slice(j * 2 * HEAD, (j + 1) * 2 * HEAD)
                x = dq_ref[rows, lanes]
                pq_ref[rows, lanes] = (x * cosine - lane_swap(x) * sine).astype(BF16)
            cosine, sine = keys_only(cosine, sine)
            x = jnp.concatenate([dk_ref[rows, :], dv_ref[rows, :]], axis=1)
            pkv_ref[rows, :] = (x * cosine - lane_swap(x) * sine).astype(BF16)
            dn_ref[rows, :] = (
                mm_t(pq_ref[rows, :], qw_ref[...]) + mm_t(pkv_ref[rows, :], kvw_ref[...])
            ).astype(BF16)
            return carry

        lax.fori_loop(0, total // block, close_up, 0)

        def weigh(i, carry):
            cols = pl.ds(pl.multiple_of(i * 512, 512), 512)
            dqkv_ref[cols, :q_cols] = t_mm(n_ref[:, cols], pq_ref[...]).astype(BF16)
            dqkv_ref[cols, q_cols:] = t_mm(n_ref[:, cols], pkv_ref[...]).astype(BF16)
            dwo_ref[:, cols] = t_mm(a_ref[...], bg_ref[:, cols]).astype(BF16)
            return carry

        lax.fori_loop(0, width // 512, weigh, 0)

    return pl.pallas_call(
        kernel,
        out_shape=(
            jax.ShapeDtypeStruct((total, width), BF16),
            jax.ShapeDtypeStruct((width, q_cols + 2 * HEAD), BF16),
            jax.ShapeDtypeStruct((q_cols, width), BF16),
        ),
        in_specs=[VMEM] * 8 + [SMEM, VMEM],
        out_specs=[VMEM] * 3,
        scratch_shapes=[
            pltpu.VMEM((total, q_cols), BF16),
            pltpu.VMEM((total, q_cols), F32),
            pltpu.VMEM((total, HEAD), F32),
            pltpu.VMEM((total, HEAD), F32),
            pltpu.VMEM((total, q_cols), BF16),
            pltpu.VMEM((total, 2 * HEAD), BF16),
        ],
        compiler_params=pltpu.CompilerParams(vmem_limit_bytes=56 << 20),
        cost_estimate=pl.CostEstimate(flops=30_000_000_000, bytes_accessed=30 << 20, transcendentals=total * total),
        name="attention_backward",
    )(branch_grad, output_weight, attention, q, kv, normed, q_weight, kv_weight, lengths, freq)


def ffn_rows(nf, act_grad, wg, wu):
    gate, up = mm(nf, wg), mm(nf, wu)
    act_grad = act_grad.astype(F32)
    sigmoid = 1.0 / (1.0 + jnp.exp(-gate))
    silu = gate * sigmoid
    activated = (silu * up).astype(BF16)
    gate_grad = (act_grad * up * sigmoid * (1.0 + gate * (1.0 - sigmoid))).astype(BF16)
    return activated, gate_grad, (act_grad * silu).astype(BF16)


def ffn_own(group, nf, act_grads, wg, wu):
    groups, total, cols = act_grads.shape
    width = nf.shape[1]
    block = 256

    def kernel(g_ref, nf_ref, ag_ref, wg_ref, wu_ref, na_ref, act_ref, gg_ref, ug_ref, dn_ref):
        nf = nf_ref[...]
        act, gg, ug = ffn_rows(nf, ag_ref[0], wg_ref[...], wu_ref[...])
        na_ref[0], act_ref[0], gg_ref[0], ug_ref[0] = nf, act, gg, ug
        dn_ref[...] = (mm_t(gg, wg_ref[...]) + mm_t(ug, wu_ref[...])).astype(BF16)

    mine = pl.BlockSpec((1, block, width), lambda i, g: (g[0], i, 0))
    hid = pl.BlockSpec((1, block, cols), lambda i, g: (g[0], i, 0))
    plain = pl.BlockSpec((block, width), lambda i, g: (i, 0))
    whole = [
        pl.BlockSpec(w.shape, lambda i, g: (0, 0), pipeline_mode=pl.Buffered(1)) for w in (wg, wu)
    ]
    hidden = jax.ShapeDtypeStruct((groups, total, cols), BF16)
    return pl.pallas_call(
        kernel,
        grid_spec=pltpu.PrefetchScalarGridSpec(
            num_scalar_prefetch=1,
            grid=(total // block,),
            in_specs=[plain, hid] + whole,
            out_specs=[mine, hid, hid, hid, plain],
        ),
        out_shape=(
            jax.ShapeDtypeStruct((groups, total, width), BF16),
            hidden,
            hidden,
            hidden,
            jax.ShapeDtypeStruct((total, width), BF16),
        ),
        compiler_params=pltpu.CompilerParams(vmem_limit_bytes=48 << 20),
        cost_estimate=pl.CostEstimate(
            flops=12 * total * width * cols, bytes_accessed=40 << 20, transcendentals=total * cols
        ),
        name="ffn_own",
    )(group, nf, act_grads, wg, wu)


def ffn_other(where, held, fetched, act_grads, wg, wu, filled):
    groups, total, cols = act_grads.shape
    width = held.shape[1]
    block = 256
    per_half = total // 2 // block

    def kernel(w_ref, held_ref, fetched_ref, ag_ref, wg_ref, wu_ref, *rest):
        na_ref, act_ref, gg_ref, ug_ref, nf_ref = rest[4:]
        i = pl.program_id(0)

        @pl.when(i < per_half)
        def _():
            nf_ref[...] = held_ref[...]

        @pl.when(i >= per_half)
        def _():
            nf_ref[...] = fetched_ref[...]

        nf = nf_ref[...]
        act, gg, ug = ffn_rows(nf, ag_ref[0], wg_ref[...], wu_ref[...])
        na_ref[0], act_ref[0], gg_ref[0], ug_ref[0] = nf, act, gg, ug

    def row(i, w):
        half = jnp.where(i < per_half, w[1], 1 - w[1])
        return half * per_half + lax.rem(i, per_half)

    mine = pl.BlockSpec((1, block, width), lambda i, w: (w[0], row(i, w), 0))
    hid = pl.BlockSpec((1, block, cols), lambda i, w: (w[0], row(i, w), 0))
    first = pl.BlockSpec((block, width), lambda i, w: (jnp.minimum(i, per_half - 1), 0))
    last = pl.BlockSpec((block, width), lambda i, w: (jnp.maximum(i - per_half, 0), 0))
    whole = [
        pl.BlockSpec(w.shape, lambda i, g: (0, 0), pipeline_mode=pl.Buffered(1)) for w in (wg, wu)
    ]
    hidden = jax.ShapeDtypeStruct((groups, total, cols), BF16)
    return pl.pallas_call(
        kernel,
        grid_spec=pltpu.PrefetchScalarGridSpec(
            num_scalar_prefetch=1,
            grid=(2 * per_half,),
            in_specs=[first, last, hid] + whole + [pl.BlockSpec(memory_space=pl.ANY)] * 4,
            out_specs=[mine, hid, hid, hid],
            scratch_shapes=[pltpu.VMEM((block, width), BF16)],
        ),
        out_shape=(jax.ShapeDtypeStruct((groups, total, width), BF16), hidden, hidden, hidden),
        input_output_aliases={6: 0, 7: 1, 8: 2, 9: 3},
        compiler_params=pltpu.CompilerParams(vmem_limit_bytes=48 << 20),
        cost_estimate=pl.CostEstimate(
            flops=8 * total * width * cols, bytes_accessed=40 << 20, transcendentals=total * cols
        ),
        name="ffn_other",
    )(where, held, fetched, act_grads, wg, wu, *filled)


def finish(normed, gate_grad, up_grad, activated, down_grad, output_part, qkv_part, collective_id):
    depth, width = normed.shape
    cols = gate_grad.shape[1]
    rows = width // 8
    tall = cols // rows
    steps = 8 + tall
    chunks = 4
    sums = (output_part, qkv_part)

    def kernel(
        nf_hbm, gg_hbm, ug_hbm, act_hbm, dg_hbm, o_in, qkv_in,
        gate_out, up_out, down_out, o_out, qkv_out,
        gg, ug, dg, left, stage, tall_stage, o_mid, qkv_mid, o_last, qkv_last,
        load_sems, left_sems, own_sems, tall_sems, push_sems, relay_sems,
    ):
        me = lax.axis_index("shard")
        group = lax.axis_index("rep")
        inner = (group == 1) | (group == 2)
        outer = (group == 0) | (group == 3)
        beside = group + 1 - 2 * lax.rem(group, 2)
        across = 3 - group

        def peer_of(i):
            mask = 7 - i
            index = 0
            for weight in (1, 2, 4):
                bits = lax.rem(lax.div(me, weight), 2) + lax.rem(lax.div(mask, weight), 2)
                index = index + weight * lax.rem(bits, 2)
            return index

        def start_left(i, slot):
            @pl.when(i < 8)
            def _():
                first = pl.multiple_of(peer_of(i) * rows, rows)
                pltpu.make_async_copy(
                    nf_hbm.at[:, pl.ds(first, rows)], left.at[slot], left_sems.at[slot]
                ).start()

            @pl.when((i >= 8) & (i < steps))
            def _():
                first = pl.multiple_of((i - 8) * rows, rows)
                pltpu.make_async_copy(
                    act_hbm.at[:, pl.ds(first, rows)], left.at[slot], left_sems.at[slot]
                ).start()

        def wait_left(slot):
            pltpu.make_async_copy(
                nf_hbm.at[:, pl.ds(0, rows)], left.at[slot], left_sems.at[slot]
            ).wait()

        loads = [
            pltpu.make_async_copy(source, target, load_sems.at[k])
            for k, (source, target) in enumerate(((gg_hbm, gg), (ug_hbm, ug), (dg_hbm, dg)))
        ]
        start_left(0, 0)
        for load in loads:
            load.start()
        barrier = pltpu.get_barrier_semaphore()
        for mask in range(1, 8):
            pl.semaphore_signal(
                barrier, inc=1, device_id={"shard": flip(me, mask)}, device_id_type=MESH
            )
        for neighbour in (beside, across):
            pl.semaphore_signal(
                barrier, inc=1, device_id={"rep": neighbour}, device_id_type=MESH
            )
        pl.semaphore_wait(barrier, 9)

        arrays = ((o_in, o_mid, o_last, o_out), (qkv_in, qkv_mid, qkv_last, qkv_out))

        def relay_copy(stage_index, k, c, target):
            start, mid, last, out = arrays[k]
            size = start.shape[0] // chunks
            part = pl.ds(pl.multiple_of(c * size, size), size)
            source, arrived = ((start, mid), (mid, last), (out, out))[stage_index]
            return pltpu.make_async_remote_copy(
                src_ref=source.at[part],
                dst_ref=arrived.at[part],
                send_sem=relay_sems.at[0, stage_index, k * chunks + c],
                recv_sem=relay_sems.at[1, stage_index, k * chunks + c],
                device_id={"rep": target},
                device_id_type=MESH,
            )

        @pl.when(outer)
        def _():
            for c in range(chunks):
                for k in range(2):
                    relay_copy(0, k, c, beside).start()

        def relay(t):
            def part_of(k, c):
                size = arrays[k][0].shape[0] // chunks
                return pl.ds(pl.multiple_of(c * size, size), size)

            @pl.when(inner & (t < chunks))
            def _():
                for k in range(2):
                    start, mid, last, out = arrays[k]
                    part = part_of(k, t)
                    relay_copy(0, k, t, beside).wait_recv()
                    mid[part, :] = (start[part, :].astype(F32) + mid[part, :].astype(F32)).astype(BF16)
                    relay_copy(1, k, t, across).start()

            @pl.when(inner & (t >= 1) & (t <= chunks))
            def _():
                for k in range(2):
                    start, mid, last, out = arrays[k]
                    part = part_of(k, t - 1)
                    relay_copy(1, k, t - 1, across).wait_recv()
                    out[part, :] = (mid[part, :].astype(F32) + last[part, :].astype(F32)).astype(BF16)
                    relay_copy(2, k, t - 1, beside).start()

            @pl.when(outer & (t >= 2) & (t <= chunks + 1))
            def _():
                for k in range(2):
                    relay_copy(2, k, t - 2, beside).wait_recv()

        outputs = (gate_out, up_out)
        own_columns = pl.ds(pl.multiple_of(me * cols, cols), cols)

        def push(i, j, target):
            return send(
                stage.at[i, j], outputs[j].at[:, own_columns], push_sems, 2 * i + j, target
            )

        def wide(i, carry):
            slot = lax.rem(i, 2)
            start_left(i + 1, 1 - slot)
            wait_left(slot)
            for j, right in enumerate((gg, ug)):

                @pl.when(i == 0)
                def _():
                    loads[j].wait()

                stage[i, j] = t_mm(left[slot], right[...]).astype(BF16)

                @pl.when(i < 7)
                def _():
                    push(i, j, peer_of(i)).start()

                @pl.when(i == 7)
                def _():
                    pltpu.make_async_copy(
                        stage.at[7, j], outputs[j].at[:, own_columns], own_sems.at[j]
                    ).start()

            @pl.when(lax.rem(i, 2) == 1)
            def _():
                relay(lax.div(i, 2))

            return carry

        lax.fori_loop(0, 8, wide, 0)
        loads[2].wait()

        def tall_copy(i):
            slot = lax.rem(i, 2)
            first = pl.multiple_of((i - 8) * rows, rows)
            return pltpu.make_async_copy(
                tall_stage.at[slot], down_out.at[pl.ds(first, rows), :], tall_sems.at[slot]
            )

        def high(i, carry):
            slot = lax.rem(i, 2)
            start_left(i + 1, 1 - slot)
            wait_left(slot)

            @pl.when(i >= 10)
            def _():
                tall_copy(i - 2).wait()

            tall_stage[slot] = t_mm(left[slot], dg[...]).astype(BF16)
            tall_copy(i).start()

            @pl.when(lax.rem(i, 2) == 1)
            def _():
                relay(lax.div(i, 2))

            return carry

        lax.fori_loop(8, steps, high, 0)
        for i in (steps - 2, steps - 1):
            tall_copy(i).wait()
        for j in range(2):
            pltpu.make_async_copy(
                stage.at[7, j], outputs[j].at[:, own_columns], own_sems.at[j]
            ).wait()
        for t in range(steps // 2, chunks + 2):
            relay(t)

        def drain(i, carry):
            for j in range(2):
                push(i, j, peer_of(i)).wait()
            return carry

        lax.fori_loop(0, 7, drain, 0)

        @pl.when(outer)
        def _():
            for c in range(chunks):
                for k in range(2):
                    relay_copy(0, k, c, beside).wait_send()

        @pl.when(inner)
        def _():
            for c in range(chunks):
                for k in range(2):
                    relay_copy(1, k, c, across).wait_send()
                    relay_copy(2, k, c, beside).wait_send()

    exchanged = jax.ShapeDtypeStruct((rows, 8 * cols), BF16)
    return pl.pallas_call(
        kernel,
        out_shape=(
            exchanged,
            exchanged,
            jax.ShapeDtypeStruct((cols, width), BF16),
            jax.ShapeDtypeStruct(output_part.shape, BF16),
            jax.ShapeDtypeStruct(qkv_part.shape, BF16),
        ),
        in_specs=[ANY] * 5 + [VMEM] * 2,
        out_specs=[ANY] * 3 + [VMEM] * 2,
        scratch_shapes=[
            pltpu.VMEM((depth, cols), BF16),
            pltpu.VMEM((depth, cols), BF16),
            pltpu.VMEM((depth, width), BF16),
            pltpu.VMEM((2, depth, rows), BF16),
            pltpu.VMEM((8, 2, rows, cols), BF16),
            pltpu.VMEM((2, rows, width), BF16),
        ]
        + [pltpu.VMEM(x.shape, BF16) for unused in range(2) for x in sums]
        + [
            pltpu.SemaphoreType.DMA((3,)),
            pltpu.SemaphoreType.DMA((2,)),
            pltpu.SemaphoreType.DMA((2,)),
            pltpu.SemaphoreType.DMA((2,)),
            pltpu.SemaphoreType.DMA((2, 14)),
            pltpu.SemaphoreType.DMA((2, 3, 2 * chunks)),
        ],
        compiler_params=comm_params(collective_id, 62),
        cost_estimate=pl.CostEstimate(
            flops=120_000_000_000, bytes_accessed=80 << 20, transcendentals=0
        ),
        name="finish",
    )(normed, gate_grad, up_grad, activated, down_grad, output_part, qkv_part)


def widen(gate, up, down, out, heads, q_cols):
    rows, wide = gate.shape
    tall, width = down.shape
    n = heads.shape[0]
    steps = 16
    block, high = rows // steps, tall // steps

    def kernel(g_ref, u_ref, d_ref, o_ref, h_ref, g_out, u_out, d_out, o_out, q_out, k_out, v_out):
        g_out[...] = g_ref[...].astype(F32)
        u_out[...] = u_ref[...].astype(F32)
        d_out[...] = d_ref[...].astype(F32)
        o_out[...] = o_ref[...].astype(F32)
        for i in range(n):
            q_out[:, i * q_cols : (i + 1) * q_cols] = h_ref[i, :, :q_cols].astype(F32)
        kv = [h_ref[i, :, q_cols:].astype(F32) for i in range(n)]
        k_out[...] = jnp.concatenate([x[:, :HEAD] for x in kv], axis=1)
        v_out[...] = jnp.concatenate([x[:, HEAD:] for x in kv], axis=1)

    def spec(height, across):
        return pl.BlockSpec((height, across), lambda i: (i, 0))

    shapes = [(rows, wide), (rows, wide), (tall, width), (rows, width)]
    blocks = [spec(block, wide), spec(block, wide), spec(high, width), spec(block, width)]
    narrow = [n * q_cols, n * HEAD, n * HEAD]
    return pl.pallas_call(
        kernel,
        grid=(steps,),
        in_specs=blocks + [pl.BlockSpec((n, block, heads.shape[2]), lambda i: (0, i, 0))],
        out_specs=blocks + [spec(block, across) for across in narrow],
        out_shape=[jax.ShapeDtypeStruct(shape, F32) for shape in shapes]
        + [jax.ShapeDtypeStruct((rows, across), F32) for across in narrow],
        compiler_params=pltpu.CompilerParams(vmem_limit_bytes=24 << 20),
        cost_estimate=pl.CostEstimate(
            flops=4 * rows * wide, bytes_accessed=20 * rows * wide, transcendentals=0
        ),
        name="widen",
    )(gate, up, down, out, heads)


def per_device_plane(
    tokens, attn_gain, query_weight, key_weight, value_weight, output_weight, ffn_gain,
    gate_weight, up_weight, down_weight, dealing, lengths, cotangent,
):
    n = 8
    here = lax.axis_index("shard")
    group = lax.axis_index("rep")
    replicas = lax.axis_size("rep")
    local, width = tokens.shape
    total = local * n
    rows = query_weight.shape[0]
    q_cols = query_weight.shape[1] // n
    ff_cols = gate_weight.shape[1] // n
    core = lax.rem(here, 2)
    half = HEAD // 2
    freq = ROPE_BASE ** (-(jnp.arange(half, dtype=F32) * 2.0) / (2.0 * half))
    freq = jnp.tile(freq, 4)[None, :]

    (
        normed, q, kv, attention, q_weight, kv_weight, gate_cols, up_cols,
        middle, normed_ffn, down_grads, act_grads, cot_own, held,
    ) = front(
        tokens, attn_gain, query_weight, key_weight, value_weight, output_weight, ffn_gain,
        gate_weight, up_weight, down_weight, dealing, lengths, cotangent, freq, replicas,
    )

    def shift(x, by):
        return lax.ppermute(x, "rep", [(i, (i + by) % replicas) for i in range(replicas)])

    def fetch(x):
        return lax.ppermute(x, "shard", [(i, i ^ 1) for i in range(n)])

    before, after = shift(held, 1), shift(held, replicas - 1)
    *filled, normed_ffn_part = ffn_own(
        group.astype(jnp.int32)[None], normed_ffn, act_grads, gate_cols, up_cols
    )
    middle_grad, ffn_gain_part, branch_grad, output_part = pull_gather(
        normed_ffn_part, middle, ffn_gain, cot_own, filled[1], down_weight, dealing.reshape(total, 1), 2
    )
    normed_part, qkv_grad, output_grad = attention_backward(
        branch_grad.reshape(total, width), output_weight, attention, q, kv, normed, q_weight, kv_weight,
        lengths, freq,
    )
    before, after, unused_part = lax.optimization_barrier((before, after, normed_part))
    opposite = shift(before, 1)
    qkv_part = exchange(qkv_grad.reshape(n, rows, q_cols + 2 * HEAD))
    tokens_grad, layer_output, gains, *filled, unused_half = pull_tokens(
        normed_part, output_part, tokens, attn_gain, middle_grad, ffn_gain_part,
        (before, after), act_grads, gate_cols, up_cols, filled, replicas, 3,
    )
    opposite, unused_rows = lax.optimization_barrier((opposite, tokens_grad))
    where = jnp.stack([lax.rem(group + replicas - 2, replicas), core]).astype(jnp.int32)
    filled = ffn_other(where, opposite, fetch(opposite), act_grads, gate_cols, up_cols, filled)
    left, *rights = [x.reshape(replicas * total, -1) for x in (filled[0], filled[2], filled[3])]
    gate_grad, up_grad, down_grad, output_grad, qkv_grad = finish(
        left, *rights, filled[1].reshape(replicas * total, -1), down_grads.reshape(replicas * total, -1),
        output_grad, qkv_part.reshape(width, -1), 4,
    )
    gate_grad, up_grad, down_grad, output_grad, q_grad, k_grad, v_grad = widen(
        gate_grad, up_grad, down_grad, output_grad, qkv_grad.reshape(n, rows, -1), q_cols
    )
    return (
        layer_output, tokens_grad, gains[0], q_grad, k_grad, v_grad, output_grad, gains[1],
        gate_grad, up_grad, down_grad,
    )


def per_device(
    tokens,
    attn_gain,
    query_weight,
    key_weight,
    value_weight,
    output_weight,
    ffn_gain,
    gate_weight,
    up_weight,
    down_weight,
    dealing,
    lengths,
    cotangent,
):
    n = lax.axis_size("shard")
    here = lax.axis_index("shard")
    local, width = tokens.shape
    total = local * n
    rows = query_weight.shape[0]
    ff_cols = gate_weight.shape[1] // n
    q_cols = query_weight.shape[1] // n
    copies = n // KV_HEADS
    own = here * local

    packed = jnp.arange(total, dtype=jnp.int32)
    segment, position = places(packed, lengths[0])
    cos_q, sin_q = rope_tables(position, q_cols)
    cos_k, sin_k = cos_q[:, :HEAD], sin_q[:, :HEAD]
    dealt = (dealing[0][:, None] == packed[None, :]).astype(BF16)

    def column_blocks(weight, cols):
        return weight.reshape(rows, n, cols).transpose(1, 0, 2)

    def head_blocks(weight):
        blocks = weight.reshape(rows, KV_HEADS, HEAD).transpose(1, 0, 2)
        return jnp.repeat(blocks, copies, axis=0)

    spread_cotangent = lax.all_gather(cotangent, ("rep", "shard"), axis=0, tiled=True)
    all_dealing = lax.all_gather(dealing, "rep", axis=0, tiled=True)
    qkv = exchange(
        jnp.concatenate(
            [column_blocks(query_weight, q_cols), head_blocks(key_weight), head_blocks(value_weight)],
            axis=2,
        )
    ).reshape(width, q_cols + 2 * HEAD)
    gate_cols = exchange(column_blocks(gate_weight, ff_cols)).reshape(width, ff_cols)
    up_cols = exchange(column_blocks(up_weight, ff_cols)).reshape(width, ff_cols)

    normed = gather_rows(rms_scale(tokens.astype(F32), attn_gain).astype(BF16))
    pre = mm(normed, qkv)
    queries = rotate(pre[:, :q_cols], cos_q, sin_q).astype(BF16)
    keys = rotate(pre[:, q_cols : q_cols + HEAD], cos_k, sin_k).astype(BF16)
    values = pre[:, q_cols + HEAD :].astype(BF16)
    attention = attention_forward(queries, jnp.concatenate([keys, values], axis=1), lengths)
    branch = scatter_rows(mm(attention, output_weight).astype(BF16))
    middle = tokens.astype(F32) + RESIDUAL_SCALE * branch.astype(F32)
    normed_ffn = gather_rows(rms_scale(middle, ffn_gain).astype(BF16))
    own_normed = lax.dynamic_slice_in_dim(normed_ffn, own, local)
    all_normed = lax.all_gather(own_normed, ("rep", "shard"), axis=0, tiled=True)

    reps = lax.axis_size("rep")
    group = lax.axis_index("rep")
    deals = (all_dealing[:, :, None] == packed[None, None, :]).astype(BF16)
    out_grad_all = lax.dot_general(
        deals,
        spread_cotangent.reshape(reps, total, width),
        (((1,), (1,)), ((0,), (0,))),
        preferred_element_type=F32,
    ).reshape(reps * total, width)
    down_grad_all = (RESIDUAL_SCALE * out_grad_all).astype(BF16)
    out_grad = lax.dynamic_slice_in_dim(out_grad_all, group * total + own, local)
    act_grad_all = mm_t(down_grad_all, down_weight)

    def ffn(rows_in, act_grad):
        gate = mm(rows_in, gate_cols)
        up = mm(rows_in, up_cols)
        sigmoid = jax.nn.sigmoid(gate)
        activated = (gate * sigmoid * up).astype(BF16)
        gate_grad = (act_grad * up * sigmoid * (1.0 + gate * (1.0 - sigmoid))).astype(BF16)
        up_grad = (act_grad * gate * sigmoid).astype(BF16)
        return activated, gate_grad, up_grad

    activated, gate_grad, up_grad = ffn(
        normed_ffn, lax.dynamic_slice_in_dim(act_grad_all, group * total, total)
    )
    normed_ffn_part = (mm_t(gate_grad, gate_cols) + mm_t(up_grad, up_cols)).astype(BF16)
    middle_part, ffn_gain_part = norm_pull(
        middle, ffn_gain, scatter_rows(normed_ffn_part).astype(F32)
    )
    middle_grad = out_grad + middle_part
    branch_grad = gather_rows((RESIDUAL_SCALE * middle_grad).astype(BF16))

    own_columns = lax.dynamic_slice_in_dim(dealt, own, local, axis=1)
    layer_output = scatter_rows(
        (
            RESIDUAL_SCALE * mm(mm(dealt, activated).astype(BF16), down_weight)
            + mm(own_columns, middle.astype(BF16))
        ).astype(BF16)
    )

    attention_grad = mm_t(branch_grad, output_weight).astype(BF16)
    dq, dk, dv = attention_gradients(
        queries, jnp.concatenate([keys, values], axis=1), attention_grad, lengths
    )
    pre_grad = jnp.concatenate(
        [
            unrotate(dq, cos_q, sin_q).astype(BF16),
            unrotate(dk, cos_k, sin_k).astype(BF16),
            dv.astype(BF16),
        ],
        axis=1,
    )
    normed_part = mm_t(pre_grad, qkv).astype(BF16)
    hidden_part, attn_gain_part = norm_pull(
        tokens.astype(F32), attn_gain, scatter_rows(normed_part).astype(F32)
    )
    tokens_grad = middle_grad + hidden_part

    activated, gate_grad, up_grad = ffn(all_normed, act_grad_all)
    gate_part = exchange(t_mm(all_normed, gate_grad).astype(BF16).reshape(n, rows, ff_cols))
    up_part = exchange(t_mm(all_normed, up_grad).astype(BF16).reshape(n, rows, ff_cols))
    down_part = t_mm(activated, down_grad_all)
    output_part = rep_sum(t_mm(attention, branch_grad).astype(BF16))
    qkv_part = rep_sum(exchange(t_mm(normed, pre_grad).astype(BF16).reshape(n, rows, q_cols + 2 * HEAD)))

    def join(blocks):
        return blocks.transpose(1, 0, 2).reshape(rows, -1).astype(F32)

    def join_heads(blocks):
        blocks = blocks.astype(F32).reshape(KV_HEADS, copies, rows, HEAD).sum(axis=1)
        return blocks.transpose(1, 0, 2).reshape(rows, KV_HEADS * HEAD)

    gain_grads = lax.psum(jnp.concatenate([attn_gain_part, ffn_gain_part]), ("rep", "shard"))
    return (
        layer_output,
        tokens_grad,
        gain_grads[0],
        join(qkv_part[:, :, :q_cols]),
        join_heads(qkv_part[:, :, q_cols : q_cols + HEAD]),
        join_heads(qkv_part[:, :, q_cols + HEAD :]),
        output_part.astype(F32),
        gain_grads[1],
        join(gate_part),
        join(up_part),
        down_part,
    )


def solution(mesh):
    both = P(("rep", "shard"), None)
    rowed = P("shard", None)
    return jax.shard_map(
        per_device_plane if (mesh.shape["rep"], mesh.shape["shard"]) == (4, 8) else per_device,
        mesh=mesh,
        in_specs=(
            both, P(), rowed, rowed, rowed, rowed, P(), rowed, rowed, rowed,
            P("rep", None), P("rep", None), both,
        ),
        out_specs=(both, both, P(), rowed, rowed, rowed, rowed, P(), rowed, rowed, rowed),
        check_vma=False,
    )
```

```python
import functools

import jax
import jax.numpy as jnp
from jax import lax
from jax.experimental import pallas as pl
from jax.experimental.pallas import tpu as pltpu
from jax.sharding import PartitionSpec as P

HEADS = 32
KV_HEADS = 8
HEAD = 64
EPSILON = 1e-05
RESIDUAL_SCALE = 0.22
SCORE_SCALE = 0.015625
ROPE_BASE = 10000000.0
MASKED = -1e30
BF16 = jnp.bfloat16
F32 = jnp.float32


def mm(a, b):
    return jnp.dot(a, b, preferred_element_type=F32)


def mm_t(a, b):
    return lax.dot_general(a, b, (((1,), (1,)), ((), ())), preferred_element_type=F32)


def t_mm(a, b):
    return lax.dot_general(a, b, (((0,), (0,)), ((), ())), preferred_element_type=F32)


def rms_scale(hidden, gain_vector):
    return (
        hidden
        * lax.rsqrt(jnp.mean(hidden * hidden, axis=-1, keepdims=True) + EPSILON)
        * gain_vector
    )


def places(packed_index, seq_lengths):
    seq_ends = jnp.cumsum(seq_lengths)
    starts = seq_ends - seq_lengths
    segment = jnp.sum((packed_index[:, None] >= seq_ends[None, :]).astype(jnp.int32), axis=1)
    chosen = segment[:, None] == jnp.arange(seq_lengths.shape[0], dtype=jnp.int32)[None, :]
    position = packed_index - jnp.sum(jnp.where(chosen, starts[None, :], 0), axis=1)
    return segment, position


def rope_tables(position, width):
    half = HEAD // 2
    frequency = ROPE_BASE ** (-(jnp.arange(half, dtype=F32) * 2.0) / (2.0 * half))
    turned = position.astype(F32)[:, None] * frequency[None, :]
    cosine, sine = jnp.cos(turned), jnp.sin(turned)
    cos_full = jnp.concatenate([cosine, cosine], axis=-1)
    sin_full = jnp.concatenate([-sine, sine], axis=-1)
    return jnp.tile(cos_full, (1, width // HEAD)), jnp.tile(sin_full, (1, width // HEAD))


def swap_halves(x):
    rows, width = x.shape
    half = HEAD // 2
    y = x.reshape(rows, width // HEAD, 2, half)
    return jnp.concatenate([y[:, :, 1:], y[:, :, :1]], axis=2).reshape(rows, width)


def rotate(x, cos_full, sin_full):
    return x * cos_full + swap_halves(x) * sin_full


def unrotate(x, cos_full, sin_full):
    return x * cos_full - swap_halves(x) * sin_full


def gather_rows(x):
    return lax.all_gather(x, "shard", axis=0, tiled=True)


def scatter_rows(x):
    return lax.psum_scatter(x, "shard", scatter_dimension=0, tiled=True)


def exchange(blocks):
    return lax.all_to_all(blocks, "shard", split_axis=0, concat_axis=0, tiled=True)


def rep_sum(x):
    count = lax.axis_size("rep")
    where = lax.axis_index("rep")
    half = count // 2
    for hop in range(half - 1):
        moved = lax.ppermute(
            x, "rep", [(hop, hop + 1), (count - 1 - hop, count - 2 - hop)]
        )
        x = (x.astype(F32) + moved.astype(F32)).astype(BF16)
    moved = lax.ppermute(x, "rep", [(half - 1, half), (half, half - 1)])
    x = (x.astype(F32) + moved.astype(F32)).astype(BF16)
    for hop in range(half - 1):
        near, far = half - 1 - hop, half + hop
        moved = lax.ppermute(x, "rep", [(near, near - 1), (far, far + 1)])
        x = jnp.where((where == near - 1) | (where == far + 1), moved, x)
    return x


MESH = pl.DeviceIdType.MESH


def flip(index, bits):
    for weight in (1, 2, 4):
        if bits & weight:
            index = index + weight - 2 * weight * lax.rem(lax.div(index, weight), 2)
    return index


def send(src, dst, sems, k, target):
    return pltpu.make_async_remote_copy(
        src_ref=src,
        dst_ref=dst,
        send_sem=sems.at[0, k],
        recv_sem=sems.at[1, k],
        device_id={"shard": target},
        device_id_type=MESH,
    )


def greet(me, masks):
    barrier = pltpu.get_barrier_semaphore()
    for mask in masks:
        pl.semaphore_signal(
            barrier, inc=1, device_id={"shard": flip(me, mask)}, device_id_type=MESH
        )
    pl.semaphore_wait(barrier, len(masks))


GATHER_SEMS = 13
BULK = (12, 2, 2)


def gather_steps(me, out, sems):
    core, px, py, diag = (flip(me, mask) for mask in (1, 2, 4, 6))
    half = out.shape[1] // 2
    low, high, whole = pl.ds(0, half), pl.ds(half, half), pl.ds(0, 2 * half)

    def move(k, block, rows, target):
        ref = out.at[block, rows]
        copy = send(ref, ref, sems, k, target)
        copy.start()
        return copy

    x_low, y_high = move(0, me, low, px), move(1, me, high, py)
    own = move(2, me, whole, core)
    x_high, y_low = move(3, me, high, px), move(4, me, low, py)
    yield
    x_low.wait_recv()
    diag_low = move(5, px, low, py)
    pieces = [own, move(6, px, low, core)]
    yield
    y_high.wait_recv()
    diag_high = move(7, py, high, px)
    pieces.append(move(8, py, high, core))
    yield
    x_high.wait_recv()
    pieces.append(move(9, px, high, core))
    yield
    y_low.wait_recv()
    pieces.append(move(10, py, low, core))
    yield
    diag_low.wait_recv()
    pieces.append(move(11, diag, low, core))
    diag_high.wait_recv()
    pieces.append(move(12, diag, high, core))
    yield
    for copy in pieces:
        copy.wait_recv()
    for copy in [x_low, y_high, x_high, y_low, diag_low, diag_high] + pieces:
        copy.wait_send()


def gather_blocks(me, out, sems):
    for unused_step in gather_steps(me, out, sems):
        pass


SCATTER_SEMS = 10


def scatter_steps(me, partial, sib_out, sib_in, acc, x_out, x_in, y_out, y_in, sems):
    core, px, py = (flip(me, mask) for mask in (1, 2, 4))
    half = acc.shape[1] // 2
    masks = (6, 2, 4, 0)
    low, high = pl.ds(0, half), pl.ds(half, half)
    copies = []

    def move(src, dst, k, target):
        copy = send(src, dst, sems, k, target)
        copy.start()
        copies.append(copy)
        return copy

    inside = []
    for i, mask in enumerate(masks):
        sib_out[i] = partial(flip(core, mask)).astype(BF16)
        inside.append(move(sib_out.at[i], sib_in.at[i], i, core))
    yield
    for i, mask in enumerate(masks):
        term = partial(flip(me, mask))
        inside[i].wait_recv()
        acc[i] = term + sib_in[i].astype(F32)
        if mask == 6:
            x_out[0] = acc[i, low].astype(BF16)
            x_diag = move(x_out.at[0], x_in.at[0], 4, px)
            y_out[0] = acc[i, high].astype(BF16)
            y_diag = move(y_out.at[0], y_in.at[0], 5, py)
        if mask == 2:
            x_out[1] = acc[i, low].astype(BF16)
            x_near = move(x_out.at[1], x_in.at[1], 6, px)
        if mask == 4:
            y_out[1] = acc[i, high].astype(BF16)
            y_near = move(y_out.at[1], y_in.at[1], 7, py)
    yield
    x_diag.wait_recv()
    y_out[2] = (acc[2, low] + x_in[0].astype(F32)).astype(BF16)
    y_last = move(y_out.at[2], y_in.at[2], 8, py)
    y_diag.wait_recv()
    x_out[2] = (acc[1, high] + y_in[0].astype(F32)).astype(BF16)
    x_last = move(x_out.at[2], x_in.at[2], 9, px)
    yield
    x_near.wait_recv()
    y_near.wait_recv()
    y_last.wait_recv()
    acc[3, low] = acc[3, low] + x_in[1].astype(F32) + y_in[2].astype(F32)
    x_last.wait_recv()
    acc[3, high] = acc[3, high] + y_in[1].astype(F32) + x_in[2].astype(F32)
    yield
    for copy in copies:
        copy.wait_send()


def scatter_blocks(me, partial, *buffers):
    for unused_step in scatter_steps(me, partial, *buffers):
        pass
    return buffers[2][3]


def scatter_scratch(rows, width):
    half = rows // 2
    return [
        pltpu.VMEM((4, rows, width), BF16),
        pltpu.VMEM((4, rows, width), BF16),
        pltpu.VMEM((4, rows, width), F32),
        pltpu.VMEM((3, half, width), BF16),
        pltpu.VMEM((3, half, width), BF16),
        pltpu.VMEM((3, half, width), BF16),
        pltpu.VMEM((3, half, width), BF16),
        pltpu.SemaphoreType.DMA((2, SCATTER_SEMS)),
    ]


VMEM = pl.BlockSpec(memory_space=pltpu.VMEM)
SMEM = pl.BlockSpec(memory_space=pltpu.SMEM)
ANY = pl.BlockSpec(memory_space=pl.ANY)


def comm_params(collective_id, mebibytes):
    return pltpu.CompilerParams(
        collective_id=collective_id, has_side_effects=True, vmem_limit_bytes=mebibytes << 20
    )


def front(
    tokens, attn_gain, query_weight, key_weight, value_weight, output_weight, ffn_gain,
    gate_weight, up_weight, down_weight, dealing, lengths, cotangent, freq, replicas,
):
    local, width = tokens.shape
    total = 8 * local
    shard_rows = query_weight.shape[0]
    q_cols = query_weight.shape[1] // 8
    ff_cols = gate_weight.shape[1] // 8
    block = 256
    others = (1, 2, 3, 4, 5, 6, 7)

    def kernel(
        tok_ref, gain_ref, wq_hbm, wk_ref, wv_ref, wo_ref, fgain_ref, wg_hbm, wu_hbm,
        wd_ref, deal_ref, len_ref, cot_ref, freq_ref,
        n_ref, q_ref, kv_ref, att_ref, qw_ref, kvw_ref, wg_out, wu_out, mid_ref, nf_ref, dg_out, ag_out, cot_out, half_out,
        kv_stage, c_all, dg_own, ag_stage,
        sib_out, sib_in, acc, x_out, x_in, y_out, y_in, scatter_sems,
        n_sems, c_sems, nf_sems, qkv_sems, bulk_sems, ring_sems, pair_sems, local_sems,
    ):
        me = lax.axis_index("shard")
        group = lax.axis_index("rep")
        core = lax.rem(me, 2)
        after = lax.rem(group + 1, replicas)
        before = lax.rem(group + replicas - 1, replicas)

        barrier = pltpu.get_barrier_semaphore()
        for mask in others:
            pl.semaphore_signal(
                barrier, inc=1, device_id={"shard": flip(me, mask)}, device_id_type=MESH
            )
        for neighbour in (after, before):
            pl.semaphore_signal(
                barrier, inc=1, device_id={"rep": neighbour}, device_id_type=MESH
            )
        c_all[me] = cot_ref[...]
        for d in range(8):
            lanes = slice(d * HEAD, (d + 1) * HEAD)
            kv_stage[d] = jnp.concatenate([wk_ref[:, lanes], wv_ref[:, lanes]], axis=1)
        pl.semaphore_wait(barrier, len(others) + 2)

        gather_c = gather_steps(me, c_all, c_sems)
        next(gather_c)
        n_ref[me] = rms_scale(tok_ref[...].astype(F32), gain_ref[...]).astype(BF16)
        weights = []
        for mask in others:
            peer = flip(me, mask)
            columns = pl.ds(pl.multiple_of(peer * q_cols, q_cols), q_cols)
            weights.append(send(wq_hbm.at[:, columns], qw_ref.at[me], qkv_sems, 2 * mask - 2, peer))
            weights.append(send(kv_stage.at[peer], kvw_ref.at[me], qkv_sems, 2 * mask - 1, peer))
        own_columns = pl.ds(pl.multiple_of(me * ff_cols, ff_cols), ff_cols)
        own_q = pl.ds(pl.multiple_of(me * q_cols, q_cols), q_cols)
        gate_slot, up_slot = ag_stage.at[:shard_rows], ag_stage.at[pl.ds(shard_rows, shard_rows)]
        kept = [
            pltpu.make_async_copy(wg_hbm.at[:, own_columns], gate_slot, local_sems.at[0]),
            pltpu.make_async_copy(wu_hbm.at[:, own_columns], up_slot, local_sems.at[1]),
            pltpu.make_async_copy(wq_hbm.at[:, own_q], qw_ref.at[me], local_sems.at[2]),
        ]
        for copy in kept:
            copy.start()
        kvw_ref[me] = kv_stage[me]

        bulk, waiting = [], []
        for source, target in ((wg_hbm, wg_out), (wu_hbm, wu_out)):
            for part in range(2):
                rows = pl.ds(part * (shard_rows // 2), shard_rows // 2)
                for mask in (2, 4, 6, 3, 5, 7, 1):
                    waiting.append((source, target, rows, mask))

        def more(count):
            for unused in range(min(count, len(waiting))):
                source, target, rows, mask = waiting.pop(0)
                peer = flip(me, mask)
                columns = pl.ds(pl.multiple_of(peer * ff_cols, ff_cols), ff_cols)
                copy = send(
                    source.at[rows, columns], target.at[me, rows], bulk_sems, len(bulk), peer
                )
                copy.start()
                bulk.append(copy)

        for unused in gather_c:
            pass
        gather_n = gather_steps(me, n_ref, n_sems)
        next(gather_n)
        for copy in weights:
            copy.start()

        def permute(first):
            def step(i, carry):
                row0 = pl.multiple_of(first + i * block, block)
                packed = row0 + lax.broadcasted_iota(jnp.int32, (block, total), 0)
                chosen = (deal_ref[...] == packed).astype(BF16)
                dealt = mm(chosen, c_all[...].reshape(total, width))
                dg_own[pl.ds(row0, block), :] = (RESIDUAL_SCALE * dealt).astype(BF16)
                return carry

            lax.fori_loop(0, total // 2 // block, step, 0)

        near = pl.multiple_of(core * (total // 2), total // 2)
        far = pl.multiple_of((1 - core) * (total // 2), total // 2)
        half = pl.ds(near, total // 2)

        opposite = lax.rem(group + 2, replicas)
        held_groups = (before, after, opposite)

        def pass_on(k):
            ref = dg_out.at[before if k == 2 else group, half]
            copy = pltpu.make_async_remote_copy(
                src_ref=ref if k == 2 else dg_own.at[half],
                dst_ref=ref,
                send_sem=ring_sems.at[0, k],
                recv_sem=ring_sems.at[1, k],
                device_id={"rep": before if k == 1 else after},
                device_id_type=MESH,
            )
            copy.start()
            return copy

        def share(k):
            ref = dg_out.at[held_groups[k], half]
            copy = send(ref, ref, pair_sems, k, flip(me, 1))
            copy.start()
            return copy

        permute(near)
        hops = [pass_on(0)]
        for unused in range(4):
            next(gather_n)
        permute(far)
        packed = me * local + lax.broadcasted_iota(jnp.int32, (local, total), 0)
        chosen = (deal_ref[...] == packed).astype(BF16)
        cot_out[...] = mm(chosen, c_all[...].reshape(total, width)).astype(BF16)
        store = pltpu.make_async_copy(dg_own, dg_out.at[group], local_sems.at[3])
        store.start()
        for unused in gather_n:
            pass
        for copy in kept:
            copy.wait()
        kept = [
            pltpu.make_async_copy(gate_slot, wg_out.at[me], local_sems.at[0]),
            pltpu.make_async_copy(up_slot, wu_out.at[me], local_sems.at[1]),
        ]
        for copy in kept:
            copy.start()
        for copy in weights:
            copy.wait_recv()
        more(BULK[0])
        def project(i, carry):
            row0 = pl.multiple_of(i * block, block)
            rows = pl.ds(row0, block)
            x = n_ref[pl.ds(i * (block // local), block // local)].reshape(block, width)
            cosine, sine = lane_rope(row0, block, freq_ref[...], len_ref)
            pre = mm(x, qw_ref[...].reshape(width, q_cols))
            for j in range(q_cols // (2 * HEAD)):
                lanes = slice(j * 2 * HEAD, (j + 1) * 2 * HEAD)
                y = pre[:, lanes]
                q_ref[rows, lanes] = (y * cosine + lane_swap(y) * sine).astype(BF16)
            cosine, sine = keys_only(cosine, sine)
            y = mm(x, kvw_ref[...].reshape(width, 2 * HEAD))
            kv_ref[rows, :] = (y * cosine + lane_swap(y) * sine).astype(BF16)
            return carry

        lax.fori_loop(0, total // block, project, 0)
        hops.append(pass_on(1))
        attend(q_cols // HEAD, block, q_ref, kv_ref, len_ref, att_ref)

        def partial(d):
            return mm(att_ref[pl.ds(pl.multiple_of(d * local, local), local), :], wo_ref[...])

        pending = {}

        def act_grad(held, first, loaded):
            rows = pl.ds(first, total // 2)
            if not loaded:
                load = pltpu.make_async_copy(
                    dg_out.at[held, rows], dg_own.at[rows], local_sems.at[3]
                )
                load.start()
                load.wait()
            slot = 0 if first is near else 1
            if slot in pending:
                pending[slot].wait()

            def step(i, carry):
                part = pl.ds(pl.multiple_of(first + i * block, block), block)
                ag_stage[part, :] = mm_t(dg_own[part, :], wd_ref[...]).astype(BF16)
                return carry

            lax.fori_loop(0, total // 2 // block, step, 0)
            pending[slot] = pltpu.make_async_copy(
                ag_stage.at[rows], ag_out.at[held, rows], local_sems.at[5 + slot]
            )
            pending[slot].start()

        hops[0].wait_recv()
        hops.append(pass_on(2))
        shares = [share(0)]
        scatter = scatter_steps(
            me, partial, sib_out, sib_in, acc, x_out, x_in, y_out, y_in, scatter_sems
        )
        next(scatter)
        more(BULK[1])
        for unused in scatter:
            pass
        branch = acc[3]
        middle = tok_ref[...].astype(F32) + RESIDUAL_SCALE * branch
        mid_ref[...] = middle
        nf_ref[me] = rms_scale(middle, fgain_ref[...]).astype(BF16)
        gather_nf = gather_steps(me, nf_ref, nf_sems)
        next(gather_nf)
        more(BULK[2])
        for unused in gather_nf:
            pass
        more(len(waiting))
        give = pltpu.make_async_copy(nf_ref.at[pl.ds(4 * core, 4)], half_out, local_sems.at[4])
        give.start()
        store.wait()
        for copy in kept:
            copy.wait()
        act_grad(group, near, True)
        act_grad(group, far, True)
        hops[0].wait_send()
        hops[1].wait_send()
        for k in range(3):
            if k > 0:
                hops[k].wait_recv()
                shares.append(share(k))
            act_grad(held_groups[k], near, False)
            shares[k].wait_recv()
            act_grad(held_groups[k], far, False)
        for copy in pending.values():
            copy.wait()
        give.wait()
        for copy in bulk:
            copy.wait_recv()
        for copy in weights + bulk + hops[2:] + shares:
            copy.wait_send()

    rows8 = jax.ShapeDtypeStruct((8, local, width), BF16)
    half_sems = pltpu.SemaphoreType.DMA
    outs = pl.pallas_call(
        kernel,
        out_shape=(
            rows8,
            jax.ShapeDtypeStruct((total, q_cols), BF16),
            jax.ShapeDtypeStruct((total, 2 * HEAD), BF16),
            jax.ShapeDtypeStruct((total, q_cols), BF16),
            jax.ShapeDtypeStruct((8, shard_rows, q_cols), BF16),
            jax.ShapeDtypeStruct((8, shard_rows, 2 * HEAD), BF16),
            jax.ShapeDtypeStruct((8, shard_rows, ff_cols), BF16),
            jax.ShapeDtypeStruct((8, shard_rows, ff_cols), BF16),
            jax.ShapeDtypeStruct((local, width), F32),
            rows8,
            jax.ShapeDtypeStruct((replicas, total, width), BF16),
            jax.ShapeDtypeStruct((replicas, total, ff_cols), BF16),
            jax.ShapeDtypeStruct((local, width), BF16),
            jax.ShapeDtypeStruct((4, local, width), BF16),
        ),
        in_specs=[VMEM, VMEM, ANY, VMEM, VMEM, VMEM, VMEM, ANY, ANY, VMEM, VMEM, SMEM, VMEM, VMEM],
        out_specs=[VMEM] * 6 + [ANY, ANY, VMEM, VMEM, ANY, ANY, VMEM, ANY],
        scratch_shapes=[
            pltpu.VMEM((8, shard_rows, 2 * HEAD), BF16),
            pltpu.VMEM((8, local, width), BF16),
            pltpu.VMEM((total, width), BF16),
            pltpu.VMEM((total, ff_cols), BF16),
        ]
        + scatter_scratch(local, width)
        + [
            half_sems((2, GATHER_SEMS)),
            half_sems((2, GATHER_SEMS)),
            half_sems((2, GATHER_SEMS)),
            half_sems((2, 14)),
            half_sems((2, 28)),
            half_sems((2, replicas)),
            half_sems((2, replicas)),
            half_sems((7,)),
        ],
        compiler_params=comm_params(0, 56),
        cost_estimate=pl.CostEstimate(
            flops=200_000_000_000, bytes_accessed=50 << 20, transcendentals=total * total
        ),
        name="front",
    )(
        tokens, attn_gain[None, :], query_weight, key_weight, value_weight, output_weight,
        ffn_gain[None, :], gate_weight, up_weight, down_weight, dealing, lengths, cotangent, freq,
    )
    normed, q, kv, attention, qw, kvw, wg, wu, middle, nf, dg, ag, cot, held = outs
    return (
        normed.reshape(total, width), q, kv, attention,
        qw.reshape(width, q_cols), kvw.reshape(width, 2 * HEAD),
        wg.reshape(width, ff_cols), wu.reshape(width, ff_cols),
        middle, nf.reshape(total, width), dg, ag, cot,
        held.reshape(total // 2, width),
    )


def norm_pull(x, gain, grad):
    scale = lax.rsqrt(jnp.mean(x * x, axis=-1, keepdims=True) + EPSILON)
    pulled = gain * grad
    rows_part = scale * pulled - x * (
        scale * scale * scale * jnp.mean(pulled * x, axis=-1, keepdims=True)
    )
    return rows_part, jnp.sum(grad * x * scale, axis=0, keepdims=True)


def pull_gather(part, middle, gain, out_grad, activated, down_weight, deal, collective_id):
    rows, width = middle.shape
    groups, total, cols = activated.shape
    block = 256

    def kernel(
        p_ref, m_ref, gain_ref, g_ref, act_hbm, wd_ref, deal_ref,
        mg_ref, gain_part, out, dealt_ref, act_ref, packed_ref, act_sem, *scratch,
    ):
        me = lax.axis_index("shard")
        *buffers, scatter_sems, sems = scratch
        load = pltpu.make_async_copy(act_hbm.at[lax.axis_index("rep")], act_ref, act_sem.at[0])
        load.start()
        greet(me, (1, 2, 4))

        def down(i, carry):
            chunk = pl.ds(pl.multiple_of(i * block, block), block)
            packed_ref[chunk, :] = (RESIDUAL_SCALE * mm(act_ref[chunk, :], wd_ref[...])).astype(BF16)
            return carry

        def deal_out(i, carry):
            chunk = pl.ds(pl.multiple_of(i * block, block), block)
            packed = lax.broadcasted_iota(jnp.int32, (block, total), 1)
            chosen = (deal_ref[chunk, :] == packed).astype(BF16)
            dealt_ref[chunk, :] = mm(chosen, packed_ref[...]).astype(BF16)
            return carry

        half = total // block // 2
        scatter = scatter_steps(
            me,
            lambda d: p_ref[pl.ds(pl.multiple_of(d * rows, rows), rows), :].astype(F32),
            *buffers,
            scatter_sems,
        )
        next(scatter)
        load.wait()
        lax.fori_loop(0, half, down, 0)
        next(scatter)
        lax.fori_loop(half, 2 * half, down, 0)
        own = pl.ds(pl.multiple_of(me * rows, rows), rows)
        packed_ref[own, :] = (packed_ref[own, :].astype(F32) + m_ref[...]).astype(BF16)
        next(scatter)
        for unused in scatter:
            pass
        rows_part, gain_row = norm_pull(m_ref[...], gain_ref[...], buffers[2][3])
        gain_part[...] = gain_row
        middle_grad = g_ref[...].astype(F32) + rows_part
        mg_ref[...] = middle_grad
        out[me] = (RESIDUAL_SCALE * middle_grad).astype(BF16)
        gather = gather_steps(me, out, sems)
        next(gather)
        lax.fori_loop(0, half, deal_out, 0)
        for unused in range(2):
            next(gather)
        lax.fori_loop(half, 2 * half, deal_out, 0)
        for unused in gather:
            pass

    return pl.pallas_call(
        kernel,
        out_shape=(
            jax.ShapeDtypeStruct((rows, width), F32),
            jax.ShapeDtypeStruct((1, width), F32),
            jax.ShapeDtypeStruct((8, rows, width), BF16),
            jax.ShapeDtypeStruct((total, width), BF16),
        ),
        in_specs=[VMEM] * 4 + [ANY] + [VMEM] * 2,
        out_specs=[VMEM] * 4,
        scratch_shapes=[
            pltpu.VMEM((total, cols), BF16),
            pltpu.VMEM((total, width), BF16),
            pltpu.SemaphoreType.DMA((1,)),
        ]
        + scatter_scratch(rows, width)
        + [pltpu.SemaphoreType.DMA((2, GATHER_SEMS))],
        compiler_params=comm_params(collective_id, 56),
        cost_estimate=pl.CostEstimate(
            flops=60_000_000_000, bytes_accessed=50 * rows * width, transcendentals=rows
        ),
        name="pull_gather",
    )(part, middle, gain[None, :], out_grad, activated, down_weight, deal)


def pull_tokens(
    part, out_part, qkv, hidden, gain, middle_grad, other_gain, near, act_grads, wg, wu, filled, replicas,
    collective_id,
):
    rows, width = middle_grad.shape
    groups, total, cols = act_grads.shape
    block = 256
    levels = [("shard", 1), ("shard", 2), ("shard", 4)]
    level = 1
    while level < replicas:
        levels.append(("rep", level))
        level *= 2
    per_half = total // 2 // block

    def kernel(
        p_ref, o_ref, h_ref, gain_ref, mg_ref, og_ref, wg_ref, wu_ref, ag_hbm,
        before_held, after_held, qkv_hbm, unused_na, unused_act, unused_gg, unused_ug,
        out, lay, gains, na_hbm, act_hbm, gg_hbm, ug_hbm, fetched, qkv_out, share_sems, qkv_sems, own_sem,
        nf_buf, ag_buf, done_buf, in_sems, out_sems, gain_in, gain_out, gain_sems, *scratch,
    ):
        me = lax.axis_index("shard")
        group = lax.axis_index("rep")
        core = lax.rem(me, 2)
        before = lax.rem(group + replicas - 1, replicas)
        after = lax.rem(group + 1, replicas)
        first, second = scratch[:8], scratch[8:]
        parts = (
            (before, before_held, core),
            (after, after_held, core),
            (before, fetched.at[0], 1 - core),
            (after, fetched.at[1], 1 - core),
        )

        def rows_of(p, r):
            return pl.ds(pl.multiple_of((parts[p][2] * per_half + r) * block, block), block)

        def loads(p, r):
            held, source, unused = parts[p]
            slot = (p % 2) * per_half + r
            return [
                pltpu.make_async_copy(
                    source.at[pl.ds(pl.multiple_of(r * block, block), block)],
                    nf_buf.at[slot],
                    in_sems.at[0, slot],
                ),
                pltpu.make_async_copy(ag_hbm.at[held, rows_of(p, r)], ag_buf.at[slot], in_sems.at[1, slot]),
            ]

        def stores(p, r):
            held = parts[p][0]
            slot = (p % 2) * per_half + r
            where = rows_of(p, r)
            return [
                pltpu.make_async_copy(nf_buf.at[slot], na_hbm.at[held, where], out_sems.at[0, slot])
            ] + [
                pltpu.make_async_copy(done_buf.at[k, slot], target.at[held, where], out_sems.at[k + 1, slot])
                for k, target in enumerate((act_hbm, gg_hbm, ug_hbm))
            ]

        def start_loads(p):
            for r in range(per_half):
                for copy in loads(p, r):
                    copy.start()

        def wait_stores(p):
            for r in range(per_half):
                for copy in stores(p, r):
                    copy.wait()

        def fill(p):
            if p > 0:
                wait_stores(p - 1)
            if p in (1, 2):
                shares[p - 1].wait_recv()
            if p + 1 < len(parts):
                start_loads(p + 1)

            def step(r, carry):
                slot = (p % 2) * per_half + r
                for copy in loads(p, r):
                    copy.wait()
                results = ffn_rows(nf_buf[slot], ag_buf[slot], wg_ref[...], wu_ref[...])
                for k, result in enumerate(results):
                    done_buf[k, slot] = result
                for copy in stores(p, r):
                    copy.start()
                return carry

            lax.fori_loop(0, per_half, step, 0)

        start_loads(0)
        barrier = pltpu.get_barrier_semaphore()
        peers = []
        for axis, weight in levels:
            index = me if axis == "shard" else group
            peers.append({axis: index + weight - 2 * weight * lax.rem(lax.div(index, weight), 2)})
        far = [{"shard": flip(me, mask)} for mask in (3, 5, 6, 7)]
        for peer in peers + far:
            pl.semaphore_signal(barrier, inc=1, device_id=peer, device_id_type=MESH)
        pl.semaphore_wait(barrier, len(peers) + len(far))

        def blocks_of(ref):
            return lambda d: ref[pl.ds(pl.multiple_of(d * rows, rows), rows), :].astype(F32)

        grads = scatter_steps(me, blocks_of(p_ref), *first)
        outputs = scatter_steps(me, blocks_of(o_ref), *second)
        next(grads)
        next(outputs)
        shares = [
            send(source, fetched.at[k], share_sems, k, flip(me, 1))
            for k, source in enumerate((before_held, after_held))
        ]
        for copy in shares:
            copy.start()
        exchange_qkv = []
        for mask in range(1, 8):
            peer = flip(me, mask)
            exchange_qkv.append(send(qkv_hbm.at[peer], qkv_out.at[me], qkv_sems, mask - 1, peer))
        own_qkv = pltpu.make_async_copy(qkv_hbm.at[me], qkv_out.at[me], own_sem.at[0])
        fill(0)
        next(grads)
        for copy in exchange_qkv + [own_qkv]:
            copy.start()
        fill(1)
        next(grads)
        next(outputs)
        fill(2)
        next(grads)
        next(outputs)
        rows_part, gain_row = norm_pull(h_ref[...].astype(F32), gain_ref[...], first[2][3])
        out[...] = mg_ref[...] + rows_part
        sums = jnp.concatenate([gain_row, og_ref[...]], axis=0)
        for i, peer in enumerate(peers):
            gain_out[i] = sums
            copy = pltpu.make_async_remote_copy(
                src_ref=gain_out.at[i],
                dst_ref=gain_in.at[i],
                send_sem=gain_sems.at[0, i],
                recv_sem=gain_sems.at[1, i],
                device_id=peer,
                device_id_type=MESH,
            )
            copy.start()
            if i == 0:
                fill(3)
            copy.wait()
            sums = sums + gain_in[i]
        gains[...] = sums
        next(outputs)
        lay[...] = second[2][3].astype(BF16)
        for steps in (grads, outputs):
            for unused in steps:
                pass
        wait_stores(3)
        own_qkv.wait()
        for copy in exchange_qkv:
            copy.wait_recv()
        for copy in shares + exchange_qkv:
            copy.wait_send()

    hidden_shape = jax.ShapeDtypeStruct((groups, total, cols), BF16)
    return pl.pallas_call(
        kernel,
        out_shape=(
            jax.ShapeDtypeStruct((rows, width), F32),
            jax.ShapeDtypeStruct((rows, width), BF16),
            jax.ShapeDtypeStruct((2, width), F32),
            jax.ShapeDtypeStruct((groups, total, width), BF16),
            hidden_shape,
            hidden_shape,
            hidden_shape,
            jax.ShapeDtypeStruct((2, total // 2, width), BF16),
            jax.ShapeDtypeStruct(qkv.shape, BF16),
        ),
        in_specs=[VMEM] * 8 + [ANY] * 8,
        out_specs=[VMEM] * 3 + [ANY] * 6,
        input_output_aliases={12: 3, 13: 4, 14: 5, 15: 6},
        scratch_shapes=[
            pltpu.SemaphoreType.DMA((2, 2)),
            pltpu.SemaphoreType.DMA((2, 7)),
            pltpu.SemaphoreType.DMA((1,)),
            pltpu.VMEM((2 * per_half, block, width), BF16),
            pltpu.VMEM((2 * per_half, block, cols), BF16),
            pltpu.VMEM((3, 2 * per_half, block, cols), BF16),
            pltpu.SemaphoreType.DMA((2, 2 * per_half)),
            pltpu.SemaphoreType.DMA((4, 2 * per_half)),
            pltpu.VMEM((len(levels), 2, width), F32),
            pltpu.VMEM((len(levels), 2, width), F32),
            pltpu.SemaphoreType.DMA((2, len(levels))),
        ]
        + scatter_scratch(rows, width)
        + scatter_scratch(rows, width),
        compiler_params=comm_params(collective_id, 62),
        cost_estimate=pl.CostEstimate(
            flops=60_000_000_000, bytes_accessed=50 * rows * width, transcendentals=rows
        ),
        name="pull_tokens",
    )(
        part, out_part, hidden, gain[None, :], middle_grad, other_gain, wg, wu, act_grads, *near, qkv, *filled
    )


def softmax_block(q, k, allowed):
    scores = SCORE_SCALE * mm_t(q, k)
    scores = jnp.where(allowed, scores, MASKED)
    top = jnp.max(scores, axis=-1, keepdims=True)
    weight = jnp.exp(scores - top)
    return weight * (1.0 / jnp.sum(weight, axis=-1, keepdims=True))


def allowed_block(row0, cols, start):
    shape = (start.shape[0], cols)
    query = row0 + lax.broadcasted_iota(jnp.int32, shape, 0)
    key = lax.broadcasted_iota(jnp.int32, shape, 1)
    return (key >= start) & (key <= query)


def sequence_starts(row0, shape, lengths_ref):
    row = row0 + lax.broadcasted_iota(jnp.int32, shape, 0)
    start = jnp.zeros(shape, jnp.int32)
    end = 0
    for i in range(lengths_ref.shape[1]):
        length = lengths_ref[0, i]
        end = end + length
        start = start + jnp.where(row >= end, length, 0)
    return start


def attend(heads, block, q_ref, kv_ref, lengths_ref, o_ref):
    total = kv_ref.shape[0]
    for i in range(total // block):
        cols = (i + 1) * block
        rows = pl.ds(i * block, block)
        allowed = allowed_block(
            i * block, cols, sequence_starts(i * block, (block, 1), lengths_ref)
        )
        kv = kv_ref[:cols, :]
        k, v = kv[:, :HEAD], kv[:, HEAD:]
        for h in range(heads):
            lanes = slice(h * HEAD, (h + 1) * HEAD)
            probs = softmax_block(q_ref[rows, lanes], k, allowed)
            o_ref[rows, lanes] = mm(probs.astype(BF16), v).astype(BF16)


def attend_back(heads, block, q_ref, kv_ref, g_ref, lengths_ref, dq_ref, dk_ref, dv_ref):
    total = kv_ref.shape[0]
    dk_ref[...] = jnp.zeros_like(dk_ref)
    dv_ref[...] = jnp.zeros_like(dv_ref)
    for i in range(total // block):
        cols = (i + 1) * block
        rows = pl.ds(i * block, block)
        allowed = allowed_block(
            i * block, cols, sequence_starts(i * block, (block, 1), lengths_ref)
        )
        kv = kv_ref[:cols, :]
        k, v = kv[:, :HEAD], kv[:, HEAD:]
        for h in range(heads):
            lanes = slice(h * HEAD, (h + 1) * HEAD)
            q, g = q_ref[rows, lanes], g_ref[rows, lanes]
            probs = softmax_block(q, k, allowed)
            probs_grad = mm_t(g, v)
            delta = jnp.sum(probs * probs_grad, axis=-1, keepdims=True)
            score_grad = (probs * (probs_grad - delta)).astype(BF16)
            dq_ref[rows, lanes] = SCORE_SCALE * mm(score_grad, k)
            dk_ref[:cols, :] += SCORE_SCALE * t_mm(score_grad, q)
            dv_ref[:cols, :] += t_mm(probs.astype(BF16), g)


def attention_forward(q, kv, lengths):
    total, width = q.shape

    def kernel(q_ref, kv_ref, lengths_ref, o_ref):
        attend(width // HEAD, 256, q_ref, kv_ref, lengths_ref, o_ref)

    return pl.pallas_call(
        kernel,
        out_shape=jax.ShapeDtypeStruct((total, width), BF16),
        in_specs=[VMEM, VMEM, SMEM],
        out_specs=VMEM,
        compiler_params=pltpu.CompilerParams(vmem_limit_bytes=40 << 20),
        name="attention_forward",
    )(q, kv, lengths)


def attention_gradients(q, kv, grad, lengths):
    total, width = q.shape

    def kernel(q_ref, kv_ref, g_ref, lengths_ref, dq_ref, dk_ref, dv_ref):
        attend_back(width // HEAD, 256, q_ref, kv_ref, g_ref, lengths_ref, dq_ref, dk_ref, dv_ref)

    return pl.pallas_call(
        kernel,
        out_shape=(
            jax.ShapeDtypeStruct((total, width), F32),
            jax.ShapeDtypeStruct((total, HEAD), F32),
            jax.ShapeDtypeStruct((total, HEAD), F32),
        ),
        in_specs=[VMEM, VMEM, VMEM, SMEM],
        out_specs=[VMEM] * 3,
        compiler_params=pltpu.CompilerParams(vmem_limit_bytes=40 << 20),
        name="attention_gradients",
    )(q, kv, grad, lengths)


def lane_rope(row0, rows, freq, lengths_ref):
    shape = (rows, 2 * HEAD)
    row = row0 + lax.broadcasted_iota(jnp.int32, shape, 0)
    position = row - sequence_starts(row0, shape, lengths_ref)
    turned = position.astype(F32) * freq
    lane = lax.broadcasted_iota(jnp.int32, shape, 1)
    first = lax.rem(lane, HEAD) < HEAD // 2
    sine = jnp.sin(turned)
    return jnp.cos(turned), jnp.where(first, -sine, sine)


def lane_swap(x):
    half = HEAD // 2
    lane = lax.broadcasted_iota(jnp.int32, x.shape, 1)
    first = lax.rem(lane, HEAD) < half
    return jnp.where(first, pltpu.roll(x, 2 * HEAD - half, 1), pltpu.roll(x, half, 1))


def keys_only(cosine, sine):
    lane = lax.broadcasted_iota(jnp.int32, cosine.shape, 1)
    return jnp.where(lane < HEAD, cosine, 1.0), jnp.where(lane < HEAD, sine, 0.0)


def attention_backward(
    branch_grad, output_weight, attention, q, kv, normed, q_weight, kv_weight, lengths, freq
):
    total, q_cols = q.shape
    width = normed.shape[1]
    block = 256

    def kernel(
        bg_ref, wo_ref, a_ref, q_ref, kv_ref, n_ref, qw_ref, kvw_ref, len_ref, freq_ref,
        dn_ref, dqkv_ref, dwo_ref, g_ref, dq_ref, dk_ref, dv_ref, pq_ref, pkv_ref,
    ):
        def open_up(i, carry):
            rows = pl.ds(pl.multiple_of(i * block, block), block)
            g_ref[rows, :] = mm_t(bg_ref[rows, :], wo_ref[...]).astype(BF16)
            return carry

        lax.fori_loop(0, total // block, open_up, 0)
        attend_back(
            q_cols // HEAD, block, q_ref, kv_ref, g_ref, len_ref, dq_ref, dk_ref, dv_ref
        )
        def close_up(i, carry):
            row0 = pl.multiple_of(i * block, block)
            rows = pl.ds(row0, block)
            cosine, sine = lane_rope(row0, block, freq_ref[...], len_ref)
            for j in range(q_cols // (2 * HEAD)):
                lanes = slice(j * 2 * HEAD, (j + 1) * 2 * HEAD)
                x = dq_ref[rows, lanes]
                pq_ref[rows, lanes] = (x * cosine - lane_swap(x) * sine).astype(BF16)
            cosine, sine = keys_only(cosine, sine)
            x = jnp.concatenate([dk_ref[rows, :], dv_ref[rows, :]], axis=1)
            pkv_ref[rows, :] = (x * cosine - lane_swap(x) * sine).astype(BF16)
            dn_ref[rows, :] = (
                mm_t(pq_ref[rows, :], qw_ref[...]) + mm_t(pkv_ref[rows, :], kvw_ref[...])
            ).astype(BF16)
            return carry

        lax.fori_loop(0, total // block, close_up, 0)

        for i in range(width // 512):
            cols = slice(i * 512, (i + 1) * 512)
            dqkv_ref[cols, :q_cols] = t_mm(n_ref[:, cols], pq_ref[...]).astype(BF16)
            dqkv_ref[cols, q_cols:] = t_mm(n_ref[:, cols], pkv_ref[...]).astype(BF16)
            dwo_ref[:, cols] = t_mm(a_ref[...], bg_ref[:, cols]).astype(BF16)

    return pl.pallas_call(
        kernel,
        out_shape=(
            jax.ShapeDtypeStruct((total, width), BF16),
            jax.ShapeDtypeStruct((width, q_cols + 2 * HEAD), BF16),
            jax.ShapeDtypeStruct((q_cols, width), BF16),
        ),
        in_specs=[VMEM] * 8 + [SMEM, VMEM],
        out_specs=[VMEM] * 3,
        scratch_shapes=[
            pltpu.VMEM((total, q_cols), BF16),
            pltpu.VMEM((total, q_cols), F32),
            pltpu.VMEM((total, HEAD), F32),
            pltpu.VMEM((total, HEAD), F32),
            pltpu.VMEM((total, q_cols), BF16),
            pltpu.VMEM((total, 2 * HEAD), BF16),
        ],
        compiler_params=pltpu.CompilerParams(vmem_limit_bytes=56 << 20),
        cost_estimate=pl.CostEstimate(flops=30_000_000_000, bytes_accessed=30 << 20, transcendentals=total * total),
        name="attention_backward",
    )(branch_grad, output_weight, attention, q, kv, normed, q_weight, kv_weight, lengths, freq)


def ffn_rows(nf, act_grad, wg, wu):
    gate, up = mm(nf, wg), mm(nf, wu)
    act_grad = act_grad.astype(F32)
    sigmoid = 1.0 / (1.0 + jnp.exp(-gate))
    silu = gate * sigmoid
    activated = (silu * up).astype(BF16)
    gate_grad = (act_grad * up * sigmoid * (1.0 + gate * (1.0 - sigmoid))).astype(BF16)
    return activated, gate_grad, (act_grad * silu).astype(BF16)


def ffn_own(group, nf, act_grads, wg, wu):
    groups, total, cols = act_grads.shape
    width = nf.shape[1]
    block = 256

    def kernel(g_ref, nf_ref, ag_ref, wg_ref, wu_ref, na_ref, act_ref, gg_ref, ug_ref, dn_ref):
        nf = nf_ref[...]
        act, gg, ug = ffn_rows(nf, ag_ref[0], wg_ref[...], wu_ref[...])
        na_ref[0], act_ref[0], gg_ref[0], ug_ref[0] = nf, act, gg, ug
        dn_ref[...] = (mm_t(gg, wg_ref[...]) + mm_t(ug, wu_ref[...])).astype(BF16)

    mine = pl.BlockSpec((1, block, width), lambda i, g: (g[0], i, 0))
    hid = pl.BlockSpec((1, block, cols), lambda i, g: (g[0], i, 0))
    plain = pl.BlockSpec((block, width), lambda i, g: (i, 0))
    whole = [
        pl.BlockSpec(w.shape, lambda i, g: (0, 0), pipeline_mode=pl.Buffered(1)) for w in (wg, wu)
    ]
    hidden = jax.ShapeDtypeStruct((groups, total, cols), BF16)
    return pl.pallas_call(
        kernel,
        grid_spec=pltpu.PrefetchScalarGridSpec(
            num_scalar_prefetch=1,
            grid=(total // block,),
            in_specs=[plain, hid] + whole,
            out_specs=[mine, hid, hid, hid, plain],
        ),
        out_shape=(
            jax.ShapeDtypeStruct((groups, total, width), BF16),
            hidden,
            hidden,
            hidden,
            jax.ShapeDtypeStruct((total, width), BF16),
        ),
        compiler_params=pltpu.CompilerParams(vmem_limit_bytes=62 << 20),
        cost_estimate=pl.CostEstimate(
            flops=12 * total * width * cols, bytes_accessed=40 << 20, transcendentals=total * cols
        ),
        name="ffn_own",
    )(group, nf, act_grads, wg, wu)


def ffn_other(where, held, fetched, act_grads, wg, wu, filled):
    groups, total, cols = act_grads.shape
    width = held.shape[1]
    block = 256
    per_half = total // 2 // block

    def kernel(w_ref, held_ref, fetched_ref, ag_ref, wg_ref, wu_ref, *rest):
        na_ref, act_ref, gg_ref, ug_ref, nf_ref = rest[4:]
        i = pl.program_id(0)

        @pl.when(i < per_half)
        def _():
            nf_ref[...] = held_ref[...]

        @pl.when(i >= per_half)
        def _():
            nf_ref[...] = fetched_ref[...]

        nf = nf_ref[...]
        act, gg, ug = ffn_rows(nf, ag_ref[0], wg_ref[...], wu_ref[...])
        na_ref[0], act_ref[0], gg_ref[0], ug_ref[0] = nf, act, gg, ug

    def row(i, w):
        half = jnp.where(i < per_half, w[1], 1 - w[1])
        return half * per_half + lax.rem(i, per_half)

    mine = pl.BlockSpec((1, block, width), lambda i, w: (w[0], row(i, w), 0))
    hid = pl.BlockSpec((1, block, cols), lambda i, w: (w[0], row(i, w), 0))
    first = pl.BlockSpec((block, width), lambda i, w: (jnp.minimum(i, per_half - 1), 0))
    last = pl.BlockSpec((block, width), lambda i, w: (jnp.maximum(i - per_half, 0), 0))
    whole = [
        pl.BlockSpec(w.shape, lambda i, g: (0, 0), pipeline_mode=pl.Buffered(1)) for w in (wg, wu)
    ]
    hidden = jax.ShapeDtypeStruct((groups, total, cols), BF16)
    return pl.pallas_call(
        kernel,
        grid_spec=pltpu.PrefetchScalarGridSpec(
            num_scalar_prefetch=1,
            grid=(2 * per_half,),
            in_specs=[first, last, hid] + whole + [pl.BlockSpec(memory_space=pl.ANY)] * 4,
            out_specs=[mine, hid, hid, hid],
            scratch_shapes=[pltpu.VMEM((block, width), BF16)],
        ),
        out_shape=(jax.ShapeDtypeStruct((groups, total, width), BF16), hidden, hidden, hidden),
        input_output_aliases={6: 0, 7: 1, 8: 2, 9: 3},
        compiler_params=pltpu.CompilerParams(vmem_limit_bytes=62 << 20),
        cost_estimate=pl.CostEstimate(
            flops=8 * total * width * cols, bytes_accessed=40 << 20, transcendentals=total * cols
        ),
        name="ffn_other",
    )(where, held, fetched, act_grads, wg, wu, *filled)


def finish(normed, gate_grad, up_grad, activated, down_grad, output_part, qkv_part, collective_id):
    depth, width = normed.shape
    cols = gate_grad.shape[1]
    rows = width // 8
    tall = cols // rows
    steps = 8 + tall
    chunks = 4
    sums = (output_part, qkv_part)

    def kernel(
        nf_hbm, gg_hbm, ug_hbm, act_hbm, dg_hbm, o_in, qkv_in,
        gate_out, up_out, down_out, o_out, qkv_out,
        gg, ug, dg, left, stage, tall_stage, o_mid, qkv_mid, o_last, qkv_last,
        load_sems, left_sems, own_sems, tall_sems, push_sems, relay_sems,
    ):
        me = lax.axis_index("shard")
        group = lax.axis_index("rep")
        inner = (group == 1) | (group == 2)
        outer = (group == 0) | (group == 3)
        beside = group + 1 - 2 * lax.rem(group, 2)
        across = 3 - group

        def peer_of(i):
            mask = 7 - i
            index = 0
            for weight in (1, 2, 4):
                bits = lax.rem(lax.div(me, weight), 2) + lax.rem(lax.div(mask, weight), 2)
                index = index + weight * lax.rem(bits, 2)
            return index

        def start_left(i, slot):
            @pl.when(i < 8)
            def _():
                first = pl.multiple_of(peer_of(i) * rows, rows)
                pltpu.make_async_copy(
                    nf_hbm.at[:, pl.ds(first, rows)], left.at[slot], left_sems.at[slot]
                ).start()

            @pl.when((i >= 8) & (i < steps))
            def _():
                first = pl.multiple_of((i - 8) * rows, rows)
                pltpu.make_async_copy(
                    act_hbm.at[:, pl.ds(first, rows)], left.at[slot], left_sems.at[slot]
                ).start()

        def wait_left(slot):
            pltpu.make_async_copy(
                nf_hbm.at[:, pl.ds(0, rows)], left.at[slot], left_sems.at[slot]
            ).wait()

        loads = [
            pltpu.make_async_copy(source, target, load_sems.at[k])
            for k, (source, target) in enumerate(((gg_hbm, gg), (ug_hbm, ug), (dg_hbm, dg)))
        ]
        start_left(0, 0)
        for load in loads:
            load.start()
        barrier = pltpu.get_barrier_semaphore()
        for mask in range(1, 8):
            pl.semaphore_signal(
                barrier, inc=1, device_id={"shard": flip(me, mask)}, device_id_type=MESH
            )
        for neighbour in (beside, across):
            pl.semaphore_signal(
                barrier, inc=1, device_id={"rep": neighbour}, device_id_type=MESH
            )
        pl.semaphore_wait(barrier, 9)

        arrays = ((o_in, o_mid, o_last, o_out), (qkv_in, qkv_mid, qkv_last, qkv_out))

        def relay_copy(stage_index, k, c, target):
            start, mid, last, out = arrays[k]
            size = start.shape[0] // chunks
            part = pl.ds(pl.multiple_of(c * size, size), size)
            source, arrived = ((start, mid), (mid, last), (out, out))[stage_index]
            return pltpu.make_async_remote_copy(
                src_ref=source.at[part],
                dst_ref=arrived.at[part],
                send_sem=relay_sems.at[0, stage_index, k * chunks + c],
                recv_sem=relay_sems.at[1, stage_index, k * chunks + c],
                device_id={"rep": target},
                device_id_type=MESH,
            )

        @pl.when(outer)
        def _():
            for c in range(chunks):
                for k in range(2):
                    relay_copy(0, k, c, beside).start()

        def relay(t):
            def part_of(k, c):
                size = arrays[k][0].shape[0] // chunks
                return pl.ds(pl.multiple_of(c * size, size), size)

            @pl.when(inner & (t < chunks))
            def _():
                for k in range(2):
                    start, mid, last, out = arrays[k]
                    part = part_of(k, t)
                    relay_copy(0, k, t, beside).wait_recv()
                    mid[part, :] = (start[part, :].astype(F32) + mid[part, :].astype(F32)).astype(BF16)
                    relay_copy(1, k, t, across).start()

            @pl.when(inner & (t >= 1) & (t <= chunks))
            def _():
                for k in range(2):
                    start, mid, last, out = arrays[k]
                    part = part_of(k, t - 1)
                    relay_copy(1, k, t - 1, across).wait_recv()
                    out[part, :] = (mid[part, :].astype(F32) + last[part, :].astype(F32)).astype(BF16)
                    relay_copy(2, k, t - 1, beside).start()

            @pl.when(outer & (t >= 2) & (t <= chunks + 1))
            def _():
                for k in range(2):
                    relay_copy(2, k, t - 2, beside).wait_recv()

        outputs = (gate_out, up_out)
        own_columns = pl.ds(pl.multiple_of(me * cols, cols), cols)

        def push(i, j, target):
            return send(
                stage.at[i, j], outputs[j].at[:, own_columns], push_sems, 2 * i + j, target
            )

        def wide(i, carry):
            slot = lax.rem(i, 2)
            start_left(i + 1, 1 - slot)
            wait_left(slot)
            for j, right in enumerate((gg, ug)):

                @pl.when(i == 0)
                def _():
                    loads[j].wait()

                stage[i, j] = t_mm(left[slot], right[...]).astype(BF16)

                @pl.when(i < 7)
                def _():
                    push(i, j, peer_of(i)).start()

                @pl.when(i == 7)
                def _():
                    pltpu.make_async_copy(
                        stage.at[7, j], outputs[j].at[:, own_columns], own_sems.at[j]
                    ).start()

            @pl.when(lax.rem(i, 2) == 1)
            def _():
                relay(lax.div(i, 2))

            return carry

        lax.fori_loop(0, 8, wide, 0)
        loads[2].wait()

        def tall_copy(i):
            slot = lax.rem(i, 2)
            first = pl.multiple_of((i - 8) * rows, rows)
            return pltpu.make_async_copy(
                tall_stage.at[slot], down_out.at[pl.ds(first, rows), :], tall_sems.at[slot]
            )

        def high(i, carry):
            slot = lax.rem(i, 2)
            start_left(i + 1, 1 - slot)
            wait_left(slot)

            @pl.when(i >= 10)
            def _():
                tall_copy(i - 2).wait()

            tall_stage[slot] = t_mm(left[slot], dg[...]).astype(BF16)
            tall_copy(i).start()

            @pl.when(lax.rem(i, 2) == 1)
            def _():
                relay(lax.div(i, 2))

            return carry

        lax.fori_loop(8, steps, high, 0)
        for i in (steps - 2, steps - 1):
            tall_copy(i).wait()
        for j in range(2):
            pltpu.make_async_copy(
                stage.at[7, j], outputs[j].at[:, own_columns], own_sems.at[j]
            ).wait()
        for t in range(steps // 2, chunks + 2):
            relay(t)

        def drain(i, carry):
            for j in range(2):
                push(i, j, peer_of(i)).wait()
            return carry

        lax.fori_loop(0, 7, drain, 0)

        @pl.when(outer)
        def _():
            for c in range(chunks):
                for k in range(2):
                    relay_copy(0, k, c, beside).wait_send()

        @pl.when(inner)
        def _():
            for c in range(chunks):
                for k in range(2):
                    relay_copy(1, k, c, across).wait_send()
                    relay_copy(2, k, c, beside).wait_send()

    exchanged = jax.ShapeDtypeStruct((rows, 8 * cols), BF16)
    return pl.pallas_call(
        kernel,
        out_shape=(
            exchanged,
            exchanged,
            jax.ShapeDtypeStruct((cols, width), BF16),
            jax.ShapeDtypeStruct(output_part.shape, BF16),
            jax.ShapeDtypeStruct(qkv_part.shape, BF16),
        ),
        in_specs=[ANY] * 5 + [VMEM] * 2,
        out_specs=[ANY] * 3 + [VMEM] * 2,
        scratch_shapes=[
            pltpu.VMEM((depth, cols), BF16),
            pltpu.VMEM((depth, cols), BF16),
            pltpu.VMEM((depth, width), BF16),
            pltpu.VMEM((2, depth, rows), BF16),
            pltpu.VMEM((8, 2, rows, cols), BF16),
            pltpu.VMEM((2, rows, width), BF16),
        ]
        + [pltpu.VMEM(x.shape, BF16) for unused in range(2) for x in sums]
        + [
            pltpu.SemaphoreType.DMA((3,)),
            pltpu.SemaphoreType.DMA((2,)),
            pltpu.SemaphoreType.DMA((2,)),
            pltpu.SemaphoreType.DMA((2,)),
            pltpu.SemaphoreType.DMA((2, 14)),
            pltpu.SemaphoreType.DMA((2, 3, 2 * chunks)),
        ],
        compiler_params=comm_params(collective_id, 62),
        cost_estimate=pl.CostEstimate(
            flops=120_000_000_000, bytes_accessed=80 << 20, transcendentals=0
        ),
        name="finish",
    )(normed, gate_grad, up_grad, activated, down_grad, output_part, qkv_part)


def widen(gate, up, down, out, heads, q_cols):
    rows, wide = gate.shape
    tall, width = down.shape
    n = heads.shape[0]
    steps = 16
    block, high = rows // steps, tall // steps

    def kernel(g_ref, u_ref, d_ref, o_ref, h_ref, g_out, u_out, d_out, o_out, q_out, k_out, v_out):
        g_out[...] = g_ref[...].astype(F32)
        u_out[...] = u_ref[...].astype(F32)
        d_out[...] = d_ref[...].astype(F32)
        o_out[...] = o_ref[...].astype(F32)
        for i in range(n):
            q_out[:, i * q_cols : (i + 1) * q_cols] = h_ref[i, :, :q_cols].astype(F32)
        kv = [h_ref[i, :, q_cols:].astype(F32) for i in range(n)]
        k_out[...] = jnp.concatenate([x[:, :HEAD] for x in kv], axis=1)
        v_out[...] = jnp.concatenate([x[:, HEAD:] for x in kv], axis=1)

    def spec(height, across):
        return pl.BlockSpec((height, across), lambda i: (i, 0))

    shapes = [(rows, wide), (rows, wide), (tall, width), (rows, width)]
    blocks = [spec(block, wide), spec(block, wide), spec(high, width), spec(block, width)]
    narrow = [n * q_cols, n * HEAD, n * HEAD]
    return pl.pallas_call(
        kernel,
        grid=(steps,),
        in_specs=blocks + [pl.BlockSpec((n, block, heads.shape[2]), lambda i: (0, i, 0))],
        out_specs=blocks + [spec(block, across) for across in narrow],
        out_shape=[jax.ShapeDtypeStruct(shape, F32) for shape in shapes]
        + [jax.ShapeDtypeStruct((rows, across), F32) for across in narrow],
        compiler_params=pltpu.CompilerParams(vmem_limit_bytes=62 << 20),
        cost_estimate=pl.CostEstimate(
            flops=4 * rows * wide, bytes_accessed=20 * rows * wide, transcendentals=0
        ),
        name="widen",
    )(gate, up, down, out, heads)


def per_device_plane(
    tokens, attn_gain, query_weight, key_weight, value_weight, output_weight, ffn_gain,
    gate_weight, up_weight, down_weight, dealing, lengths, cotangent,
):
    n = 8
    here = lax.axis_index("shard")
    group = lax.axis_index("rep")
    replicas = lax.axis_size("rep")
    local, width = tokens.shape
    total = local * n
    rows = query_weight.shape[0]
    q_cols = query_weight.shape[1] // n
    ff_cols = gate_weight.shape[1] // n
    core = lax.rem(here, 2)
    half = HEAD // 2
    freq = ROPE_BASE ** (-(jnp.arange(half, dtype=F32) * 2.0) / (2.0 * half))
    freq = jnp.tile(freq, 4)[None, :]

    (
        normed, q, kv, attention, q_weight, kv_weight, gate_cols, up_cols,
        middle, normed_ffn, down_grads, act_grads, cot_own, held,
    ) = front(
        tokens, attn_gain, query_weight, key_weight, value_weight, output_weight, ffn_gain,
        gate_weight, up_weight, down_weight, dealing, lengths, cotangent, freq, replicas,
    )

    def shift(x, by):
        return lax.ppermute(x, "rep", [(i, (i + by) % replicas) for i in range(replicas)])

    def fetch(x):
        return lax.ppermute(x, "shard", [(i, i ^ 1) for i in range(n)])

    before, after = shift(held, 1), shift(held, replicas - 1)
    *filled, normed_ffn_part = ffn_own(
        group.astype(jnp.int32)[None], normed_ffn, act_grads, gate_cols, up_cols
    )
    middle_grad, ffn_gain_part, branch_grad, output_part = pull_gather(
        normed_ffn_part, middle, ffn_gain, cot_own, filled[1], down_weight, dealing.reshape(total, 1), 2
    )
    normed_part, qkv_grad, output_grad = attention_backward(
        branch_grad.reshape(total, width), output_weight, attention, q, kv, normed, q_weight, kv_weight,
        lengths, freq,
    )
    before, after, unused_part = lax.optimization_barrier((before, after, normed_part))
    opposite = shift(before, 1)
    tokens_grad, layer_output, gains, *filled, unused_half, qkv_part = pull_tokens(
        normed_part, output_part, qkv_grad.reshape(n, rows, q_cols + 2 * HEAD), tokens, attn_gain, middle_grad, ffn_gain_part,
        (before, after), act_grads, gate_cols, up_cols, filled, replicas, 3,
    )
    opposite, unused_rows = lax.optimization_barrier((opposite, tokens_grad))
    where = jnp.stack([lax.rem(group + replicas - 2, replicas), core]).astype(jnp.int32)
    filled = ffn_other(where, opposite, fetch(opposite), act_grads, gate_cols, up_cols, filled)
    left, *rights = [x.reshape(replicas * total, -1) for x in (filled[0], filled[2], filled[3])]
    gate_grad, up_grad, down_grad, output_grad, qkv_grad = finish(
        left, *rights, filled[1].reshape(replicas * total, -1), down_grads.reshape(replicas * total, -1),
        output_grad, qkv_part.reshape(width, -1), 4,
    )
    gate_grad, up_grad, down_grad, output_grad, q_grad, k_grad, v_grad = widen(
        gate_grad, up_grad, down_grad, output_grad, qkv_grad.reshape(n, rows, -1), q_cols
    )
    return (
        layer_output, tokens_grad, gains[0], q_grad, k_grad, v_grad, output_grad, gains[1],
        gate_grad, up_grad, down_grad,
    )


def per_device(
    tokens,
    attn_gain,
    query_weight,
    key_weight,
    value_weight,
    output_weight,
    ffn_gain,
    gate_weight,
    up_weight,
    down_weight,
    dealing,
    lengths,
    cotangent,
):
    n = lax.axis_size("shard")
    here = lax.axis_index("shard")
    local, width = tokens.shape
    total = local * n
    rows = query_weight.shape[0]
    ff_cols = gate_weight.shape[1] // n
    q_cols = query_weight.shape[1] // n
    copies = n // KV_HEADS
    own = here * local

    packed = jnp.arange(total, dtype=jnp.int32)
    segment, position = places(packed, lengths[0])
    cos_q, sin_q = rope_tables(position, q_cols)
    cos_k, sin_k = cos_q[:, :HEAD], sin_q[:, :HEAD]
    dealt = (dealing[0][:, None] == packed[None, :]).astype(BF16)

    def column_blocks(weight, cols):
        return weight.reshape(rows, n, cols).transpose(1, 0, 2)

    def head_blocks(weight):
        blocks = weight.reshape(rows, KV_HEADS, HEAD).transpose(1, 0, 2)
        return jnp.repeat(blocks, copies, axis=0)

    spread_cotangent = lax.all_gather(cotangent, ("rep", "shard"), axis=0, tiled=True)
    all_dealing = lax.all_gather(dealing, "rep", axis=0, tiled=True)
    qkv = exchange(
        jnp.concatenate(
            [column_blocks(query_weight, q_cols), head_blocks(key_weight), head_blocks(value_weight)],
            axis=2,
        )
    ).reshape(width, q_cols + 2 * HEAD)
    gate_cols = exchange(column_blocks(gate_weight, ff_cols)).reshape(width, ff_cols)
    up_cols = exchange(column_blocks(up_weight, ff_cols)).reshape(width, ff_cols)

    normed = gather_rows(rms_scale(tokens.astype(F32), attn_gain).astype(BF16))
    pre = mm(normed, qkv)
    queries = rotate(pre[:, :q_cols], cos_q, sin_q).astype(BF16)
    keys = rotate(pre[:, q_cols : q_cols + HEAD], cos_k, sin_k).astype(BF16)
    values = pre[:, q_cols + HEAD :].astype(BF16)
    attention = attention_forward(queries, jnp.concatenate([keys, values], axis=1), lengths)
    branch = scatter_rows(mm(attention, output_weight).astype(BF16))
    middle = tokens.astype(F32) + RESIDUAL_SCALE * branch.astype(F32)
    normed_ffn = gather_rows(rms_scale(middle, ffn_gain).astype(BF16))
    own_normed = lax.dynamic_slice_in_dim(normed_ffn, own, local)
    all_normed = lax.all_gather(own_normed, ("rep", "shard"), axis=0, tiled=True)

    reps = lax.axis_size("rep")
    group = lax.axis_index("rep")
    deals = (all_dealing[:, :, None] == packed[None, None, :]).astype(BF16)
    out_grad_all = lax.dot_general(
        deals,
        spread_cotangent.reshape(reps, total, width),
        (((1,), (1,)), ((0,), (0,))),
        preferred_element_type=F32,
    ).reshape(reps * total, width)
    down_grad_all = (RESIDUAL_SCALE * out_grad_all).astype(BF16)
    out_grad = lax.dynamic_slice_in_dim(out_grad_all, group * total + own, local)
    act_grad_all = mm_t(down_grad_all, down_weight)

    def ffn(rows_in, act_grad):
        gate = mm(rows_in, gate_cols)
        up = mm(rows_in, up_cols)
        sigmoid = jax.nn.sigmoid(gate)
        activated = (gate * sigmoid * up).astype(BF16)
        gate_grad = (act_grad * up * sigmoid * (1.0 + gate * (1.0 - sigmoid))).astype(BF16)
        up_grad = (act_grad * gate * sigmoid).astype(BF16)
        return activated, gate_grad, up_grad

    activated, gate_grad, up_grad = ffn(
        normed_ffn, lax.dynamic_slice_in_dim(act_grad_all, group * total, total)
    )
    normed_ffn_part = (mm_t(gate_grad, gate_cols) + mm_t(up_grad, up_cols)).astype(BF16)
    middle_part, ffn_gain_part = norm_pull(
        middle, ffn_gain, scatter_rows(normed_ffn_part).astype(F32)
    )
    middle_grad = out_grad + middle_part
    branch_grad = gather_rows((RESIDUAL_SCALE * middle_grad).astype(BF16))

    own_columns = lax.dynamic_slice_in_dim(dealt, own, local, axis=1)
    layer_output = scatter_rows(
        (
            RESIDUAL_SCALE * mm(mm(dealt, activated).astype(BF16), down_weight)
            + mm(own_columns, middle.astype(BF16))
        ).astype(BF16)
    )

    attention_grad = mm_t(branch_grad, output_weight).astype(BF16)
    dq, dk, dv = attention_gradients(
        queries, jnp.concatenate([keys, values], axis=1), attention_grad, lengths
    )
    pre_grad = jnp.concatenate(
        [
            unrotate(dq, cos_q, sin_q).astype(BF16),
            unrotate(dk, cos_k, sin_k).astype(BF16),
            dv.astype(BF16),
        ],
        axis=1,
    )
    normed_part = mm_t(pre_grad, qkv).astype(BF16)
    hidden_part, attn_gain_part = norm_pull(
        tokens.astype(F32), attn_gain, scatter_rows(normed_part).astype(F32)
    )
    tokens_grad = middle_grad + hidden_part

    activated, gate_grad, up_grad = ffn(all_normed, act_grad_all)
    gate_part = exchange(t_mm(all_normed, gate_grad).astype(BF16).reshape(n, rows, ff_cols))
    up_part = exchange(t_mm(all_normed, up_grad).astype(BF16).reshape(n, rows, ff_cols))
    down_part = t_mm(activated, down_grad_all)
    output_part = rep_sum(t_mm(attention, branch_grad).astype(BF16))
    qkv_part = rep_sum(exchange(t_mm(normed, pre_grad).astype(BF16).reshape(n, rows, q_cols + 2 * HEAD)))

    def join(blocks):
        return blocks.transpose(1, 0, 2).reshape(rows, -1).astype(F32)

    def join_heads(blocks):
        blocks = blocks.astype(F32).reshape(KV_HEADS, copies, rows, HEAD).sum(axis=1)
        return blocks.transpose(1, 0, 2).reshape(rows, KV_HEADS * HEAD)

    gain_grads = lax.psum(jnp.concatenate([attn_gain_part, ffn_gain_part]), ("rep", "shard"))
    return (
        layer_output,
        tokens_grad,
        gain_grads[0],
        join(qkv_part[:, :, :q_cols]),
        join_heads(qkv_part[:, :, q_cols : q_cols + HEAD]),
        join_heads(qkv_part[:, :, q_cols + HEAD :]),
        output_part.astype(F32),
        gain_grads[1],
        join(gate_part),
        join(up_part),
        down_part,
    )


def solution(mesh):
    both = P(("rep", "shard"), None)
    rowed = P("shard", None)
    return jax.shard_map(
        per_device_plane if (mesh.shape["rep"], mesh.shape["shard"]) == (4, 8) else per_device,
        mesh=mesh,
        in_specs=(
            both, P(), rowed, rowed, rowed, rowed, P(), rowed, rowed, rowed,
            P("rep", None), P("rep", None), both,
        ),
        out_specs=(both, both, P(), rowed, rowed, rowed, rowed, P(), rowed, rowed, rowed),
        check_vma=False,
    )
```

```python
import functools

import jax
import jax.numpy as jnp
from jax import lax
from jax.experimental import pallas as pl
from jax.experimental.pallas import tpu as pltpu
from jax.sharding import PartitionSpec as P

HEADS = 32
KV_HEADS = 8
HEAD = 64
EPSILON = 1e-05
RESIDUAL_SCALE = 0.22
SCORE_SCALE = 0.015625
ROPE_BASE = 10000000.0
MASKED = -1e30
BF16 = jnp.bfloat16
F32 = jnp.float32


def mm(a, b):
    return jnp.dot(a, b, preferred_element_type=F32)


def mm_t(a, b):
    return lax.dot_general(a, b, (((1,), (1,)), ((), ())), preferred_element_type=F32)


def t_mm(a, b):
    return lax.dot_general(a, b, (((0,), (0,)), ((), ())), preferred_element_type=F32)


def rms_scale(hidden, gain_vector):
    return (
        hidden
        * lax.rsqrt(jnp.mean(hidden * hidden, axis=-1, keepdims=True) + EPSILON)
        * gain_vector
    )


def places(packed_index, seq_lengths):
    seq_ends = jnp.cumsum(seq_lengths)
    starts = seq_ends - seq_lengths
    segment = jnp.sum((packed_index[:, None] >= seq_ends[None, :]).astype(jnp.int32), axis=1)
    chosen = segment[:, None] == jnp.arange(seq_lengths.shape[0], dtype=jnp.int32)[None, :]
    position = packed_index - jnp.sum(jnp.where(chosen, starts[None, :], 0), axis=1)
    return segment, position


def rope_tables(position, width):
    half = HEAD // 2
    frequency = ROPE_BASE ** (-(jnp.arange(half, dtype=F32) * 2.0) / (2.0 * half))
    turned = position.astype(F32)[:, None] * frequency[None, :]
    cosine, sine = jnp.cos(turned), jnp.sin(turned)
    cos_full = jnp.concatenate([cosine, cosine], axis=-1)
    sin_full = jnp.concatenate([-sine, sine], axis=-1)
    return jnp.tile(cos_full, (1, width // HEAD)), jnp.tile(sin_full, (1, width // HEAD))


def swap_halves(x):
    rows, width = x.shape
    half = HEAD // 2
    y = x.reshape(rows, width // HEAD, 2, half)
    return jnp.concatenate([y[:, :, 1:], y[:, :, :1]], axis=2).reshape(rows, width)


def rotate(x, cos_full, sin_full):
    return x * cos_full + swap_halves(x) * sin_full


def unrotate(x, cos_full, sin_full):
    return x * cos_full - swap_halves(x) * sin_full


def gather_rows(x):
    return lax.all_gather(x, "shard", axis=0, tiled=True)


def scatter_rows(x):
    return lax.psum_scatter(x, "shard", scatter_dimension=0, tiled=True)


def exchange(blocks):
    return lax.all_to_all(blocks, "shard", split_axis=0, concat_axis=0, tiled=True)


def rep_sum(x):
    count = lax.axis_size("rep")
    where = lax.axis_index("rep")
    half = count // 2
    for hop in range(half - 1):
        moved = lax.ppermute(
            x, "rep", [(hop, hop + 1), (count - 1 - hop, count - 2 - hop)]
        )
        x = (x.astype(F32) + moved.astype(F32)).astype(BF16)
    moved = lax.ppermute(x, "rep", [(half - 1, half), (half, half - 1)])
    x = (x.astype(F32) + moved.astype(F32)).astype(BF16)
    for hop in range(half - 1):
        near, far = half - 1 - hop, half + hop
        moved = lax.ppermute(x, "rep", [(near, near - 1), (far, far + 1)])
        x = jnp.where((where == near - 1) | (where == far + 1), moved, x)
    return x


MESH = pl.DeviceIdType.MESH


def flip(index, bits):
    for weight in (1, 2, 4):
        if bits & weight:
            index = index + weight - 2 * weight * lax.rem(lax.div(index, weight), 2)
    return index


def send(src, dst, sems, k, target):
    return pltpu.make_async_remote_copy(
        src_ref=src,
        dst_ref=dst,
        send_sem=sems.at[0, k],
        recv_sem=sems.at[1, k],
        device_id={"shard": target},
        device_id_type=MESH,
    )


def greet(me, masks):
    barrier = pltpu.get_barrier_semaphore()
    for mask in masks:
        pl.semaphore_signal(
            barrier, inc=1, device_id={"shard": flip(me, mask)}, device_id_type=MESH
        )
    pl.semaphore_wait(barrier, len(masks))


GATHER_SEMS = 13
BULK = (12, 2, 2)


def gather_steps(me, out, sems):
    core, px, py, diag = (flip(me, mask) for mask in (1, 2, 4, 6))
    half = out.shape[1] // 2
    low, high, whole = pl.ds(0, half), pl.ds(half, half), pl.ds(0, 2 * half)

    def move(k, block, rows, target):
        ref = out.at[block, rows]
        copy = send(ref, ref, sems, k, target)
        copy.start()
        return copy

    x_low, y_high = move(0, me, low, px), move(1, me, high, py)
    own = move(2, me, whole, core)
    x_high, y_low = move(3, me, high, px), move(4, me, low, py)
    yield
    x_low.wait_recv()
    diag_low = move(5, px, low, py)
    pieces = [own, move(6, px, low, core)]
    yield
    y_high.wait_recv()
    diag_high = move(7, py, high, px)
    pieces.append(move(8, py, high, core))
    yield
    x_high.wait_recv()
    pieces.append(move(9, px, high, core))
    yield
    y_low.wait_recv()
    pieces.append(move(10, py, low, core))
    yield
    diag_low.wait_recv()
    pieces.append(move(11, diag, low, core))
    diag_high.wait_recv()
    pieces.append(move(12, diag, high, core))
    yield
    for copy in pieces:
        copy.wait_recv()
    for copy in [x_low, y_high, x_high, y_low, diag_low, diag_high] + pieces:
        copy.wait_send()


def gather_blocks(me, out, sems):
    for unused_step in gather_steps(me, out, sems):
        pass


SCATTER_SEMS = 10


def scatter_steps(me, partial, sib_out, sib_in, acc, x_out, x_in, y_out, y_in, sems):
    core, px, py = (flip(me, mask) for mask in (1, 2, 4))
    half = acc.shape[1] // 2
    masks = (6, 2, 4, 0)
    low, high = pl.ds(0, half), pl.ds(half, half)
    copies = []

    def move(src, dst, k, target):
        copy = send(src, dst, sems, k, target)
        copy.start()
        copies.append(copy)
        return copy

    inside = []
    for i, mask in enumerate(masks):
        sib_out[i] = partial(flip(core, mask)).astype(BF16)
        inside.append(move(sib_out.at[i], sib_in.at[i], i, core))
    yield
    for i, mask in enumerate(masks):
        term = partial(flip(me, mask))
        inside[i].wait_recv()
        acc[i] = term + sib_in[i].astype(F32)
        if mask == 6:
            x_out[0] = acc[i, low].astype(BF16)
            x_diag = move(x_out.at[0], x_in.at[0], 4, px)
            y_out[0] = acc[i, high].astype(BF16)
            y_diag = move(y_out.at[0], y_in.at[0], 5, py)
        if mask == 2:
            x_out[1] = acc[i, low].astype(BF16)
            x_near = move(x_out.at[1], x_in.at[1], 6, px)
        if mask == 4:
            y_out[1] = acc[i, high].astype(BF16)
            y_near = move(y_out.at[1], y_in.at[1], 7, py)
    yield
    x_diag.wait_recv()
    y_out[2] = (acc[2, low] + x_in[0].astype(F32)).astype(BF16)
    y_last = move(y_out.at[2], y_in.at[2], 8, py)
    y_diag.wait_recv()
    x_out[2] = (acc[1, high] + y_in[0].astype(F32)).astype(BF16)
    x_last = move(x_out.at[2], x_in.at[2], 9, px)
    yield
    x_near.wait_recv()
    y_near.wait_recv()
    y_last.wait_recv()
    acc[3, low] = acc[3, low] + x_in[1].astype(F32) + y_in[2].astype(F32)
    x_last.wait_recv()
    acc[3, high] = acc[3, high] + y_in[1].astype(F32) + x_in[2].astype(F32)
    yield
    for copy in copies:
        copy.wait_send()


def scatter_blocks(me, partial, *buffers):
    for unused_step in scatter_steps(me, partial, *buffers):
        pass
    return buffers[2][3]


def scatter_scratch(rows, width):
    half = rows // 2
    return [
        pltpu.VMEM((4, rows, width), BF16),
        pltpu.VMEM((4, rows, width), BF16),
        pltpu.VMEM((4, rows, width), F32),
        pltpu.VMEM((3, half, width), BF16),
        pltpu.VMEM((3, half, width), BF16),
        pltpu.VMEM((3, half, width), BF16),
        pltpu.VMEM((3, half, width), BF16),
        pltpu.SemaphoreType.DMA((2, SCATTER_SEMS)),
    ]


VMEM = pl.BlockSpec(memory_space=pltpu.VMEM)
SMEM = pl.BlockSpec(memory_space=pltpu.SMEM)
ANY = pl.BlockSpec(memory_space=pl.ANY)


def comm_params(collective_id, mebibytes):
    return pltpu.CompilerParams(
        collective_id=collective_id, has_side_effects=True, vmem_limit_bytes=mebibytes << 20
    )


def front(
    tokens, attn_gain, query_weight, key_weight, value_weight, output_weight, ffn_gain,
    gate_weight, up_weight, down_weight, dealing, lengths, cotangent, freq, replicas,
):
    local, width = tokens.shape
    total = 8 * local
    shard_rows = query_weight.shape[0]
    q_cols = query_weight.shape[1] // 8
    ff_cols = gate_weight.shape[1] // 8
    block = 256
    others = (1, 2, 3, 4, 5, 6, 7)

    def kernel(
        tok_ref, gain_ref, wq_hbm, wk_ref, wv_ref, wo_ref, fgain_ref, wg_hbm, wu_hbm,
        wd_ref, deal_ref, len_ref, cot_ref, freq_ref,
        n_ref, q_ref, kv_ref, att_ref, qw_ref, kvw_ref, wg_out, wu_out, mid_ref, nf_ref, dg_out, ag_out, cot_out, half_out,
        kv_stage, c_all, dg_own, ag_stage,
        sib_out, sib_in, acc, x_out, x_in, y_out, y_in, scatter_sems,
        n_sems, c_sems, nf_sems, qkv_sems, bulk_sems, ring_sems, pair_sems, local_sems,
    ):
        me = lax.axis_index("shard")
        group = lax.axis_index("rep")
        core = lax.rem(me, 2)
        after = lax.rem(group + 1, replicas)
        before = lax.rem(group + replicas - 1, replicas)

        barrier = pltpu.get_barrier_semaphore()
        for mask in others:
            pl.semaphore_signal(
                barrier, inc=1, device_id={"shard": flip(me, mask)}, device_id_type=MESH
            )
        for neighbour in (after, before):
            pl.semaphore_signal(
                barrier, inc=1, device_id={"rep": neighbour}, device_id_type=MESH
            )
        c_all[me] = cot_ref[...]
        for d in range(8):
            lanes = slice(d * HEAD, (d + 1) * HEAD)
            kv_stage[d] = jnp.concatenate([wk_ref[:, lanes], wv_ref[:, lanes]], axis=1)
        pl.semaphore_wait(barrier, len(others) + 2)

        gather_c = gather_steps(me, c_all, c_sems)
        next(gather_c)
        n_ref[me] = rms_scale(tok_ref[...].astype(F32), gain_ref[...]).astype(BF16)
        weights = []
        for mask in others:
            peer = flip(me, mask)
            columns = pl.ds(pl.multiple_of(peer * q_cols, q_cols), q_cols)
            weights.append(send(wq_hbm.at[:, columns], qw_ref.at[me], qkv_sems, 2 * mask - 2, peer))
            weights.append(send(kv_stage.at[peer], kvw_ref.at[me], qkv_sems, 2 * mask - 1, peer))
        own_columns = pl.ds(pl.multiple_of(me * ff_cols, ff_cols), ff_cols)
        own_q = pl.ds(pl.multiple_of(me * q_cols, q_cols), q_cols)
        gate_slot, up_slot = ag_stage.at[:shard_rows], ag_stage.at[pl.ds(shard_rows, shard_rows)]
        kept = [
            pltpu.make_async_copy(wg_hbm.at[:, own_columns], gate_slot, local_sems.at[0]),
            pltpu.make_async_copy(wu_hbm.at[:, own_columns], up_slot, local_sems.at[1]),
            pltpu.make_async_copy(wq_hbm.at[:, own_q], qw_ref.at[me], local_sems.at[2]),
        ]
        for copy in kept:
            copy.start()
        kvw_ref[me] = kv_stage[me]

        bulk, waiting = [], []
        for source, target in ((wg_hbm, wg_out), (wu_hbm, wu_out)):
            for part in range(2):
                rows = pl.ds(part * (shard_rows // 2), shard_rows // 2)
                for mask in (2, 4, 6, 3, 5, 7, 1):
                    waiting.append((source, target, rows, mask))

        def more(count):
            for unused in range(min(count, len(waiting))):
                source, target, rows, mask = waiting.pop(0)
                peer = flip(me, mask)
                columns = pl.ds(pl.multiple_of(peer * ff_cols, ff_cols), ff_cols)
                copy = send(
                    source.at[rows, columns], target.at[me, rows], bulk_sems, len(bulk), peer
                )
                copy.start()
                bulk.append(copy)

        for unused in gather_c:
            pass
        gather_n = gather_steps(me, n_ref, n_sems)
        next(gather_n)
        for copy in weights:
            copy.start()

        def permute(first):
            def step(i, carry):
                row0 = pl.multiple_of(first + i * block, block)
                packed = row0 + lax.broadcasted_iota(jnp.int32, (block, total), 0)
                chosen = (deal_ref[...] == packed).astype(BF16)
                dealt = mm(chosen, c_all[...].reshape(total, width))
                dg_own[pl.ds(row0, block), :] = (RESIDUAL_SCALE * dealt).astype(BF16)
                return carry

            lax.fori_loop(0, total // 2 // block, step, 0)

        near = pl.multiple_of(core * (total // 2), total // 2)
        far = pl.multiple_of((1 - core) * (total // 2), total // 2)
        half = pl.ds(near, total // 2)

        opposite = lax.rem(group + 2, replicas)
        held_groups = (before, after, opposite)

        def pass_on(k):
            ref = dg_out.at[before if k == 2 else group, half]
            copy = pltpu.make_async_remote_copy(
                src_ref=ref if k == 2 else dg_own.at[half],
                dst_ref=ref,
                send_sem=ring_sems.at[0, k],
                recv_sem=ring_sems.at[1, k],
                device_id={"rep": before if k == 1 else after},
                device_id_type=MESH,
            )
            copy.start()
            return copy

        def share(k):
            ref = dg_out.at[held_groups[k], half]
            copy = send(ref, ref, pair_sems, k, flip(me, 1))
            copy.start()
            return copy

        permute(near)
        hops = [pass_on(0)]
        for unused in range(4):
            next(gather_n)
        permute(far)
        packed = me * local + lax.broadcasted_iota(jnp.int32, (local, total), 0)
        chosen = (deal_ref[...] == packed).astype(BF16)
        cot_out[...] = mm(chosen, c_all[...].reshape(total, width)).astype(BF16)
        store = pltpu.make_async_copy(dg_own, dg_out.at[group], local_sems.at[3])
        store.start()
        for unused in gather_n:
            pass
        for copy in kept:
            copy.wait()
        kept = [
            pltpu.make_async_copy(gate_slot, wg_out.at[me], local_sems.at[0]),
            pltpu.make_async_copy(up_slot, wu_out.at[me], local_sems.at[1]),
        ]
        for copy in kept:
            copy.start()
        for copy in weights:
            copy.wait_recv()
        more(BULK[0])
        def project(i, carry):
            row0 = pl.multiple_of(i * block, block)
            rows = pl.ds(row0, block)
            x = n_ref[pl.ds(i * (block // local), block // local)].reshape(block, width)
            cosine, sine = lane_rope(row0, block, freq_ref[...], len_ref)
            pre = mm(x, qw_ref[...].reshape(width, q_cols))
            for j in range(q_cols // (2 * HEAD)):
                lanes = slice(j * 2 * HEAD, (j + 1) * 2 * HEAD)
                y = pre[:, lanes]
                q_ref[rows, lanes] = (y * cosine + lane_swap(y) * sine).astype(BF16)
            cosine, sine = keys_only(cosine, sine)
            y = mm(x, kvw_ref[...].reshape(width, 2 * HEAD))
            kv_ref[rows, :] = (y * cosine + lane_swap(y) * sine).astype(BF16)
            return carry

        lax.fori_loop(0, total // block, project, 0)
        hops.append(pass_on(1))
        attend(q_cols // HEAD, block, q_ref, kv_ref, len_ref, att_ref)

        def partial(d):
            return mm(att_ref[pl.ds(pl.multiple_of(d * local, local), local), :], wo_ref[...])

        pending = {}

        def act_grad(held, first, loaded):
            rows = pl.ds(first, total // 2)
            if not loaded:
                load = pltpu.make_async_copy(
                    dg_out.at[held, rows], dg_own.at[rows], local_sems.at[3]
                )
                load.start()
                load.wait()
            slot = 0 if first is near else 1
            if slot in pending:
                pending[slot].wait()

            def step(i, carry):
                part = pl.ds(pl.multiple_of(first + i * block, block), block)
                ag_stage[part, :] = mm_t(dg_own[part, :], wd_ref[...]).astype(BF16)
                return carry

            lax.fori_loop(0, total // 2 // block, step, 0)
            pending[slot] = pltpu.make_async_copy(
                ag_stage.at[rows], ag_out.at[held, rows], local_sems.at[5 + slot]
            )
            pending[slot].start()

        hops[0].wait_recv()
        hops.append(pass_on(2))
        shares = [share(0)]
        scatter = scatter_steps(
            me, partial, sib_out, sib_in, acc, x_out, x_in, y_out, y_in, scatter_sems
        )
        next(scatter)
        more(BULK[1])
        for unused in scatter:
            pass
        branch = acc[3]
        middle = tok_ref[...].astype(F32) + RESIDUAL_SCALE * branch
        mid_ref[...] = middle
        nf_ref[me] = rms_scale(middle, fgain_ref[...]).astype(BF16)
        gather_nf = gather_steps(me, nf_ref, nf_sems)
        next(gather_nf)
        more(BULK[2])
        for unused in gather_nf:
            pass
        more(len(waiting))
        give = pltpu.make_async_copy(nf_ref.at[pl.ds(4 * core, 4)], half_out, local_sems.at[4])
        give.start()
        store.wait()
        for copy in kept:
            copy.wait()
        act_grad(group, near, True)
        act_grad(group, far, True)
        hops[0].wait_send()
        hops[1].wait_send()
        for k in range(3):
            if k > 0:
                hops[k].wait_recv()
                shares.append(share(k))
            act_grad(held_groups[k], near, False)
            shares[k].wait_recv()
            act_grad(held_groups[k], far, False)
        for copy in pending.values():
            copy.wait()
        give.wait()
        for copy in bulk:
            copy.wait_recv()
        for copy in weights + bulk + hops[2:] + shares:
            copy.wait_send()

    rows8 = jax.ShapeDtypeStruct((8, local, width), BF16)
    half_sems = pltpu.SemaphoreType.DMA
    outs = pl.pallas_call(
        kernel,
        out_shape=(
            rows8,
            jax.ShapeDtypeStruct((total, q_cols), BF16),
            jax.ShapeDtypeStruct((total, 2 * HEAD), BF16),
            jax.ShapeDtypeStruct((total, q_cols), BF16),
            jax.ShapeDtypeStruct((8, shard_rows, q_cols), BF16),
            jax.ShapeDtypeStruct((8, shard_rows, 2 * HEAD), BF16),
            jax.ShapeDtypeStruct((8, shard_rows, ff_cols), BF16),
            jax.ShapeDtypeStruct((8, shard_rows, ff_cols), BF16),
            jax.ShapeDtypeStruct((local, width), F32),
            rows8,
            jax.ShapeDtypeStruct((replicas, total, width), BF16),
            jax.ShapeDtypeStruct((replicas, total, ff_cols), BF16),
            jax.ShapeDtypeStruct((local, width), BF16),
            jax.ShapeDtypeStruct((4, local, width), BF16),
        ),
        in_specs=[VMEM, VMEM, ANY, VMEM, VMEM, VMEM, VMEM, ANY, ANY, VMEM, VMEM, SMEM, VMEM, VMEM],
        out_specs=[VMEM] * 6 + [ANY, ANY, VMEM, VMEM, ANY, ANY, VMEM, ANY],
        scratch_shapes=[
            pltpu.VMEM((8, shard_rows, 2 * HEAD), BF16),
            pltpu.VMEM((8, local, width), BF16),
            pltpu.VMEM((total, width), BF16),
            pltpu.VMEM((total, ff_cols), BF16),
        ]
        + scatter_scratch(local, width)
        + [
            half_sems((2, GATHER_SEMS)),
            half_sems((2, GATHER_SEMS)),
            half_sems((2, GATHER_SEMS)),
            half_sems((2, 14)),
            half_sems((2, 28)),
            half_sems((2, replicas)),
            half_sems((2, replicas)),
            half_sems((7,)),
        ],
        compiler_params=comm_params(0, 56),
        cost_estimate=pl.CostEstimate(
            flops=200_000_000_000, bytes_accessed=50 << 20, transcendentals=total * total
        ),
        name="front",
    )(
        tokens, attn_gain[None, :], query_weight, key_weight, value_weight, output_weight,
        ffn_gain[None, :], gate_weight, up_weight, down_weight, dealing, lengths, cotangent, freq,
    )
    normed, q, kv, attention, qw, kvw, wg, wu, middle, nf, dg, ag, cot, held = outs
    return (
        normed.reshape(total, width), q, kv, attention,
        qw.reshape(width, q_cols), kvw.reshape(width, 2 * HEAD),
        wg.reshape(width, ff_cols), wu.reshape(width, ff_cols),
        middle, nf.reshape(total, width), dg, ag, cot,
        held.reshape(total // 2, width),
    )


def norm_pull(x, gain, grad):
    scale = lax.rsqrt(jnp.mean(x * x, axis=-1, keepdims=True) + EPSILON)
    pulled = gain * grad
    rows_part = scale * pulled - x * (
        scale * scale * scale * jnp.mean(pulled * x, axis=-1, keepdims=True)
    )
    return rows_part, jnp.sum(grad * x * scale, axis=0, keepdims=True)


def pull_gather(part, middle, gain, out_grad, activated, down_weight, deal, collective_id):
    rows, width = middle.shape
    groups, total, cols = activated.shape
    block = 256

    def kernel(
        p_ref, m_ref, gain_ref, g_ref, act_hbm, wd_ref, deal_ref,
        mg_ref, gain_part, out, dealt_ref, act_ref, packed_ref, act_sem, *scratch,
    ):
        me = lax.axis_index("shard")
        *buffers, scatter_sems, sems = scratch
        load = pltpu.make_async_copy(act_hbm.at[lax.axis_index("rep")], act_ref, act_sem.at[0])
        load.start()
        greet(me, (1, 2, 4))

        def down(i, carry):
            chunk = pl.ds(pl.multiple_of(i * block, block), block)
            packed_ref[chunk, :] = (RESIDUAL_SCALE * mm(act_ref[chunk, :], wd_ref[...])).astype(BF16)
            return carry

        def deal_out(i, carry):
            chunk = pl.ds(pl.multiple_of(i * block, block), block)
            packed = lax.broadcasted_iota(jnp.int32, (block, total), 1)
            chosen = (deal_ref[chunk, :] == packed).astype(BF16)
            dealt_ref[chunk, :] = mm(chosen, packed_ref[...]).astype(BF16)
            return carry

        half = total // block // 2
        scatter = scatter_steps(
            me,
            lambda d: p_ref[pl.ds(pl.multiple_of(d * rows, rows), rows), :].astype(F32),
            *buffers,
            scatter_sems,
        )
        next(scatter)
        load.wait()
        lax.fori_loop(0, half, down, 0)
        next(scatter)
        lax.fori_loop(half, 2 * half, down, 0)
        own = pl.ds(pl.multiple_of(me * rows, rows), rows)
        packed_ref[own, :] = (packed_ref[own, :].astype(F32) + m_ref[...]).astype(BF16)
        next(scatter)
        for unused in scatter:
            pass
        rows_part, gain_row = norm_pull(m_ref[...], gain_ref[...], buffers[2][3])
        gain_part[...] = gain_row
        middle_grad = g_ref[...].astype(F32) + rows_part
        mg_ref[...] = middle_grad
        out[me] = (RESIDUAL_SCALE * middle_grad).astype(BF16)
        gather = gather_steps(me, out, sems)
        next(gather)
        lax.fori_loop(0, half, deal_out, 0)
        for unused in range(2):
            next(gather)
        lax.fori_loop(half, 2 * half, deal_out, 0)
        for unused in gather:
            pass

    return pl.pallas_call(
        kernel,
        out_shape=(
            jax.ShapeDtypeStruct((rows, width), F32),
            jax.ShapeDtypeStruct((1, width), F32),
            jax.ShapeDtypeStruct((8, rows, width), BF16),
            jax.ShapeDtypeStruct((total, width), BF16),
        ),
        in_specs=[VMEM] * 4 + [ANY] + [VMEM] * 2,
        out_specs=[VMEM] * 4,
        scratch_shapes=[
            pltpu.VMEM((total, cols), BF16),
            pltpu.VMEM((total, width), BF16),
            pltpu.SemaphoreType.DMA((1,)),
        ]
        + scatter_scratch(rows, width)
        + [pltpu.SemaphoreType.DMA((2, GATHER_SEMS))],
        compiler_params=comm_params(collective_id, 56),
        cost_estimate=pl.CostEstimate(
            flops=60_000_000_000, bytes_accessed=50 * rows * width, transcendentals=rows
        ),
        name="pull_gather",
    )(part, middle, gain[None, :], out_grad, activated, down_weight, deal)


def pull_tokens(
    part, out_part, qkv, hidden, gain, middle_grad, other_gain, near, act_grads, wg, wu, filled, replicas,
    collective_id,
):
    rows, width = middle_grad.shape
    groups, total, cols = act_grads.shape
    block = 256
    levels = [("shard", 1), ("shard", 2), ("shard", 4)]
    level = 1
    while level < replicas:
        levels.append(("rep", level))
        level *= 2
    per_half = total // 2 // block

    def kernel(
        p_ref, o_ref, h_ref, gain_ref, mg_ref, og_ref, wg_ref, wu_ref, ag_hbm,
        before_held, after_held, qkv_hbm, unused_na, unused_act, unused_gg, unused_ug,
        out, lay, gains, na_hbm, act_hbm, gg_hbm, ug_hbm, fetched, qkv_out, share_sems, qkv_sems, own_sem, own_block,
        nf_buf, ag_buf, done_buf, in_sems, out_sems, gain_in, gain_out, gain_sems, *scratch,
    ):
        me = lax.axis_index("shard")
        group = lax.axis_index("rep")
        core = lax.rem(me, 2)
        before = lax.rem(group + replicas - 1, replicas)
        after = lax.rem(group + 1, replicas)
        first, second = scratch[:8], scratch[8:]
        parts = (
            (before, before_held, core),
            (after, after_held, core),
            (before, fetched.at[0], 1 - core),
            (after, fetched.at[1], 1 - core),
        )

        def rows_of(p, r):
            return pl.ds(pl.multiple_of((parts[p][2] * per_half + r) * block, block), block)

        def loads(p, r):
            held, source, unused = parts[p]
            slot = (p % 2) * per_half + r
            return [
                pltpu.make_async_copy(
                    source.at[pl.ds(pl.multiple_of(r * block, block), block)],
                    nf_buf.at[slot],
                    in_sems.at[0, slot],
                ),
                pltpu.make_async_copy(ag_hbm.at[held, rows_of(p, r)], ag_buf.at[slot], in_sems.at[1, slot]),
            ]

        def stores(p, r):
            held = parts[p][0]
            slot = (p % 2) * per_half + r
            where = rows_of(p, r)
            return [
                pltpu.make_async_copy(nf_buf.at[slot], na_hbm.at[held, where], out_sems.at[0, slot])
            ] + [
                pltpu.make_async_copy(done_buf.at[k, slot], target.at[held, where], out_sems.at[k + 1, slot])
                for k, target in enumerate((act_hbm, gg_hbm, ug_hbm))
            ]

        def start_loads(p):
            for r in range(per_half):
                for copy in loads(p, r):
                    copy.start()

        def wait_stores(p):
            for r in range(per_half):
                for copy in stores(p, r):
                    copy.wait()

        def fill(p):
            if p > 0:
                wait_stores(p - 1)
            if p in (1, 2):
                shares[p - 1].wait_recv()
            if p + 1 < len(parts):
                start_loads(p + 1)

            def step(r, carry):
                slot = (p % 2) * per_half + r
                for copy in loads(p, r):
                    copy.wait()
                results = ffn_rows(nf_buf[slot], ag_buf[slot], wg_ref[...], wu_ref[...])
                for k, result in enumerate(results):
                    done_buf[k, slot] = result
                for copy in stores(p, r):
                    copy.start()
                return carry

            lax.fori_loop(0, per_half, step, 0)

        start_loads(0)
        barrier = pltpu.get_barrier_semaphore()
        peers = []
        for axis, weight in levels:
            index = me if axis == "shard" else group
            peers.append({axis: index + weight - 2 * weight * lax.rem(lax.div(index, weight), 2)})
        far = [{"shard": flip(me, mask)} for mask in (3, 5, 6, 7)]
        for peer in peers + far:
            pl.semaphore_signal(barrier, inc=1, device_id=peer, device_id_type=MESH)
        pl.semaphore_wait(barrier, len(peers) + len(far))

        def blocks_of(ref):
            return lambda d: ref[pl.ds(pl.multiple_of(d * rows, rows), rows), :].astype(F32)

        grads = scatter_steps(me, blocks_of(p_ref), *first)
        outputs = scatter_steps(me, blocks_of(o_ref), *second)
        next(grads)
        next(outputs)
        shares = [
            send(source, fetched.at[k], share_sems, k, flip(me, 1))
            for k, source in enumerate((before_held, after_held))
        ]
        for copy in shares:
            copy.start()
        exchange_qkv = []
        for mask in range(1, 8):
            peer = flip(me, mask)
            exchange_qkv.append(send(qkv_hbm.at[peer], qkv_out.at[me], qkv_sems, mask - 1, peer))
        own_in = pltpu.make_async_copy(qkv_hbm.at[me], own_block, own_sem.at[0])
        own_in.start()
        own_qkv = pltpu.make_async_copy(own_block, qkv_out.at[me], own_sem.at[1])
        fill(0)
        next(grads)
        fill(1)
        next(grads)
        next(outputs)
        own_in.wait()
        for copy in exchange_qkv + [own_qkv]:
            copy.start()
        fill(2)
        next(grads)
        next(outputs)
        rows_part, gain_row = norm_pull(h_ref[...].astype(F32), gain_ref[...], first[2][3])
        out[...] = mg_ref[...] + rows_part
        sums = jnp.concatenate([gain_row, og_ref[...]], axis=0)
        for i, peer in enumerate(peers):
            gain_out[i] = sums
            copy = pltpu.make_async_remote_copy(
                src_ref=gain_out.at[i],
                dst_ref=gain_in.at[i],
                send_sem=gain_sems.at[0, i],
                recv_sem=gain_sems.at[1, i],
                device_id=peer,
                device_id_type=MESH,
            )
            copy.start()
            if i == 0:
                fill(3)
            copy.wait()
            sums = sums + gain_in[i]
        gains[...] = sums
        next(outputs)
        lay[...] = second[2][3].astype(BF16)
        for steps in (grads, outputs):
            for unused in steps:
                pass
        wait_stores(3)
        own_qkv.wait()
        for copy in exchange_qkv:
            copy.wait_recv()
        for copy in shares + exchange_qkv:
            copy.wait_send()

    hidden_shape = jax.ShapeDtypeStruct((groups, total, cols), BF16)
    return pl.pallas_call(
        kernel,
        out_shape=(
            jax.ShapeDtypeStruct((rows, width), F32),
            jax.ShapeDtypeStruct((rows, width), BF16),
            jax.ShapeDtypeStruct((2, width), F32),
            jax.ShapeDtypeStruct((groups, total, width), BF16),
            hidden_shape,
            hidden_shape,
            hidden_shape,
            jax.ShapeDtypeStruct((2, total // 2, width), BF16),
            jax.ShapeDtypeStruct(qkv.shape, BF16),
        ),
        in_specs=[VMEM] * 8 + [ANY] * 8,
        out_specs=[VMEM] * 3 + [ANY] * 6,
        input_output_aliases={12: 3, 13: 4, 14: 5, 15: 6},
        scratch_shapes=[
            pltpu.SemaphoreType.DMA((2, 2)),
            pltpu.SemaphoreType.DMA((2, 7)),
            pltpu.SemaphoreType.DMA((2,)),
            pltpu.VMEM(qkv.shape[1:], BF16),
            pltpu.VMEM((2 * per_half, block, width), BF16),
            pltpu.VMEM((2 * per_half, block, cols), BF16),
            pltpu.VMEM((3, 2 * per_half, block, cols), BF16),
            pltpu.SemaphoreType.DMA((2, 2 * per_half)),
            pltpu.SemaphoreType.DMA((4, 2 * per_half)),
            pltpu.VMEM((len(levels), 2, width), F32),
            pltpu.VMEM((len(levels), 2, width), F32),
            pltpu.SemaphoreType.DMA((2, len(levels))),
        ]
        + scatter_scratch(rows, width)
        + scatter_scratch(rows, width),
        compiler_params=comm_params(collective_id, 62),
        cost_estimate=pl.CostEstimate(
            flops=60_000_000_000, bytes_accessed=50 * rows * width, transcendentals=rows
        ),
        name="pull_tokens",
    )(
        part, out_part, hidden, gain[None, :], middle_grad, other_gain, wg, wu, act_grads, *near, qkv, *filled
    )


def softmax_block(q, k, allowed):
    scores = SCORE_SCALE * mm_t(q, k)
    scores = jnp.where(allowed, scores, MASKED)
    top = jnp.max(scores, axis=-1, keepdims=True)
    weight = jnp.exp(scores - top)
    return weight * (1.0 / jnp.sum(weight, axis=-1, keepdims=True))


def allowed_block(row0, cols, start):
    shape = (start.shape[0], cols)
    query = row0 + lax.broadcasted_iota(jnp.int32, shape, 0)
    key = lax.broadcasted_iota(jnp.int32, shape, 1)
    return (key >= start) & (key <= query)


def sequence_starts(row0, shape, lengths_ref):
    row = row0 + lax.broadcasted_iota(jnp.int32, shape, 0)
    start = jnp.zeros(shape, jnp.int32)
    end = 0
    for i in range(lengths_ref.shape[1]):
        length = lengths_ref[0, i]
        end = end + length
        start = start + jnp.where(row >= end, length, 0)
    return start


def attend(heads, block, q_ref, kv_ref, lengths_ref, o_ref):
    total = kv_ref.shape[0]
    for i in range(total // block):
        cols = (i + 1) * block
        rows = pl.ds(i * block, block)
        allowed = allowed_block(
            i * block, cols, sequence_starts(i * block, (block, 1), lengths_ref)
        )
        kv = kv_ref[:cols, :]
        k, v = kv[:, :HEAD], kv[:, HEAD:]
        for h in range(heads):
            lanes = slice(h * HEAD, (h + 1) * HEAD)
            probs = softmax_block(q_ref[rows, lanes], k, allowed)
            o_ref[rows, lanes] = mm(probs.astype(BF16), v).astype(BF16)


def attend_back(heads, block, q_ref, kv_ref, g_ref, lengths_ref, dq_ref, dk_ref, dv_ref):
    total = kv_ref.shape[0]
    dk_ref[...] = jnp.zeros_like(dk_ref)
    dv_ref[...] = jnp.zeros_like(dv_ref)
    for i in range(total // block):
        cols = (i + 1) * block
        rows = pl.ds(i * block, block)
        allowed = allowed_block(
            i * block, cols, sequence_starts(i * block, (block, 1), lengths_ref)
        )
        kv = kv_ref[:cols, :]
        k, v = kv[:, :HEAD], kv[:, HEAD:]
        for h in range(heads):
            lanes = slice(h * HEAD, (h + 1) * HEAD)
            q, g = q_ref[rows, lanes], g_ref[rows, lanes]
            probs = softmax_block(q, k, allowed)
            probs_grad = mm_t(g, v)
            delta = jnp.sum(probs * probs_grad, axis=-1, keepdims=True)
            score_grad = (probs * (probs_grad - delta)).astype(BF16)
            dq_ref[rows, lanes] = SCORE_SCALE * mm(score_grad, k)
            dk_ref[:cols, :] += SCORE_SCALE * t_mm(score_grad, q)
            dv_ref[:cols, :] += t_mm(probs.astype(BF16), g)


def attention_forward(q, kv, lengths):
    total, width = q.shape

    def kernel(q_ref, kv_ref, lengths_ref, o_ref):
        attend(width // HEAD, 256, q_ref, kv_ref, lengths_ref, o_ref)

    return pl.pallas_call(
        kernel,
        out_shape=jax.ShapeDtypeStruct((total, width), BF16),
        in_specs=[VMEM, VMEM, SMEM],
        out_specs=VMEM,
        compiler_params=pltpu.CompilerParams(vmem_limit_bytes=40 << 20),
        name="attention_forward",
    )(q, kv, lengths)


def attention_gradients(q, kv, grad, lengths):
    total, width = q.shape

    def kernel(q_ref, kv_ref, g_ref, lengths_ref, dq_ref, dk_ref, dv_ref):
        attend_back(width // HEAD, 256, q_ref, kv_ref, g_ref, lengths_ref, dq_ref, dk_ref, dv_ref)

    return pl.pallas_call(
        kernel,
        out_shape=(
            jax.ShapeDtypeStruct((total, width), F32),
            jax.ShapeDtypeStruct((total, HEAD), F32),
            jax.ShapeDtypeStruct((total, HEAD), F32),
        ),
        in_specs=[VMEM, VMEM, VMEM, SMEM],
        out_specs=[VMEM] * 3,
        compiler_params=pltpu.CompilerParams(vmem_limit_bytes=40 << 20),
        name="attention_gradients",
    )(q, kv, grad, lengths)


def lane_rope(row0, rows, freq, lengths_ref):
    shape = (rows, 2 * HEAD)
    row = row0 + lax.broadcasted_iota(jnp.int32, shape, 0)
    position = row - sequence_starts(row0, shape, lengths_ref)
    turned = position.astype(F32) * freq
    lane = lax.broadcasted_iota(jnp.int32, shape, 1)
    first = lax.rem(lane, HEAD) < HEAD // 2
    sine = jnp.sin(turned)
    return jnp.cos(turned), jnp.where(first, -sine, sine)


def lane_swap(x):
    half = HEAD // 2
    lane = lax.broadcasted_iota(jnp.int32, x.shape, 1)
    first = lax.rem(lane, HEAD) < half
    return jnp.where(first, pltpu.roll(x, 2 * HEAD - half, 1), pltpu.roll(x, half, 1))


def keys_only(cosine, sine):
    lane = lax.broadcasted_iota(jnp.int32, cosine.shape, 1)
    return jnp.where(lane < HEAD, cosine, 1.0), jnp.where(lane < HEAD, sine, 0.0)


def attention_backward(
    branch_grad, output_weight, attention, q, kv, normed, q_weight, kv_weight, lengths, freq
):
    total, q_cols = q.shape
    width = normed.shape[1]
    block = 256

    def kernel(
        bg_ref, wo_ref, a_ref, q_ref, kv_ref, n_ref, qw_ref, kvw_ref, len_ref, freq_ref,
        dn_ref, dqkv_ref, dwo_ref, g_ref, dq_ref, dk_ref, dv_ref, pq_ref, pkv_ref,
    ):
        def open_up(i, carry):
            rows = pl.ds(pl.multiple_of(i * block, block), block)
            g_ref[rows, :] = mm_t(bg_ref[rows, :], wo_ref[...]).astype(BF16)
            return carry

        lax.fori_loop(0, total // block, open_up, 0)
        attend_back(
            q_cols // HEAD, block, q_ref, kv_ref, g_ref, len_ref, dq_ref, dk_ref, dv_ref
        )
        def close_up(i, carry):
            row0 = pl.multiple_of(i * block, block)
            rows = pl.ds(row0, block)
            cosine, sine = lane_rope(row0, block, freq_ref[...], len_ref)
            for j in range(q_cols // (2 * HEAD)):
                lanes = slice(j * 2 * HEAD, (j + 1) * 2 * HEAD)
                x = dq_ref[rows, lanes]
                pq_ref[rows, lanes] = (x * cosine - lane_swap(x) * sine).astype(BF16)
            cosine, sine = keys_only(cosine, sine)
            x = jnp.concatenate([dk_ref[rows, :], dv_ref[rows, :]], axis=1)
            pkv_ref[rows, :] = (x * cosine - lane_swap(x) * sine).astype(BF16)
            dn_ref[rows, :] = (
                mm_t(pq_ref[rows, :], qw_ref[...]) + mm_t(pkv_ref[rows, :], kvw_ref[...])
            ).astype(BF16)
            return carry

        lax.fori_loop(0, total // block, close_up, 0)

        for i in range(width // 512):
            cols = slice(i * 512, (i + 1) * 512)
            dqkv_ref[cols, :q_cols] = t_mm(n_ref[:, cols], pq_ref[...]).astype(BF16)
            dqkv_ref[cols, q_cols:] = t_mm(n_ref[:, cols], pkv_ref[...]).astype(BF16)
            dwo_ref[:, cols] = t_mm(a_ref[...], bg_ref[:, cols]).astype(BF16)

    return pl.pallas_call(
        kernel,
        out_shape=(
            jax.ShapeDtypeStruct((total, width), BF16),
            jax.ShapeDtypeStruct((width, q_cols + 2 * HEAD), BF16),
            jax.ShapeDtypeStruct((q_cols, width), BF16),
        ),
        in_specs=[VMEM] * 8 + [SMEM, VMEM],
        out_specs=[VMEM] * 3,
        scratch_shapes=[
            pltpu.VMEM((total, q_cols), BF16),
            pltpu.VMEM((total, q_cols), F32),
            pltpu.VMEM((total, HEAD), F32),
            pltpu.VMEM((total, HEAD), F32),
            pltpu.VMEM((total, q_cols), BF16),
            pltpu.VMEM((total, 2 * HEAD), BF16),
        ],
        compiler_params=pltpu.CompilerParams(vmem_limit_bytes=56 << 20),
        cost_estimate=pl.CostEstimate(flops=30_000_000_000, bytes_accessed=30 << 20, transcendentals=total * total),
        name="attention_backward",
    )(branch_grad, output_weight, attention, q, kv, normed, q_weight, kv_weight, lengths, freq)


def ffn_rows(nf, act_grad, wg, wu):
    gate, up = mm(nf, wg), mm(nf, wu)
    act_grad = act_grad.astype(F32)
    sigmoid = 1.0 / (1.0 + jnp.exp(-gate))
    silu = gate * sigmoid
    activated = (silu * up).astype(BF16)
    gate_grad = (act_grad * up * sigmoid * (1.0 + gate * (1.0 - sigmoid))).astype(BF16)
    return activated, gate_grad, (act_grad * silu).astype(BF16)


def ffn_own(group, nf, act_grads, wg, wu):
    groups, total, cols = act_grads.shape
    width = nf.shape[1]
    block = 256

    def kernel(g_ref, nf_ref, ag_ref, wg_ref, wu_ref, na_ref, act_ref, gg_ref, ug_ref, dn_ref):
        nf = nf_ref[...]
        act, gg, ug = ffn_rows(nf, ag_ref[0], wg_ref[...], wu_ref[...])
        na_ref[0], act_ref[0], gg_ref[0], ug_ref[0] = nf, act, gg, ug
        dn_ref[...] = (mm_t(gg, wg_ref[...]) + mm_t(ug, wu_ref[...])).astype(BF16)

    mine = pl.BlockSpec((1, block, width), lambda i, g: (g[0], i, 0))
    hid = pl.BlockSpec((1, block, cols), lambda i, g: (g[0], i, 0))
    plain = pl.BlockSpec((block, width), lambda i, g: (i, 0))
    whole = [
        pl.BlockSpec(w.shape, lambda i, g: (0, 0), pipeline_mode=pl.Buffered(1)) for w in (wg, wu)
    ]
    hidden = jax.ShapeDtypeStruct((groups, total, cols), BF16)
    return pl.pallas_call(
        kernel,
        grid_spec=pltpu.PrefetchScalarGridSpec(
            num_scalar_prefetch=1,
            grid=(total // block,),
            in_specs=[plain, hid] + whole,
            out_specs=[mine, hid, hid, hid, plain],
        ),
        out_shape=(
            jax.ShapeDtypeStruct((groups, total, width), BF16),
            hidden,
            hidden,
            hidden,
            jax.ShapeDtypeStruct((total, width), BF16),
        ),
        compiler_params=pltpu.CompilerParams(vmem_limit_bytes=62 << 20),
        cost_estimate=pl.CostEstimate(
            flops=12 * total * width * cols, bytes_accessed=40 << 20, transcendentals=total * cols
        ),
        name="ffn_own",
    )(group, nf, act_grads, wg, wu)


def ffn_other(where, held, fetched, act_grads, wg, wu, filled):
    groups, total, cols = act_grads.shape
    width = held.shape[1]
    block = 256
    per_half = total // 2 // block

    def kernel(w_ref, held_ref, fetched_ref, ag_ref, wg_ref, wu_ref, *rest):
        na_ref, act_ref, gg_ref, ug_ref, nf_ref = rest[4:]
        i = pl.program_id(0)

        @pl.when(i < per_half)
        def _():
            nf_ref[...] = held_ref[...]

        @pl.when(i >= per_half)
        def _():
            nf_ref[...] = fetched_ref[...]

        nf = nf_ref[...]
        act, gg, ug = ffn_rows(nf, ag_ref[0], wg_ref[...], wu_ref[...])
        na_ref[0], act_ref[0], gg_ref[0], ug_ref[0] = nf, act, gg, ug

    def row(i, w):
        half = jnp.where(i < per_half, w[1], 1 - w[1])
        return half * per_half + lax.rem(i, per_half)

    mine = pl.BlockSpec((1, block, width), lambda i, w: (w[0], row(i, w), 0))
    hid = pl.BlockSpec((1, block, cols), lambda i, w: (w[0], row(i, w), 0))
    first = pl.BlockSpec((block, width), lambda i, w: (jnp.minimum(i, per_half - 1), 0))
    last = pl.BlockSpec((block, width), lambda i, w: (jnp.maximum(i - per_half, 0), 0))
    whole = [
        pl.BlockSpec(w.shape, lambda i, g: (0, 0), pipeline_mode=pl.Buffered(1)) for w in (wg, wu)
    ]
    hidden = jax.ShapeDtypeStruct((groups, total, cols), BF16)
    return pl.pallas_call(
        kernel,
        grid_spec=pltpu.PrefetchScalarGridSpec(
            num_scalar_prefetch=1,
            grid=(2 * per_half,),
            in_specs=[first, last, hid] + whole + [pl.BlockSpec(memory_space=pl.ANY)] * 4,
            out_specs=[mine, hid, hid, hid],
            scratch_shapes=[pltpu.VMEM((block, width), BF16)],
        ),
        out_shape=(jax.ShapeDtypeStruct((groups, total, width), BF16), hidden, hidden, hidden),
        input_output_aliases={6: 0, 7: 1, 8: 2, 9: 3},
        compiler_params=pltpu.CompilerParams(vmem_limit_bytes=62 << 20),
        cost_estimate=pl.CostEstimate(
            flops=8 * total * width * cols, bytes_accessed=40 << 20, transcendentals=total * cols
        ),
        name="ffn_other",
    )(where, held, fetched, act_grads, wg, wu, *filled)


def finish(normed, gate_grad, up_grad, activated, down_grad, output_part, qkv_part, collective_id):
    depth, width = normed.shape
    cols = gate_grad.shape[1]
    rows = width // 8
    tall = cols // rows
    steps = 8 + tall
    chunks = 4
    sums = (output_part, qkv_part)

    def kernel(
        nf_hbm, gg_hbm, ug_hbm, act_hbm, dg_hbm, o_in, qkv_in,
        gate_out, up_out, down_out, o_out, qkv_out,
        gg, ug, dg, left, stage, tall_stage, o_mid, qkv_mid, o_last, qkv_last,
        load_sems, left_sems, own_sems, tall_sems, push_sems, relay_sems,
    ):
        me = lax.axis_index("shard")
        group = lax.axis_index("rep")
        inner = (group == 1) | (group == 2)
        outer = (group == 0) | (group == 3)
        beside = group + 1 - 2 * lax.rem(group, 2)
        across = 3 - group

        def peer_of(i):
            mask = 7 - i
            index = 0
            for weight in (1, 2, 4):
                bits = lax.rem(lax.div(me, weight), 2) + lax.rem(lax.div(mask, weight), 2)
                index = index + weight * lax.rem(bits, 2)
            return index

        def start_left(i, slot):
            @pl.when(i < 8)
            def _():
                first = pl.multiple_of(peer_of(i) * rows, rows)
                pltpu.make_async_copy(
                    nf_hbm.at[:, pl.ds(first, rows)], left.at[slot], left_sems.at[slot]
                ).start()

            @pl.when((i >= 8) & (i < steps))
            def _():
                first = pl.multiple_of((i - 8) * rows, rows)
                pltpu.make_async_copy(
                    act_hbm.at[:, pl.ds(first, rows)], left.at[slot], left_sems.at[slot]
                ).start()

        def wait_left(slot):
            pltpu.make_async_copy(
                nf_hbm.at[:, pl.ds(0, rows)], left.at[slot], left_sems.at[slot]
            ).wait()

        loads = [
            pltpu.make_async_copy(source, target, load_sems.at[k])
            for k, (source, target) in enumerate(((gg_hbm, gg), (ug_hbm, ug), (dg_hbm, dg)))
        ]
        start_left(0, 0)
        for load in loads:
            load.start()
        barrier = pltpu.get_barrier_semaphore()
        for mask in range(1, 8):
            pl.semaphore_signal(
                barrier, inc=1, device_id={"shard": flip(me, mask)}, device_id_type=MESH
            )
        for neighbour in (beside, across):
            pl.semaphore_signal(
                barrier, inc=1, device_id={"rep": neighbour}, device_id_type=MESH
            )
        pl.semaphore_wait(barrier, 9)

        arrays = ((o_in, o_mid, o_last, o_out), (qkv_in, qkv_mid, qkv_last, qkv_out))

        def relay_copy(stage_index, k, c, target):
            start, mid, last, out = arrays[k]
            size = start.shape[0] // chunks
            part = pl.ds(pl.multiple_of(c * size, size), size)
            source, arrived = ((start, mid), (mid, last), (out, out))[stage_index]
            return pltpu.make_async_remote_copy(
                src_ref=source.at[part],
                dst_ref=arrived.at[part],
                send_sem=relay_sems.at[0, stage_index, k * chunks + c],
                recv_sem=relay_sems.at[1, stage_index, k * chunks + c],
                device_id={"rep": target},
                device_id_type=MESH,
            )

        @pl.when(outer)
        def _():
            for c in range(chunks):
                for k in range(2):
                    relay_copy(0, k, c, beside).start()

        def relay(t):
            def part_of(k, c):
                size = arrays[k][0].shape[0] // chunks
                return pl.ds(pl.multiple_of(c * size, size), size)

            @pl.when(inner & (t < chunks))
            def _():
                for k in range(2):
                    start, mid, last, out = arrays[k]
                    part = part_of(k, t)
                    relay_copy(0, k, t, beside).wait_recv()
                    mid[part, :] = (start[part, :].astype(F32) + mid[part, :].astype(F32)).astype(BF16)
                    relay_copy(1, k, t, across).start()

            @pl.when(inner & (t >= 1) & (t <= chunks))
            def _():
                for k in range(2):
                    start, mid, last, out = arrays[k]
                    part = part_of(k, t - 1)
                    relay_copy(1, k, t - 1, across).wait_recv()
                    out[part, :] = (mid[part, :].astype(F32) + last[part, :].astype(F32)).astype(BF16)
                    relay_copy(2, k, t - 1, beside).start()

            @pl.when(outer & (t >= 2) & (t <= chunks + 1))
            def _():
                for k in range(2):
                    relay_copy(2, k, t - 2, beside).wait_recv()

        outputs = (gate_out, up_out)
        own_columns = pl.ds(pl.multiple_of(me * cols, cols), cols)

        def push(i, j, target):
            return send(
                stage.at[i, j], outputs[j].at[:, own_columns], push_sems, 2 * i + j, target
            )

        def wide(i, carry):
            slot = lax.rem(i, 2)
            start_left(i + 1, 1 - slot)
            wait_left(slot)
            for j, right in enumerate((gg, ug)):

                @pl.when(i == 0)
                def _():
                    loads[j].wait()

                stage[i, j] = t_mm(left[slot], right[...]).astype(BF16)

                @pl.when(i < 7)
                def _():
                    push(i, j, peer_of(i)).start()

                @pl.when(i == 7)
                def _():
                    pltpu.make_async_copy(
                        stage.at[7, j], outputs[j].at[:, own_columns], own_sems.at[j]
                    ).start()

            @pl.when(lax.rem(i, 2) == 1)
            def _():
                relay(lax.div(i, 2))

            return carry

        lax.fori_loop(0, 8, wide, 0)
        loads[2].wait()

        def tall_copy(i):
            slot = lax.rem(i, 2)
            first = pl.multiple_of((i - 8) * rows, rows)
            return pltpu.make_async_copy(
                tall_stage.at[slot], down_out.at[pl.ds(first, rows), :], tall_sems.at[slot]
            )

        def high(i, carry):
            slot = lax.rem(i, 2)
            start_left(i + 1, 1 - slot)
            wait_left(slot)

            @pl.when(i >= 10)
            def _():
                tall_copy(i - 2).wait()

            tall_stage[slot] = t_mm(left[slot], dg[...]).astype(BF16)
            tall_copy(i).start()

            @pl.when(lax.rem(i, 2) == 1)
            def _():
                relay(lax.div(i, 2))

            return carry

        lax.fori_loop(8, steps, high, 0)
        for i in (steps - 2, steps - 1):
            tall_copy(i).wait()
        for j in range(2):
            pltpu.make_async_copy(
                stage.at[7, j], outputs[j].at[:, own_columns], own_sems.at[j]
            ).wait()
        for t in range(steps // 2, chunks + 2):
            relay(t)

        def drain(i, carry):
            for j in range(2):
                push(i, j, peer_of(i)).wait()
            return carry

        lax.fori_loop(0, 7, drain, 0)

        @pl.when(outer)
        def _():
            for c in range(chunks):
                for k in range(2):
                    relay_copy(0, k, c, beside).wait_send()

        @pl.when(inner)
        def _():
            for c in range(chunks):
                for k in range(2):
                    relay_copy(1, k, c, across).wait_send()
                    relay_copy(2, k, c, beside).wait_send()

    exchanged = jax.ShapeDtypeStruct((rows, 8 * cols), BF16)
    return pl.pallas_call(
        kernel,
        out_shape=(
            exchanged,
            exchanged,
            jax.ShapeDtypeStruct((cols, width), BF16),
            jax.ShapeDtypeStruct(output_part.shape, BF16),
            jax.ShapeDtypeStruct(qkv_part.shape, BF16),
        ),
        in_specs=[ANY] * 5 + [VMEM] * 2,
        out_specs=[ANY] * 3 + [VMEM] * 2,
        scratch_shapes=[
            pltpu.VMEM((depth, cols), BF16),
            pltpu.VMEM((depth, cols), BF16),
            pltpu.VMEM((depth, width), BF16),
            pltpu.VMEM((2, depth, rows), BF16),
            pltpu.VMEM((8, 2, rows, cols), BF16),
            pltpu.VMEM((2, rows, width), BF16),
        ]
        + [pltpu.VMEM(x.shape, BF16) for unused in range(2) for x in sums]
        + [
            pltpu.SemaphoreType.DMA((3,)),
            pltpu.SemaphoreType.DMA((2,)),
            pltpu.SemaphoreType.DMA((2,)),
            pltpu.SemaphoreType.DMA((2,)),
            pltpu.SemaphoreType.DMA((2, 14)),
            pltpu.SemaphoreType.DMA((2, 3, 2 * chunks)),
        ],
        compiler_params=comm_params(collective_id, 62),
        cost_estimate=pl.CostEstimate(
            flops=120_000_000_000, bytes_accessed=80 << 20, transcendentals=0
        ),
        name="finish",
    )(normed, gate_grad, up_grad, activated, down_grad, output_part, qkv_part)


def widen(gate, up, down, out, heads, q_cols):
    rows, wide = gate.shape
    tall, width = down.shape
    n = heads.shape[0]
    steps = 16
    block, high = rows // steps, tall // steps

    def kernel(g_ref, u_ref, d_ref, o_ref, h_ref, g_out, u_out, d_out, o_out, q_out, k_out, v_out):
        g_out[...] = g_ref[...].astype(F32)
        u_out[...] = u_ref[...].astype(F32)
        d_out[...] = d_ref[...].astype(F32)
        o_out[...] = o_ref[...].astype(F32)
        for i in range(n):
            q_out[:, i * q_cols : (i + 1) * q_cols] = h_ref[i, :, :q_cols].astype(F32)
        kv = [h_ref[i, :, q_cols:].astype(F32) for i in range(n)]
        k_out[...] = jnp.concatenate([x[:, :HEAD] for x in kv], axis=1)
        v_out[...] = jnp.concatenate([x[:, HEAD:] for x in kv], axis=1)

    def spec(height, across):
        return pl.BlockSpec((height, across), lambda i: (i, 0))

    shapes = [(rows, wide), (rows, wide), (tall, width), (rows, width)]
    blocks = [spec(block, wide), spec(block, wide), spec(high, width), spec(block, width)]
    narrow = [n * q_cols, n * HEAD, n * HEAD]
    return pl.pallas_call(
        kernel,
        grid=(steps,),
        in_specs=blocks + [pl.BlockSpec((n, block, heads.shape[2]), lambda i: (0, i, 0))],
        out_specs=blocks + [spec(block, across) for across in narrow],
        out_shape=[jax.ShapeDtypeStruct(shape, F32) for shape in shapes]
        + [jax.ShapeDtypeStruct((rows, across), F32) for across in narrow],
        compiler_params=pltpu.CompilerParams(vmem_limit_bytes=62 << 20),
        cost_estimate=pl.CostEstimate(
            flops=4 * rows * wide, bytes_accessed=20 * rows * wide, transcendentals=0
        ),
        name="widen",
    )(gate, up, down, out, heads)


def per_device_plane(
    tokens, attn_gain, query_weight, key_weight, value_weight, output_weight, ffn_gain,
    gate_weight, up_weight, down_weight, dealing, lengths, cotangent,
):
    n = 8
    here = lax.axis_index("shard")
    group = lax.axis_index("rep")
    replicas = lax.axis_size("rep")
    local, width = tokens.shape
    total = local * n
    rows = query_weight.shape[0]
    q_cols = query_weight.shape[1] // n
    ff_cols = gate_weight.shape[1] // n
    core = lax.rem(here, 2)
    half = HEAD // 2
    freq = ROPE_BASE ** (-(jnp.arange(half, dtype=F32) * 2.0) / (2.0 * half))
    freq = jnp.tile(freq, 4)[None, :]

    (
        normed, q, kv, attention, q_weight, kv_weight, gate_cols, up_cols,
        middle, normed_ffn, down_grads, act_grads, cot_own, held,
    ) = front(
        tokens, attn_gain, query_weight, key_weight, value_weight, output_weight, ffn_gain,
        gate_weight, up_weight, down_weight, dealing, lengths, cotangent, freq, replicas,
    )

    def shift(x, by):
        return lax.ppermute(x, "rep", [(i, (i + by) % replicas) for i in range(replicas)])

    def fetch(x):
        return lax.ppermute(x, "shard", [(i, i ^ 1) for i in range(n)])

    before, after = shift(held, 1), shift(held, replicas - 1)
    *filled, normed_ffn_part = ffn_own(
        group.astype(jnp.int32)[None], normed_ffn, act_grads, gate_cols, up_cols
    )
    middle_grad, ffn_gain_part, branch_grad, output_part = pull_gather(
        normed_ffn_part, middle, ffn_gain, cot_own, filled[1], down_weight, dealing.reshape(total, 1), 2
    )
    normed_part, qkv_grad, output_grad = attention_backward(
        branch_grad.reshape(total, width), output_weight, attention, q, kv, normed, q_weight, kv_weight,
        lengths, freq,
    )
    before, after, unused_part = lax.optimization_barrier((before, after, normed_part))
    opposite = shift(before, 1)
    tokens_grad, layer_output, gains, *filled, unused_half, qkv_part = pull_tokens(
        normed_part, output_part, qkv_grad.reshape(n, rows, q_cols + 2 * HEAD), tokens, attn_gain, middle_grad, ffn_gain_part,
        (before, after), act_grads, gate_cols, up_cols, filled, replicas, 3,
    )
    opposite, unused_rows = lax.optimization_barrier((opposite, tokens_grad))
    where = jnp.stack([lax.rem(group + replicas - 2, replicas), core]).astype(jnp.int32)
    filled = ffn_other(where, opposite, fetch(opposite), act_grads, gate_cols, up_cols, filled)
    left, *rights = [x.reshape(replicas * total, -1) for x in (filled[0], filled[2], filled[3])]
    gate_grad, up_grad, down_grad, output_grad, qkv_grad = finish(
        left, *rights, filled[1].reshape(replicas * total, -1), down_grads.reshape(replicas * total, -1),
        output_grad, qkv_part.reshape(width, -1), 4,
    )
    gate_grad, up_grad, down_grad, output_grad, q_grad, k_grad, v_grad = widen(
        gate_grad, up_grad, down_grad, output_grad, qkv_grad.reshape(n, rows, -1), q_cols
    )
    return (
        layer_output, tokens_grad, gains[0], q_grad, k_grad, v_grad, output_grad, gains[1],
        gate_grad, up_grad, down_grad,
    )


def per_device(
    tokens,
    attn_gain,
    query_weight,
    key_weight,
    value_weight,
    output_weight,
    ffn_gain,
    gate_weight,
    up_weight,
    down_weight,
    dealing,
    lengths,
    cotangent,
):
    n = lax.axis_size("shard")
    here = lax.axis_index("shard")
    local, width = tokens.shape
    total = local * n
    rows = query_weight.shape[0]
    ff_cols = gate_weight.shape[1] // n
    q_cols = query_weight.shape[1] // n
    copies = n // KV_HEADS
    own = here * local

    packed = jnp.arange(total, dtype=jnp.int32)
    segment, position = places(packed, lengths[0])
    cos_q, sin_q = rope_tables(position, q_cols)
    cos_k, sin_k = cos_q[:, :HEAD], sin_q[:, :HEAD]
    dealt = (dealing[0][:, None] == packed[None, :]).astype(BF16)

    def column_blocks(weight, cols):
        return weight.reshape(rows, n, cols).transpose(1, 0, 2)

    def head_blocks(weight):
        blocks = weight.reshape(rows, KV_HEADS, HEAD).transpose(1, 0, 2)
        return jnp.repeat(blocks, copies, axis=0)

    spread_cotangent = lax.all_gather(cotangent, ("rep", "shard"), axis=0, tiled=True)
    all_dealing = lax.all_gather(dealing, "rep", axis=0, tiled=True)
    qkv = exchange(
        jnp.concatenate(
            [column_blocks(query_weight, q_cols), head_blocks(key_weight), head_blocks(value_weight)],
            axis=2,
        )
    ).reshape(width, q_cols + 2 * HEAD)
    gate_cols = exchange(column_blocks(gate_weight, ff_cols)).reshape(width, ff_cols)
    up_cols = exchange(column_blocks(up_weight, ff_cols)).reshape(width, ff_cols)

    normed = gather_rows(rms_scale(tokens.astype(F32), attn_gain).astype(BF16))
    pre = mm(normed, qkv)
    queries = rotate(pre[:, :q_cols], cos_q, sin_q).astype(BF16)
    keys = rotate(pre[:, q_cols : q_cols + HEAD], cos_k, sin_k).astype(BF16)
    values = pre[:, q_cols + HEAD :].astype(BF16)
    attention = attention_forward(queries, jnp.concatenate([keys, values], axis=1), lengths)
    branch = scatter_rows(mm(attention, output_weight).astype(BF16))
    middle = tokens.astype(F32) + RESIDUAL_SCALE * branch.astype(F32)
    normed_ffn = gather_rows(rms_scale(middle, ffn_gain).astype(BF16))
    own_normed = lax.dynamic_slice_in_dim(normed_ffn, own, local)
    all_normed = lax.all_gather(own_normed, ("rep", "shard"), axis=0, tiled=True)

    reps = lax.axis_size("rep")
    group = lax.axis_index("rep")
    deals = (all_dealing[:, :, None] == packed[None, None, :]).astype(BF16)
    out_grad_all = lax.dot_general(
        deals,
        spread_cotangent.reshape(reps, total, width),
        (((1,), (1,)), ((0,), (0,))),
        preferred_element_type=F32,
    ).reshape(reps * total, width)
    down_grad_all = (RESIDUAL_SCALE * out_grad_all).astype(BF16)
    out_grad = lax.dynamic_slice_in_dim(out_grad_all, group * total + own, local)
    act_grad_all = mm_t(down_grad_all, down_weight)

    def ffn(rows_in, act_grad):
        gate = mm(rows_in, gate_cols)
        up = mm(rows_in, up_cols)
        sigmoid = jax.nn.sigmoid(gate)
        activated = (gate * sigmoid * up).astype(BF16)
        gate_grad = (act_grad * up * sigmoid * (1.0 + gate * (1.0 - sigmoid))).astype(BF16)
        up_grad = (act_grad * gate * sigmoid).astype(BF16)
        return activated, gate_grad, up_grad

    activated, gate_grad, up_grad = ffn(
        normed_ffn, lax.dynamic_slice_in_dim(act_grad_all, group * total, total)
    )
    normed_ffn_part = (mm_t(gate_grad, gate_cols) + mm_t(up_grad, up_cols)).astype(BF16)
    middle_part, ffn_gain_part = norm_pull(
        middle, ffn_gain, scatter_rows(normed_ffn_part).astype(F32)
    )
    middle_grad = out_grad + middle_part
    branch_grad = gather_rows((RESIDUAL_SCALE * middle_grad).astype(BF16))

    own_columns = lax.dynamic_slice_in_dim(dealt, own, local, axis=1)
    layer_output = scatter_rows(
        (
            RESIDUAL_SCALE * mm(mm(dealt, activated).astype(BF16), down_weight)
            + mm(own_columns, middle.astype(BF16))
        ).astype(BF16)
    )

    attention_grad = mm_t(branch_grad, output_weight).astype(BF16)
    dq, dk, dv = attention_gradients(
        queries, jnp.concatenate([keys, values], axis=1), attention_grad, lengths
    )
    pre_grad = jnp.concatenate(
        [
            unrotate(dq, cos_q, sin_q).astype(BF16),
            unrotate(dk, cos_k, sin_k).astype(BF16),
            dv.astype(BF16),
        ],
        axis=1,
    )
    normed_part = mm_t(pre_grad, qkv).astype(BF16)
    hidden_part, attn_gain_part = norm_pull(
        tokens.astype(F32), attn_gain, scatter_rows(normed_part).astype(F32)
    )
    tokens_grad = middle_grad + hidden_part

    activated, gate_grad, up_grad = ffn(all_normed, act_grad_all)
    gate_part = exchange(t_mm(all_normed, gate_grad).astype(BF16).reshape(n, rows, ff_cols))
    up_part = exchange(t_mm(all_normed, up_grad).astype(BF16).reshape(n, rows, ff_cols))
    down_part = t_mm(activated, down_grad_all)
    output_part = rep_sum(t_mm(attention, branch_grad).astype(BF16))
    qkv_part = rep_sum(exchange(t_mm(normed, pre_grad).astype(BF16).reshape(n, rows, q_cols + 2 * HEAD)))

    def join(blocks):
        return blocks.transpose(1, 0, 2).reshape(rows, -1).astype(F32)

    def join_heads(blocks):
        blocks = blocks.astype(F32).reshape(KV_HEADS, copies, rows, HEAD).sum(axis=1)
        return blocks.transpose(1, 0, 2).reshape(rows, KV_HEADS * HEAD)

    gain_grads = lax.psum(jnp.concatenate([attn_gain_part, ffn_gain_part]), ("rep", "shard"))
    return (
        layer_output,
        tokens_grad,
        gain_grads[0],
        join(qkv_part[:, :, :q_cols]),
        join_heads(qkv_part[:, :, q_cols : q_cols + HEAD]),
        join_heads(qkv_part[:, :, q_cols + HEAD :]),
        output_part.astype(F32),
        gain_grads[1],
        join(gate_part),
        join(up_part),
        down_part,
    )


def solution(mesh):
    both = P(("rep", "shard"), None)
    rowed = P("shard", None)
    return jax.shard_map(
        per_device_plane if (mesh.shape["rep"], mesh.shape["shard"]) == (4, 8) else per_device,
        mesh=mesh,
        in_specs=(
            both, P(), rowed, rowed, rowed, rowed, P(), rowed, rowed, rowed,
            P("rep", None), P("rep", None), both,
        ),
        out_specs=(both, both, P(), rowed, rowed, rowed, rowed, P(), rowed, rowed, rowed),
        check_vma=False,
    )
```

```python
import functools

import jax
import jax.numpy as jnp
from jax import lax
from jax.experimental import pallas as pl
from jax.experimental.pallas import tpu as pltpu
from jax.sharding import PartitionSpec as P

HEADS = 32
KV_HEADS = 8
HEAD = 64
EPSILON = 1e-05
RESIDUAL_SCALE = 0.22
SCORE_SCALE = 0.015625
ROPE_BASE = 10000000.0
MASKED = -1e30
BF16 = jnp.bfloat16
F32 = jnp.float32


def mm(a, b):
    return jnp.dot(a, b, preferred_element_type=F32)


def mm_t(a, b):
    return lax.dot_general(a, b, (((1,), (1,)), ((), ())), preferred_element_type=F32)


def t_mm(a, b):
    return lax.dot_general(a, b, (((0,), (0,)), ((), ())), preferred_element_type=F32)


def rms_scale(hidden, gain_vector):
    return (
        hidden
        * lax.rsqrt(jnp.mean(hidden * hidden, axis=-1, keepdims=True) + EPSILON)
        * gain_vector
    )


def places(packed_index, seq_lengths):
    seq_ends = jnp.cumsum(seq_lengths)
    starts = seq_ends - seq_lengths
    segment = jnp.sum((packed_index[:, None] >= seq_ends[None, :]).astype(jnp.int32), axis=1)
    chosen = segment[:, None] == jnp.arange(seq_lengths.shape[0], dtype=jnp.int32)[None, :]
    position = packed_index - jnp.sum(jnp.where(chosen, starts[None, :], 0), axis=1)
    return segment, position


def rope_tables(position, width):
    half = HEAD // 2
    frequency = ROPE_BASE ** (-(jnp.arange(half, dtype=F32) * 2.0) / (2.0 * half))
    turned = position.astype(F32)[:, None] * frequency[None, :]
    cosine, sine = jnp.cos(turned), jnp.sin(turned)
    cos_full = jnp.concatenate([cosine, cosine], axis=-1)
    sin_full = jnp.concatenate([-sine, sine], axis=-1)
    return jnp.tile(cos_full, (1, width // HEAD)), jnp.tile(sin_full, (1, width // HEAD))


def swap_halves(x):
    rows, width = x.shape
    half = HEAD // 2
    y = x.reshape(rows, width // HEAD, 2, half)
    return jnp.concatenate([y[:, :, 1:], y[:, :, :1]], axis=2).reshape(rows, width)


def rotate(x, cos_full, sin_full):
    return x * cos_full + swap_halves(x) * sin_full


def unrotate(x, cos_full, sin_full):
    return x * cos_full - swap_halves(x) * sin_full


def gather_rows(x):
    return lax.all_gather(x, "shard", axis=0, tiled=True)


def scatter_rows(x):
    return lax.psum_scatter(x, "shard", scatter_dimension=0, tiled=True)


def exchange(blocks):
    return lax.all_to_all(blocks, "shard", split_axis=0, concat_axis=0, tiled=True)


def rep_sum(x):
    count = lax.axis_size("rep")
    where = lax.axis_index("rep")
    half = count // 2
    for hop in range(half - 1):
        moved = lax.ppermute(
            x, "rep", [(hop, hop + 1), (count - 1 - hop, count - 2 - hop)]
        )
        x = (x.astype(F32) + moved.astype(F32)).astype(BF16)
    moved = lax.ppermute(x, "rep", [(half - 1, half), (half, half - 1)])
    x = (x.astype(F32) + moved.astype(F32)).astype(BF16)
    for hop in range(half - 1):
        near, far = half - 1 - hop, half + hop
        moved = lax.ppermute(x, "rep", [(near, near - 1), (far, far + 1)])
        x = jnp.where((where == near - 1) | (where == far + 1), moved, x)
    return x


MESH = pl.DeviceIdType.MESH


def flip(index, bits):
    for weight in (1, 2, 4):
        if bits & weight:
            index = index + weight - 2 * weight * lax.rem(lax.div(index, weight), 2)
    return index


def send(src, dst, sems, k, target):
    return pltpu.make_async_remote_copy(
        src_ref=src,
        dst_ref=dst,
        send_sem=sems.at[0, k],
        recv_sem=sems.at[1, k],
        device_id={"shard": target},
        device_id_type=MESH,
    )


def greet(me, masks):
    barrier = pltpu.get_barrier_semaphore()
    for mask in masks:
        pl.semaphore_signal(
            barrier, inc=1, device_id={"shard": flip(me, mask)}, device_id_type=MESH
        )
    pl.semaphore_wait(barrier, len(masks))


GATHER_SEMS = 13
BULK = (12, 2, 2)


def gather_steps(me, out, sems):
    core, px, py, diag = (flip(me, mask) for mask in (1, 2, 4, 6))
    half = out.shape[1] // 2
    low, high, whole = pl.ds(0, half), pl.ds(half, half), pl.ds(0, 2 * half)

    def move(k, block, rows, target):
        ref = out.at[block, rows]
        copy = send(ref, ref, sems, k, target)
        copy.start()
        return copy

    x_low, y_high = move(0, me, low, px), move(1, me, high, py)
    own = move(2, me, whole, core)
    x_high, y_low = move(3, me, high, px), move(4, me, low, py)
    yield
    x_low.wait_recv()
    diag_low = move(5, px, low, py)
    pieces = [own, move(6, px, low, core)]
    yield
    y_high.wait_recv()
    diag_high = move(7, py, high, px)
    pieces.append(move(8, py, high, core))
    yield
    x_high.wait_recv()
    pieces.append(move(9, px, high, core))
    yield
    y_low.wait_recv()
    pieces.append(move(10, py, low, core))
    yield
    diag_low.wait_recv()
    pieces.append(move(11, diag, low, core))
    diag_high.wait_recv()
    pieces.append(move(12, diag, high, core))
    yield
    for copy in pieces:
        copy.wait_recv()
    for copy in [x_low, y_high, x_high, y_low, diag_low, diag_high] + pieces:
        copy.wait_send()


def gather_blocks(me, out, sems):
    for unused_step in gather_steps(me, out, sems):
        pass


SCATTER_SEMS = 10


def scatter_steps(me, partial, sib_out, sib_in, acc, x_out, x_in, y_out, y_in, sems):
    core, px, py = (flip(me, mask) for mask in (1, 2, 4))
    half = acc.shape[1] // 2
    masks = (6, 2, 4, 0)
    low, high = pl.ds(0, half), pl.ds(half, half)
    copies = []

    def move(src, dst, k, target):
        copy = send(src, dst, sems, k, target)
        copy.start()
        copies.append(copy)
        return copy

    inside = []
    for i, mask in enumerate(masks):
        sib_out[i] = partial(flip(core, mask)).astype(BF16)
        inside.append(move(sib_out.at[i], sib_in.at[i], i, core))
    yield
    for i, mask in enumerate(masks):
        term = partial(flip(me, mask))
        inside[i].wait_recv()
        acc[i] = term + sib_in[i].astype(F32)
        if mask == 6:
            x_out[0] = acc[i, low].astype(BF16)
            x_diag = move(x_out.at[0], x_in.at[0], 4, px)
            y_out[0] = acc[i, high].astype(BF16)
            y_diag = move(y_out.at[0], y_in.at[0], 5, py)
        if mask == 2:
            x_out[1] = acc[i, low].astype(BF16)
            x_near = move(x_out.at[1], x_in.at[1], 6, px)
        if mask == 4:
            y_out[1] = acc[i, high].astype(BF16)
            y_near = move(y_out.at[1], y_in.at[1], 7, py)
    yield
    x_diag.wait_recv()
    y_out[2] = (acc[2, low] + x_in[0].astype(F32)).astype(BF16)
    y_last = move(y_out.at[2], y_in.at[2], 8, py)
    y_diag.wait_recv()
    x_out[2] = (acc[1, high] + y_in[0].astype(F32)).astype(BF16)
    x_last = move(x_out.at[2], x_in.at[2], 9, px)
    yield
    x_near.wait_recv()
    y_near.wait_recv()
    y_last.wait_recv()
    acc[3, low] = acc[3, low] + x_in[1].astype(F32) + y_in[2].astype(F32)
    x_last.wait_recv()
    acc[3, high] = acc[3, high] + y_in[1].astype(F32) + x_in[2].astype(F32)
    yield
    for copy in copies:
        copy.wait_send()


def scatter_blocks(me, partial, *buffers):
    for unused_step in scatter_steps(me, partial, *buffers):
        pass
    return buffers[2][3]


def scatter_scratch(rows, width):
    half = rows // 2
    return [
        pltpu.VMEM((4, rows, width), BF16),
        pltpu.VMEM((4, rows, width), BF16),
        pltpu.VMEM((4, rows, width), F32),
        pltpu.VMEM((3, half, width), BF16),
        pltpu.VMEM((3, half, width), BF16),
        pltpu.VMEM((3, half, width), BF16),
        pltpu.VMEM((3, half, width), BF16),
        pltpu.SemaphoreType.DMA((2, SCATTER_SEMS)),
    ]


VMEM = pl.BlockSpec(memory_space=pltpu.VMEM)
SMEM = pl.BlockSpec(memory_space=pltpu.SMEM)
ANY = pl.BlockSpec(memory_space=pl.ANY)


def comm_params(collective_id, mebibytes):
    return pltpu.CompilerParams(
        collective_id=collective_id, has_side_effects=True, vmem_limit_bytes=mebibytes << 20
    )


def front(
    tokens, attn_gain, query_weight, key_weight, value_weight, output_weight, ffn_gain,
    gate_weight, up_weight, down_weight, dealing, lengths, cotangent, freq, replicas,
):
    local, width = tokens.shape
    total = 8 * local
    shard_rows = query_weight.shape[0]
    q_cols = query_weight.shape[1] // 8
    ff_cols = gate_weight.shape[1] // 8
    block = 256
    others = (1, 2, 3, 4, 5, 6, 7)

    def kernel(
        tok_ref, gain_ref, wq_hbm, wk_ref, wv_ref, wo_ref, fgain_ref, wg_hbm, wu_hbm,
        wd_ref, deal_ref, len_ref, cot_ref, freq_ref,
        n_ref, q_ref, kv_ref, att_ref, qw_ref, kvw_ref, wg_out, wu_out, mid_ref, nf_ref, dg_out, ag_out, cot_out, half_out,
        kv_stage, c_all, dg_own, ag_stage,
        sib_out, sib_in, acc, x_out, x_in, y_out, y_in, scatter_sems,
        n_sems, c_sems, nf_sems, qkv_sems, bulk_sems, ring_sems, pair_sems, local_sems,
    ):
        me = lax.axis_index("shard")
        group = lax.axis_index("rep")
        core = lax.rem(me, 2)
        after = lax.rem(group + 1, replicas)
        before = lax.rem(group + replicas - 1, replicas)

        barrier = pltpu.get_barrier_semaphore()
        for mask in others:
            pl.semaphore_signal(
                barrier, inc=1, device_id={"shard": flip(me, mask)}, device_id_type=MESH
            )
        for neighbour in (after, before):
            pl.semaphore_signal(
                barrier, inc=1, device_id={"rep": neighbour}, device_id_type=MESH
            )
        c_all[me] = cot_ref[...]
        for d in range(8):
            lanes = slice(d * HEAD, (d + 1) * HEAD)
            kv_stage[d] = jnp.concatenate([wk_ref[:, lanes], wv_ref[:, lanes]], axis=1)
        pl.semaphore_wait(barrier, len(others) + 2)

        gather_c = gather_steps(me, c_all, c_sems)
        next(gather_c)
        n_ref[me] = rms_scale(tok_ref[...].astype(F32), gain_ref[...]).astype(BF16)
        weights = []
        for mask in others:
            peer = flip(me, mask)
            columns = pl.ds(pl.multiple_of(peer * q_cols, q_cols), q_cols)
            weights.append(send(wq_hbm.at[:, columns], qw_ref.at[me], qkv_sems, 2 * mask - 2, peer))
            weights.append(send(kv_stage.at[peer], kvw_ref.at[me], qkv_sems, 2 * mask - 1, peer))
        own_columns = pl.ds(pl.multiple_of(me * ff_cols, ff_cols), ff_cols)
        own_q = pl.ds(pl.multiple_of(me * q_cols, q_cols), q_cols)
        gate_slot, up_slot = ag_stage.at[:shard_rows], ag_stage.at[pl.ds(shard_rows, shard_rows)]
        kept = [
            pltpu.make_async_copy(wg_hbm.at[:, own_columns], gate_slot, local_sems.at[0]),
            pltpu.make_async_copy(wu_hbm.at[:, own_columns], up_slot, local_sems.at[1]),
            pltpu.make_async_copy(wq_hbm.at[:, own_q], qw_ref.at[me], local_sems.at[2]),
        ]
        for copy in kept:
            copy.start()
        kvw_ref[me] = kv_stage[me]

        bulk, waiting = [], []
        for source, target in ((wg_hbm, wg_out), (wu_hbm, wu_out)):
            for part in range(2):
                rows = pl.ds(part * (shard_rows // 2), shard_rows // 2)
                for mask in (2, 4, 6, 3, 5, 7, 1):
                    waiting.append((source, target, rows, mask))

        def more(count):
            for unused in range(min(count, len(waiting))):
                source, target, rows, mask = waiting.pop(0)
                peer = flip(me, mask)
                columns = pl.ds(pl.multiple_of(peer * ff_cols, ff_cols), ff_cols)
                copy = send(
                    source.at[rows, columns], target.at[me, rows], bulk_sems, len(bulk), peer
                )
                copy.start()
                bulk.append(copy)

        for unused in gather_c:
            pass
        gather_n = gather_steps(me, n_ref, n_sems)
        next(gather_n)
        for copy in weights:
            copy.start()

        def permute(first):
            def step(i, carry):
                row0 = pl.multiple_of(first + i * block, block)
                packed = row0 + lax.broadcasted_iota(jnp.int32, (block, total), 0)
                chosen = (deal_ref[...] == packed).astype(BF16)
                dealt = mm(chosen, c_all[...].reshape(total, width))
                dg_own[pl.ds(row0, block), :] = (RESIDUAL_SCALE * dealt).astype(BF16)
                return carry

            lax.fori_loop(0, total // 2 // block, step, 0)

        near = pl.multiple_of(core * (total // 2), total // 2)
        far = pl.multiple_of((1 - core) * (total // 2), total // 2)
        half = pl.ds(near, total // 2)

        opposite = lax.rem(group + 2, replicas)
        held_groups = (before, after, opposite)

        def pass_on(k):
            ref = dg_out.at[before if k == 2 else group, half]
            copy = pltpu.make_async_remote_copy(
                src_ref=ref if k == 2 else dg_own.at[half],
                dst_ref=ref,
                send_sem=ring_sems.at[0, k],
                recv_sem=ring_sems.at[1, k],
                device_id={"rep": before if k == 1 else after},
                device_id_type=MESH,
            )
            copy.start()
            return copy

        def share(k):
            ref = dg_out.at[held_groups[k], half]
            copy = send(ref, ref, pair_sems, k, flip(me, 1))
            copy.start()
            return copy

        permute(near)
        hops = [pass_on(0)]
        for unused in range(4):
            next(gather_n)
        permute(far)
        packed = me * local + lax.broadcasted_iota(jnp.int32, (local, total), 0)
        chosen = (deal_ref[...] == packed).astype(BF16)
        cot_out[...] = mm(chosen, c_all[...].reshape(total, width)).astype(BF16)
        store = pltpu.make_async_copy(dg_own, dg_out.at[group], local_sems.at[3])
        store.start()
        for unused in gather_n:
            pass
        for copy in kept:
            copy.wait()
        kept = [
            pltpu.make_async_copy(gate_slot, wg_out.at[me], local_sems.at[0]),
            pltpu.make_async_copy(up_slot, wu_out.at[me], local_sems.at[1]),
        ]
        for copy in kept:
            copy.start()
        for copy in weights:
            copy.wait_recv()
        more(BULK[0])
        def project(i, carry):
            row0 = pl.multiple_of(i * block, block)
            rows = pl.ds(row0, block)
            x = n_ref[pl.ds(i * (block // local), block // local)].reshape(block, width)
            cosine, sine = lane_rope(row0, block, freq_ref[...], len_ref)
            pre = mm(x, qw_ref[...].reshape(width, q_cols))
            for j in range(q_cols // (2 * HEAD)):
                lanes = slice(j * 2 * HEAD, (j + 1) * 2 * HEAD)
                y = pre[:, lanes]
                q_ref[rows, lanes] = (y * cosine + lane_swap(y) * sine).astype(BF16)
            cosine, sine = keys_only(cosine, sine)
            y = mm(x, kvw_ref[...].reshape(width, 2 * HEAD))
            kv_ref[rows, :] = (y * cosine + lane_swap(y) * sine).astype(BF16)
            return carry

        lax.fori_loop(0, total // block, project, 0)
        hops.append(pass_on(1))
        attend(q_cols // HEAD, block, q_ref, kv_ref, len_ref, att_ref)

        def partial(d):
            return mm(att_ref[pl.ds(pl.multiple_of(d * local, local), local), :], wo_ref[...])

        pending = {}

        def act_grad(held, first, loaded):
            rows = pl.ds(first, total // 2)
            if not loaded:
                load = pltpu.make_async_copy(
                    dg_out.at[held, rows], dg_own.at[rows], local_sems.at[3]
                )
                load.start()
                load.wait()
            slot = 0 if first is near else 1
            if slot in pending:
                pending[slot].wait()

            def step(i, carry):
                part = pl.ds(pl.multiple_of(first + i * block, block), block)
                ag_stage[part, :] = mm_t(dg_own[part, :], wd_ref[...]).astype(BF16)
                return carry

            lax.fori_loop(0, total // 2 // block, step, 0)
            pending[slot] = pltpu.make_async_copy(
                ag_stage.at[rows], ag_out.at[held, rows], local_sems.at[5 + slot]
            )
            pending[slot].start()

        hops[0].wait_recv()
        hops.append(pass_on(2))
        shares = [share(0)]
        scatter = scatter_steps(
            me, partial, sib_out, sib_in, acc, x_out, x_in, y_out, y_in, scatter_sems
        )
        next(scatter)
        more(BULK[1])
        for unused in scatter:
            pass
        branch = acc[3]
        middle = tok_ref[...].astype(F32) + RESIDUAL_SCALE * branch
        mid_ref[...] = middle
        nf_ref[me] = rms_scale(middle, fgain_ref[...]).astype(BF16)
        gather_nf = gather_steps(me, nf_ref, nf_sems)
        next(gather_nf)
        more(BULK[2])
        for unused in gather_nf:
            pass
        more(len(waiting))
        give = pltpu.make_async_copy(nf_ref.at[pl.ds(4 * core, 4)], half_out, local_sems.at[4])
        give.start()
        store.wait()
        for copy in kept:
            copy.wait()
        act_grad(group, near, True)
        act_grad(group, far, True)
        hops[0].wait_send()
        hops[1].wait_send()
        for k in range(3):
            if k > 0:
                hops[k].wait_recv()
                shares.append(share(k))
            act_grad(held_groups[k], near, False)
            shares[k].wait_recv()
            act_grad(held_groups[k], far, False)
        for copy in pending.values():
            copy.wait()
        give.wait()
        for copy in bulk:
            copy.wait_recv()
        for copy in weights + bulk + hops[2:] + shares:
            copy.wait_send()

    rows8 = jax.ShapeDtypeStruct((8, local, width), BF16)
    half_sems = pltpu.SemaphoreType.DMA
    outs = pl.pallas_call(
        kernel,
        out_shape=(
            rows8,
            jax.ShapeDtypeStruct((total, q_cols), BF16),
            jax.ShapeDtypeStruct((total, 2 * HEAD), BF16),
            jax.ShapeDtypeStruct((total, q_cols), BF16),
            jax.ShapeDtypeStruct((8, shard_rows, q_cols), BF16),
            jax.ShapeDtypeStruct((8, shard_rows, 2 * HEAD), BF16),
            jax.ShapeDtypeStruct((8, shard_rows, ff_cols), BF16),
            jax.ShapeDtypeStruct((8, shard_rows, ff_cols), BF16),
            jax.ShapeDtypeStruct((local, width), F32),
            rows8,
            jax.ShapeDtypeStruct((replicas, total, width), BF16),
            jax.ShapeDtypeStruct((replicas, total, ff_cols), BF16),
            jax.ShapeDtypeStruct((local, width), BF16),
            jax.ShapeDtypeStruct((4, local, width), BF16),
        ),
        in_specs=[VMEM, VMEM, ANY, VMEM, VMEM, VMEM, VMEM, ANY, ANY, VMEM, VMEM, SMEM, VMEM, VMEM],
        out_specs=[VMEM] * 6 + [ANY, ANY, VMEM, VMEM, ANY, ANY, VMEM, ANY],
        scratch_shapes=[
            pltpu.VMEM((8, shard_rows, 2 * HEAD), BF16),
            pltpu.VMEM((8, local, width), BF16),
            pltpu.VMEM((total, width), BF16),
            pltpu.VMEM((total, ff_cols), BF16),
        ]
        + scatter_scratch(local, width)
        + [
            half_sems((2, GATHER_SEMS)),
            half_sems((2, GATHER_SEMS)),
            half_sems((2, GATHER_SEMS)),
            half_sems((2, 14)),
            half_sems((2, 28)),
            half_sems((2, replicas)),
            half_sems((2, replicas)),
            half_sems((7,)),
        ],
        compiler_params=comm_params(0, 56),
        cost_estimate=pl.CostEstimate(
            flops=200_000_000_000, bytes_accessed=50 << 20, transcendentals=total * total
        ),
        name="front",
    )(
        tokens, attn_gain[None, :], query_weight, key_weight, value_weight, output_weight,
        ffn_gain[None, :], gate_weight, up_weight, down_weight, dealing, lengths, cotangent, freq,
    )
    normed, q, kv, attention, qw, kvw, wg, wu, middle, nf, dg, ag, cot, held = outs
    return (
        normed.reshape(total, width), q, kv, attention,
        qw.reshape(width, q_cols), kvw.reshape(width, 2 * HEAD),
        wg.reshape(width, ff_cols), wu.reshape(width, ff_cols),
        middle, nf.reshape(total, width), dg, ag, cot,
        held.reshape(total // 2, width),
    )


def norm_pull(x, gain, grad):
    scale = lax.rsqrt(jnp.mean(x * x, axis=-1, keepdims=True) + EPSILON)
    pulled = gain * grad
    rows_part = scale * pulled - x * (
        scale * scale * scale * jnp.mean(pulled * x, axis=-1, keepdims=True)
    )
    return rows_part, jnp.sum(grad * x * scale, axis=0, keepdims=True)


def pull_gather(part, middle, gain, out_grad, activated, down_weight, deal, collective_id):
    rows, width = middle.shape
    groups, total, cols = activated.shape
    block = 256

    def kernel(
        p_ref, m_ref, gain_ref, g_ref, act_hbm, wd_ref, deal_ref,
        mg_ref, gain_part, out, dealt_ref, act_ref, packed_ref, act_sem, *scratch,
    ):
        me = lax.axis_index("shard")
        *buffers, scatter_sems, sems = scratch
        load = pltpu.make_async_copy(act_hbm.at[lax.axis_index("rep")], act_ref, act_sem.at[0])
        load.start()
        greet(me, (1, 2, 4))

        def down(i, carry):
            chunk = pl.ds(pl.multiple_of(i * block, block), block)
            packed_ref[chunk, :] = (RESIDUAL_SCALE * mm(act_ref[chunk, :], wd_ref[...])).astype(BF16)
            return carry

        def deal_out(i, carry):
            chunk = pl.ds(pl.multiple_of(i * block, block), block)
            packed = lax.broadcasted_iota(jnp.int32, (block, total), 1)
            chosen = (deal_ref[chunk, :] == packed).astype(BF16)
            dealt_ref[chunk, :] = mm(chosen, packed_ref[...]).astype(BF16)
            return carry

        half = total // block // 2
        scatter = scatter_steps(
            me,
            lambda d: p_ref[pl.ds(pl.multiple_of(d * rows, rows), rows), :].astype(F32),
            *buffers,
            scatter_sems,
        )
        next(scatter)
        load.wait()
        lax.fori_loop(0, half, down, 0)
        next(scatter)
        lax.fori_loop(half, 2 * half, down, 0)
        own = pl.ds(pl.multiple_of(me * rows, rows), rows)
        packed_ref[own, :] = (packed_ref[own, :].astype(F32) + m_ref[...]).astype(BF16)
        next(scatter)
        for unused in scatter:
            pass
        rows_part, gain_row = norm_pull(m_ref[...], gain_ref[...], buffers[2][3])
        gain_part[...] = gain_row
        middle_grad = g_ref[...].astype(F32) + rows_part
        mg_ref[...] = middle_grad
        out[me] = (RESIDUAL_SCALE * middle_grad).astype(BF16)
        gather = gather_steps(me, out, sems)
        next(gather)
        lax.fori_loop(0, half, deal_out, 0)
        for unused in range(2):
            next(gather)
        lax.fori_loop(half, 2 * half, deal_out, 0)
        for unused in gather:
            pass

    return pl.pallas_call(
        kernel,
        out_shape=(
            jax.ShapeDtypeStruct((rows, width), F32),
            jax.ShapeDtypeStruct((1, width), F32),
            jax.ShapeDtypeStruct((8, rows, width), BF16),
            jax.ShapeDtypeStruct((total, width), BF16),
        ),
        in_specs=[VMEM] * 4 + [ANY] + [VMEM] * 2,
        out_specs=[VMEM] * 4,
        scratch_shapes=[
            pltpu.VMEM((total, cols), BF16),
            pltpu.VMEM((total, width), BF16),
            pltpu.SemaphoreType.DMA((1,)),
        ]
        + scatter_scratch(rows, width)
        + [pltpu.SemaphoreType.DMA((2, GATHER_SEMS))],
        compiler_params=comm_params(collective_id, 56),
        cost_estimate=pl.CostEstimate(
            flops=60_000_000_000, bytes_accessed=50 * rows * width, transcendentals=rows
        ),
        name="pull_gather",
    )(part, middle, gain[None, :], out_grad, activated, down_weight, deal)


def pull_tokens(
    part, out_part, hidden, gain, middle_grad, other_gain, near, act_grads, wg, wu, filled, replicas, collective_id
):
    rows, width = middle_grad.shape
    groups, total, cols = act_grads.shape
    block = 256
    levels = [("shard", 1), ("shard", 2), ("shard", 4)]
    level = 1
    while level < replicas:
        levels.append(("rep", level))
        level *= 2
    per_half = total // 2 // block

    def kernel(
        p_ref, o_ref, h_ref, gain_ref, mg_ref, og_ref, wg_ref, wu_ref, ag_hbm,
        before_held, after_held, unused_na, unused_act, unused_gg, unused_ug,
        out, lay, gains, na_hbm, act_hbm, gg_hbm, ug_hbm, fetched, share_sems,
        nf_buf, ag_buf, done_buf, in_sems, out_sems, gain_in, gain_out, gain_sems, *scratch,
    ):
        me = lax.axis_index("shard")
        group = lax.axis_index("rep")
        core = lax.rem(me, 2)
        before = lax.rem(group + replicas - 1, replicas)
        after = lax.rem(group + 1, replicas)
        first, second = scratch[:8], scratch[8:]
        parts = (
            (before, before_held, core),
            (after, after_held, core),
            (before, fetched.at[0], 1 - core),
            (after, fetched.at[1], 1 - core),
        )

        def rows_of(p, r):
            return pl.ds(pl.multiple_of((parts[p][2] * per_half + r) * block, block), block)

        def loads(p, r):
            held, source, unused = parts[p]
            slot = (p % 2) * per_half + r
            return [
                pltpu.make_async_copy(
                    source.at[pl.ds(pl.multiple_of(r * block, block), block)],
                    nf_buf.at[slot],
                    in_sems.at[0, slot],
                ),
                pltpu.make_async_copy(ag_hbm.at[held, rows_of(p, r)], ag_buf.at[slot], in_sems.at[1, slot]),
            ]

        def stores(p, r):
            held = parts[p][0]
            slot = (p % 2) * per_half + r
            where = rows_of(p, r)
            return [
                pltpu.make_async_copy(nf_buf.at[slot], na_hbm.at[held, where], out_sems.at[0, slot])
            ] + [
                pltpu.make_async_copy(done_buf.at[k, slot], target.at[held, where], out_sems.at[k + 1, slot])
                for k, target in enumerate((act_hbm, gg_hbm, ug_hbm))
            ]

        def start_loads(p):
            for r in range(per_half):
                for copy in loads(p, r):
                    copy.start()

        def wait_stores(p):
            for r in range(per_half):
                for copy in stores(p, r):
                    copy.wait()

        def fill(p):
            if p > 0:
                wait_stores(p - 1)
            if p in (1, 2):
                shares[p - 1].wait_recv()
            if p + 1 < len(parts):
                start_loads(p + 1)

            def step(r, carry):
                slot = (p % 2) * per_half + r
                for copy in loads(p, r):
                    copy.wait()
                results = ffn_rows(nf_buf[slot], ag_buf[slot], wg_ref[...], wu_ref[...])
                for k, result in enumerate(results):
                    done_buf[k, slot] = result
                for copy in stores(p, r):
                    copy.start()
                return carry

            lax.fori_loop(0, per_half, step, 0)

        start_loads(0)
        barrier = pltpu.get_barrier_semaphore()
        peers = []
        for axis, weight in levels:
            index = me if axis == "shard" else group
            peers.append({axis: index + weight - 2 * weight * lax.rem(lax.div(index, weight), 2)})
        for peer in peers:
            pl.semaphore_signal(barrier, inc=1, device_id=peer, device_id_type=MESH)
        pl.semaphore_wait(barrier, len(peers))

        def blocks_of(ref):
            return lambda d: ref[pl.ds(pl.multiple_of(d * rows, rows), rows), :].astype(F32)

        grads = scatter_steps(me, blocks_of(p_ref), *first)
        outputs = scatter_steps(me, blocks_of(o_ref), *second)
        next(grads)
        next(outputs)
        shares = [
            send(source, fetched.at[k], share_sems, k, flip(me, 1))
            for k, source in enumerate((before_held, after_held))
        ]
        for copy in shares:
            copy.start()
        fill(0)
        next(grads)
        fill(1)
        next(grads)
        next(outputs)
        fill(2)
        next(grads)
        next(outputs)
        rows_part, gain_row = norm_pull(h_ref[...].astype(F32), gain_ref[...], first[2][3])
        out[...] = mg_ref[...] + rows_part
        sums = jnp.concatenate([gain_row, og_ref[...]], axis=0)
        for i, peer in enumerate(peers):
            gain_out[i] = sums
            copy = pltpu.make_async_remote_copy(
                src_ref=gain_out.at[i],
                dst_ref=gain_in.at[i],
                send_sem=gain_sems.at[0, i],
                recv_sem=gain_sems.at[1, i],
                device_id=peer,
                device_id_type=MESH,
            )
            copy.start()
            if i == 0:
                fill(3)
            copy.wait()
            sums = sums + gain_in[i]
        gains[...] = sums
        next(outputs)
        lay[...] = second[2][3].astype(BF16)
        for steps in (grads, outputs):
            for unused in steps:
                pass
        wait_stores(3)
        for copy in shares:
            copy.wait_send()

    hidden_shape = jax.ShapeDtypeStruct((groups, total, cols), BF16)
    return pl.pallas_call(
        kernel,
        out_shape=(
            jax.ShapeDtypeStruct((rows, width), F32),
            jax.ShapeDtypeStruct((rows, width), BF16),
            jax.ShapeDtypeStruct((2, width), F32),
            jax.ShapeDtypeStruct((groups, total, width), BF16),
            hidden_shape,
            hidden_shape,
            hidden_shape,
            jax.ShapeDtypeStruct((2, total // 2, width), BF16),
        ),
        in_specs=[VMEM] * 8 + [ANY] * 7,
        out_specs=[VMEM] * 3 + [ANY] * 5,
        input_output_aliases={11: 3, 12: 4, 13: 5, 14: 6},
        scratch_shapes=[
            pltpu.SemaphoreType.DMA((2, 2)),
            pltpu.VMEM((2 * per_half, block, width), BF16),
            pltpu.VMEM((2 * per_half, block, cols), BF16),
            pltpu.VMEM((3, 2 * per_half, block, cols), BF16),
            pltpu.SemaphoreType.DMA((2, 2 * per_half)),
            pltpu.SemaphoreType.DMA((4, 2 * per_half)),
            pltpu.VMEM((len(levels), 2, width), F32),
            pltpu.VMEM((len(levels), 2, width), F32),
            pltpu.SemaphoreType.DMA((2, len(levels))),
        ]
        + scatter_scratch(rows, width)
        + scatter_scratch(rows, width),
        compiler_params=comm_params(collective_id, 62),
        cost_estimate=pl.CostEstimate(
            flops=60_000_000_000, bytes_accessed=50 * rows * width, transcendentals=rows
        ),
        name="pull_tokens",
    )(
        part, out_part, hidden, gain[None, :], middle_grad, other_gain, wg, wu, act_grads, *near, *filled
    )


def softmax_block(q, k, allowed):
    scores = SCORE_SCALE * mm_t(q, k)
    scores = jnp.where(allowed, scores, MASKED)
    top = jnp.max(scores, axis=-1, keepdims=True)
    weight = jnp.exp(scores - top)
    return weight * (1.0 / jnp.sum(weight, axis=-1, keepdims=True))


def allowed_block(row0, cols, start):
    shape = (start.shape[0], cols)
    query = row0 + lax.broadcasted_iota(jnp.int32, shape, 0)
    key = lax.broadcasted_iota(jnp.int32, shape, 1)
    return (key >= start) & (key <= query)


def sequence_starts(row0, shape, lengths_ref):
    row = row0 + lax.broadcasted_iota(jnp.int32, shape, 0)
    start = jnp.zeros(shape, jnp.int32)
    end = 0
    for i in range(lengths_ref.shape[1]):
        length = lengths_ref[0, i]
        end = end + length
        start = start + jnp.where(row >= end, length, 0)
    return start


def attend(heads, block, q_ref, kv_ref, lengths_ref, o_ref):
    total = kv_ref.shape[0]
    for i in range(total // block):
        cols = (i + 1) * block
        rows = pl.ds(i * block, block)
        allowed = allowed_block(
            i * block, cols, sequence_starts(i * block, (block, 1), lengths_ref)
        )
        kv = kv_ref[:cols, :]
        k, v = kv[:, :HEAD], kv[:, HEAD:]
        for h in range(heads):
            lanes = slice(h * HEAD, (h + 1) * HEAD)
            probs = softmax_block(q_ref[rows, lanes], k, allowed)
            o_ref[rows, lanes] = mm(probs.astype(BF16), v).astype(BF16)


def attend_back(heads, block, q_ref, kv_ref, g_ref, lengths_ref, dq_ref, dk_ref, dv_ref):
    total = kv_ref.shape[0]
    dk_ref[...] = jnp.zeros_like(dk_ref)
    dv_ref[...] = jnp.zeros_like(dv_ref)
    for i in range(total // block):
        cols = (i + 1) * block
        rows = pl.ds(i * block, block)
        allowed = allowed_block(
            i * block, cols, sequence_starts(i * block, (block, 1), lengths_ref)
        )
        kv = kv_ref[:cols, :]
        k, v = kv[:, :HEAD], kv[:, HEAD:]
        for h in range(heads):
            lanes = slice(h * HEAD, (h + 1) * HEAD)
            q, g = q_ref[rows, lanes], g_ref[rows, lanes]
            probs = softmax_block(q, k, allowed)
            probs_grad = mm_t(g, v)
            delta = jnp.sum(probs * probs_grad, axis=-1, keepdims=True)
            score_grad = (probs * (probs_grad - delta)).astype(BF16)
            dq_ref[rows, lanes] = SCORE_SCALE * mm(score_grad, k)
            dk_ref[:cols, :] += SCORE_SCALE * t_mm(score_grad, q)
            dv_ref[:cols, :] += t_mm(probs.astype(BF16), g)


def attention_forward(q, kv, lengths):
    total, width = q.shape

    def kernel(q_ref, kv_ref, lengths_ref, o_ref):
        attend(width // HEAD, 256, q_ref, kv_ref, lengths_ref, o_ref)

    return pl.pallas_call(
        kernel,
        out_shape=jax.ShapeDtypeStruct((total, width), BF16),
        in_specs=[VMEM, VMEM, SMEM],
        out_specs=VMEM,
        compiler_params=pltpu.CompilerParams(vmem_limit_bytes=40 << 20),
        name="attention_forward",
    )(q, kv, lengths)


def attention_gradients(q, kv, grad, lengths):
    total, width = q.shape

    def kernel(q_ref, kv_ref, g_ref, lengths_ref, dq_ref, dk_ref, dv_ref):
        attend_back(width // HEAD, 256, q_ref, kv_ref, g_ref, lengths_ref, dq_ref, dk_ref, dv_ref)

    return pl.pallas_call(
        kernel,
        out_shape=(
            jax.ShapeDtypeStruct((total, width), F32),
            jax.ShapeDtypeStruct((total, HEAD), F32),
            jax.ShapeDtypeStruct((total, HEAD), F32),
        ),
        in_specs=[VMEM, VMEM, VMEM, SMEM],
        out_specs=[VMEM] * 3,
        compiler_params=pltpu.CompilerParams(vmem_limit_bytes=40 << 20),
        name="attention_gradients",
    )(q, kv, grad, lengths)


def lane_rope(row0, rows, freq, lengths_ref):
    shape = (rows, 2 * HEAD)
    row = row0 + lax.broadcasted_iota(jnp.int32, shape, 0)
    position = row - sequence_starts(row0, shape, lengths_ref)
    turned = position.astype(F32) * freq
    lane = lax.broadcasted_iota(jnp.int32, shape, 1)
    first = lax.rem(lane, HEAD) < HEAD // 2
    sine = jnp.sin(turned)
    return jnp.cos(turned), jnp.where(first, -sine, sine)


def lane_swap(x):
    half = HEAD // 2
    lane = lax.broadcasted_iota(jnp.int32, x.shape, 1)
    first = lax.rem(lane, HEAD) < half
    return jnp.where(first, pltpu.roll(x, 2 * HEAD - half, 1), pltpu.roll(x, half, 1))


def keys_only(cosine, sine):
    lane = lax.broadcasted_iota(jnp.int32, cosine.shape, 1)
    return jnp.where(lane < HEAD, cosine, 1.0), jnp.where(lane < HEAD, sine, 0.0)


def attention_backward(
    branch_grad, output_weight, attention, q, kv, normed, q_weight, kv_weight, lengths, freq
):
    total, q_cols = q.shape
    width = normed.shape[1]
    block = 256

    def kernel(
        bg_ref, wo_ref, a_ref, q_ref, kv_ref, n_ref, qw_ref, kvw_ref, len_ref, freq_ref,
        dn_ref, dqkv_ref, dwo_ref, g_ref, dq_ref, dk_ref, dv_ref, pq_ref, pkv_ref,
    ):
        def open_up(i, carry):
            rows = pl.ds(pl.multiple_of(i * block, block), block)
            g_ref[rows, :] = mm_t(bg_ref[rows, :], wo_ref[...]).astype(BF16)
            return carry

        lax.fori_loop(0, total // block, open_up, 0)
        attend_back(
            q_cols // HEAD, block, q_ref, kv_ref, g_ref, len_ref, dq_ref, dk_ref, dv_ref
        )
        def close_up(i, carry):
            row0 = pl.multiple_of(i * block, block)
            rows = pl.ds(row0, block)
            cosine, sine = lane_rope(row0, block, freq_ref[...], len_ref)
            for j in range(q_cols // (2 * HEAD)):
                lanes = slice(j * 2 * HEAD, (j + 1) * 2 * HEAD)
                x = dq_ref[rows, lanes]
                pq_ref[rows, lanes] = (x * cosine - lane_swap(x) * sine).astype(BF16)
            cosine, sine = keys_only(cosine, sine)
            x = jnp.concatenate([dk_ref[rows, :], dv_ref[rows, :]], axis=1)
            pkv_ref[rows, :] = (x * cosine - lane_swap(x) * sine).astype(BF16)
            dn_ref[rows, :] = (
                mm_t(pq_ref[rows, :], qw_ref[...]) + mm_t(pkv_ref[rows, :], kvw_ref[...])
            ).astype(BF16)
            return carry

        lax.fori_loop(0, total // block, close_up, 0)

        for i in range(width // 512):
            cols = slice(i * 512, (i + 1) * 512)
            dqkv_ref[cols, :q_cols] = t_mm(n_ref[:, cols], pq_ref[...]).astype(BF16)
            dqkv_ref[cols, q_cols:] = t_mm(n_ref[:, cols], pkv_ref[...]).astype(BF16)
            dwo_ref[:, cols] = t_mm(a_ref[...], bg_ref[:, cols]).astype(BF16)

    return pl.pallas_call(
        kernel,
        out_shape=(
            jax.ShapeDtypeStruct((total, width), BF16),
            jax.ShapeDtypeStruct((width, q_cols + 2 * HEAD), BF16),
            jax.ShapeDtypeStruct((q_cols, width), BF16),
        ),
        in_specs=[VMEM] * 8 + [SMEM, VMEM],
        out_specs=[VMEM] * 3,
        scratch_shapes=[
            pltpu.VMEM((total, q_cols), BF16),
            pltpu.VMEM((total, q_cols), F32),
            pltpu.VMEM((total, HEAD), F32),
            pltpu.VMEM((total, HEAD), F32),
            pltpu.VMEM((total, q_cols), BF16),
            pltpu.VMEM((total, 2 * HEAD), BF16),
        ],
        compiler_params=pltpu.CompilerParams(vmem_limit_bytes=56 << 20),
        cost_estimate=pl.CostEstimate(flops=30_000_000_000, bytes_accessed=30 << 20, transcendentals=total * total),
        name="attention_backward",
    )(branch_grad, output_weight, attention, q, kv, normed, q_weight, kv_weight, lengths, freq)


def ffn_rows(nf, act_grad, wg, wu):
    gate, up = mm(nf, wg), mm(nf, wu)
    act_grad = act_grad.astype(F32)
    sigmoid = 1.0 / (1.0 + jnp.exp(-gate))
    silu = gate * sigmoid
    activated = (silu * up).astype(BF16)
    gate_grad = (act_grad * up * sigmoid * (1.0 + gate * (1.0 - sigmoid))).astype(BF16)
    return activated, gate_grad, (act_grad * silu).astype(BF16)


def ffn_own(group, nf, act_grads, wg, wu):
    groups, total, cols = act_grads.shape
    width = nf.shape[1]
    block = 256

    def kernel(g_ref, nf_ref, ag_ref, wg_ref, wu_ref, na_ref, act_ref, gg_ref, ug_ref, dn_ref):
        nf = nf_ref[...]
        act, gg, ug = ffn_rows(nf, ag_ref[0], wg_ref[...], wu_ref[...])
        na_ref[0], act_ref[0], gg_ref[0], ug_ref[0] = nf, act, gg, ug
        dn_ref[...] = (mm_t(gg, wg_ref[...]) + mm_t(ug, wu_ref[...])).astype(BF16)

    mine = pl.BlockSpec((1, block, width), lambda i, g: (g[0], i, 0))
    hid = pl.BlockSpec((1, block, cols), lambda i, g: (g[0], i, 0))
    plain = pl.BlockSpec((block, width), lambda i, g: (i, 0))
    whole = [
        pl.BlockSpec(w.shape, lambda i, g: (0, 0), pipeline_mode=pl.Buffered(1)) for w in (wg, wu)
    ]
    hidden = jax.ShapeDtypeStruct((groups, total, cols), BF16)
    return pl.pallas_call(
        kernel,
        grid_spec=pltpu.PrefetchScalarGridSpec(
            num_scalar_prefetch=1,
            grid=(total // block,),
            in_specs=[plain, hid] + whole,
            out_specs=[mine, hid, hid, hid, plain],
        ),
        out_shape=(
            jax.ShapeDtypeStruct((groups, total, width), BF16),
            hidden,
            hidden,
            hidden,
            jax.ShapeDtypeStruct((total, width), BF16),
        ),
        compiler_params=pltpu.CompilerParams(vmem_limit_bytes=62 << 20),
        cost_estimate=pl.CostEstimate(
            flops=12 * total * width * cols, bytes_accessed=40 << 20, transcendentals=total * cols
        ),
        name="ffn_own",
    )(group, nf, act_grads, wg, wu)


def ffn_other(where, held, fetched, act_grads, wg, wu, filled):
    groups, total, cols = act_grads.shape
    width = held.shape[1]
    block = 256
    per_half = total // 2 // block

    def kernel(w_ref, held_ref, fetched_ref, ag_ref, wg_ref, wu_ref, *rest):
        na_ref, act_ref, gg_ref, ug_ref, nf_ref = rest[4:]
        i = pl.program_id(0)

        @pl.when(i < per_half)
        def _():
            nf_ref[...] = held_ref[...]

        @pl.when(i >= per_half)
        def _():
            nf_ref[...] = fetched_ref[...]

        nf = nf_ref[...]
        act, gg, ug = ffn_rows(nf, ag_ref[0], wg_ref[...], wu_ref[...])
        na_ref[0], act_ref[0], gg_ref[0], ug_ref[0] = nf, act, gg, ug

    def row(i, w):
        half = jnp.where(i < per_half, w[1], 1 - w[1])
        return half * per_half + lax.rem(i, per_half)

    mine = pl.BlockSpec((1, block, width), lambda i, w: (w[0], row(i, w), 0))
    hid = pl.BlockSpec((1, block, cols), lambda i, w: (w[0], row(i, w), 0))
    first = pl.BlockSpec((block, width), lambda i, w: (jnp.minimum(i, per_half - 1), 0))
    last = pl.BlockSpec((block, width), lambda i, w: (jnp.maximum(i - per_half, 0), 0))
    whole = [
        pl.BlockSpec(w.shape, lambda i, g: (0, 0), pipeline_mode=pl.Buffered(1)) for w in (wg, wu)
    ]
    hidden = jax.ShapeDtypeStruct((groups, total, cols), BF16)
    return pl.pallas_call(
        kernel,
        grid_spec=pltpu.PrefetchScalarGridSpec(
            num_scalar_prefetch=1,
            grid=(2 * per_half,),
            in_specs=[first, last, hid] + whole + [pl.BlockSpec(memory_space=pl.ANY)] * 4,
            out_specs=[mine, hid, hid, hid],
            scratch_shapes=[pltpu.VMEM((block, width), BF16)],
        ),
        out_shape=(jax.ShapeDtypeStruct((groups, total, width), BF16), hidden, hidden, hidden),
        input_output_aliases={6: 0, 7: 1, 8: 2, 9: 3},
        compiler_params=pltpu.CompilerParams(vmem_limit_bytes=62 << 20),
        cost_estimate=pl.CostEstimate(
            flops=8 * total * width * cols, bytes_accessed=40 << 20, transcendentals=total * cols
        ),
        name="ffn_other",
    )(where, held, fetched, act_grads, wg, wu, *filled)


def finish(normed, gate_grad, up_grad, activated, down_grad, output_part, qkv_part, collective_id):
    depth, width = normed.shape
    cols = gate_grad.shape[1]
    rows = width // 8
    tall = cols // rows
    steps = 8 + tall
    chunks = 4
    sums = (output_part, qkv_part)

    def kernel(
        nf_hbm, gg_hbm, ug_hbm, act_hbm, dg_hbm, o_in, qkv_in,
        gate_out, up_out, down_out, o_out, qkv_out,
        gg, ug, dg, left, stage, tall_stage, o_mid, qkv_mid, o_last, qkv_last,
        load_sems, left_sems, own_sems, tall_sems, push_sems, relay_sems,
    ):
        me = lax.axis_index("shard")
        group = lax.axis_index("rep")
        inner = (group == 1) | (group == 2)
        outer = (group == 0) | (group == 3)
        beside = group + 1 - 2 * lax.rem(group, 2)
        across = 3 - group

        def peer_of(i):
            mask = 7 - i
            index = 0
            for weight in (1, 2, 4):
                bits = lax.rem(lax.div(me, weight), 2) + lax.rem(lax.div(mask, weight), 2)
                index = index + weight * lax.rem(bits, 2)
            return index

        def start_left(i, slot):
            @pl.when(i < 8)
            def _():
                first = pl.multiple_of(peer_of(i) * rows, rows)
                pltpu.make_async_copy(
                    nf_hbm.at[:, pl.ds(first, rows)], left.at[slot], left_sems.at[slot]
                ).start()

            @pl.when((i >= 8) & (i < steps))
            def _():
                first = pl.multiple_of((i - 8) * rows, rows)
                pltpu.make_async_copy(
                    act_hbm.at[:, pl.ds(first, rows)], left.at[slot], left_sems.at[slot]
                ).start()

        def wait_left(slot):
            pltpu.make_async_copy(
                nf_hbm.at[:, pl.ds(0, rows)], left.at[slot], left_sems.at[slot]
            ).wait()

        loads = [
            pltpu.make_async_copy(source, target, load_sems.at[k])
            for k, (source, target) in enumerate(((gg_hbm, gg), (ug_hbm, ug), (dg_hbm, dg)))
        ]
        start_left(0, 0)
        for load in loads:
            load.start()
        barrier = pltpu.get_barrier_semaphore()
        for mask in range(1, 8):
            pl.semaphore_signal(
                barrier, inc=1, device_id={"shard": flip(me, mask)}, device_id_type=MESH
            )
        for neighbour in (beside, across):
            pl.semaphore_signal(
                barrier, inc=1, device_id={"rep": neighbour}, device_id_type=MESH
            )
        pl.semaphore_wait(barrier, 9)

        arrays = ((o_in, o_mid, o_last, o_out), (qkv_in, qkv_mid, qkv_last, qkv_out))

        def relay_copy(stage_index, k, c, target):
            start, mid, last, out = arrays[k]
            size = start.shape[0] // chunks
            part = pl.ds(pl.multiple_of(c * size, size), size)
            source, arrived = ((start, mid), (mid, last), (out, out))[stage_index]
            return pltpu.make_async_remote_copy(
                src_ref=source.at[part],
                dst_ref=arrived.at[part],
                send_sem=relay_sems.at[0, stage_index, k * chunks + c],
                recv_sem=relay_sems.at[1, stage_index, k * chunks + c],
                device_id={"rep": target},
                device_id_type=MESH,
            )

        @pl.when(outer)
        def _():
            for c in range(chunks):
                for k in range(2):
                    relay_copy(0, k, c, beside).start()

        def relay(t):
            def part_of(k, c):
                size = arrays[k][0].shape[0] // chunks
                return pl.ds(pl.multiple_of(c * size, size), size)

            @pl.when(inner & (t < chunks))
            def _():
                for k in range(2):
                    start, mid, last, out = arrays[k]
                    part = part_of(k, t)
                    relay_copy(0, k, t, beside).wait_recv()
                    mid[part, :] = (start[part, :].astype(F32) + mid[part, :].astype(F32)).astype(BF16)
                    relay_copy(1, k, t, across).start()

            @pl.when(inner & (t >= 1) & (t <= chunks))
            def _():
                for k in range(2):
                    start, mid, last, out = arrays[k]
                    part = part_of(k, t - 1)
                    relay_copy(1, k, t - 1, across).wait_recv()
                    out[part, :] = (mid[part, :].astype(F32) + last[part, :].astype(F32)).astype(BF16)
                    relay_copy(2, k, t - 1, beside).start()

            @pl.when(outer & (t >= 2) & (t <= chunks + 1))
            def _():
                for k in range(2):
                    relay_copy(2, k, t - 2, beside).wait_recv()

        outputs = (gate_out, up_out)
        own_columns = pl.ds(pl.multiple_of(me * cols, cols), cols)

        def push(i, j, target):
            return send(
                stage.at[i, j], outputs[j].at[:, own_columns], push_sems, 2 * i + j, target
            )

        def wide(i, carry):
            slot = lax.rem(i, 2)
            start_left(i + 1, 1 - slot)
            wait_left(slot)
            for j, right in enumerate((gg, ug)):

                @pl.when(i == 0)
                def _():
                    loads[j].wait()

                stage[i, j] = t_mm(left[slot], right[...]).astype(BF16)

                @pl.when(i < 7)
                def _():
                    push(i, j, peer_of(i)).start()

                @pl.when(i == 7)
                def _():
                    pltpu.make_async_copy(
                        stage.at[7, j], outputs[j].at[:, own_columns], own_sems.at[j]
                    ).start()

            @pl.when(lax.rem(i, 2) == 1)
            def _():
                relay(lax.div(i, 2))

            return carry

        lax.fori_loop(0, 8, wide, 0)
        loads[2].wait()

        def tall_copy(i):
            slot = lax.rem(i, 2)
            first = pl.multiple_of((i - 8) * rows, rows)
            return pltpu.make_async_copy(
                tall_stage.at[slot], down_out.at[pl.ds(first, rows), :], tall_sems.at[slot]
            )

        def high(i, carry):
            slot = lax.rem(i, 2)
            start_left(i + 1, 1 - slot)
            wait_left(slot)

            @pl.when(i >= 10)
            def _():
                tall_copy(i - 2).wait()

            tall_stage[slot] = t_mm(left[slot], dg[...]).astype(BF16)
            tall_copy(i).start()

            @pl.when(lax.rem(i, 2) == 1)
            def _():
                relay(lax.div(i, 2))

            return carry

        lax.fori_loop(8, steps, high, 0)
        for i in (steps - 2, steps - 1):
            tall_copy(i).wait()
        for j in range(2):
            pltpu.make_async_copy(
                stage.at[7, j], outputs[j].at[:, own_columns], own_sems.at[j]
            ).wait()
        for t in range(steps // 2, chunks + 2):
            relay(t)

        def drain(i, carry):
            for j in range(2):
                push(i, j, peer_of(i)).wait()
            return carry

        lax.fori_loop(0, 7, drain, 0)

        @pl.when(outer)
        def _():
            for c in range(chunks):
                for k in range(2):
                    relay_copy(0, k, c, beside).wait_send()

        @pl.when(inner)
        def _():
            for c in range(chunks):
                for k in range(2):
                    relay_copy(1, k, c, across).wait_send()
                    relay_copy(2, k, c, beside).wait_send()

    exchanged = jax.ShapeDtypeStruct((rows, 8 * cols), BF16)
    return pl.pallas_call(
        kernel,
        out_shape=(
            exchanged,
            exchanged,
            jax.ShapeDtypeStruct((cols, width), BF16),
            jax.ShapeDtypeStruct(output_part.shape, BF16),
            jax.ShapeDtypeStruct(qkv_part.shape, BF16),
        ),
        in_specs=[ANY] * 5 + [VMEM] * 2,
        out_specs=[ANY] * 3 + [VMEM] * 2,
        scratch_shapes=[
            pltpu.VMEM((depth, cols), BF16),
            pltpu.VMEM((depth, cols), BF16),
            pltpu.VMEM((depth, width), BF16),
            pltpu.VMEM((2, depth, rows), BF16),
            pltpu.VMEM((8, 2, rows, cols), BF16),
            pltpu.VMEM((2, rows, width), BF16),
        ]
        + [pltpu.VMEM(x.shape, BF16) for unused in range(2) for x in sums]
        + [
            pltpu.SemaphoreType.DMA((3,)),
            pltpu.SemaphoreType.DMA((2,)),
            pltpu.SemaphoreType.DMA((2,)),
            pltpu.SemaphoreType.DMA((2,)),
            pltpu.SemaphoreType.DMA((2, 14)),
            pltpu.SemaphoreType.DMA((2, 3, 2 * chunks)),
        ],
        compiler_params=comm_params(collective_id, 62),
        cost_estimate=pl.CostEstimate(
            flops=120_000_000_000, bytes_accessed=80 << 20, transcendentals=0
        ),
        name="finish",
    )(normed, gate_grad, up_grad, activated, down_grad, output_part, qkv_part)


def widen(gate, up, down, out, heads, q_cols):
    rows, wide = gate.shape
    tall, width = down.shape
    n = heads.shape[0]
    steps = 16
    block, high = rows // steps, tall // steps

    def kernel(g_ref, u_ref, d_ref, o_ref, h_ref, g_out, u_out, d_out, o_out, q_out, k_out, v_out):
        g_out[...] = g_ref[...].astype(F32)
        u_out[...] = u_ref[...].astype(F32)
        d_out[...] = d_ref[...].astype(F32)
        o_out[...] = o_ref[...].astype(F32)
        for i in range(n):
            q_out[:, i * q_cols : (i + 1) * q_cols] = h_ref[i, :, :q_cols].astype(F32)
        kv = [h_ref[i, :, q_cols:].astype(F32) for i in range(n)]
        k_out[...] = jnp.concatenate([x[:, :HEAD] for x in kv], axis=1)
        v_out[...] = jnp.concatenate([x[:, HEAD:] for x in kv], axis=1)

    def spec(height, across):
        return pl.BlockSpec((height, across), lambda i: (i, 0))

    shapes = [(rows, wide), (rows, wide), (tall, width), (rows, width)]
    blocks = [spec(block, wide), spec(block, wide), spec(high, width), spec(block, width)]
    narrow = [n * q_cols, n * HEAD, n * HEAD]
    return pl.pallas_call(
        kernel,
        grid=(steps,),
        in_specs=blocks + [pl.BlockSpec((n, block, heads.shape[2]), lambda i: (0, i, 0))],
        out_specs=blocks + [spec(block, across) for across in narrow],
        out_shape=[jax.ShapeDtypeStruct(shape, F32) for shape in shapes]
        + [jax.ShapeDtypeStruct((rows, across), F32) for across in narrow],
        compiler_params=pltpu.CompilerParams(vmem_limit_bytes=62 << 20),
        cost_estimate=pl.CostEstimate(
            flops=4 * rows * wide, bytes_accessed=20 * rows * wide, transcendentals=0
        ),
        name="widen",
    )(gate, up, down, out, heads)


def per_device_plane(
    tokens, attn_gain, query_weight, key_weight, value_weight, output_weight, ffn_gain,
    gate_weight, up_weight, down_weight, dealing, lengths, cotangent,
):
    n = 8
    here = lax.axis_index("shard")
    group = lax.axis_index("rep")
    replicas = lax.axis_size("rep")
    local, width = tokens.shape
    total = local * n
    rows = query_weight.shape[0]
    q_cols = query_weight.shape[1] // n
    ff_cols = gate_weight.shape[1] // n
    core = lax.rem(here, 2)
    half = HEAD // 2
    freq = ROPE_BASE ** (-(jnp.arange(half, dtype=F32) * 2.0) / (2.0 * half))
    freq = jnp.tile(freq, 4)[None, :]

    (
        normed, q, kv, attention, q_weight, kv_weight, gate_cols, up_cols,
        middle, normed_ffn, down_grads, act_grads, cot_own, held,
    ) = front(
        tokens, attn_gain, query_weight, key_weight, value_weight, output_weight, ffn_gain,
        gate_weight, up_weight, down_weight, dealing, lengths, cotangent, freq, replicas,
    )

    def shift(x, by):
        return lax.ppermute(x, "rep", [(i, (i + by) % replicas) for i in range(replicas)])

    def fetch(x):
        return lax.ppermute(x, "shard", [(i, i ^ 1) for i in range(n)])

    before, after = shift(held, 1), shift(held, replicas - 1)
    *filled, normed_ffn_part = ffn_own(
        group.astype(jnp.int32)[None], normed_ffn, act_grads, gate_cols, up_cols
    )
    middle_grad, ffn_gain_part, branch_grad, output_part = pull_gather(
        normed_ffn_part, middle, ffn_gain, cot_own, filled[1], down_weight, dealing.reshape(total, 1), 2
    )
    normed_part, qkv_grad, output_grad = attention_backward(
        branch_grad.reshape(total, width), output_weight, attention, q, kv, normed, q_weight, kv_weight,
        lengths, freq,
    )
    before, after, unused_part = lax.optimization_barrier((before, after, normed_part))
    opposite = shift(before, 1)
    qkv_part = exchange(qkv_grad.reshape(n, rows, q_cols + 2 * HEAD))
    tokens_grad, layer_output, gains, *filled, unused_half = pull_tokens(
        normed_part, output_part, tokens, attn_gain, middle_grad, ffn_gain_part,
        (before, after), act_grads, gate_cols, up_cols, filled, replicas, 3,
    )
    opposite, unused_rows = lax.optimization_barrier((opposite, tokens_grad))
    where = jnp.stack([lax.rem(group + replicas - 2, replicas), core]).astype(jnp.int32)
    filled = ffn_other(where, opposite, fetch(opposite), act_grads, gate_cols, up_cols, filled)
    left, *rights = [x.reshape(replicas * total, -1) for x in (filled[0], filled[2], filled[3])]
    gate_grad, up_grad, down_grad, output_grad, qkv_grad = finish(
        left, *rights, filled[1].reshape(replicas * total, -1), down_grads.reshape(replicas * total, -1),
        output_grad, qkv_part.reshape(width, -1), 4,
    )
    gate_grad, up_grad, down_grad, output_grad, q_grad, k_grad, v_grad = widen(
        gate_grad, up_grad, down_grad, output_grad, qkv_grad.reshape(n, rows, -1), q_cols
    )
    return (
        layer_output, tokens_grad, gains[0], q_grad, k_grad, v_grad, output_grad, gains[1],
        gate_grad, up_grad, down_grad,
    )


def per_device(
    tokens,
    attn_gain,
    query_weight,
    key_weight,
    value_weight,
    output_weight,
    ffn_gain,
    gate_weight,
    up_weight,
    down_weight,
    dealing,
    lengths,
    cotangent,
):
    n = lax.axis_size("shard")
    here = lax.axis_index("shard")
    local, width = tokens.shape
    total = local * n
    rows = query_weight.shape[0]
    ff_cols = gate_weight.shape[1] // n
    q_cols = query_weight.shape[1] // n
    copies = n // KV_HEADS
    own = here * local

    packed = jnp.arange(total, dtype=jnp.int32)
    segment, position = places(packed, lengths[0])
    cos_q, sin_q = rope_tables(position, q_cols)
    cos_k, sin_k = cos_q[:, :HEAD], sin_q[:, :HEAD]
    dealt = (dealing[0][:, None] == packed[None, :]).astype(BF16)

    def column_blocks(weight, cols):
        return weight.reshape(rows, n, cols).transpose(1, 0, 2)

    def head_blocks(weight):
        blocks = weight.reshape(rows, KV_HEADS, HEAD).transpose(1, 0, 2)
        return jnp.repeat(blocks, copies, axis=0)

    spread_cotangent = lax.all_gather(cotangent, ("rep", "shard"), axis=0, tiled=True)
    all_dealing = lax.all_gather(dealing, "rep", axis=0, tiled=True)
    qkv = exchange(
        jnp.concatenate(
            [column_blocks(query_weight, q_cols), head_blocks(key_weight), head_blocks(value_weight)],
            axis=2,
        )
    ).reshape(width, q_cols + 2 * HEAD)
    gate_cols = exchange(column_blocks(gate_weight, ff_cols)).reshape(width, ff_cols)
    up_cols = exchange(column_blocks(up_weight, ff_cols)).reshape(width, ff_cols)

    normed = gather_rows(rms_scale(tokens.astype(F32), attn_gain).astype(BF16))
    pre = mm(normed, qkv)
    queries = rotate(pre[:, :q_cols], cos_q, sin_q).astype(BF16)
    keys = rotate(pre[:, q_cols : q_cols + HEAD], cos_k, sin_k).astype(BF16)
    values = pre[:, q_cols + HEAD :].astype(BF16)
    attention = attention_forward(queries, jnp.concatenate([keys, values], axis=1), lengths)
    branch = scatter_rows(mm(attention, output_weight).astype(BF16))
    middle = tokens.astype(F32) + RESIDUAL_SCALE * branch.astype(F32)
    normed_ffn = gather_rows(rms_scale(middle, ffn_gain).astype(BF16))
    own_normed = lax.dynamic_slice_in_dim(normed_ffn, own, local)
    all_normed = lax.all_gather(own_normed, ("rep", "shard"), axis=0, tiled=True)

    reps = lax.axis_size("rep")
    group = lax.axis_index("rep")
    deals = (all_dealing[:, :, None] == packed[None, None, :]).astype(BF16)
    out_grad_all = lax.dot_general(
        deals,
        spread_cotangent.reshape(reps, total, width),
        (((1,), (1,)), ((0,), (0,))),
        preferred_element_type=F32,
    ).reshape(reps * total, width)
    down_grad_all = (RESIDUAL_SCALE * out_grad_all).astype(BF16)
    out_grad = lax.dynamic_slice_in_dim(out_grad_all, group * total + own, local)
    act_grad_all = mm_t(down_grad_all, down_weight)

    def ffn(rows_in, act_grad):
        gate = mm(rows_in, gate_cols)
        up = mm(rows_in, up_cols)
        sigmoid = jax.nn.sigmoid(gate)
        activated = (gate * sigmoid * up).astype(BF16)
        gate_grad = (act_grad * up * sigmoid * (1.0 + gate * (1.0 - sigmoid))).astype(BF16)
        up_grad = (act_grad * gate * sigmoid).astype(BF16)
        return activated, gate_grad, up_grad

    activated, gate_grad, up_grad = ffn(
        normed_ffn, lax.dynamic_slice_in_dim(act_grad_all, group * total, total)
    )
    normed_ffn_part = (mm_t(gate_grad, gate_cols) + mm_t(up_grad, up_cols)).astype(BF16)
    middle_part, ffn_gain_part = norm_pull(
        middle, ffn_gain, scatter_rows(normed_ffn_part).astype(F32)
    )
    middle_grad = out_grad + middle_part
    branch_grad = gather_rows((RESIDUAL_SCALE * middle_grad).astype(BF16))

    own_columns = lax.dynamic_slice_in_dim(dealt, own, local, axis=1)
    layer_output = scatter_rows(
        (
            RESIDUAL_SCALE * mm(mm(dealt, activated).astype(BF16), down_weight)
            + mm(own_columns, middle.astype(BF16))
        ).astype(BF16)
    )

    attention_grad = mm_t(branch_grad, output_weight).astype(BF16)
    dq, dk, dv = attention_gradients(
        queries, jnp.concatenate([keys, values], axis=1), attention_grad, lengths
    )
    pre_grad = jnp.concatenate(
        [
            unrotate(dq, cos_q, sin_q).astype(BF16),
            unrotate(dk, cos_k, sin_k).astype(BF16),
            dv.astype(BF16),
        ],
        axis=1,
    )
    normed_part = mm_t(pre_grad, qkv).astype(BF16)
    hidden_part, attn_gain_part = norm_pull(
        tokens.astype(F32), attn_gain, scatter_rows(normed_part).astype(F32)
    )
    tokens_grad = middle_grad + hidden_part

    activated, gate_grad, up_grad = ffn(all_normed, act_grad_all)
    gate_part = exchange(t_mm(all_normed, gate_grad).astype(BF16).reshape(n, rows, ff_cols))
    up_part = exchange(t_mm(all_normed, up_grad).astype(BF16).reshape(n, rows, ff_cols))
    down_part = t_mm(activated, down_grad_all)
    output_part = rep_sum(t_mm(attention, branch_grad).astype(BF16))
    qkv_part = rep_sum(exchange(t_mm(normed, pre_grad).astype(BF16).reshape(n, rows, q_cols + 2 * HEAD)))

    def join(blocks):
        return blocks.transpose(1, 0, 2).reshape(rows, -1).astype(F32)

    def join_heads(blocks):
        blocks = blocks.astype(F32).reshape(KV_HEADS, copies, rows, HEAD).sum(axis=1)
        return blocks.transpose(1, 0, 2).reshape(rows, KV_HEADS * HEAD)

    gain_grads = lax.psum(jnp.concatenate([attn_gain_part, ffn_gain_part]), ("rep", "shard"))
    return (
        layer_output,
        tokens_grad,
        gain_grads[0],
        join(qkv_part[:, :, :q_cols]),
        join_heads(qkv_part[:, :, q_cols : q_cols + HEAD]),
        join_heads(qkv_part[:, :, q_cols + HEAD :]),
        output_part.astype(F32),
        gain_grads[1],
        join(gate_part),
        join(up_part),
        down_part,
    )


def solution(mesh):
    both = P(("rep", "shard"), None)
    rowed = P("shard", None)
    return jax.shard_map(
        per_device_plane if (mesh.shape["rep"], mesh.shape["shard"]) == (4, 8) else per_device,
        mesh=mesh,
        in_specs=(
            both, P(), rowed, rowed, rowed, rowed, P(), rowed, rowed, rowed,
            P("rep", None), P("rep", None), both,
        ),
        out_specs=(both, both, P(), rowed, rowed, rowed, rowed, P(), rowed, rowed, rowed),
        check_vma=False,
    )
```
